32 devices in a mesh: dp: 8 (over z, x), fsdp: 4 (over y, core).
Axes of the slice: x: 2, y: 2, z: 4, core: 2. Of those that a mesh axis runs over, the one named last changes fastest.
Arguments:
- tokens: bfloat16 [32768, 768], P(('dp', 'fsdp')), may hold values from -6 to 6
- counts: int32 [32], P(('dp', 'fsdp')), may hold values from 512 to 1024, as said below
- cotangent: bfloat16 [32768, 768], P(('dp', 'fsdp')), may hold values from -6 to 6
- qkv_weight: float32 [768, 2304], P('dp', 'fsdp'), may hold values from -0.21875 to 0.21875
- out_weight: float32 [768, 768], P('dp', 'fsdp'), may hold values from -1.75 to 1.75
- up_weight: float32 [768, 3072], P('dp', 'fsdp'), may hold values from -0.21875 to 0.21875
- down_weight: float32 [3072, 768], P('dp', 'fsdp'), may hold values from -0.109375 to 0.109375
- small_params: float32 [9216], replicated
- statistics: float32 [32, 2, 768, 768], P(('dp', 'fsdp')), as said below
- inverse_roots: float32 [32, 2, 768, 768], P(('dp', 'fsdp')), as said below
- owners: int32 [12], replicated, may hold values from 0 to 31, as said below
Outputs:
- layer_out: bfloat16 [32768, 768], P(('dp', 'fsdp'))
- input_grad: bfloat16 [32768, 768], P(('dp', 'fsdp'))
- grad_qkv: float32 [768, 2304], P('dp', 'fsdp')
- grad_out: float32 [768, 768], P('dp', 'fsdp')
- grad_up: float32 [768, 3072], P('dp', 'fsdp')
- grad_down: float32 [3072, 768], P('dp', 'fsdp')
- grad_small: float32 [9216], replicated
- new_statistics: float32 [32, 2, 768, 768], P(('dp', 'fsdp'))
- new_qkv: float32 [768, 2304], P('dp', 'fsdp')
- new_out: float32 [768, 768], P('dp', 'fsdp')
- new_up: float32 [768, 3072], P('dp', 'fsdp')
- new_down: float32 [3072, 768], P('dp', 'fsdp')
- new_small: float32 [9216], replicated
The draws below stay inside these ranges and needn't reach their ends.
Inputs may be any that keep to these rules, and one draw needn't show every extreme that they name: `counts`: true patch count of each clip; 1024 is reached by one clip and 512 by another. `owners`: distinct device ranks, rank = dp index * 4 + fsdp index. `statistics`: each slot's two matrices are symmetric. `inverse_roots`: each slot's two matrices are symmetric.
All inputs are finite; a program needn't handle non-finite values.
Results may differ from the reference program's by a relative error of at most 0.017.
Values may be sent and summed in bfloat16 or wider, within the bound.
A program may use at most 320 MiB of HBM per device.

```python
import math
import jax
import jax.numpy as jnp
from jax import lax

D = 768
HEADS = 12
HD = 64
FF = 3072
SLOTS = 1024
CLIPS = 32
TOKENS = 32768
BLOCKS = 12
N_DP = 8
N_FSDP = 4


def draw_counts(key, part):
    first, second, third = jax.random.split(key, 3)
    lengths = jax.random.randint(first, (CLIPS,), SLOTS // 2, SLOTS + 1)
    longest = jax.random.randint(second, (), 0, CLIPS)
    shortest = (longest + 1 + jax.random.randint(third, (), 0, CLIPS - 1)) % CLIPS
    return lengths.at[longest].set(SLOTS).at[shortest].set(SLOTS // 2).astype(jnp.int32)


def draw_owners(key, part):
    first, second = jax.random.split(key)
    devices = N_DP * N_FSDP
    inner = jax.random.permutation(first, devices - 2)[:BLOCKS - 2] + 1
    picked = jnp.concatenate([jnp.array([0, devices - 1], jnp.int32), inner.astype(jnp.int32)])
    return picked[jax.random.permutation(second, BLOCKS)].astype(jnp.int32)


def draw_small_params(key, part):
    offsets = jnp.concatenate([jnp.ones((D,), jnp.float32), jnp.zeros((D,), jnp.float32), jnp.ones((D,), jnp.float32), jnp.zeros((5 * D + FF,), jnp.float32)])
    noise = 0.2 * jax.random.normal(key, (8 * D + FF,), jnp.float32)
    return offsets + noise


def symmetric_draw(key, base, floor_value, ceil_value):
    first, second = jax.random.split(key)
    devices = N_DP * N_FSDP
    diagonal = jax.random.uniform(first, (devices, 2, D), jnp.float32, floor_value, ceil_value)
    noise = jax.random.normal(second, (devices, 2, D, D), jnp.float32)
    paired = (noise + jnp.swapaxes(noise, -1, -2)) * (0.3 / math.sqrt(2.0 * D))
    rooted = jnp.sqrt(diagonal)
    identity = jnp.eye(D, dtype=jnp.float32)
    return base * (identity * diagonal[..., None, :] + (1.0 - identity) * paired * rooted[..., :, None] * rooted[..., None, :])


def draw_statistics(key, part):
    return symmetric_draw(jax.random.fold_in(key, 11), D * TOKENS * 12.0, 1.0, 4.0)


def draw_inverse_roots(key, part):
    return symmetric_draw(jax.random.fold_in(key, 23), (D * TOKENS / 5.0) ** (-0.25), 0.7, 1.4)


def block_levels(rng, extent, cuts, least, largest):
    def one(axis_at, blocks):
        steps = jax.random.uniform(jax.random.fold_in(jax.random.fold_in(rng, 6), axis_at), (blocks,), jnp.float32, least / len(cuts), largest / len(cuts))
        return jnp.repeat(jnp.exp(steps), extent[axis_at] // blocks).reshape((-1,) + (1,) * (len(extent) - axis_at - 1))

    gain = one(*cuts[0])
    for cut in cuts[1:]:
        gain = gain * one(*cut)
    return gain


def bell_draw(key, extent, width, reach, shards=(), kind=jnp.bfloat16):
    values = width * jax.random.normal(key, extent, jnp.float32)
    if shards:
        values = values * block_levels(key, extent, shards, -0.22, 0.18)
    return jnp.clip(values, -reach, reach).astype(kind)


def setup_inputs(seed: int = 0) -> dict:
    keys = jax.random.split(jax.random.key(seed), 12)
    tokens = bell_draw(keys[0], (TOKENS, D), 1.0, 6.0, ((0, 32),))
    counts = draw_counts(jax.random.fold_in(keys[11], 71), 0)
    cotangent = bell_draw(keys[2], (TOKENS, D), 1.0, 6.0, ((0, 32),))
    qkv_weight = bell_draw(keys[3], (D, 3 * D), D ** -0.5, 0.21875, ((0, 8), (1, 4)), jnp.float32)
    out_weight = bell_draw(keys[4], (D, D), (D * 16 // SLOTS) ** -0.5, 1.75, ((0, 8), (1, 4)), jnp.float32)
    up_weight = bell_draw(keys[5], (D, FF), D ** -0.5, 0.21875, ((0, 8), (1, 4)), jnp.float32)
    down_weight = bell_draw(keys[6], (FF, D), FF ** -0.5, 0.109375, ((0, 8), (1, 4)), jnp.float32)
    small_params = draw_small_params(jax.random.fold_in(keys[11], 71), 0)
    statistics = draw_statistics(jax.random.fold_in(keys[11], 71), 0)
    inverse_roots = draw_inverse_roots(jax.random.fold_in(keys[11], 71), 0)
    owners = draw_owners(jax.random.fold_in(keys[11], 71), 0)
    return dict(tokens=tokens, counts=counts, cotangent=cotangent, qkv_weight=qkv_weight, out_weight=out_weight, up_weight=up_weight, down_weight=down_weight, small_params=small_params, statistics=statistics, inverse_roots=inverse_roots, owners=owners)


@jax.custom_vjp
def low(v):
    return lax.optimization_barrier(v.astype(jnp.bfloat16)).astype(jnp.float32)

@jax.custom_vjp
def low_back(v):
    return v

def low_keep(v):
    return (low(v), None)

def low_pass(kept, grad):
    return (grad,)

def back_keep(v):
    return (v, None)

def back_low(kept, grad):
    return (low(grad),)
low.defvjp(low_keep, low_pass)
low_back.defvjp(back_keep, back_low)
masked_score = -1000000000.0
decay_rate = 0.5
step_rate = 1.0
small_rate = 0.3
highest = lax.Precision.HIGHEST

def product(left, right):
    return jnp.dot(left, right, precision=highest, preferred_element_type=jnp.float32)

def layer_norm(values, scale_row, shift_row):
    center = values - lax.optimization_barrier(jnp.mean(values, axis=-1, keepdims=True))
    spread = lax.optimization_barrier(jnp.mean(center * center, axis=-1, keepdims=True))
    return center * lax.rsqrt(spread + 1e-06) * scale_row + shift_row

def unpack(small_params):
    pieces = [small_params[number * D:(number + 1) * D] for number in range(8)]
    return pieces + [small_params[8 * D:8 * D + FF]]

def clip_forward(clip_tokens, length, weights, small_params):
    qkv_low, out_low, up_low, down_low = weights
    gain_one, shift_one, gain_two, shift_two, bias_query, bias_value, bias_out, bias_down, bias_up = unpack(small_params)
    normed = low(layer_norm(clip_tokens, gain_one, shift_one))
    projected = product(normed, qkv_low)
    queries = low_back(low(projected[:, :D] + bias_query)).reshape(SLOTS, HEADS, HD)
    key_rows = low_back(low(projected[:, D:2 * D])).reshape(SLOTS, HEADS, HD)
    value_rows = low_back(low(projected[:, 2 * D:] + bias_value)).reshape(SLOTS, HEADS, HD)
    scores = jnp.einsum('qhd,khd->hqk', queries, key_rows, precision=highest) * float(HD) ** (-0.5)
    scores = low_back(scores)
    visible = (jnp.arange(SLOTS) < length)[None, None, :]
    scores = jnp.where(visible, scores, masked_score)
    row_top = lax.optimization_barrier(jnp.max(scores, axis=-1, keepdims=True))
    raised = jnp.exp(scores - row_top)
    softmax_weights = raised / lax.optimization_barrier(jnp.sum(raised, axis=-1, keepdims=True))
    attended = jnp.einsum('hqk,khd->qhd', low(softmax_weights), value_rows, precision=highest).reshape(SLOTS, D)
    attended = low_back(low(attended))
    branch = low_back(product(attended, out_low) + bias_out)
    middle = clip_tokens + branch
    normed_two = low(layer_norm(middle, gain_two, shift_two))
    hidden = low_back(product(normed_two, up_low) + bias_up)
    active = low(jax.nn.gelu(hidden, approximate=False))
    return middle + product(active, down_low) + bias_down

def reference(tokens, counts, cotangent, qkv_weight, out_weight, up_weight, down_weight, small_params, statistics, inverse_roots, owners):
    inputs = tokens.astype(jnp.float32).reshape(CLIPS, SLOTS, D)
    back_rows = cotangent.astype(jnp.float32).reshape(CLIPS, SLOTS, D)

    def whole_layer(inputs, qkv_master, out_master, up_master, down_master, small_values):
        weights = (low(qkv_master), low(out_master), low(up_master), low(down_master))

        def one_clip(clip_pair):
            return jax.checkpoint(clip_forward)(clip_pair[0], clip_pair[1], weights, small_values)
        return lax.map(one_clip, (inputs, counts))
    layer_rows, pullback = jax.vjp(whole_layer, inputs, qkv_weight, out_weight, up_weight, down_weight, small_params)
    input_rows, grad_qkv, grad_out, grad_up, grad_down, grad_small = pullback(back_rows)
    blocks = [grad_qkv[:, column * D:(column + 1) * D] for column in range(3)]
    blocks = blocks + [grad_out]
    blocks = blocks + [grad_up[:, column * D:(column + 1) * D] for column in range(FF // D)]
    blocks = blocks + [grad_down[column * D:(column + 1) * D, :] for column in range(FF // D)]
    new_statistics = statistics
    updates = []
    for number in range(BLOCKS):
        gradient = blocks[number]
        owner_rank = owners[number]
        left_stat = decay_rate * statistics[owner_rank, 0] + (1.0 - decay_rate) * product(gradient, gradient.T)
        right_stat = decay_rate * statistics[owner_rank, 1] + (1.0 - decay_rate) * product(gradient.T, gradient)
        new_statistics = new_statistics.at[owner_rank].set(jnp.stack([left_stat, right_stat]))
        updates.append(product(product(inverse_roots[owner_rank, 0], gradient), inverse_roots[owner_rank, 1]))
    new_qkv = qkv_weight - step_rate * jnp.concatenate(updates[0:3], axis=1)
    new_out = out_weight - step_rate * updates[3]
    new_up = up_weight - step_rate * jnp.concatenate(updates[4:4 + FF // D], axis=1)
    new_down = down_weight - step_rate * jnp.concatenate(updates[4 + FF // D:], axis=0)
    new_small = small_params - small_rate * grad_small * lax.rsqrt(jnp.mean(grad_small * grad_small) + 1e-06)
    return (layer_rows.reshape(TOKENS, D).astype(jnp.bfloat16), input_rows.reshape(TOKENS, D).astype(jnp.bfloat16), grad_qkv, grad_out, grad_up, grad_down, grad_small, new_statistics, new_qkv, new_out, new_up, new_down, new_small)
```

```python
from functools import partial

import jax
import jax.numpy as jnp
from jax import lax
from jax.experimental import pallas as pl
from jax.experimental.pallas import tpu as pltpu
from jax.sharding import PartitionSpec as P

MESH = pl.DeviceIdType.MESH
ANY = pl.BlockSpec(memory_space=pl.ANY)
VM = pl.BlockSpec(memory_space=pltpu.VMEM)


class Grid:
    def __init__(self, n_dp, n_fsdp):
        self.Z = 4
        self.X = n_dp // 4
        self.Y = n_fsdp // 2
        self.swap = self.X == self.Y
        self.A, self.B = self.X, self.Y

    def here(self):
        dp, fs = lax.axis_index("dp"), lax.axis_index("fsdp")
        self.z, self.x = dp // self.X, dp % self.X
        self.y, self.c = fs // 2, fs % 2
        if self.swap:
            self.a = self.x + self.c * (self.y - self.x)
            self.b = self.y + self.c * (self.x - self.y)
        else:
            self.a, self.b = self.x, self.y
        return self

    def xy(self, a, b, c):
        if self.swap:
            return a + c * (b - a), b + c * (a - b)
        return a, b

    def device(self, z, a, b, c, frame=None):
        x, y = self.xy(a, b, self.c if frame is None else frame)
        return {"dp": z * self.X + x, "fsdp": y * 2 + c}

    def shape(self, order, r, w):
        if order == "j":
            return (self.Y, 2, self.Z, self.X, r, w)
        return (self.Z, self.X, self.Y, 2, r, w)

    def at(self, ref, order, y, c, z, x):
        return ref.at[y, c, z, x] if order == "j" else ref.at[z, x, y, c]

    def peers(self):
        out = [self.device((self.z + k) % self.Z, self.a, self.b, self.c) for k in range(1, self.Z)]
        out += [self.device(self.z, (self.a + k) % self.A, self.b, self.c) for k in range(1, self.A)]
        out += [self.device(self.z, self.a, (self.b + k) % self.B, self.c) for k in range(1, self.B)]
        out += [{"dp": self.z * self.X + self.x, "fsdp": self.y * 2 + 1 - self.c}]
        return out

    def barrier(self):
        sem = pltpu.get_barrier_semaphore()
        peers = self.peers()
        for peer in peers:
            pl.semaphore_signal(sem, inc=1, device_id=peer, device_id_type=MESH)
        pl.semaphore_wait(sem, len(peers))


class Gather:
    def __init__(self, grid, order, src, out, local, send, recv):
        g = self.g = grid
        self.order, self.src, self.out = order, src, out
        self.local, self.send, self.recv = local, send, recv
        self.copies = {}

    @staticmethod
    def slots(g):
        return (g.Z - 1) + 2 * (g.A - 1) + 2 * (g.B - 1) * g.A + 1

    def _copy(self, stage, slot, src, dst, device):
        cp = pltpu.make_async_remote_copy(
            src_ref=src, dst_ref=dst, send_sem=self.send.at[slot], recv_sem=self.recv.at[slot],
            device_id=device, device_id_type=MESH)
        cp.start()
        self.copies.setdefault(stage, []).append(cp)

    def _piece(self, a, b, c, z=slice(None)):
        x, y = self.g.xy(a, b, self.g.c)
        return self.g.at(self.out, self.order, y, c, z, x)

    def start(self):
        g = self.g
        self.own = pltpu.make_async_copy(self.src, self._piece(g.a, g.b, g.c, g.z), self.local)
        self.own.start()
        for k in range(1, g.Z):
            self._copy("z", k - 1, self.src, self._piece(g.a, g.b, g.c, g.z),
                       g.device((g.z + k) % g.Z, g.a, g.b, g.c))

    def _sibling(self, stage, slot, a, b):
        g = self.g
        ref = self._piece(a, b, g.c)
        self._copy(stage, slot, ref, ref, {"dp": g.z * g.X + g.x, "fsdp": g.y * 2 + 1 - g.c})

    def after_z(self):
        g = self.g
        self.own.wait()
        for cp in self.copies["z"]:
            cp.wait_recv()
        base = g.Z - 1
        ref = self._piece(g.a, g.b, g.c)
        for k in range(1, g.A):
            self._copy("a", base + k - 1, ref, ref, g.device(g.z, (g.a + k) % g.A, g.b, g.c))
        self._sibling("d", base + g.A - 1, g.a, g.b)

    def after_a(self):
        g = self.g
        for cp in self.copies["a"]:
            cp.wait_recv()
        base = g.Z - 1 + g.A
        for a in range(g.A):
            ref = self._piece(a, g.b, g.c)
            for k in range(1, g.B):
                self._copy("b", base + a * (g.B - 1) + k - 1, ref, ref,
                           g.device(g.z, a * 0 + g.a, (g.b + k) % g.B, g.c))
        base += g.A * (g.B - 1)
        for k in range(1, g.A):
            self._sibling("d", base + k - 1, (g.a - k + g.A) % g.A, g.b)

    def after_b(self):
        g = self.g
        for cp in self.copies["b"]:
            cp.wait_recv()
        base = g.Z - 1 + g.A + g.A * (g.B - 1) + g.A - 1
        for a in range(g.A):
            for k in range(1, g.B):
                self._sibling("d", base + a * (g.B - 1) + k - 1, a, (g.b - k + g.B) % g.B)

    def arrive(self):
        for cp in self.copies["d"]:
            cp.wait_recv()

    def finish(self):
        for group in self.copies.values():
            for cp in group:
                cp.wait_send()


class Scatter:
    def __init__(self, grid, order, src, work, recv_b, recv_a, recv_z, mine, local, send, recv):
        self.g, self.order, self.src = grid, order, src
        self.work, self.recv_b, self.recv_a, self.recv_z, self.mine = work, recv_b, recv_a, recv_z, mine
        self.local, self.send, self.recv = local, send, recv
        self.copies = {}

    @staticmethod
    def slots(g):
        return g.A * g.B + (g.B - 1) + (g.A - 1) + (g.Z - 1)

    @staticmethod
    def scratch(g, r, w, staged=True):
        return [
            pltpu.VMEM((g.B, g.Z, g.A, r, w), jnp.bfloat16),
            pltpu.VMEM((max(g.B - 1, 1), g.Z, g.A, r, w), jnp.bfloat16),
            pltpu.VMEM((max(g.A - 1, 1), g.Z, r, w), jnp.bfloat16),
            pltpu.VMEM((g.Z - 1, r, w), jnp.bfloat16),
            pltpu.VMEM((g.B, g.Z, g.A, r, w), jnp.bfloat16),
        ]

    def _copy(self, stage, slot, src, dst, device):
        cp = pltpu.make_async_remote_copy(
            src_ref=src, dst_ref=dst, send_sem=self.send.at[slot], recv_sem=self.recv.at[slot],
            device_id=device, device_id_type=MESH)
        cp.start()
        self.copies.setdefault(stage, []).append(cp)

    def start(self):
        g = self.g
        other = 1 - g.c
        self.owns = []
        for b in range(g.B):
            for a in range(g.A):
                x, y = g.xy(a, b, other)
                self._copy("d", b * g.A + a, g.at(self.src, self.order, y, other, slice(None), x),
                           self.work.at[b, :, a], {"dp": g.z * g.X + g.x, "fsdp": g.y * 2 + other})
        for b in range(g.B):
            for a in range(g.A):
                x, y = g.xy(a, b, g.c)
                cp = pltpu.make_async_copy(g.at(self.src, self.order, y, g.c, slice(None), x),
                                           self.mine.at[b, :, a], self.local.at[b * g.A + a])
                cp.start()
                self.owns.append(cp)

    def after_d(self):
        g = self.g
        for cp in self.owns:
            cp.wait()
        for cp in self.copies["d"]:
            cp.wait_recv()

        def add(n, carry):
            b, z, a = n // (g.Z * g.A), n // g.A % g.Z, n % g.A
            self.work[b, z, a] = (self.work[b, z, a].astype(jnp.float32)
                                  + self.mine[b, z, a].astype(jnp.float32)).astype(jnp.bfloat16)
            return carry

        lax.fori_loop(0, g.B * g.Z * g.A, add, 0)
        base = g.A * g.B
        for k in range(1, g.B):
            b = (g.b + k) % g.B
            self._copy("b", base + k - 1, self.work.at[b], self.recv_b.at[k - 1], g.device(g.z, g.a, b, g.c))

    def after_b(self):
        g = self.g
        for cp in self.copies.get("b", []):
            cp.wait_recv()

        def add(n, carry):
            z, a = n // g.A, n % g.A
            total = self.work[g.b, z, a].astype(jnp.float32)
            for k in range(1, g.B):
                total = total + self.recv_b[k - 1, z, a].astype(jnp.float32)
            self.work[g.b, z, a] = total.astype(jnp.bfloat16)
            return carry

        lax.fori_loop(0, g.Z * g.A, add, 0)
        base = g.A * g.B + g.B - 1
        for k in range(1, g.A):
            a = (g.a + k) % g.A
            self._copy("a", base + k - 1, self.work.at[g.b, :, a], self.recv_a.at[k - 1],
                       g.device(g.z, a, g.b, g.c))

    def after_a(self):
        g = self.g
        for cp in self.copies.get("a", []):
            cp.wait_recv()

        def add(z, carry):
            total = self.work[g.b, z, g.a].astype(jnp.float32)
            for k in range(1, g.A):
                total = total + self.recv_a[k - 1, z].astype(jnp.float32)
            self.work[g.b, z, g.a] = total.astype(jnp.bfloat16)
            return carry

        lax.fori_loop(0, g.Z, add, 0)
        base = g.A * g.B + g.B - 1 + g.A - 1
        for k in range(1, g.Z):
            z = (g.z + k) % g.Z
            self._copy("z", base + k - 1, self.work.at[g.b, z, g.a], self.recv_z.at[k - 1],
                       g.device(z, g.a, g.b, g.c))

    def total(self):
        g = self.g
        for cp in self.copies["z"]:
            cp.wait_recv()
        total = self.work[g.b, g.z, g.a].astype(jnp.float32)
        for k in range(1, g.Z):
            total = total + self.recv_z[k - 1].astype(jnp.float32)
        return total

    def finish(self):
        for group in self.copies.values():
            for cp in group:
                cp.wait_send()


def gather_all(n_dp, n_fsdp, shards, orders, collective_id):
    grid = Grid(n_dp, n_fsdp)
    count = len(shards)
    slots = Gather.slots(grid)

    def kernel(*refs):
        ins, outs, (local, send, recv) = refs[:count], refs[count : 2 * count], refs[2 * count :]
        g = grid.here()
        g.barrier()
        jobs = [Gather(g, orders[n], ins[n], outs[n], local.at[n], send.at[n], recv.at[n]) for n in range(count)]
        for job in jobs:
            job.start()
        stages = ["after_z", "after_a", "after_b", "arrive"]
        for step in range(count + len(stages) - 1):
            for s in reversed(range(len(stages))):
                if 0 <= step - s < count:
                    getattr(jobs[step - s], stages[s])()
        for job in jobs:
            job.finish()

    return pl.pallas_call(
        kernel,
        out_shape=[jax.ShapeDtypeStruct(grid.shape(o, *s.shape), s.dtype) for s, o in zip(shards, orders)],
        in_specs=[ANY] * count,
        out_specs=[ANY] * count,
        scratch_shapes=[pltpu.SemaphoreType.DMA((count,)), pltpu.SemaphoreType.DMA((count, slots)),
                        pltpu.SemaphoreType.DMA((count, slots))],
        compiler_params=pltpu.CompilerParams(collective_id=collective_id, has_side_effects=True),
        name="gather_all",
    )(*shards)


def scatter_all(n_dp, n_fsdp, wholes, orders, collective_id):
    grid = Grid(n_dp, n_fsdp)
    count = len(wholes)
    slots = Scatter.slots(grid)
    sizes = [w.shape[-2:] for w in wholes]

    def kernel(*refs):
        ins, outs = refs[:count], refs[count : 2 * count]
        bufs, (local, send, recv) = refs[2 * count : 2 * count + 5 * count], refs[7 * count :]
        g = grid.here()
        g.barrier()
        jobs = [Scatter(g, orders[n], ins[n], *bufs[5 * n : 5 * n + 5], local.at[n], send.at[n], recv.at[n])
                for n in range(count)]
        for job in jobs:
            job.start()

        stages = ["after_d", "after_b", "after_a", "total"]
        for step in range(count + len(stages) - 1):
            for s in reversed(range(len(stages))):
                n = step - s
                if 0 <= n < count:
                    if stages[s] == "total":
                        outs[n][...] = jobs[n].total()
                    else:
                        getattr(jobs[n], stages[s])()
        for job in jobs:
            job.finish()

    scratch = []
    for r, w in sizes:
        scratch += Scatter.scratch(grid, r, w)
    return pl.pallas_call(
        kernel,
        out_shape=[jax.ShapeDtypeStruct(s, jnp.float32) for s in sizes],
        in_specs=[ANY] * count,
        out_specs=[VM] * count,
        scratch_shapes=scratch + [pltpu.SemaphoreType.DMA((count, grid.A * grid.B)),
                                  pltpu.SemaphoreType.DMA((count, slots)), pltpu.SemaphoreType.DMA((count, slots))],
        compiler_params=pltpu.CompilerParams(collective_id=collective_id, has_side_effects=True,
                                             vmem_limit_bytes=60 * 1024 * 1024),
        name="scatter_all",
    )(*wholes)


D = 768
HEADS = 12
HD = 64
FF = 3072
BLOCKS = 12


masked_score = -1000000000.0
decay_rate = 0.5
step_rate = 1.0
small_rate = 0.3
highest = lax.Precision.HIGHEST


def broadcast(value, axis, source):
    kept = jnp.where(lax.axis_index(axis) == source, value, 0).astype(value.dtype)
    return lax.psum(kept, axis)


def layer_norm(values, scale_row, shift_row):
    center = values - jnp.mean(values, axis=-1, keepdims=True)
    spread = jnp.mean(center * center, axis=-1, keepdims=True)
    return center * lax.rsqrt(spread + 1e-06) * scale_row + shift_row


def unpack(small_params):
    pieces = [small_params[number * D : (number + 1) * D] for number in range(8)]
    return pieces + [small_params[8 * D : 8 * D + FF]]


def row_dot(left, right):
    return jnp.dot(left, right, preferred_element_type=jnp.float32)


def column_dot(left, right):
    return lax.dot_general(
        left, right, (((0,), (0,)), ((), ())), preferred_element_type=jnp.float32
    )


def transposed_dot(left, right):
    return lax.dot_general(
        left, right, (((1,), (1,)), ((), ())), preferred_element_type=jnp.float32
    )


def block_split(array, block_rows):
    slots = array.shape[-1]
    return array.reshape(HEADS, HD, slots // block_rows, block_rows).transpose(2, 0, 1, 3)


def block_join(array):
    return array.transpose(0, 3, 1, 2).reshape(-1, D)


def attend_clip(queries, key_rows, value_rows, length):
    slots = queries.shape[-1]
    block_rows = min(512, slots)
    score_scale = float(HD) ** (-0.5)
    visible = (jnp.arange(slots) < length)[None, None, :]

    def one_block(query_block):
        scores = (
            jnp.einsum("hdq,hdk->hqk", query_block, key_rows, preferred_element_type=jnp.float32)
            * score_scale
        )
        scores = jnp.where(visible, scores, masked_score)
        row_top = jnp.max(scores, axis=-1, keepdims=True)
        raised = jnp.exp(scores - row_top)
        row_total = jnp.sum(raised, axis=-1, keepdims=True)
        softmax_weights = (raised / row_total).astype(jnp.bfloat16)
        attended = jnp.einsum(
            "hqk,hdk->hdq", softmax_weights, value_rows, preferred_element_type=jnp.float32
        )
        return (attended.astype(jnp.bfloat16), (row_top + jnp.log(row_total))[:, :, 0])

    attended, log_totals = lax.map(one_block, block_split(queries, block_rows))
    return (block_join(attended), log_totals)


def attend_back(queries, key_rows, value_rows, length, log_totals, out_grads):
    slots = queries.shape[-1]
    block_rows = min(512, slots)
    score_scale = float(HD) ** (-0.5)
    visible = (jnp.arange(slots) < length)[None, None, :]

    def one_block(carry, pieces):
        key_grad, value_grad = carry
        query_block, grad_block, log_block = pieces
        scores = (
            jnp.einsum("hdq,hdk->hqk", query_block, key_rows, preferred_element_type=jnp.float32)
            * score_scale
        )
        scores = jnp.where(visible, scores, masked_score)
        softmax_weights = jnp.exp(scores - log_block[:, :, None])
        weight_grad = jnp.einsum(
            "hdq,hdk->hqk", grad_block, value_rows, preferred_element_type=jnp.float32
        )
        inner_sum = jnp.sum(softmax_weights * weight_grad, axis=-1, keepdims=True)
        score_grad = (softmax_weights * (weight_grad - inner_sum)).astype(jnp.bfloat16)
        query_grad = (
            jnp.einsum("hqk,hdk->hdq", score_grad, key_rows, preferred_element_type=jnp.float32)
            * score_scale
        )
        key_grad = (
            key_grad
            + jnp.einsum(
                "hqk,hdq->hdk", score_grad, query_block, preferred_element_type=jnp.float32
            )
            * score_scale
        )
        value_grad = value_grad + jnp.einsum(
            "hqk,hdq->hdk",
            softmax_weights.astype(jnp.bfloat16),
            grad_block,
            preferred_element_type=jnp.float32,
        )
        return ((key_grad, value_grad), query_grad)

    blank = jnp.zeros((HEADS, HD, slots), jnp.float32)
    (key_grad, value_grad), query_grad = lax.scan(
        one_block,
        (blank, blank),
        (block_split(queries, block_rows), block_split(out_grads, block_rows), log_totals),
    )
    key_rows_grad = key_grad.transpose(2, 0, 1).reshape(slots, D)
    value_rows_grad = value_grad.transpose(2, 0, 1).reshape(slots, D)
    return (block_join(query_grad), key_rows_grad, value_rows_grad)


def take_columns(operands, member, start):
    return lax.slice_in_dim(operands[member], start, start + D, axis=1)


def take_rows(operands, member, start):
    return lax.slice_in_dim(operands[member], start, start + D, axis=0)


def block_pickers():
    pickers = [partial(take_columns, member=0, start=column * D) for column in range(3)]
    pickers.append(partial(take_columns, member=1, start=0))
    pickers = pickers + [
        partial(take_columns, member=2, start=column * D) for column in range(FF // D)
    ]
    pickers = pickers + [
        partial(take_rows, member=3, start=column * D) for column in range(FF // D)
    ]
    return pickers


def wholes_of(pieces, orders):
    out = []
    for piece, order in zip(pieces, orders):
        rows, columns = piece.shape[-2:]
        if order == "j":
            folded = piece.reshape(piece.shape[0] * piece.shape[1], -1, columns)
        else:
            folded = piece.reshape(piece.shape[0] * piece.shape[1], -1, columns)
        out.append(folded.transpose(1, 0, 2).reshape(folded.shape[1], -1))
    return out


def pieces_of(whole, order, n_dp, n_fsdp):
    grid = Grid(n_dp, n_fsdp)
    n_rows, n_columns = (n_dp, n_fsdp) if order == "j" else (n_fsdp, n_dp)
    rows, columns = whole.shape[0] // n_rows, whole.shape[1] // n_columns
    folded = whole.reshape(whole.shape[0], n_columns, columns).transpose(1, 0, 2)
    return folded.reshape(grid.shape(order, rows, columns))


def local(
    sizes,
    tokens,
    counts,
    cotangent,
    qkv_weight,
    out_weight,
    up_weight,
    down_weight,
    small_params,
    statistics,
    inverse_roots,
    owners,
):
    clips_here = counts.shape[0]
    slots = tokens.shape[0] // clips_here
    qkv_low = qkv_weight.astype(jnp.bfloat16)
    out_low = out_weight.astype(jnp.bfloat16)
    up_low = up_weight.astype(jnp.bfloat16)
    down_low = down_weight.astype(jnp.bfloat16)
    n_dp, n_fsdp = sizes
    orders = ("j", "j", "j", "i")
    gathered = gather_all(n_dp, n_fsdp, (qkv_low, out_low, up_low, down_low.T), orders, 1)
    qkv_full, out_full, up_full, down_full_t = wholes_of(gathered, orders)
    (
        gain_one,
        shift_one,
        gain_two,
        shift_two,
        bias_query,
        bias_value,
        bias_out,
        bias_down,
        bias_up,
    ) = unpack(small_params)

    def heads_view(array):
        return array.reshape(clips_here, slots, HEADS, HD).transpose(0, 2, 3, 1)

    def clip_forward(clip_group):
        return attend_clip(clip_group[0], clip_group[1], clip_group[2], clip_group[3])

    def clip_backward(clip_group):
        return attend_back(
            clip_group[0], clip_group[1], clip_group[2], clip_group[3], clip_group[4], clip_group[5]
        )

    inputs = tokens.astype(jnp.float32)
    normed = layer_norm(inputs, gain_one, shift_one).astype(jnp.bfloat16)
    projected = row_dot(normed, qkv_full)
    queries = heads_view((projected[:, :D] + bias_query).astype(jnp.bfloat16))
    key_rows = heads_view(projected[:, D : 2 * D].astype(jnp.bfloat16))
    value_rows = heads_view((projected[:, 2 * D :] + bias_value).astype(jnp.bfloat16))
    attended, log_totals = lax.map(clip_forward, (queries, key_rows, value_rows, counts))
    attended = attended.reshape(-1, D)
    middle = inputs + (row_dot(attended, out_full) + bias_out)
    normed_two = layer_norm(middle, gain_two, shift_two).astype(jnp.bfloat16)
    hidden = row_dot(normed_two, up_full) + bias_up
    active = jax.nn.gelu(hidden, approximate=False).astype(jnp.bfloat16)
    layer_rows = (middle + transposed_dot(active, down_full_t) + bias_down).astype(jnp.bfloat16)
    grad_down_t = column_dot(cotangent, active)
    grad_bias_down = jnp.sum(cotangent.astype(jnp.float32), axis=0)
    active_grad = row_dot(cotangent, down_full_t)
    unused_value, gelu_pull = jax.vjp(partial(jax.nn.gelu, approximate=False), hidden)
    hidden_grad = gelu_pull(active_grad)[0].astype(jnp.bfloat16)
    grad_up = column_dot(normed_two, hidden_grad)
    grad_bias_up = jnp.sum(hidden_grad.astype(jnp.float32), axis=0)
    normed_two_grad = transposed_dot(hidden_grad, up_full)
    unused_norm, norm_two_pull = jax.vjp(layer_norm, middle, gain_two, shift_two)
    middle_grad, grad_gain_two, grad_shift_two = norm_two_pull(normed_two_grad)
    middle_grad = middle_grad + cotangent.astype(jnp.float32)
    branch_grad = middle_grad.astype(jnp.bfloat16)
    grad_out = column_dot(attended, branch_grad)
    grad_bias_out = jnp.sum(branch_grad.astype(jnp.float32), axis=0)
    attended_grad = transposed_dot(branch_grad, out_full).astype(jnp.bfloat16)
    query_grad, key_grad, value_grad = lax.map(
        clip_backward,
        (queries, key_rows, value_rows, counts, log_totals, heads_view(attended_grad)),
    )
    projected_grad = (
        jnp.concatenate([query_grad, key_grad, value_grad], axis=-1)
        .reshape(-1, 3 * D)
        .astype(jnp.bfloat16)
    )
    grad_qkv = column_dot(normed, projected_grad)
    grad_bias_query = jnp.sum(projected_grad[:, :D].astype(jnp.float32), axis=0)
    grad_bias_value = jnp.sum(projected_grad[:, 2 * D :].astype(jnp.float32), axis=0)
    normed_grad = transposed_dot(projected_grad, qkv_full)
    unused_first, norm_one_pull = jax.vjp(layer_norm, inputs, gain_one, shift_one)
    input_rows_grad, grad_gain_one, grad_shift_one = norm_one_pull(normed_grad)
    input_grad = (middle_grad + input_rows_grad).astype(jnp.bfloat16)
    small_grad = jnp.concatenate(
        [
            grad_gain_one,
            grad_shift_one,
            grad_gain_two,
            grad_shift_two,
            grad_bias_query,
            grad_bias_value,
            grad_bias_out,
            grad_bias_down,
            grad_bias_up,
        ]
    )
    whole_small = lax.psum(small_grad, ("dp", "fsdp"))
    split = [
        pieces_of(grad.astype(jnp.bfloat16), order, n_dp, n_fsdp)
        for grad, order in zip((grad_qkv, grad_out, grad_up, grad_down_t), orders)
    ]
    shards = scatter_all(n_dp, n_fsdp, split, orders, 2)
    shard_qkv, shard_out, shard_up, shard_down_t = shards
    gradients = gather_all(n_dp, n_fsdp, [s.astype(jnp.bfloat16) for s in shards], orders, 3)
    whole_qkv, whole_out, whole_up, whole_down_t = wholes_of(gradients, orders)
    shard_down = shard_down_t.T
    rank = lax.axis_index(("dp", "fsdp"))
    row_index = lax.axis_index("dp")
    column_index = lax.axis_index("fsdp")
    numbers = jnp.arange(BLOCKS, dtype=jnp.int32)
    matches = owners == rank
    mine = jnp.sum(jnp.where(matches, numbers, 0))
    owning = jnp.any(matches)

    def update_slot(gradient):
        left_stat = decay_rate * statistics[0, 0] + (1.0 - decay_rate) * transposed_dot(gradient, gradient)
        right_stat = decay_rate * statistics[0, 1] + (1.0 - decay_rate) * column_dot(gradient, gradient)
        wide = gradient.astype(jnp.float32)
        left_step = jnp.dot(
            inverse_roots[0, 0], wide, precision=highest, preferred_element_type=jnp.float32
        )
        update = jnp.dot(
            left_step, inverse_roots[0, 1], precision=highest, preferred_element_type=jnp.float32
        )
        return (jnp.stack([left_stat, right_stat])[None], update.astype(jnp.bfloat16))

    def keep_slot(gradient):
        return (statistics, jnp.zeros((D, D), jnp.bfloat16))

    whole_down = whole_down_t.T
    gradient = lax.switch(mine, block_pickers(), (whole_qkv, whole_out, whole_up, whole_down))
    new_statistics, update = lax.cond(owning, update_slot, keep_slot, gradient)
    zero = jnp.zeros((D, D), jnp.bfloat16)
    steps = [jnp.where(owners[number] == rank, update, zero) for number in range(BLOCKS)]
    update_t = update.T
    turned = [jnp.where(owners[number] == rank, update_t, zero) for number in range(4 + FF // D, BLOCKS)]
    masked = (
        jnp.concatenate(steps[0:3], axis=1),
        steps[3],
        jnp.concatenate(steps[4 : 4 + FF // D], axis=1),
        jnp.concatenate(turned, axis=1),
    )
    split = [pieces_of(whole, order, n_dp, n_fsdp) for whole, order in zip(masked, orders)]
    tile_qkv, tile_out, tile_up, tile_down_t = scatter_all(n_dp, n_fsdp, split, orders, 4)
    tile_down = tile_down_t.T
    new_qkv = qkv_weight - step_rate * tile_qkv
    new_out = out_weight - step_rate * tile_out
    new_up = up_weight - step_rate * tile_up
    new_down = down_weight - step_rate * tile_down
    new_small = small_params - small_rate * whole_small * lax.rsqrt(
        jnp.mean(whole_small * whole_small) + 1e-06
    )
    return (
        layer_rows,
        input_grad,
        shard_qkv,
        shard_out,
        shard_up,
        shard_down,
        whole_small,
        new_statistics,
        new_qkv,
        new_out,
        new_up,
        new_down,
        new_small,
    )


def solution(mesh):
    placed = (
        P(("dp", "fsdp"), None),
        P(("dp", "fsdp")),
        P(("dp", "fsdp"), None),
        P("dp", "fsdp"),
        P("dp", "fsdp"),
        P("dp", "fsdp"),
        P("dp", "fsdp"),
        P(),
        P(("dp", "fsdp"), None, None, None),
        P(("dp", "fsdp"), None, None, None),
        P(),
    )
    return jax.shard_map(
        partial(local, (mesh.shape["dp"], mesh.shape["fsdp"])),
        mesh=mesh,
        in_specs=placed,
        out_specs=(
            P(("dp", "fsdp"), None),
            P(("dp", "fsdp"), None),
            P("dp", "fsdp"),
            P("dp", "fsdp"),
            P("dp", "fsdp"),
            P("dp", "fsdp"),
            P(),
            P(("dp", "fsdp"), None, None, None),
            P("dp", "fsdp"),
            P("dp", "fsdp"),
            P("dp", "fsdp"),
            P("dp", "fsdp"),
            P(),
        ),
        check_vma=False,
    )
```

```python
from functools import partial

import jax
import jax.numpy as jnp
from jax import lax
from jax.experimental import pallas as pl
from jax.experimental.pallas import tpu as pltpu
from jax.sharding import PartitionSpec as P

MESH = pl.DeviceIdType.MESH
ANY = pl.BlockSpec(memory_space=pl.ANY)
VM = pl.BlockSpec(memory_space=pltpu.VMEM)


class Grid:
    def __init__(self, n_dp, n_fsdp):
        self.Z = 4
        self.X = n_dp // 4
        self.Y = n_fsdp // 2
        self.swap = self.X == self.Y
        self.A, self.B = self.X, self.Y

    def here(self):
        dp, fs = lax.axis_index("dp"), lax.axis_index("fsdp")
        self.z, self.x = dp // self.X, dp % self.X
        self.y, self.c = fs // 2, fs % 2
        if self.swap:
            self.a = self.x + self.c * (self.y - self.x)
            self.b = self.y + self.c * (self.x - self.y)
        else:
            self.a, self.b = self.x, self.y
        return self

    def xy(self, a, b, c):
        if self.swap:
            return a + c * (b - a), b + c * (a - b)
        return a, b

    def device(self, z, a, b, c, frame=None):
        x, y = self.xy(a, b, self.c if frame is None else frame)
        return {"dp": z * self.X + x, "fsdp": y * 2 + c}

    def shape(self, order, r, w):
        if order == "j":
            return (self.Y, 2, self.Z, self.X, r, w)
        return (self.Z, self.X, self.Y, 2, r, w)

    def at(self, ref, order, y, c, z, x):
        return ref.at[y, c, z, x] if order == "j" else ref.at[z, x, y, c]

    def peers(self):
        out = [self.device((self.z + k) % self.Z, self.a, self.b, self.c) for k in range(1, self.Z)]
        out += [self.device(self.z, (self.a + k) % self.A, self.b, self.c) for k in range(1, self.A)]
        out += [self.device(self.z, self.a, (self.b + k) % self.B, self.c) for k in range(1, self.B)]
        out += [{"dp": self.z * self.X + self.x, "fsdp": self.y * 2 + 1 - self.c}]
        return out

    def barrier(self):
        sem = pltpu.get_barrier_semaphore()
        peers = self.peers()
        for peer in peers:
            pl.semaphore_signal(sem, inc=1, device_id=peer, device_id_type=MESH)
        pl.semaphore_wait(sem, len(peers))


def remote(src, dst, send, recv, slot, device):
    return pltpu.make_async_remote_copy(
        src_ref=src, dst_ref=dst, send_sem=send.at[slot], recv_sem=recv.at[slot], device_id=device, device_id_type=MESH
    )


def start_all(copies):
    for copy in copies:
        copy.start()


def arrived(copies):
    for copy in copies:
        copy.wait_recv()


def sent(copies):
    for copy in copies:
        copy.wait_send()


class Gather:
    def __init__(self, g, order, path, rows, src, out, local, send, recv):
        size = {"z": g.Z, "a": g.A, "b": g.B}
        place = {"z": g.z, "a": g.a, "b": g.b}

        def piece(cell):
            x, y = g.xy(cell["a"], cell["b"], g.c)
            return g.at(out, order, y, g.c, cell["z"], x).at[..., rows, :]

        def cells(full):
            out = [dict(place)]
            for axis in full:
                if axis == "z":
                    out = [dict(cell, z=slice(None)) for cell in out]
                else:
                    out = [dict(cell, **{axis: n}) for cell in out for n in range(size[axis])]
            return out

        near = {"dp": g.z * g.X + g.x, "fsdp": g.y * 2 + 1 - g.c}
        self.slot = 0

        def copy(start, end, device):
            self.slot += 1
            return remote(start, end, send, recv, self.slot - 1, device)

        own = src.at[rows, :]
        self.own = pltpu.make_async_copy(own, piece(place), local)
        self.stages, self.near = [], [[copy(own, piece(place), near)]]
        full = ""
        for axis in path:
            out_copies, near_copies = [], []
            for cell in cells(full):
                start = piece(cell) if full else own
                for k in range(1, size[axis]):
                    to = dict(place, **{axis: (place[axis] + k) % size[axis]})
                    out_copies.append(copy(start, piece(cell), g.device(to["z"], to["a"], to["b"], g.c)))
                    came = piece(dict(cell, **{axis: (place[axis] - k + size[axis]) % size[axis]}))
                    near_copies.append(copy(came, came, near))
            self.stages.append(out_copies)
            self.near.append(near_copies)
            full += axis

    @staticmethod
    def slots(g):
        zab = (g.Z - 1) + (g.A - 1) + g.A * (g.B - 1)
        abz = (g.A - 1) + g.A * (g.B - 1) + g.A * g.B * (g.Z - 1)
        return 1 + 2 * max(zab, abz)

    def step(self, number):
        if number == 0:
            self.own.start()
        else:
            if number == 1:
                self.own.wait()
            arrived(self.stages[number - 1])
        start_all(self.near[number])
        if number < 3:
            start_all(self.stages[number])

    def finish(self):
        for group in self.near:
            arrived(group)
        for group in self.near + self.stages:
            sent(group)


class Scatter:
    def __init__(self, g, order, path, rows, src, bufs, local, send, recv):
        self.g, self.path, self.count = g, path, rows.size
        self.work, self.mine = bufs[0], bufs[1]
        self.recv = dict(zip(path, bufs[2:]))
        work, other = self.work, 1 - g.c
        size = {"z": g.Z, "a": g.A, "b": g.B}
        place = {"z": g.z, "a": g.a, "b": g.b}
        self.size = size
        self.slot = 0

        def copy(start, end, device):
            self.slot += 1
            return remote(start, end, send, recv, self.slot - 1, device)

        self.owns, near = [], []
        for b in range(g.B):
            for a in range(g.A):
                x, y = g.xy(a, b, other)
                near.append(copy(g.at(src, order, y, other, slice(None), x).at[:, rows, :], work.at[b, :, a],
                                 {"dp": g.z * g.X + g.x, "fsdp": g.y * 2 + other}))
                x, y = g.xy(a, b, g.c)
                self.owns.append(pltpu.make_async_copy(g.at(src, order, y, g.c, slice(None), x).at[:, rows, :],
                                                       self.mine.at[b, :, a], local.at[b * g.A + a]))
        self.stages = [near]
        done = ""
        for axis in path:
            copies = []
            for k in range(1, size[axis]):
                to = dict(place, **{axis: (place[axis] + k) % size[axis]})
                where = {name: (place[name] if name in done else slice(None)) for name in "bza"}
                where[axis] = to[axis]
                copies.append(copy(work.at[where["b"], where["z"], where["a"]], self.recv[axis].at[k - 1],
                                   g.device(to["z"], to["a"], to["b"], g.c)))
            self.stages.append(copies)
            done += axis

    @staticmethod
    def slots(g):
        return g.A * g.B + (g.B - 1) + (g.A - 1) + (g.Z - 1)

    @staticmethod
    def scratch(g, path, r, w):
        size = {"z": g.Z, "a": g.A, "b": g.B}
        out = [pltpu.VMEM((g.B, g.Z, g.A, r, w), jnp.bfloat16)] * 2
        done = ""
        for axis in path:
            done += axis
            out.append(pltpu.VMEM((size[axis] - 1,) + tuple(size[n] for n in "bza" if n not in done) + (r, w), jnp.bfloat16))
        return out

    def _cell(self, index, done):
        place = {"z": self.g.z, "a": self.g.a, "b": self.g.b}
        return [place[n] if n in done else index[n] for n in "bza"]

    def _add(self, number):
        g, done = self.g, self.path[:number]
        left = [n for n in "bza" if n not in done]
        total = 1
        for name in left:
            total *= self.size[name]

        def add(n, carry):
            index = {}
            for name in reversed(left):
                index[name] = n % self.size[name]
                n = n // self.size[name]
            b, z, a = self._cell(index, done)
            if number == 0:
                summed = self.work[b, z, a].astype(jnp.float32) + self.mine[b, z, a].astype(jnp.float32)
            else:
                summed = self._sum(number, b, z, a, [index[name] for name in left])
            self.work[b, z, a] = summed.astype(jnp.bfloat16)
            return carry

        lax.fori_loop(0, total, add, 0)

    def _sum(self, number, b, z, a, index):
        axis = self.path[number - 1]
        summed = self.work[b, z, a].astype(jnp.float32)
        for k in range(self.size[axis] - 1):
            summed = summed + self.recv[axis][tuple([k] + index)].astype(jnp.float32)
        return summed

    def step(self, number):
        if number == 0:
            start_all(self.stages[0] + self.owns)
            return
        if number == 1:
            for copy in self.owns:
                copy.wait()
        arrived(self.stages[number - 1])
        self._add(number - 1)
        start_all(self.stages[number])

    def total(self):
        arrived(self.stages[3])
        return self._sum(3, self.g.b, self.g.z, self.g.a, [])

    def finish(self):
        for group in self.stages:
            sent(group)


GATHER_PATHS = ("zab", "abz")
SCATTER_PATHS = ("baz", "zba")


def row_parts(rows):
    first = rows * 2 // 3 // 16 * 16
    if first == 0 or first == rows:
        return [(0, pl.ds(0, rows))]
    return [(0, pl.ds(0, first)), (1, pl.ds(first, rows - first))]


def job_list(sizes):
    return [(n, path, rows) for n, (r, _) in enumerate(sizes) for path, rows in row_parts(r)]


def rounds(jobs, last):
    return [(n, step) for step in range(last + 1) for n in range(len(jobs))]


def gather_scratch(g, count):
    lanes = Gather.slots(g)
    dma = pltpu.SemaphoreType.DMA
    return [dma((count,)), dma((count, lanes)), dma((count, lanes))]


def gather_all(n_dp, n_fsdp, shards, orders, collective_id):
    grid = Grid(n_dp, n_fsdp)
    count = len(shards)
    jobs = job_list([s.shape for s in shards])

    def kernel(*refs):
        ins, outs, (local, send, recv) = refs[:count], refs[count : 2 * count], refs[2 * count :]
        g = grid.here()
        g.barrier()
        work = [Gather(g, orders[n], GATHER_PATHS[path], rows, ins[n], outs[n], local.at[j], send.at[j], recv.at[j])
                for j, (n, path, rows) in enumerate(jobs)]
        for j, step in rounds(jobs, 3):
            work[j].step(step)
        for job in work:
            job.finish()

    return pl.pallas_call(
        kernel,
        out_shape=[jax.ShapeDtypeStruct(grid.shape(o, *s.shape), s.dtype) for s, o in zip(shards, orders)],
        in_specs=[ANY] * count,
        out_specs=[ANY] * count,
        scratch_shapes=gather_scratch(grid, len(jobs)),
        compiler_params=pltpu.CompilerParams(collective_id=collective_id, has_side_effects=True),
        name="gather_all",
    )(*shards)


def scatter_scratch(g, sizes, jobs):
    out = []
    for n, path, rows in jobs:
        out += Scatter.scratch(g, SCATTER_PATHS[path], rows.size, sizes[n][1])
    dma = pltpu.SemaphoreType.DMA
    lanes = Scatter.slots(g)
    return out + [dma((len(jobs), g.A * g.B)), dma((len(jobs), lanes)), dma((len(jobs), lanes))]


def scatter_jobs(g, orders, jobs, ins, scratch):
    local, send, recv = scratch[5 * len(jobs) :]
    return [Scatter(g, orders[n], SCATTER_PATHS[path], rows, ins[n], scratch[5 * j : 5 * j + 5], local.at[j], send.at[j],
                    recv.at[j]) for j, (n, path, rows) in enumerate(jobs)]


def scatter_all(n_dp, n_fsdp, wholes, orders, collective_id, dtype=jnp.float32):
    grid = Grid(n_dp, n_fsdp)
    count = len(wholes)
    sizes = [w.shape[-2:] for w in wholes]
    jobs = job_list(sizes)

    def kernel(*refs):
        ins, outs, scratch = refs[:count], refs[count : 2 * count], refs[2 * count :]
        g = grid.here()
        g.barrier()
        work = scatter_jobs(g, orders, jobs, ins, scratch)
        for j, step in rounds(jobs, 3):
            work[j].step(step)
        for job, (n, path, rows) in zip(work, jobs):
            outs[n][rows, :] = job.total().astype(dtype)
        for job in work:
            job.finish()

    return pl.pallas_call(
        kernel,
        out_shape=[jax.ShapeDtypeStruct(s, dtype) for s in sizes],
        in_specs=[ANY] * count,
        out_specs=[VM] * count,
        scratch_shapes=scatter_scratch(grid, sizes, jobs),
        compiler_params=pltpu.CompilerParams(collective_id=collective_id, has_side_effects=True,
                                             vmem_limit_bytes=60 * 1024 * 1024),
        name="scatter_all",
    )(*wholes)


HEAD = 64
PAIR = 128


def last_dot(left, right):
    return lax.dot_general(left, right, (((1,), (1,)), ((), ())), preferred_element_type=jnp.float32)


def plain_dot(left, right):
    return lax.dot_general(left, right, (((1,), (0,)), ((), ())), preferred_element_type=jnp.float32)


def attend_block(length, start, size, q_heads, k_ref, v_turned, o_ref, lse_ref):
    slots = k_ref.shape[0]
    half = slots // 2
    keys = k_ref[...]
    key_index = lax.broadcasted_iota(jnp.int32, (slots - half, size), 0) + half
    scores, tops = [], []
    for head in range(2):
        q = q_heads[head, pl.ds(start, size), :]
        low = last_dot(keys[:half], q)
        high = jnp.where(key_index < length, last_dot(keys[half:], q), -1000000000.0)
        tops.append(jnp.maximum(jnp.max(low, axis=0, keepdims=True), jnp.max(high, axis=0, keepdims=True)))
        scores.append((low, high))
    raised = [[jnp.exp(s - tops[head]).astype(jnp.bfloat16) for s in scores[head]] for head in range(2)]
    parts = []
    for head in range(2):
        summed = plain_dot(v_turned[head][:, :half], raised[head][0])
        summed = summed + plain_dot(v_turned[head][:, half:], raised[head][1])
        mine = summed[head * HEAD : (head + 1) * HEAD]
        total = summed[(1 - head) * HEAD : (1 - head) * HEAD + 1]
        parts.append(mine * (1.0 / total))
        lse_ref[head, pl.ds(start, size)] = (tops[head] + jnp.log(total))[0]
    o_ref[pl.ds(start, size), :] = jnp.concatenate(parts, axis=0).T.astype(jnp.bfloat16)


def attend_prepare(q_ref, v_ref, q_heads, v_turned):
    slots = q_ref.shape[0]
    lane = lax.broadcasted_iota(jnp.int32, (slots, PAIR), 1)
    row = lax.broadcasted_iota(jnp.int32, (PAIR, slots), 0)
    q = q_ref[...].astype(jnp.float32) * (HEAD ** (-0.5))
    v = v_ref[...].astype(jnp.float32).T
    for head in range(2):
        q_heads[head] = jnp.where(lane // HEAD == head, q, 0.0).astype(jnp.bfloat16)
        v_turned[head] = jnp.where(row // HEAD == head, v, 1.0).astype(jnp.bfloat16)


def attend_kernel(size, count_ref, q_ref, k_ref, v_ref, o_ref, lse_ref, q_heads, v_turned):
    attend_prepare(q_ref, v_ref, q_heads, v_turned)
    length = count_ref[0]

    def step(n, carry):
        attend_block(length, pl.multiple_of(n * size, size), size, q_heads, k_ref, v_turned, o_ref, lse_ref.at[0])
        return carry

    lax.fori_loop(0, q_ref.shape[0] // size, step, 0)


def attend(counts, projected, size=256):
    slots, width = projected.shape
    d = width // 3
    pairs = d // PAIR
    spec = lambda part: pl.BlockSpec((slots, PAIR), lambda p, n, part=part: (0, part * pairs + p))
    return pl.pallas_call(
        partial(attend_kernel, size),
        out_shape=[jax.ShapeDtypeStruct((slots, d), jnp.bfloat16),
                   jax.ShapeDtypeStruct((pairs, 2, slots), jnp.float32)],
        grid_spec=pltpu.PrefetchScalarGridSpec(
            num_scalar_prefetch=1, grid=(pairs,),
            in_specs=[spec(0), spec(1), spec(2)],
            out_specs=[pl.BlockSpec((slots, PAIR), lambda p, n: (0, p)),
                       pl.BlockSpec((1, 2, slots), lambda p, n: (p, 0, 0))],
            scratch_shapes=[pltpu.VMEM((2, slots, PAIR), jnp.bfloat16), pltpu.VMEM((2, PAIR, slots), jnp.bfloat16)]),
        compiler_params=pltpu.CompilerParams(vmem_limit_bytes=48 * 1024 * 1024),
        name="attend",
    )(counts, projected, projected, projected)


def attend_back_scratch(slots):
    return [pltpu.VMEM((2, slots, PAIR), jnp.bfloat16), pltpu.VMEM((2, slots, PAIR), jnp.bfloat16),
            pltpu.VMEM((2, PAIR, slots), jnp.bfloat16), pltpu.VMEM((2, slots), jnp.float32),
            pltpu.VMEM((slots, PAIR), jnp.float32), pltpu.VMEM((slots, PAIR), jnp.float32)]


def attend_back_body(size, count_ref, q_ref, k_ref, v_ref, o_ref, do_ref, lse_ref, out_ref,
                     q_heads, do_heads, k_turned, inner, dk_sum, dv_sum, hook):
    slots = q_ref.shape[0]
    length = count_ref[0]
    lane = lax.broadcasted_iota(jnp.int32, (slots, PAIR), 1)
    row = lax.broadcasted_iota(jnp.int32, (PAIR, slots), 0)
    q = q_ref[...].astype(jnp.float32) * (HEAD ** (-0.5))
    do = do_ref[...].astype(jnp.float32)
    k = k_ref[...].astype(jnp.float32).T * (HEAD ** (-0.5))
    product = (do * o_ref[...].astype(jnp.float32)).T
    for head in range(2):
        q_heads[head] = jnp.where(lane // HEAD == head, q, 0.0).astype(jnp.bfloat16)
        do_heads[head] = jnp.where(lane // HEAD == head, do, 0.0).astype(jnp.bfloat16)
        k_turned[head] = jnp.where(row // HEAD == head, k, 0.0).astype(jnp.bfloat16)
        inner[head] = jnp.sum(product[head * HEAD : (head + 1) * HEAD], axis=0)
    dk_sum[...] = jnp.zeros_like(dk_sum)
    dv_sum[...] = jnp.zeros_like(dv_sum)
    key_index = lax.broadcasted_iota(jnp.int32, (slots, size), 0)

    def step(n, carry):
        rows = pl.ds(pl.multiple_of(n * size, size), size)
        keys, values = k_ref[...], v_ref[...]
        dq = jnp.zeros((PAIR, size), jnp.float32)
        for head in range(2):
            q_block, do_block = q_heads[head, rows, :], do_heads[head, rows, :]
            scores = last_dot(keys, q_block)
            weights = jnp.exp(scores - lse_ref[0, head, rows][None, :])
            weights = jnp.where(key_index < length, weights, 0.0)
            weight_grad = last_dot(values, do_block)
            score_grad = (weights * (weight_grad - inner[head, rows][None, :])).astype(jnp.bfloat16)
            dv_sum[...] += plain_dot(weights.astype(jnp.bfloat16), do_block)
            dk_sum[...] += plain_dot(score_grad, q_block)
            dq = dq + plain_dot(k_turned[head], score_grad)
        out_ref[0, rows, :] = dq.T.astype(jnp.bfloat16)
        return carry

    steps = slots // size
    for half in range(2):
        hook(half)
        lax.fori_loop(half * steps // 2, (half + 1) * steps // 2, step, 0)
    out_ref[1] = dk_sum[...].astype(jnp.bfloat16)
    out_ref[2] = dv_sum[...].astype(jnp.bfloat16)


def attend_gather(n_dp, n_fsdp, counts, projected, shards, orders, plan, collective_id, size=512):
    slots, width = projected.shape
    d = width // 3
    pairs = d // PAIR
    grid = Grid(n_dp, n_fsdp)
    count = len(shards)
    jobs = job_list([s.shape for s in shards])
    steps = slots // size

    def kernel(count_ref, q_ref, k_ref, v_ref, *refs):
        ins, (o_ref, lse_ref), outs = refs[:count], refs[count : count + 2], refs[count + 2 : 2 * count + 2]
        q_heads, v_turned, local, send, recv = refs[2 * count + 2 :]
        g = grid.here()
        work = [Gather(g, orders[n], GATHER_PATHS[path], rows, ins[n], outs[n], local.at[j], send.at[j], recv.at[j])
                for j, (n, path, rows) in enumerate(jobs)]
        pair = pl.program_id(0)

        def run(when):
            for j, step in plan.get(when, []):
                work[j].step(step)

        for p in range(pairs):
            if any(p * steps == when for when in plan):

                @pl.when(pair == p)
                def _():
                    if p == 0:
                        g.barrier()
                    run(p * steps)

        attend_prepare(q_ref, v_ref, q_heads, v_turned)
        length = count_ref[0]
        for n in range(steps):
            for p in range(pairs):
                if n > 0 and p * steps + n in plan:
                    pl.when(pair == p)(partial(run, p * steps + n))

            attend_block(length, n * size, size, q_heads, k_ref, v_turned, o_ref, lse_ref.at[0])

        @pl.when(pair == pairs - 1)
        def _():
            run("end")
            for job in work:
                job.finish()

    spec = lambda part: pl.BlockSpec((slots, PAIR), lambda p, n, part=part: (0, part * pairs + p))
    return pl.pallas_call(
        kernel,
        out_shape=[jax.ShapeDtypeStruct((slots, d), jnp.bfloat16),
                   jax.ShapeDtypeStruct((pairs, 2, slots), jnp.float32)]
        + [jax.ShapeDtypeStruct(grid.shape(o, *s.shape), s.dtype) for s, o in zip(shards, orders)],
        grid_spec=pltpu.PrefetchScalarGridSpec(
            num_scalar_prefetch=1, grid=(pairs,),
            in_specs=[spec(0), spec(1), spec(2)] + [ANY] * count,
            out_specs=[pl.BlockSpec((slots, PAIR), lambda p, n: (0, p)),
                       pl.BlockSpec((1, 2, slots), lambda p, n: (p, 0, 0))] + [ANY] * count,
            scratch_shapes=[pltpu.VMEM((2, slots, PAIR), jnp.bfloat16), pltpu.VMEM((2, PAIR, slots), jnp.bfloat16)]
            + gather_scratch(grid, len(jobs))),
        compiler_params=pltpu.CompilerParams(vmem_limit_bytes=56 * 1024 * 1024, collective_id=collective_id,
                                             has_side_effects=True),
        name="attend_gather",
    )(counts, projected, projected, projected, *shards)


FORWARD_PLAN = {
    0: [(0, 0), (1, 0), (2, 0), (3, 0)],
    2: [(0, 1), (1, 1)],
    3: [(0, 2), (1, 2), (4, 0), (5, 0)],
    4: [(2, 1), (3, 1)],
    5: [(0, 3), (1, 3)],
    7: [(2, 2), (3, 2)],
    8: [(4, 1), (5, 1)],
    10: [(4, 2), (5, 2)],
    11: [(2, 3), (3, 3)],
    "end": [(4, 3), (5, 3)],
}


def attend_back_scatter(n_dp, n_fsdp, counts, projected, attended, attended_grad, lse, wholes, plan, collective_id, size=256):
    slots, width = projected.shape
    d = width // 3
    pairs = d // PAIR
    grid = Grid(n_dp, n_fsdp)
    count = len(wholes)
    sizes = [w.shape[-2:] for w in wholes]
    jobs = job_list(sizes)

    def kernel(count_ref, q_ref, k_ref, v_ref, o_ref, do_ref, lse_ref, *refs):
        ins, out_ref, outs = refs[:count], refs[count], refs[count + 1 : 2 * count + 1]
        own, scratch = refs[2 * count + 1 : 2 * count + 7], refs[2 * count + 7 :]
        g = grid.here()
        work = scatter_jobs(g, ["j"] * count, jobs, ins, scratch)
        pair = pl.program_id(0)

        def run(when):
            for j, step in plan.get(when, []):
                work[j].step(step)

        for p in range(pairs):
            for half in range(2):
                if half == 0 and p * 2 in plan:

                    @pl.when(pair == p)
                    def _():
                        if p == 0:
                            g.barrier()
                        run(p * 2)

        def hook(half):
            for p in range(pairs):
                if half and p * 2 + half in plan:
                    pl.when(pair == p)(partial(run, p * 2 + half))

        attend_back_body(size, count_ref, q_ref, k_ref, v_ref, o_ref, do_ref, lse_ref, out_ref, *own, hook)

        @pl.when(pair == pairs - 1)
        def _():
            run("end")
            for job, (n, path, rows) in zip(work, jobs):
                outs[n][rows, :] = job.total().astype(jnp.bfloat16)
            for job in work:
                job.finish()

    spec = lambda part: pl.BlockSpec((slots, PAIR), lambda p, n, part=part: (0, part * pairs + p))
    return pl.pallas_call(
        kernel,
        out_shape=[jax.ShapeDtypeStruct((3, slots, d), jnp.bfloat16)]
        + [jax.ShapeDtypeStruct(s, jnp.bfloat16) for s in sizes],
        grid_spec=pltpu.PrefetchScalarGridSpec(
            num_scalar_prefetch=1, grid=(pairs,),
            in_specs=[spec(0), spec(1), spec(2), spec(0), spec(0), pl.BlockSpec((1, 2, slots), lambda p, n: (p, 0, 0))]
            + [ANY] * count,
            out_specs=[pl.BlockSpec((3, slots, PAIR), lambda p, n: (0, 0, p))] + [VM] * count,
            scratch_shapes=attend_back_scratch(slots) + scatter_scratch(grid, sizes, jobs)),
        compiler_params=pltpu.CompilerParams(vmem_limit_bytes=60 * 1024 * 1024, collective_id=collective_id,
                                             has_side_effects=True),
        name="attend_back_scatter",
    )(counts, projected, projected, projected, attended, attended_grad, lse, *wholes)


BACKWARD_PLAN = {
    0: [(n, 0) for n in range(6)],
    3: [(0, 1), (1, 1)],
    4: [(2, 1), (3, 1), (4, 1), (5, 1)],
    6: [(0, 2), (1, 2)],
    7: [(2, 2), (3, 2), (4, 2), (5, 2)],
    9: [(0, 3), (1, 3)],
    10: [(2, 3), (3, 3), (4, 3), (5, 3)],
}


PIECE = (48, 384)


class Spread:
    def __init__(self, g, u, tiles, send, recv, base):
        qkv, out, up, down = tiles
        me = g.y * 2 + g.c
        rows = pl.ds(pl.multiple_of(g.y * 48, 16), 48)
        self.g, self.u, self.tiles, self.rows, self.me = g, u, tiles, rows, me
        self.copies = []

        def copy(src, dst, device):
            self.copies.append(remote(src, dst, send, recv, base + len(self.copies), device))

        for k in range(1, 4):
            to = (me + k) % 4
            device = {"dp": g.z * 2 + g.x, "fsdp": to}
            block, half = self.qkv_place(to)
            copy(u.at[block], qkv.at[half, rows, :], device)
            copy(u.at[3], out.at[g.c, rows, :], device)
            copy(u.at[4 + to], up.at[g.c, rows, :], device)
        for k in range(1, 4):
            to = (g.z + k) % 4
            copy(u.at[8 + to], down.at[pl.ds(pl.multiple_of(g.z * 48, 16), 48), :], {"dp": to * 2 + g.x, "fsdp": me})

    def qkv_place(self, to):
        c = self.g.c
        middle = (to + 1) // 2 % 2
        return to - to // 3 - middle * c, middle + c - 2 * middle * c

    def start(self):
        start_all(self.copies)
        g, u = self.g, self.u
        qkv, out, up, down = self.tiles
        block, half = self.qkv_place(self.me)
        qkv[half, self.rows, :] = u[block]
        out[g.c, self.rows, :] = u[3]
        up[g.c, self.rows, :] = u[4 + self.me]
        down[pl.ds(pl.multiple_of(g.z * 48, 16), 48), :] = u[8 + g.z]

    def finish(self):
        arrived(self.copies)
        sent(self.copies)


TILES = [jax.ShapeDtypeStruct((2, 96, 384), jnp.bfloat16)] * 3 + [jax.ShapeDtypeStruct((192, 384), jnp.bfloat16)]


def meet_all(g, n_dp, n_fsdp):
    count = n_dp * n_fsdp
    me = (g.z * g.X + g.x) * n_fsdp + g.y * 2 + g.c
    sem = pltpu.get_barrier_semaphore()
    ranks = [(me + k) % count for k in range(1, count)]
    peers = [{"dp": rank // n_fsdp, "fsdp": rank % n_fsdp} for rank in ranks]
    for peer in peers:
        pl.semaphore_signal(sem, inc=1, device_id=peer, device_id_type=MESH)
    pl.semaphore_wait(sem, count - 1)
    return me, ranks, peers


def to_owners(n_dp, n_fsdp, blocks_of, u, small, collective_id):
    grid = Grid(n_dp, n_fsdp)
    count = n_dp * n_fsdp

    def kernel(of_ref, u_ref, small_ref, got, all_small, qkv, out, up, down, slots, send, recv):
        g = grid.here()
        me, ranks, peers = meet_all(g, n_dp, n_fsdp)

        def fill(n, carry):
            slots[n] = u_ref[of_ref[n]]
            return carry

        lax.fori_loop(0, count, fill, 0)
        copies = []
        for k, (rank, peer) in enumerate(zip(ranks, peers)):
            copies.append(remote(slots.at[rank], got.at[me], send, recv, k, peer))
        for k, peer in enumerate(peers):
            copies.append(remote(small_ref, all_small.at[me], send, recv, count - 1 + k, peer))
        start_all(copies)
        spread = Spread(g, u_ref, (qkv, out, up, down), send, recv, 2 * count - 2)
        spread.start()
        got[me] = slots[me]
        all_small[me] = small_ref[...]
        arrived(copies)
        sent(copies)
        spread.finish()

    lanes = 2 * count - 2 + 12
    return pl.pallas_call(
        kernel,
        out_shape=[jax.ShapeDtypeStruct((count,) + PIECE, jnp.bfloat16),
                   jax.ShapeDtypeStruct((count,) + small.shape, jnp.float32)] + TILES,
        in_specs=[pl.BlockSpec(memory_space=pltpu.SMEM), VM, VM],
        out_specs=[VM] * 6,
        scratch_shapes=[pltpu.VMEM((count,) + PIECE, jnp.bfloat16), pltpu.SemaphoreType.DMA((lanes,)),
                        pltpu.SemaphoreType.DMA((lanes,))],
        compiler_params=pltpu.CompilerParams(collective_id=collective_id, has_side_effects=True),
        name="to_owners",
    )(blocks_of, u, small)


def to_tiles(n_dp, n_fsdp, owners, pieces, collective_id):
    grid = Grid(n_dp, n_fsdp)
    count = n_dp * n_fsdp

    def kernel(owners_ref, pieces_ref, qkv, out, up, down, got, u, send, recv):
        g = grid.here()
        me, ranks, peers = meet_all(g, n_dp, n_fsdp)
        copies = [remote(pieces_ref.at[rank], got.at[me], send, recv, k, peer)
                  for k, (rank, peer) in enumerate(zip(ranks, peers))]
        start_all(copies)
        got[me] = pieces_ref[me]
        arrived(copies)

        def fill(n, carry):
            u[n] = got[owners_ref[n]]
            return carry

        lax.fori_loop(0, 12, fill, 0)
        spread = Spread(g, u, (qkv, out, up, down), send, recv, count - 1)
        spread.start()
        sent(copies)
        spread.finish()

    lanes = count - 1 + 12
    return pl.pallas_call(
        kernel,
        out_shape=TILES,
        in_specs=[pl.BlockSpec(memory_space=pltpu.SMEM), VM],
        out_specs=[VM] * 4,
        scratch_shapes=[pltpu.VMEM((count,) + PIECE, jnp.bfloat16), pltpu.VMEM((12,) + PIECE, jnp.bfloat16),
                        pltpu.SemaphoreType.DMA((lanes,)), pltpu.SemaphoreType.DMA((lanes,))],
        compiler_params=pltpu.CompilerParams(collective_id=collective_id, has_side_effects=True),
        name="to_tiles",
    )(owners, pieces)


def piece_rows(turned, z, x, y, c):
    if turned:
        return 192 * (2 * y + c) + 48 * z, 384 * x
    return 96 * (2 * z + x) + 48 * y, 384 * c


def places():
    return [(z, x, y, c) for z in range(4) for x in range(2) for y in range(2) for c in range(2)]


def precondition_kernel(flags, pieces, stats, roots, new_stats, steps, block, turned):
    own, down = flags[0], flags[1]

    @pl.when(own == 0)
    def _():
        new_stats[...] = stats[...]

    @pl.when(own == 1)
    def _():
        for kind in range(2):

            @pl.when(down == kind)
            def _():
                for n, place in enumerate(places()):
                    row, column = piece_rows(kind, *place)
                    block[row : row + 48, column : column + 384] = pieces[n]

        turned[...] = block[...].astype(jnp.float32).T.astype(jnp.bfloat16)
        new_stats[down] = 0.5 * stats[down] + 0.5 * last_dot(block[...], block[...])
        new_stats[1 - down] = 0.5 * stats[1 - down] + 0.5 * last_dot(turned[...], turned[...])
        left = plain_dot(roots[down].astype(jnp.bfloat16), block[...]).astype(jnp.bfloat16)
        block[...] = plain_dot(left, roots[1 - down].astype(jnp.bfloat16)).astype(jnp.bfloat16)
        for kind in range(2):

            @pl.when(down == kind)
            def _():
                for n, place in enumerate(places()):
                    row, column = piece_rows(kind, *place)
                    steps[n] = block[row : row + 48, column : column + 384]


def precondition(flags, pieces, stats, roots):
    return pl.pallas_call(
        precondition_kernel,
        out_shape=[jax.ShapeDtypeStruct(stats.shape, jnp.float32), jax.ShapeDtypeStruct(pieces.shape, jnp.bfloat16)],
        in_specs=[pl.BlockSpec(memory_space=pltpu.SMEM), VM, VM, VM],
        out_specs=[VM, VM],
        scratch_shapes=[pltpu.VMEM(stats.shape[1:], jnp.bfloat16)] * 2,
        compiler_params=pltpu.CompilerParams(vmem_limit_bytes=56 * 1024 * 1024),
        name="precondition",
    )(flags, pieces, stats, roots)


def block_grads_kernel(turned_blocks, left, right, out, sums, left_turned):
    @pl.when(pl.program_id(0) == 0)
    def _():
        left_turned[...] = left[...].astype(jnp.float32).T.astype(jnp.bfloat16)

    values = right[...].reshape(right.shape[-2:])
    grad = plain_dot(left_turned[...], values).astype(jnp.bfloat16)
    for z, x, y, c in places():
        row, column = piece_rows(turned_blocks, z, x, y, c)
        out[y, c, z, x] = grad[row : row + 48, column : column + 384]
    sums[...] = jnp.sum(values.astype(jnp.float32), axis=0).reshape(sums.shape)


def block_grads(left, right, turned_blocks):
    rows, d = left.shape
    if right.ndim == 3:
        count = right.shape[0]
        spec = pl.BlockSpec((1, rows, d), lambda b: (b, 0, 0))
    else:
        count = right.shape[1] // d
        spec = pl.BlockSpec((rows, d), lambda b: (0, b))
    return pl.pallas_call(
        partial(block_grads_kernel, turned_blocks),
        out_shape=[jax.ShapeDtypeStruct((2, 2, 4, 2, count * 48, 384), jnp.bfloat16),
                   jax.ShapeDtypeStruct((count, 1, d), jnp.float32)],
        grid=(count,),
        in_specs=[pl.BlockSpec((rows, d), lambda b: (0, 0)), spec],
        out_specs=[pl.BlockSpec((2, 2, 4, 2, 48, 384), lambda b: (0, 0, 0, 0, b, 0)),
                   pl.BlockSpec((1, 1, d), lambda b: (b, 0, 0))],
        scratch_shapes=[pltpu.VMEM((d, rows), jnp.bfloat16)],
        compiler_params=pltpu.CompilerParams(vmem_limit_bytes=56 * 1024 * 1024),
        name="block_grads",
    )(left, right)


D = 768
HEADS = 12
HD = 64
FF = 3072
BLOCKS = 12


masked_score = -1000000000.0
decay_rate = 0.5
step_rate = 1.0
small_rate = 0.3
highest = lax.Precision.HIGHEST


def broadcast(value, axis, source):
    kept = jnp.where(lax.axis_index(axis) == source, value, 0).astype(value.dtype)
    return lax.psum(kept, axis)


def layer_norm(values, scale_row, shift_row):
    center = values - jnp.mean(values, axis=-1, keepdims=True)
    spread = jnp.mean(center * center, axis=-1, keepdims=True)
    return center * lax.rsqrt(spread + 1e-06) * scale_row + shift_row


def unpack(small_params):
    pieces = [small_params[number * D : (number + 1) * D] for number in range(8)]
    return pieces + [small_params[8 * D : 8 * D + FF]]


def row_dot(left, right):
    return jnp.dot(left, right, preferred_element_type=jnp.float32)


def column_dot(left, right):
    return lax.dot_general(
        left, right, (((0,), (0,)), ((), ())), preferred_element_type=jnp.float32
    )


def transposed_dot(left, right):
    return lax.dot_general(
        left, right, (((1,), (1,)), ((), ())), preferred_element_type=jnp.float32
    )


def block_split(array, block_rows):
    slots = array.shape[-1]
    return array.reshape(HEADS, HD, slots // block_rows, block_rows).transpose(2, 0, 1, 3)


def block_join(array):
    return array.transpose(0, 3, 1, 2).reshape(-1, D)


def attend_clip(queries, key_rows, value_rows, length):
    slots = queries.shape[-1]
    block_rows = min(512, slots)
    score_scale = float(HD) ** (-0.5)
    visible = (jnp.arange(slots) < length)[None, None, :]

    def one_block(query_block):
        scores = (
            jnp.einsum("hdq,hdk->hqk", query_block, key_rows, preferred_element_type=jnp.float32)
            * score_scale
        )
        scores = jnp.where(visible, scores, masked_score)
        row_top = jnp.max(scores, axis=-1, keepdims=True)
        raised = jnp.exp(scores - row_top)
        row_total = jnp.sum(raised, axis=-1, keepdims=True)
        softmax_weights = (raised / row_total).astype(jnp.bfloat16)
        attended = jnp.einsum(
            "hqk,hdk->hdq", softmax_weights, value_rows, preferred_element_type=jnp.float32
        )
        return (attended.astype(jnp.bfloat16), (row_top + jnp.log(row_total))[:, :, 0])

    attended, log_totals = lax.map(one_block, block_split(queries, block_rows))
    return (block_join(attended), log_totals)


def attend_back(queries, key_rows, value_rows, length, log_totals, out_grads):
    slots = queries.shape[-1]
    block_rows = min(512, slots)
    score_scale = float(HD) ** (-0.5)
    visible = (jnp.arange(slots) < length)[None, None, :]

    def one_block(carry, pieces):
        key_grad, value_grad = carry
        query_block, grad_block, log_block = pieces
        scores = (
            jnp.einsum("hdq,hdk->hqk", query_block, key_rows, preferred_element_type=jnp.float32)
            * score_scale
        )
        scores = jnp.where(visible, scores, masked_score)
        softmax_weights = jnp.exp(scores - log_block[:, :, None])
        weight_grad = jnp.einsum(
            "hdq,hdk->hqk", grad_block, value_rows, preferred_element_type=jnp.float32
        )
        inner_sum = jnp.sum(softmax_weights * weight_grad, axis=-1, keepdims=True)
        score_grad = (softmax_weights * (weight_grad - inner_sum)).astype(jnp.bfloat16)
        query_grad = (
            jnp.einsum("hqk,hdk->hdq", score_grad, key_rows, preferred_element_type=jnp.float32)
            * score_scale
        )
        key_grad = (
            key_grad
            + jnp.einsum(
                "hqk,hdq->hdk", score_grad, query_block, preferred_element_type=jnp.float32
            )
            * score_scale
        )
        value_grad = value_grad + jnp.einsum(
            "hqk,hdq->hdk",
            softmax_weights.astype(jnp.bfloat16),
            grad_block,
            preferred_element_type=jnp.float32,
        )
        return ((key_grad, value_grad), query_grad)

    blank = jnp.zeros((HEADS, HD, slots), jnp.float32)
    (key_grad, value_grad), query_grad = lax.scan(
        one_block,
        (blank, blank),
        (block_split(queries, block_rows), block_split(out_grads, block_rows), log_totals),
    )
    key_rows_grad = key_grad.transpose(2, 0, 1).reshape(slots, D)
    value_rows_grad = value_grad.transpose(2, 0, 1).reshape(slots, D)
    return (block_join(query_grad), key_rows_grad, value_rows_grad)


def take_columns(operands, member, start):
    return lax.slice_in_dim(operands[member], start, start + D, axis=1)


def take_rows(operands, member, start):
    return lax.slice_in_dim(operands[member], start, start + D, axis=0)


def block_pickers():
    pickers = [partial(take_columns, member=0, start=column * D) for column in range(3)]
    pickers.append(partial(take_columns, member=1, start=0))
    pickers = pickers + [
        partial(take_columns, member=2, start=column * D) for column in range(FF // D)
    ]
    pickers = pickers + [
        partial(take_rows, member=3, start=column * D) for column in range(FF // D)
    ]
    return pickers


def fetch_update(update, root):
    return broadcast(update.astype(jnp.bfloat16), ("dp", "fsdp"), root).astype(update.dtype)


def band_tile(band, like, column_index):
    columns_here = like.shape[1]
    return lax.dynamic_slice_in_dim(band, column_index * columns_here, columns_here, 1)


def row_band(pieces, like, row_index):
    rows_here = like.shape[0]
    start = row_index * rows_here
    return jnp.concatenate(
        [lax.dynamic_slice_in_dim(piece, start, rows_here, 0) for piece in pieces], axis=1
    )


def stacked_band(pieces, like, row_index):
    rows_here = like.shape[0]
    start = row_index * rows_here
    owner_block = start // D
    picked = jnp.zeros((rows_here, D), jnp.float32)
    for number in range(len(pieces)):
        inside = jnp.clip(start - number * D, 0, D - rows_here)
        piece = lax.dynamic_slice_in_dim(pieces[number], inside, rows_here, 0)
        picked = jnp.where(owner_block == number, piece, picked)
    return picked


def local_any(
    tokens,
    counts,
    cotangent,
    qkv_weight,
    out_weight,
    up_weight,
    down_weight,
    small_params,
    statistics,
    inverse_roots,
    owners,
):
    clips_here = counts.shape[0]
    slots = tokens.shape[0] // clips_here
    qkv_low = qkv_weight.astype(jnp.bfloat16)
    out_low = out_weight.astype(jnp.bfloat16)
    up_low = up_weight.astype(jnp.bfloat16)
    down_low = down_weight.astype(jnp.bfloat16)
    qkv_cols, out_cols, up_cols, down_cols = (
        lax.all_gather(qkv_low, "fsdp", axis=1, tiled=True),
        lax.all_gather(out_low, "fsdp", axis=1, tiled=True),
        lax.all_gather(up_low, "fsdp", axis=1, tiled=True),
        lax.all_gather(down_low, "fsdp", axis=1, tiled=True),
    )
    qkv_full, out_full, up_full, down_full = (
        lax.all_gather(qkv_cols, "dp", axis=0, tiled=True),
        lax.all_gather(out_cols, "dp", axis=0, tiled=True),
        lax.all_gather(up_cols, "dp", axis=0, tiled=True),
        lax.all_gather(down_cols, "dp", axis=0, tiled=True),
    )
    (
        gain_one,
        shift_one,
        gain_two,
        shift_two,
        bias_query,
        bias_value,
        bias_out,
        bias_down,
        bias_up,
    ) = unpack(small_params)

    def heads_view(array):
        return array.reshape(clips_here, slots, HEADS, HD).transpose(0, 2, 3, 1)

    def clip_forward(clip_group):
        return attend_clip(clip_group[0], clip_group[1], clip_group[2], clip_group[3])

    def clip_backward(clip_group):
        return attend_back(
            clip_group[0], clip_group[1], clip_group[2], clip_group[3], clip_group[4], clip_group[5]
        )

    inputs = tokens.astype(jnp.float32)
    normed = layer_norm(inputs, gain_one, shift_one).astype(jnp.bfloat16)
    projected = row_dot(normed, qkv_full)
    queries = heads_view((projected[:, :D] + bias_query).astype(jnp.bfloat16))
    key_rows = heads_view(projected[:, D : 2 * D].astype(jnp.bfloat16))
    value_rows = heads_view((projected[:, 2 * D :] + bias_value).astype(jnp.bfloat16))
    attended, log_totals = lax.map(clip_forward, (queries, key_rows, value_rows, counts))
    attended = attended.reshape(-1, D)
    middle = inputs + (row_dot(attended, out_full) + bias_out)
    normed_two = layer_norm(middle, gain_two, shift_two).astype(jnp.bfloat16)
    hidden = row_dot(normed_two, up_full) + bias_up
    active = jax.nn.gelu(hidden, approximate=False).astype(jnp.bfloat16)
    layer_rows = (middle + row_dot(active, down_full) + bias_down).astype(jnp.bfloat16)
    qkv_part, out_part, up_part, down_part = (
        lax.all_gather(qkv_low, "fsdp", axis=1, tiled=True),
        lax.all_gather(out_low, "fsdp", axis=1, tiled=True),
        lax.all_gather(up_low, "fsdp", axis=1, tiled=True),
        lax.all_gather(down_low, "fsdp", axis=1, tiled=True),
    )
    qkv_back, out_back, up_back, down_back = (
        lax.all_gather(qkv_part, "dp", axis=0, tiled=True),
        lax.all_gather(out_part, "dp", axis=0, tiled=True),
        lax.all_gather(up_part, "dp", axis=0, tiled=True),
        lax.all_gather(down_part, "dp", axis=0, tiled=True),
    )
    grad_down = column_dot(active, cotangent)
    grad_bias_down = jnp.sum(cotangent.astype(jnp.float32), axis=0)
    active_grad = transposed_dot(cotangent, down_back)
    unused_value, gelu_pull = jax.vjp(partial(jax.nn.gelu, approximate=False), hidden)
    hidden_grad = gelu_pull(active_grad)[0].astype(jnp.bfloat16)
    grad_up = column_dot(normed_two, hidden_grad)
    grad_bias_up = jnp.sum(hidden_grad.astype(jnp.float32), axis=0)
    normed_two_grad = transposed_dot(hidden_grad, up_back)
    unused_norm, norm_two_pull = jax.vjp(layer_norm, middle, gain_two, shift_two)
    middle_grad, grad_gain_two, grad_shift_two = norm_two_pull(normed_two_grad)
    middle_grad = middle_grad + cotangent.astype(jnp.float32)
    branch_grad = middle_grad.astype(jnp.bfloat16)
    grad_out = column_dot(attended, branch_grad)
    grad_bias_out = jnp.sum(branch_grad.astype(jnp.float32), axis=0)
    attended_grad = transposed_dot(branch_grad, out_back).astype(jnp.bfloat16)
    query_grad, key_grad, value_grad = lax.map(
        clip_backward,
        (queries, key_rows, value_rows, counts, log_totals, heads_view(attended_grad)),
    )
    projected_grad = (
        jnp.concatenate([query_grad, key_grad, value_grad], axis=-1)
        .reshape(-1, 3 * D)
        .astype(jnp.bfloat16)
    )
    grad_qkv = column_dot(normed, projected_grad)
    grad_bias_query = jnp.sum(projected_grad[:, :D].astype(jnp.float32), axis=0)
    grad_bias_value = jnp.sum(projected_grad[:, 2 * D :].astype(jnp.float32), axis=0)
    normed_grad = transposed_dot(projected_grad, qkv_back)
    unused_first, norm_one_pull = jax.vjp(layer_norm, inputs, gain_one, shift_one)
    input_rows_grad, grad_gain_one, grad_shift_one = norm_one_pull(normed_grad)
    input_grad = (middle_grad + input_rows_grad).astype(jnp.bfloat16)
    small_grad = jnp.concatenate(
        [
            grad_gain_one,
            grad_shift_one,
            grad_gain_two,
            grad_shift_two,
            grad_bias_query,
            grad_bias_value,
            grad_bias_out,
            grad_bias_down,
            grad_bias_up,
        ]
    )
    row_qkv, row_out, row_up, row_down, row_small = (
        lax.psum_scatter(
            grad_qkv.astype(jnp.bfloat16), "dp", scatter_dimension=0, tiled=True
        ).astype(jnp.float32),
        lax.psum_scatter(
            grad_out.astype(jnp.bfloat16), "dp", scatter_dimension=0, tiled=True
        ).astype(jnp.float32),
        lax.psum_scatter(
            grad_up.astype(jnp.bfloat16), "dp", scatter_dimension=0, tiled=True
        ).astype(jnp.float32),
        lax.psum_scatter(
            grad_down.astype(jnp.bfloat16), "dp", scatter_dimension=0, tiled=True
        ).astype(jnp.float32),
        lax.psum_scatter(
            small_grad.astype(jnp.bfloat16), "dp", scatter_dimension=0, tiled=True
        ).astype(jnp.float32),
    )
    shard_qkv, shard_out, shard_up, shard_down, shard_small = (
        lax.psum_scatter(
            row_qkv.astype(jnp.bfloat16), "fsdp", scatter_dimension=1, tiled=True
        ).astype(jnp.float32),
        lax.psum_scatter(
            row_out.astype(jnp.bfloat16), "fsdp", scatter_dimension=1, tiled=True
        ).astype(jnp.float32),
        lax.psum_scatter(
            row_up.astype(jnp.bfloat16), "fsdp", scatter_dimension=1, tiled=True
        ).astype(jnp.float32),
        lax.psum_scatter(
            row_down.astype(jnp.bfloat16), "fsdp", scatter_dimension=1, tiled=True
        ).astype(jnp.float32),
        lax.psum_scatter(
            row_small.astype(jnp.bfloat16), "fsdp", scatter_dimension=0, tiled=True
        ).astype(jnp.float32),
    )
    band_qkv, band_out, band_up, band_down, band_small = (
        lax.all_gather(shard_qkv.astype(jnp.bfloat16), "fsdp", axis=1, tiled=True).astype(
            shard_qkv.dtype
        ),
        lax.all_gather(shard_out.astype(jnp.bfloat16), "fsdp", axis=1, tiled=True).astype(
            shard_out.dtype
        ),
        lax.all_gather(shard_up.astype(jnp.bfloat16), "fsdp", axis=1, tiled=True).astype(
            shard_up.dtype
        ),
        lax.all_gather(shard_down.astype(jnp.bfloat16), "fsdp", axis=1, tiled=True).astype(
            shard_down.dtype
        ),
        lax.all_gather(shard_small.astype(jnp.bfloat16), "fsdp", axis=0, tiled=True).astype(
            shard_small.dtype
        ),
    )
    rank = lax.axis_index(("dp", "fsdp"))
    row_index = lax.axis_index("dp")
    column_index = lax.axis_index("fsdp")
    numbers = jnp.arange(BLOCKS, dtype=jnp.int32)
    matches = owners == rank
    mine = jnp.sum(jnp.where(matches, numbers, 0))
    owning = jnp.any(matches)

    def update_slot(gradient):
        left_stat = decay_rate * statistics[0, 0] + (1.0 - decay_rate) * jnp.dot(
            gradient, gradient.T, precision=highest, preferred_element_type=jnp.float32
        )
        right_stat = decay_rate * statistics[0, 1] + (1.0 - decay_rate) * jnp.dot(
            gradient.T, gradient, precision=highest, preferred_element_type=jnp.float32
        )
        left_step = jnp.dot(
            inverse_roots[0, 0], gradient, precision=highest, preferred_element_type=jnp.float32
        )
        update = jnp.dot(
            left_step, inverse_roots[0, 1], precision=highest, preferred_element_type=jnp.float32
        )
        return (jnp.stack([left_stat, right_stat])[None], update)

    def keep_slot(gradient):
        return (statistics, jnp.zeros((D, D), jnp.float32))

    whole_qkv, whole_out, whole_up, whole_down, whole_small = (
        lax.all_gather(band_qkv.astype(jnp.bfloat16), "dp", axis=0, tiled=True).astype(
            band_qkv.dtype
        ),
        lax.all_gather(band_out.astype(jnp.bfloat16), "dp", axis=0, tiled=True).astype(
            band_out.dtype
        ),
        lax.all_gather(band_up.astype(jnp.bfloat16), "dp", axis=0, tiled=True).astype(
            band_up.dtype
        ),
        lax.all_gather(band_down.astype(jnp.bfloat16), "dp", axis=0, tiled=True).astype(
            band_down.dtype
        ),
        lax.all_gather(band_small.astype(jnp.bfloat16), "dp", axis=0, tiled=True).astype(
            band_small.dtype
        ),
    )
    gradient = lax.switch(mine, block_pickers(), (whole_qkv, whole_out, whole_up, whole_down))
    new_statistics, update = lax.cond(owning, update_slot, keep_slot, gradient)
    arrivals = []
    for number in range(BLOCKS):
        arrivals.append(fetch_update(update, owners[number]))
    tile_qkv = band_tile(row_band(arrivals[0:3], qkv_weight, row_index), qkv_weight, column_index)
    tile_out = band_tile(row_band(arrivals[3:4], out_weight, row_index), out_weight, column_index)
    tile_up = band_tile(
        row_band(arrivals[4 : 4 + FF // D], up_weight, row_index), up_weight, column_index
    )
    tile_down = band_tile(
        stacked_band(arrivals[4 + FF // D :], down_weight, row_index), down_weight, column_index
    )
    new_qkv = qkv_weight - step_rate * tile_qkv
    new_out = out_weight - step_rate * tile_out
    new_up = up_weight - step_rate * tile_up
    new_down = down_weight - step_rate * tile_down
    new_small = small_params - small_rate * whole_small * lax.rsqrt(
        jnp.mean(whole_small * whole_small) + 1e-06
    )
    return (
        layer_rows,
        input_grad,
        shard_qkv,
        shard_out,
        shard_up,
        shard_down,
        whole_small,
        new_statistics,
        new_qkv,
        new_out,
        new_up,
        new_down,
        new_small,
    )


def local_staged(
    sizes,
    tokens,
    counts,
    cotangent,
    qkv_weight,
    out_weight,
    up_weight,
    down_weight,
    small_params,
    statistics,
    inverse_roots,
    owners,
):
    n_dp, n_fsdp = sizes
    qkv_low = qkv_weight.astype(jnp.bfloat16)
    later = (
        out_weight.astype(jnp.bfloat16),
        up_weight.astype(jnp.bfloat16),
        down_weight.astype(jnp.bfloat16).T,
    )
    (
        gain_one,
        shift_one,
        gain_two,
        shift_two,
        bias_query,
        bias_value,
        bias_out,
        bias_down,
        bias_up,
    ) = unpack(small_params)
    (qkv_pieces,) = gather_all(n_dp, n_fsdp, (qkv_low,), ("j",), 1)
    qkv_full = whole_of(qkv_pieces)
    inputs = tokens.astype(jnp.float32)
    normed = layer_norm(inputs, gain_one, shift_one).astype(jnp.bfloat16)
    bias_qkv = jnp.concatenate([bias_query, jnp.zeros((D,), jnp.float32), bias_value])
    projected = (row_dot(normed, qkv_full) + bias_qkv).astype(jnp.bfloat16)
    attended, log_totals, out_pieces, up_pieces, down_pieces = attend_gather(
        n_dp, n_fsdp, counts, projected, later, ("j", "j", "i"), FORWARD_PLAN, 2
    )
    out_full, up_full, down_full_t = whole_of(out_pieces), whole_of(up_pieces), whole_of(down_pieces)
    middle = inputs + (row_dot(attended, out_full) + bias_out)
    normed_two = layer_norm(middle, gain_two, shift_two).astype(jnp.bfloat16)
    hidden = row_dot(normed_two, up_full) + bias_up
    active = jax.nn.gelu(hidden, approximate=False).astype(jnp.bfloat16)
    layer_rows = (middle + transposed_dot(active, down_full_t) + bias_down).astype(jnp.bfloat16)
    grad_bias_down = jnp.sum(cotangent.astype(jnp.float32), axis=0)
    active_grad = row_dot(cotangent, down_full_t)
    unused_value, gelu_pull = jax.vjp(partial(jax.nn.gelu, approximate=False), hidden)
    hidden_grad = gelu_pull(active_grad)[0].astype(jnp.bfloat16)
    normed_two_grad = transposed_dot(hidden_grad, up_full)
    unused_norm, norm_two_pull = jax.vjp(layer_norm, middle, gain_two, shift_two)
    middle_grad, grad_gain_two, grad_shift_two = norm_two_pull(normed_two_grad)
    middle_grad = middle_grad + cotangent.astype(jnp.float32)
    branch_grad = middle_grad.astype(jnp.bfloat16)
    attended_grad = transposed_dot(branch_grad, out_full).astype(jnp.bfloat16)
    split_down, unused_sums = block_grads(cotangent, active, True)
    split_up, grad_bias_up = block_grads(normed_two, hidden_grad, False)
    split_out, grad_bias_out = block_grads(attended, branch_grad, False)
    projected_grad, mine_down, mine_up, mine_out = attend_back_scatter(
        n_dp, n_fsdp, counts, projected, attended, attended_grad, log_totals,
        (split_down, split_up, split_out), BACKWARD_PLAN, 3,
    )
    split_qkv, grad_bias_qkv = block_grads(normed, projected_grad, False)
    normed_grad = sum(
        transposed_dot(projected_grad[part], qkv_full[:, part * D : (part + 1) * D]) for part in range(3)
    )
    unused_first, norm_one_pull = jax.vjp(layer_norm, inputs, gain_one, shift_one)
    input_rows_grad, grad_gain_one, grad_shift_one = norm_one_pull(normed_grad)
    input_grad = (middle_grad + input_rows_grad).astype(jnp.bfloat16)
    small_grad = jnp.concatenate(
        [
            grad_gain_one,
            grad_shift_one,
            grad_gain_two,
            grad_shift_two,
            grad_bias_qkv[0, 0],
            grad_bias_qkv[2, 0],
            grad_bias_out.reshape(-1),
            grad_bias_down,
            grad_bias_up.reshape(-1),
        ]
    )
    devices = n_dp * n_fsdp
    small_split = jnp.pad(small_grad.astype(jnp.bfloat16).reshape(devices, -1), ((0, 0), (0, 2048 - 9216 // devices)))
    small_split = small_split.reshape(4, 2, 2, 2, 16, 128).transpose(2, 3, 0, 1, 4, 5)
    mine_qkv, mine_small = scatter_all(n_dp, n_fsdp, (split_qkv, small_split), ("j", "j"), 4)
    mine = jnp.concatenate([mine_qkv.astype(jnp.bfloat16), mine_out, mine_up, mine_down], axis=0)
    numbers = jnp.arange(BLOCKS, dtype=jnp.int32)
    ranks = jnp.arange(devices, dtype=jnp.int32)
    blocks_of = jnp.sum(jnp.where(owners[None, :] == ranks[:, None], numbers[None, :], 0), axis=1).astype(jnp.int32)
    gathered, small_pieces, *grad_tiles = to_owners(
        n_dp, n_fsdp, blocks_of, mine.reshape(BLOCKS, 48, 384), mine_small, 5
    )
    rank = lax.axis_index(("dp", "fsdp"))
    owning = jnp.any(owners == rank)
    flags = jnp.stack([owning, blocks_of[rank] >= 4 + FF // D]).astype(jnp.int32)
    new_statistics, steps = precondition(flags, gathered, statistics[0], inverse_roots[0])
    step_tiles = to_tiles(n_dp, n_fsdp, owners, steps, 6)
    column_index = lax.axis_index("fsdp")
    shard_qkv, shard_out, shard_up, shard_down = tiles_of(grad_tiles, column_index)
    tile_qkv, tile_out, tile_up, tile_down = tiles_of(step_tiles, column_index)
    new_qkv = qkv_weight - step_rate * tile_qkv
    new_out = out_weight - step_rate * tile_out
    new_up = up_weight - step_rate * tile_up
    new_down = down_weight - step_rate * tile_down
    whole_small = small_pieces.reshape(devices, 2048)[:, : 9216 // devices].reshape(-1)
    new_small = small_params - small_rate * whole_small * lax.rsqrt(
        jnp.mean(whole_small * whole_small) + 1e-06
    )
    return (
        layer_rows,
        input_grad,
        shard_qkv,
        shard_out,
        shard_up,
        shard_down,
        whole_small,
        new_statistics[None],
        new_qkv,
        new_out,
        new_up,
        new_down,
        new_small,
    )


def whole_of(pieces):
    rows, columns = pieces.shape[-2:]
    folded = pieces.reshape(pieces.shape[0] * pieces.shape[1], -1, columns)
    return folded.transpose(1, 0, 2).reshape(folded.shape[1], -1)


def tiles_of(tiles, column_index):
    qkv, out, up, down = tiles
    band = lambda halves: halves.astype(jnp.float32).transpose(1, 0, 2).reshape(96, D)
    qkv, out = band(qkv), band(out)
    qkv = jnp.where(column_index % 2 == 1, qkv[:, 192:], qkv[:, : D - 192])
    out = lax.dynamic_slice_in_dim(out, column_index * 192, 192, 1)
    return qkv, out, band(up), down.astype(jnp.float32).T


def solution(mesh):
    placed = (
        P(("dp", "fsdp"), None),
        P(("dp", "fsdp")),
        P(("dp", "fsdp"), None),
        P("dp", "fsdp"),
        P("dp", "fsdp"),
        P("dp", "fsdp"),
        P("dp", "fsdp"),
        P(),
        P(("dp", "fsdp"), None, None, None),
        P(("dp", "fsdp"), None, None, None),
        P(),
    )
    sizes = (mesh.shape["dp"], mesh.shape["fsdp"])
    local = partial(local_staged, sizes) if sizes == (8, 4) else local_any
    return jax.shard_map(
        local,
        mesh=mesh,
        in_specs=placed,
        out_specs=(
            P(("dp", "fsdp"), None),
            P(("dp", "fsdp"), None),
            P("dp", "fsdp"),
            P("dp", "fsdp"),
            P("dp", "fsdp"),
            P("dp", "fsdp"),
            P(),
            P(("dp", "fsdp"), None, None, None),
            P("dp", "fsdp"),
            P("dp", "fsdp"),
            P("dp", "fsdp"),
            P("dp", "fsdp"),
            P(),
        ),
        check_vma=False,
    )
```

```python
from functools import partial

import jax
import jax.numpy as jnp
from jax import lax
from jax.experimental import pallas as pl
from jax.experimental.pallas import tpu as pltpu
from jax.sharding import PartitionSpec as P

MESH = pl.DeviceIdType.MESH
ANY = pl.BlockSpec(memory_space=pl.ANY)
VM = pl.BlockSpec(memory_space=pltpu.VMEM)


class Grid:
    def __init__(self, n_dp, n_fsdp):
        self.Z = 4
        self.X = n_dp // 4
        self.Y = n_fsdp // 2
        self.swap = self.X == self.Y
        self.A, self.B = self.X, self.Y

    def here(self):
        dp, fs = lax.axis_index("dp"), lax.axis_index("fsdp")
        self.z, self.x = dp // self.X, dp % self.X
        self.y, self.c = fs // 2, fs % 2
        if self.swap:
            self.a = self.x + self.c * (self.y - self.x)
            self.b = self.y + self.c * (self.x - self.y)
        else:
            self.a, self.b = self.x, self.y
        return self

    def xy(self, a, b, c):
        if self.swap:
            return a + c * (b - a), b + c * (a - b)
        return a, b

    def device(self, z, a, b, c, frame=None):
        x, y = self.xy(a, b, self.c if frame is None else frame)
        return {"dp": z * self.X + x, "fsdp": y * 2 + c}

    def shape(self, order, r, w):
        if order == "j":
            return (self.Y, 2, self.Z, self.X, r, w)
        return (self.Z, self.X, self.Y, 2, r, w)

    def at(self, ref, order, y, c, z, x):
        return ref.at[y, c, z, x] if order == "j" else ref.at[z, x, y, c]

    def peers(self):
        out = [self.device((self.z + k) % self.Z, self.a, self.b, self.c) for k in range(1, self.Z)]
        out += [self.device(self.z, (self.a + k) % self.A, self.b, self.c) for k in range(1, self.A)]
        out += [self.device(self.z, self.a, (self.b + k) % self.B, self.c) for k in range(1, self.B)]
        out += [{"dp": self.z * self.X + self.x, "fsdp": self.y * 2 + 1 - self.c}]
        return out

    def barrier(self):
        sem = pltpu.get_barrier_semaphore()
        peers = self.peers()
        for peer in peers:
            pl.semaphore_signal(sem, inc=1, device_id=peer, device_id_type=MESH)
        pl.semaphore_wait(sem, len(peers))


def remote(src, dst, send, recv, slot, device):
    return pltpu.make_async_remote_copy(
        src_ref=src, dst_ref=dst, send_sem=send.at[slot], recv_sem=recv.at[slot], device_id=device, device_id_type=MESH
    )


def start_all(copies):
    for copy in copies:
        copy.start()


def arrived(copies):
    for copy in copies:
        copy.wait_recv()


def sent(copies):
    for copy in copies:
        copy.wait_send()


class Copies:
    def __init__(self, send, recv):
        self.send, self.recv, self.slot = send, recv, 0

    def add(self, group, describe):
        group.append((self.slot, describe))
        self.slot += 1

    def made(self, group):
        out = []
        for slot, describe in group:
            start, end, device = describe()
            out.append(remote(start, end, self.send, self.recv, slot, device))
        return out

    def start(self, group):
        start_all(self.made(group))

    def arrived(self, group):
        arrived(self.made(group))

    def sent(self, group):
        sent(self.made(group))


class Gather:
    def __init__(self, g, order, path, rows, src, out, local, send, recv):
        size = {"z": g.Z, "a": g.A, "b": g.B}
        self.copies = Copies(send, recv)

        def at(name, shift):
            place = {"z": g.z, "a": g.a, "b": g.b}[name]
            return (place + shift + size[name]) % size[name] if shift else place

        def piece(cell):
            where = {name: (at(name, value[1]) if isinstance(value, tuple) else value) for name, value in cell.items()}
            x, y = g.xy(where["a"], where["b"], g.c)
            return g.at(out, order, y, g.c, where["z"], x).at[..., rows, :]

        own_cell = {"z": ("own", 0), "a": ("own", 0), "b": ("own", 0)}

        def cells(full):
            out = [dict(own_cell)]
            for axis in full:
                if axis == "z":
                    out = [dict(cell, z=slice(None)) for cell in out]
                else:
                    out = [dict(cell, **{axis: n}) for cell in out for n in range(size[axis])]
            return out

        def near():
            return {"dp": g.z * g.X + g.x, "fsdp": g.y * 2 + 1 - g.c}

        def far(axis, k):
            return g.device(*[at(name, k if name == axis else 0) for name in "zab"], g.c)

        def own():
            return src.at[rows, :]

        self.own = lambda: pltpu.make_async_copy(own(), piece(own_cell), local)
        self.stages, self.near = [], [[]]
        self.copies.add(self.near[0], lambda: (own(), piece(own_cell), near()))
        full = ""
        for axis in path:
            self.stages.append([])
            self.near.append([])
            for cell in cells(full):
                for k in range(1, size[axis]):
                    from_src = not full
                    self.copies.add(self.stages[-1], lambda cell=cell, k=k, axis=axis, from_src=from_src: (
                        own() if from_src else piece(cell), piece(cell), far(axis, k)))
                    came = dict(cell, **{axis: ("own", -k)})
                    self.copies.add(self.near[-1], lambda came=came: (piece(came), piece(came), near()))
            full += axis

    @staticmethod
    def slots(g):
        zab = (g.Z - 1) + (g.A - 1) + g.A * (g.B - 1)
        abz = (g.A - 1) + g.A * (g.B - 1) + g.A * g.B * (g.Z - 1)
        return 1 + 2 * max(zab, abz)

    def step(self, number):
        if number == 0:
            self.own().start()
        else:
            if number == 1:
                self.own().wait()
            self.copies.arrived(self.stages[number - 1])
        if number < 3:
            self.copies.start(self.stages[number])
        self.copies.start(self.near[number])

    def pause(self):
        self.own().wait()
        for group in (self.stages[0], self.near[0]):
            self.copies.arrived(group)
            self.copies.sent(group)

    def resume(self):
        self.copies.start(self.stages[1])
        self.copies.start(self.near[1])

    def finish(self, first=0):
        for group in self.near[first:]:
            self.copies.arrived(group)
        for group in self.near[first:] + self.stages[first:]:
            self.copies.sent(group)


class Scatter:
    def __init__(self, g, order, path, rows, src, bufs, send, recv):
        self.g, self.path, self.order, self.rows, self.src = g, path, order, rows, src
        self.work = bufs[0]
        self.recv = dict(zip(path, bufs[1:]))
        work = self.work
        size = {"z": g.Z, "a": g.A, "b": g.B}
        self.size = size
        self.copies = Copies(send, recv)
        places = lambda: {"z": g.z, "a": g.a, "b": g.b}

        def other(b, a):
            x, y = g.xy(a, b, 1 - g.c)
            return (g.at(src, order, y, 1 - g.c, slice(None), x).at[:, rows, :], work.at[b, :, a],
                    {"dp": g.z * g.X + g.x, "fsdp": g.y * 2 + 1 - g.c})

        def onward(axis, k, done):
            place = places()
            to = dict(place, **{axis: (place[axis] + k) % size[axis]})
            where = {name: (place[name] if name in done else slice(None)) for name in "bza"}
            where[axis] = to[axis]
            return (work.at[where["b"], where["z"], where["a"]], self.recv[axis].at[k - 1],
                    g.device(to["z"], to["a"], to["b"], g.c))

        self.stages = [[]]
        for b in range(g.B):
            for a in range(g.A):
                self.copies.add(self.stages[0], partial(other, b, a))
        done = ""
        for axis in path:
            self.stages.append([])
            for k in range(1, size[axis]):
                self.copies.add(self.stages[-1], partial(onward, axis, k, done))
            done += axis

    @staticmethod
    def slots(g):
        return g.A * g.B + (g.B - 1) + (g.A - 1) + (g.Z - 1)

    @staticmethod
    def scratch(g, path, r, w):
        size = {"z": g.Z, "a": g.A, "b": g.B}
        out = [pltpu.VMEM((g.B, g.Z, g.A, r, w), jnp.bfloat16)]
        done = ""
        for axis in path:
            done += axis
            out.append(pltpu.VMEM((size[axis] - 1,) + tuple(size[n] for n in "bza" if n not in done) + (r, w), jnp.bfloat16))
        return out

    def _cell(self, index, done):
        place = {"z": self.g.z, "a": self.g.a, "b": self.g.b}
        return [place[n] if n in done else index[n] for n in "bza"]

    def _add(self, number):
        g, done = self.g, self.path[:number]
        left = [n for n in "bza" if n not in done]
        total = 1
        for name in left:
            total *= self.size[name]

        def add(n, carry):
            index = {}
            for name in reversed(left):
                index[name] = n % self.size[name]
                n = n // self.size[name]
            b, z, a = self._cell(index, done)
            if number == 0:
                x, y = g.xy(a, b, g.c)
                mine = g.at(self.src, self.order, y, g.c, z, x)[self.rows, :]
                summed = self.work[b, z, a].astype(jnp.float32) + mine.astype(jnp.float32)
            else:
                summed = self._sum(number, b, z, a, [index[name] for name in left])
            self.work[b, z, a] = summed.astype(jnp.bfloat16)
            return carry

        lax.fori_loop(0, total, add, 0)

    def _sum(self, number, b, z, a, index):
        axis = self.path[number - 1]
        summed = self.work[b, z, a].astype(jnp.float32)
        for k in range(self.size[axis] - 1):
            summed = summed + self.recv[axis][tuple([k] + index)].astype(jnp.float32)
        return summed

    def step(self, number):
        if number > 0:
            self.copies.arrived(self.stages[number - 1])
            self._add(number - 1)
        self.copies.start(self.stages[number])

    def total(self):
        self.copies.arrived(self.stages[3])
        return self._sum(3, self.g.b, self.g.z, self.g.a, [])

    def finish(self):
        for group in self.stages:
            self.copies.sent(group)


GATHER_PATHS = ("zab", "abz")
SCATTER_PATHS = ("baz", "zba")


def row_parts(rows, share=0):
    second = rows * share // 6 // 16 * 16
    parts = [(0, pl.ds(0, rows - second))]
    return parts + ([(1, pl.ds(rows - second, second))] if second else [])


def job_list(sizes, share=0):
    return [(n, path, rows) for n, (r, _) in enumerate(sizes) for path, rows in row_parts(r, share)]


def rounds(jobs, last):
    return [(n, step) for step in range(last + 1) for n in range(len(jobs))]


def gather_scratch(g, count):
    lanes = Gather.slots(g)
    dma = pltpu.SemaphoreType.DMA
    return [dma((count,)), dma((count, lanes)), dma((count, lanes))]


def gather_jobs(g, orders, jobs, ins, outs, scratch):
    local, send, recv = scratch
    return [Gather(g, orders[n], GATHER_PATHS[path], rows, ins[n], outs[n], local.at[j], send.at[j], recv.at[j])
            for j, (n, path, rows) in enumerate(jobs)]


def gather_first(n_dp, n_fsdp, shards, orders, share, collective_id):
    grid = Grid(n_dp, n_fsdp)
    count = len(shards)
    jobs = job_list([shards[0].shape]) + [(n + 1, p, r) for n, p, r in job_list([s.shape for s in shards[1:]], share)]

    def kernel(*refs):
        g = grid.here()
        g.barrier()
        whole, *others = gather_jobs(g, orders, jobs, refs[:count], refs[count : 2 * count], refs[2 * count :])
        whole.step(0)
        whole.step(1)
        for job in others:
            job.step(0)
        whole.step(2)
        whole.step(3)
        for job in others:
            job.pause()
        whole.finish()

    return pl.pallas_call(
        kernel,
        out_shape=[jax.ShapeDtypeStruct(grid.shape(o, *s.shape), s.dtype) for s, o in zip(shards, orders)],
        in_specs=[ANY] * count,
        out_specs=[ANY] * count,
        scratch_shapes=gather_scratch(grid, len(jobs)),
        compiler_params=pltpu.CompilerParams(collective_id=collective_id, has_side_effects=True),
        name="gather_first",
    )(*shards)


def scatter_scratch(g, sizes, jobs):
    out = []
    for n, path, rows in jobs:
        out += Scatter.scratch(g, SCATTER_PATHS[path], rows.size, sizes[n][1])
    dma = pltpu.SemaphoreType.DMA
    lanes = Scatter.slots(g)
    return out + [dma((len(jobs), lanes)), dma((len(jobs), lanes))]


def scatter_jobs(g, orders, jobs, ins, scratch):
    send, recv = scratch[4 * len(jobs) :]
    return [Scatter(g, orders[n], SCATTER_PATHS[path], rows, ins[n], scratch[4 * j : 4 * j + 4], send.at[j], recv.at[j])
            for j, (n, path, rows) in enumerate(jobs)]


def scatter_all(n_dp, n_fsdp, wholes, orders, collective_id, dtype=jnp.float32):
    grid = Grid(n_dp, n_fsdp)
    count = len(wholes)
    sizes = [w.shape[-2:] for w in wholes]
    jobs = job_list(sizes, 2)

    def kernel(*refs):
        ins, outs, scratch = refs[:count], refs[count : 2 * count], refs[2 * count :]
        g = grid.here()
        g.barrier()
        work = scatter_jobs(g, orders, jobs, ins, scratch)
        for j, step in rounds(jobs, 3):
            work[j].step(step)
        for job, (n, path, rows) in zip(work, jobs):
            outs[n][rows, :] = job.total().astype(dtype)
        for job in work:
            job.finish()

    return pl.pallas_call(
        kernel,
        out_shape=[jax.ShapeDtypeStruct(s, dtype) for s in sizes],
        in_specs=[VM] * count,
        out_specs=[VM] * count,
        scratch_shapes=scatter_scratch(grid, sizes, jobs),
        compiler_params=pltpu.CompilerParams(collective_id=collective_id, has_side_effects=True,
                                             vmem_limit_bytes=60 * 1024 * 1024),
        name="scatter_all",
    )(*wholes)


HEAD = 64
PAIR = 128


def last_dot(left, right):
    return lax.dot_general(left, right, (((1,), (1,)), ((), ())), preferred_element_type=jnp.float32)


def plain_dot(left, right):
    return lax.dot_general(left, right, (((1,), (0,)), ((), ())), preferred_element_type=jnp.float32)


def attend_block(length, start, size, q_heads, k_ref, v_turned, o_ref, lse_ref):
    slots = k_ref.shape[0]
    half = slots // 2
    keys = k_ref[...]
    key_index = lax.broadcasted_iota(jnp.int32, (slots - half, size), 0) + half
    scores, tops = [], []
    for head in range(2):
        q = q_heads[head, pl.ds(start, size), :]
        low = last_dot(keys[:half], q)
        high = jnp.where(key_index < length, last_dot(keys[half:], q), -1000000000.0)
        tops.append(jnp.maximum(jnp.max(low, axis=0, keepdims=True), jnp.max(high, axis=0, keepdims=True)))
        scores.append((low, high))
    raised = [[jnp.exp(s - tops[head]).astype(jnp.bfloat16) for s in scores[head]] for head in range(2)]
    parts = []
    for head in range(2):
        summed = plain_dot(v_turned[head][:, :half], raised[head][0])
        summed = summed + plain_dot(v_turned[head][:, half:], raised[head][1])
        mine = summed[head * HEAD : (head + 1) * HEAD]
        total = summed[(1 - head) * HEAD : (1 - head) * HEAD + 1]
        parts.append(mine * (1.0 / total))
        lse_ref[head, pl.ds(start, size)] = (tops[head] + jnp.log(total))[0]
    o_ref[pl.ds(start, size), :] = jnp.concatenate(parts, axis=0).T.astype(jnp.bfloat16)


def attend_prepare(q_ref, v_ref, q_heads, v_turned):
    slots = q_ref.shape[0]
    lane = lax.broadcasted_iota(jnp.int32, (slots, PAIR), 1)
    row = lax.broadcasted_iota(jnp.int32, (PAIR, slots), 0)
    q = q_ref[...].astype(jnp.float32) * (HEAD ** (-0.5))
    v = v_ref[...].astype(jnp.float32).T
    for head in range(2):
        q_heads[head] = jnp.where(lane // HEAD == head, q, 0.0).astype(jnp.bfloat16)
        v_turned[head] = jnp.where(row // HEAD == head, v, 1.0).astype(jnp.bfloat16)


def attend_kernel(size, count_ref, q_ref, k_ref, v_ref, o_ref, lse_ref, q_heads, v_turned):
    attend_prepare(q_ref, v_ref, q_heads, v_turned)
    length = count_ref[0]

    def step(n, carry):
        attend_block(length, pl.multiple_of(n * size, size), size, q_heads, k_ref, v_turned, o_ref, lse_ref.at[0])
        return carry

    lax.fori_loop(0, q_ref.shape[0] // size, step, 0)


def attend(counts, projected, size=256):
    slots, width = projected.shape
    d = width // 3
    pairs = d // PAIR
    spec = lambda part: pl.BlockSpec((slots, PAIR), lambda p, n, part=part: (0, part * pairs + p))
    return pl.pallas_call(
        partial(attend_kernel, size),
        out_shape=[jax.ShapeDtypeStruct((slots, d), jnp.bfloat16),
                   jax.ShapeDtypeStruct((pairs, 2, slots), jnp.float32)],
        grid_spec=pltpu.PrefetchScalarGridSpec(
            num_scalar_prefetch=1, grid=(pairs,),
            in_specs=[spec(0), spec(1), spec(2)],
            out_specs=[pl.BlockSpec((slots, PAIR), lambda p, n: (0, p)),
                       pl.BlockSpec((1, 2, slots), lambda p, n: (p, 0, 0))],
            scratch_shapes=[pltpu.VMEM((2, slots, PAIR), jnp.bfloat16), pltpu.VMEM((2, PAIR, slots), jnp.bfloat16)]),
        compiler_params=pltpu.CompilerParams(vmem_limit_bytes=48 * 1024 * 1024),
        name="attend",
    )(counts, projected, projected, projected)


def attend_back_scratch(slots):
    return [pltpu.VMEM((2, slots, PAIR), jnp.bfloat16), pltpu.VMEM((2, slots, PAIR), jnp.bfloat16),
            pltpu.VMEM((2, PAIR, slots), jnp.bfloat16), pltpu.VMEM((2, slots), jnp.float32),
            pltpu.VMEM((slots, PAIR), jnp.float32), pltpu.VMEM((slots, PAIR), jnp.float32)]


def attend_back_body(size, count_ref, q_ref, k_ref, v_ref, o_ref, do_ref, lse_ref, out_ref,
                     q_heads, do_heads, k_turned, inner, dk_sum, dv_sum, hook):
    slots = q_ref.shape[0]
    length = count_ref[0]
    lane = lax.broadcasted_iota(jnp.int32, (slots, PAIR), 1)
    row = lax.broadcasted_iota(jnp.int32, (PAIR, slots), 0)
    q = q_ref[...].astype(jnp.float32) * (HEAD ** (-0.5))
    do = do_ref[...].astype(jnp.float32)
    k = k_ref[...].astype(jnp.float32).T * (HEAD ** (-0.5))
    product = (do * o_ref[...].astype(jnp.float32)).T
    for head in range(2):
        q_heads[head] = jnp.where(lane // HEAD == head, q, 0.0).astype(jnp.bfloat16)
        do_heads[head] = jnp.where(lane // HEAD == head, do, 0.0).astype(jnp.bfloat16)
        k_turned[head] = jnp.where(row // HEAD == head, k, 0.0).astype(jnp.bfloat16)
        inner[head] = jnp.sum(product[head * HEAD : (head + 1) * HEAD], axis=0)
    dk_sum[...] = jnp.zeros_like(dk_sum)
    dv_sum[...] = jnp.zeros_like(dv_sum)
    key_index = lax.broadcasted_iota(jnp.int32, (slots, size), 0)

    def step(n, carry):
        rows = pl.ds(n * size, size)
        keys, values = k_ref[...], v_ref[...]
        dq = jnp.zeros((PAIR, size), jnp.float32)
        for head in range(2):
            q_block, do_block = q_heads[head, rows, :], do_heads[head, rows, :]
            scores = last_dot(keys, q_block)
            weights = jnp.exp(scores - lse_ref[0, head, rows][None, :])
            weights = jnp.where(key_index < length, weights, 0.0)
            weight_grad = last_dot(values, do_block)
            score_grad = (weights * (weight_grad - inner[head, rows][None, :])).astype(jnp.bfloat16)
            dv_sum[...] += plain_dot(weights.astype(jnp.bfloat16), do_block)
            dk_sum[...] += plain_dot(score_grad, q_block)
            dq = dq + plain_dot(k_turned[head], score_grad)
        out_ref[0, rows, :] = dq.T.astype(jnp.bfloat16)
        return carry

    for n in range(slots // size):
        hook(n)
        step(n, 0)
    out_ref[1] = dk_sum[...].astype(jnp.bfloat16)
    out_ref[2] = dv_sum[...].astype(jnp.bfloat16)


def attend_gather(n_dp, n_fsdp, counts, projected, pieces, fresh, orders, plan, collective_id, size=512):
    slots, width = projected.shape
    d = width // 3
    pairs = d // PAIR
    grid = Grid(n_dp, n_fsdp)
    begun, count = len(pieces), len(pieces) + len(fresh)
    jobs = job_list([a.shape[-2:] for a in (*pieces, *fresh)])
    shapes = [jax.ShapeDtypeStruct(p.shape, p.dtype) for p in pieces]
    shapes += [jax.ShapeDtypeStruct(grid.shape(o, *a.shape), a.dtype) for a, o in zip(fresh, orders[begun:])]
    steps = slots // size

    def kernel(count_ref, q_ref, k_ref, v_ref, *refs):
        (o_ref, lse_ref), outs = refs[count : count + 2], refs[count + 2 : 2 * count + 2]
        q_heads, v_turned = refs[2 * count + 2 : 2 * count + 4]
        g = grid.here()
        work = gather_jobs(g, orders, jobs, outs[:begun] + refs[begun:count], outs, refs[2 * count + 4 :])
        pair = pl.program_id(0)

        def run(when):
            for j, step in plan.get(when, []):
                if step == 1 and j < begun:
                    work[j].resume()
                else:
                    work[j].step(step)

        @pl.when(pair == 0)
        def _():
            g.barrier()

        def hook(n):
            for p in range(pairs):
                if (p, n) in plan:
                    pl.when(pair == p)(partial(run, (p, n)))

        hook(0)
        attend_prepare(q_ref, v_ref, q_heads, v_turned)
        length = count_ref[0]
        for n in range(steps):
            if n > 0:
                hook(n)
            attend_block(length, n * size, size, q_heads, k_ref, v_turned, o_ref, lse_ref.at[0])

        @pl.when(pair == pairs - 1)
        def _():
            run("end")
            for j, job in enumerate(work):
                job.finish(1 if j < begun else 0)

    spec = lambda part: pl.BlockSpec((slots, PAIR), lambda p, n, part=part: (0, part * pairs + p))
    return pl.pallas_call(
        kernel,
        out_shape=[jax.ShapeDtypeStruct((slots, d), jnp.bfloat16),
                   jax.ShapeDtypeStruct((pairs, 2, slots), jnp.float32)]
        + shapes,
        grid_spec=pltpu.PrefetchScalarGridSpec(
            num_scalar_prefetch=1, grid=(pairs,),
            in_specs=[spec(0), spec(1), spec(2)] + [ANY] * count,
            out_specs=[pl.BlockSpec((slots, PAIR), lambda p, n: (0, p)),
                       pl.BlockSpec((1, 2, slots), lambda p, n: (p, 0, 0))] + [ANY] * count,
            scratch_shapes=[pltpu.VMEM((2, slots, PAIR), jnp.bfloat16), pltpu.VMEM((2, PAIR, slots), jnp.bfloat16)]
            + gather_scratch(grid, len(jobs))),
        input_output_aliases={4 + n: 2 + n for n in range(begun)},
        compiler_params=pltpu.CompilerParams(vmem_limit_bytes=56 * 1024 * 1024, collective_id=collective_id,
                                             has_side_effects=True),
        name="attend_gather",
    )(counts, projected, projected, projected, *pieces, *fresh)


FORWARD_PLAN = {
    (0, 0): [(0, 1), (1, 1), (2, 0)],
    (1, 0): [(0, 2)],
    (2, 0): [(1, 2), (0, 3)],
    (3, 0): [(2, 1)],
    (4, 0): [(2, 2)],
    "end": [(1, 3), (2, 3)],
}


def cut_block(grad, turned_blocks, out, rows):
    for z, x, y, c in places():
        row, column = piece_rows(turned_blocks, z, x, y, c)
        out[y, c, z, x, rows, :] = grad[row : row + 48, column : column + 384]


def grads_attend_back(n_dp, n_fsdp, counts, projected, attended, attended_grad, lse, cotangent, active, normed, hidden_grad,
                      branch_grad, plan, collective_id, size=256):
    slots, width = projected.shape
    d = width // 3
    pairs = d // PAIR
    panels = active.shape[1] // d
    head = 2 * panels + 1
    grid = Grid(n_dp, n_fsdp)
    sizes = [(panels * 48, 384), (panels * 48, 384), (48, 384)]
    jobs = job_list(sizes)
    steps = slots // size

    def kernel(count_ref, q_ref, k_ref, v_ref, o_ref, do_ref, lse_ref, dy, z, h2, du, o_all, db, out_ref, *refs):
        outs, sums, parts, left = refs[:3], refs[3:5], refs[5:8], refs[8]
        own, scratch = refs[9:15], refs[15:]
        g = grid.here()
        work = scatter_jobs(g, ["j"] * 3, jobs, parts, scratch)
        step = pl.program_id(0)

        def run(when):
            for j, number in plan.get(when, []):
                work[j].step(number)

        @pl.when(step == 0)
        def _():
            g.barrier()

        def turn(ref):
            left[...] = ref[...].astype(jnp.float32).T.astype(jnp.bfloat16)

        for first, ref in ((0, dy), (panels, h2), (2 * panels, o_all)):
            pl.when(step == first)(partial(turn, ref))

        def blocks(part, first, right, kind):
            @pl.when((step >= first) & (step < first + (1 if part == 2 else panels)))
            def _():
                values = right[...]
                grad = plain_dot(left[...], values).astype(jnp.bfloat16)
                at = 0 if part == 2 else pl.multiple_of((step - first) * 48, 16)
                cut_block(grad, kind, parts[part], pl.ds(at, 48))
                if part > 0:
                    sums[part - 1][...] = jnp.sum(values.astype(jnp.float32), axis=0).reshape(1, 1, d)

        for when in range(head):
            if (when, 0) in plan:
                pl.when(step == when)(partial(run, (when, 0)))
        blocks(0, 0, z, True)
        blocks(1, panels, du, False)
        blocks(2, 2 * panels, db, False)

        def hook(n):
            for p in range(head, head + pairs):
                if (p, n) in plan:
                    pl.when(step == p)(partial(run, (p, n)))

        @pl.when(step >= head)
        def _():
            attend_back_body(size, count_ref, q_ref, k_ref, v_ref, o_ref, do_ref, lse_ref, out_ref, *own, hook)

        @pl.when(step == head + pairs - 1)
        def _():
            run("end")
            for job, (n, path, rows) in zip(work, jobs):
                outs[n][rows, :] = job.total().astype(jnp.bfloat16)
            for job in work:
                job.finish()

    pair_at = lambda s: jnp.maximum(s - head, 0)
    spec = lambda part: pl.BlockSpec((slots, PAIR), lambda s, n, part=part: (0, part * pairs + pair_at(s)))
    once = pl.BlockSpec((slots, d), lambda s, n: (0, 0), pipeline_mode=pl.Buffered(1))
    panel = lambda first: pl.BlockSpec((slots, d), lambda s, n: (0, jnp.clip(s - first, 0, panels - 1)))
    low, wide = jnp.bfloat16, jnp.float32
    return pl.pallas_call(
        kernel,
        out_shape=[jax.ShapeDtypeStruct((3, slots, d), low)]
        + [jax.ShapeDtypeStruct(s, low) for s in sizes]
        + [jax.ShapeDtypeStruct((panels, 1, d), wide), jax.ShapeDtypeStruct((1, 1, d), wide)],
        grid_spec=pltpu.PrefetchScalarGridSpec(
            num_scalar_prefetch=1, grid=(head + pairs,),
            in_specs=[spec(0), spec(1), spec(2), spec(0), spec(0),
                      pl.BlockSpec((1, 2, slots), lambda s, n: (pair_at(s), 0, 0)),
                      once, panel(0), once, panel(panels), once, once],
            out_specs=[pl.BlockSpec((3, slots, PAIR), lambda s, n: (0, 0, pair_at(s)))] + [VM] * 3
            + [pl.BlockSpec((1, 1, d), lambda s, n: (jnp.clip(s - panels, 0, panels - 1), 0, 0)),
               pl.BlockSpec((1, 1, d), lambda s, n: (0, 0, 0))],
            scratch_shapes=[pltpu.VMEM(grid.shape("j", *s), low) for s in sizes] + [pltpu.VMEM((d, slots), low)]
            + attend_back_scratch(slots) + scatter_scratch(grid, sizes, jobs)),
        compiler_params=pltpu.CompilerParams(vmem_limit_bytes=62 * 1024 * 1024, collective_id=collective_id,
                                             has_side_effects=True),
        name="grads_attend_back",
    )(counts, projected, projected, projected, attended, attended_grad, lse, cotangent, active, normed, hidden_grad,
      attended, branch_grad)


BACKWARD_PLAN = {
    (4, 0): [(0, 0)],
    (6, 0): [(0, 1)],
    (8, 0): [(1, 0), (0, 2)],
    (9, 0): [(2, 0), (1, 1)],
    (10, 0): [(0, 3)],
    (10, 2): [(2, 1)],
    (11, 2): [(1, 2), (2, 2)],
    (12, 2): [(1, 3), (2, 3)],
}


PIECE = (48, 384)


class Spread:
    def __init__(self, g, u, tiles, send, recv, base):
        qkv, out, up, down = tiles
        me = g.y * 2 + g.c
        rows = pl.ds(pl.multiple_of(g.y * 48, 16), 48)
        self.g, self.u, self.tiles, self.rows, self.me = g, u, tiles, rows, me
        self.copies = []

        def copy(src, dst, device):
            self.copies.append(remote(src, dst, send, recv, base + len(self.copies), device))

        for k in range(1, 4):
            to = (me + k) % 4
            device = {"dp": g.z * 2 + g.x, "fsdp": to}
            block, half = self.qkv_place(to)
            copy(u.at[block], qkv.at[half, rows, :], device)
            copy(u.at[3], out.at[g.c, rows, :], device)
            copy(u.at[4 + to], up.at[g.c, rows, :], device)
        for k in range(1, 4):
            to = (g.z + k) % 4
            copy(u.at[8 + to], down.at[pl.ds(pl.multiple_of(g.z * 48, 16), 48), :], {"dp": to * 2 + g.x, "fsdp": me})

    def qkv_place(self, to):
        c = self.g.c
        middle = (to + 1) // 2 % 2
        return to - to // 3 - middle * c, middle + c - 2 * middle * c

    def start(self):
        start_all(self.copies)
        g, u = self.g, self.u
        qkv, out, up, down = self.tiles
        block, half = self.qkv_place(self.me)
        qkv[half, self.rows, :] = u[block]
        out[g.c, self.rows, :] = u[3]
        up[g.c, self.rows, :] = u[4 + self.me]
        down[pl.ds(pl.multiple_of(g.z * 48, 16), 48), :] = u[8 + g.z]

    def finish(self):
        arrived(self.copies)
        sent(self.copies)


TILES = [jax.ShapeDtypeStruct((2, 96, 384), jnp.bfloat16)] * 3 + [jax.ShapeDtypeStruct((192, 384), jnp.bfloat16)]


def meet_all(g, n_dp, n_fsdp):
    count = n_dp * n_fsdp
    me = (g.z * g.X + g.x) * n_fsdp + g.y * 2 + g.c
    sem = pltpu.get_barrier_semaphore()
    ranks = [(me + k) % count for k in range(1, count)]
    peers = [{"dp": rank // n_fsdp, "fsdp": rank % n_fsdp} for rank in ranks]
    for peer in peers:
        pl.semaphore_signal(sem, inc=1, device_id=peer, device_id_type=MESH)
    pl.semaphore_wait(sem, count - 1)
    return me, ranks, peers


def piece_rows(turned, z, x, y, c):
    if turned:
        return 192 * (2 * y + c) + 48 * z, 384 * x
    return 96 * (2 * z + x) + 48 * y, 384 * c


def places():
    return [(z, x, y, c) for z in range(4) for x in range(2) for y in range(2) for c in range(2)]


def owner_exchange(n_dp, n_fsdp, blocks_of, owners, flags, u, small, stats, roots, collective_id):
    grid = Grid(n_dp, n_fsdp)
    count = n_dp * n_fsdp
    spread_lanes = 12

    def kernel(of_ref, owners_ref, flags_ref, u_ref, small_ref, stats_hbm, roots_hbm,
               all_small, qkv, out, up, down, s_qkv, s_out, s_up, s_down, new_stats_hbm,
               slots, got, got_steps, u_steps, stats, roots, block, turned, local, send, recv):
        g = grid.here()
        me, ranks, peers = meet_all(g, n_dp, n_fsdp)
        loads = [pltpu.make_async_copy(stats_hbm, stats, local.at[0]), pltpu.make_async_copy(roots_hbm, roots, local.at[1])]

        def fill(n, carry):
            slots[n] = u_ref[of_ref[n]]
            return carry

        lax.fori_loop(0, count, fill, 0)
        lane = 0
        copies, small_copies, step_copies = [], [], []
        for rank, peer in zip(ranks, peers):
            copies.append(remote(slots.at[rank], got.at[me], send, recv, lane, peer))
            small_copies.append(remote(small_ref, all_small.at[me], send, recv, lane + 1, peer))
            step_copies.append(remote(slots.at[rank], got_steps.at[me], send, recv, lane + 2, peer))
            lane += 3
        start_all(copies)
        for load in loads:
            load.start()
        got[me] = slots[me]
        all_small[me] = small_ref[...]
        for load in loads:
            load.wait()
        arrived(copies)
        sent(copies)
        spread = Spread(g, u_ref, (qkv, out, up, down), send, recv, lane)
        spread.start()
        start_all(small_copies)

        own, kind = flags_ref[0] == 1, flags_ref[1]
        for turn in range(2):
            for n, place in enumerate(places()):
                row, column = piece_rows(turn, *place)
                (turned if turn else block)[row : row + 48, column : column + 384] = got[n]
        block[...] = jnp.where(kind == 1, turned[...], block[...])
        turned[...] = block[...].astype(jnp.float32).T.astype(jnp.bfloat16)
        left = plain_dot(roots[kind].astype(jnp.bfloat16), block[...]).astype(jnp.bfloat16)
        step = plain_dot(left, roots[1 - kind].astype(jnp.bfloat16)).astype(jnp.bfloat16)
        for n, place in enumerate(places()):
            row, column = piece_rows(0, *place)
            other_row, other_column = piece_rows(1, *place)
            slots[n] = jnp.where(kind == 1, step[other_row : other_row + 48, other_column : other_column + 384],
                                 step[row : row + 48, column : column + 384])
        start_all(step_copies)
        got_steps[me] = slots[me]
        rows_by = last_dot(block[...], block[...])
        columns_by = last_dot(turned[...], turned[...])
        for side in range(2):
            mine, other = (rows_by, columns_by) if side == 0 else (columns_by, rows_by)
            moved = 0.5 * stats[side] + 0.5 * jnp.where(kind == 1, other, mine)
            stats[side] = jnp.where(own, moved, stats[side])
        store = pltpu.make_async_copy(stats, new_stats_hbm, local.at[0])
        store.start()
        arrived(step_copies)

        def pick(n, carry):
            u_steps[n] = got_steps[owners_ref[n]]
            return carry

        lax.fori_loop(0, 12, pick, 0)
        back = Spread(g, u_steps, (s_qkv, s_out, s_up, s_down), send, recv, lane + spread_lanes)
        back.start()
        spread.finish()
        arrived(small_copies)
        sent(small_copies + step_copies)
        back.finish()
        store.wait()

    lanes = 3 * (count - 1) + 2 * spread_lanes
    low = jnp.bfloat16
    smem = pl.BlockSpec(memory_space=pltpu.SMEM)
    return pl.pallas_call(
        kernel,
        out_shape=[jax.ShapeDtypeStruct((count,) + small.shape, jnp.float32)] + TILES + TILES
        + [jax.ShapeDtypeStruct(stats.shape, jnp.float32)],
        in_specs=[smem, smem, smem, VM, VM, ANY, ANY],
        out_specs=[VM] * 9 + [ANY],
        scratch_shapes=[pltpu.VMEM((count,) + PIECE, low), pltpu.VMEM((count,) + PIECE, low),
                        pltpu.VMEM((count,) + PIECE, low), pltpu.VMEM((12,) + PIECE, low),
                        pltpu.VMEM(stats.shape, jnp.float32), pltpu.VMEM(roots.shape, jnp.float32),
                        pltpu.VMEM(stats.shape[1:], low), pltpu.VMEM(stats.shape[1:], low),
                        pltpu.SemaphoreType.DMA((2,)), pltpu.SemaphoreType.DMA((lanes,)), pltpu.SemaphoreType.DMA((lanes,))],
        compiler_params=pltpu.CompilerParams(collective_id=collective_id, has_side_effects=True,
                                             vmem_limit_bytes=56 * 1024 * 1024),
        name="owner_exchange",
    )(blocks_of, owners, flags, u, small, stats, roots)


def block_grads_kernel(turned_blocks, left, right, out, sums, left_turned):
    @pl.when(pl.program_id(0) == 0)
    def _():
        left_turned[...] = left[...].astype(jnp.float32).T.astype(jnp.bfloat16)

    values = right[...].reshape(right.shape[-2:])
    grad = plain_dot(left_turned[...], values).astype(jnp.bfloat16)
    for z, x, y, c in places():
        row, column = piece_rows(turned_blocks, z, x, y, c)
        out[y, c, z, x] = grad[row : row + 48, column : column + 384]
    sums[...] = jnp.sum(values.astype(jnp.float32), axis=0).reshape(sums.shape)


def block_grads(left, right, turned_blocks):
    rows, d = left.shape
    if right.ndim == 3:
        count = right.shape[0]
        spec = pl.BlockSpec((1, rows, d), lambda b: (b, 0, 0))
    else:
        count = right.shape[1] // d
        spec = pl.BlockSpec((rows, d), lambda b: (0, b))
    return pl.pallas_call(
        partial(block_grads_kernel, turned_blocks),
        out_shape=[jax.ShapeDtypeStruct((2, 2, 4, 2, count * 48, 384), jnp.bfloat16),
                   jax.ShapeDtypeStruct((count, 1, d), jnp.float32)],
        grid=(count,),
        in_specs=[pl.BlockSpec((rows, d), lambda b: (0, 0)), spec],
        out_specs=[pl.BlockSpec((2, 2, 4, 2, 48, 384), lambda b: (0, 0, 0, 0, b, 0)),
                   pl.BlockSpec((1, 1, d), lambda b: (b, 0, 0))],
        scratch_shapes=[pltpu.VMEM((d, rows), jnp.bfloat16)],
        compiler_params=pltpu.CompilerParams(vmem_limit_bytes=56 * 1024 * 1024),
        name="block_grads",
    )(left, right)


def centered(values):
    center = values - jnp.mean(values, axis=-1, keepdims=True)
    spread = lax.rsqrt(jnp.mean(center * center, axis=-1, keepdims=True) + 1e-06)
    return center * spread, spread


def norm_back(grads, unit, spread, gain):
    scaled = grads * gain
    mean = jnp.mean(scaled, axis=-1, keepdims=True)
    along = jnp.mean(scaled * unit, axis=-1, keepdims=True)
    return (scaled - mean - unit * along) * spread


def middle_kernel(x, attended, dy, out_w, up_w, down_w, rows, bias_up,
                  layer, h2, active, hidden_grad, middle_grad, branch_grad, attended_grad, sums):
    gain, shift, bias_out, bias_down = rows[0:1], rows[1:2], rows[2:3], rows[3:4]
    middle = x[...].astype(jnp.float32) + (plain_dot(attended[...], out_w[...]) + bias_out)
    unit, spread = centered(middle)
    normed = (unit * gain + shift).astype(jnp.bfloat16)
    h2[...] = normed
    grad_rows = dy[...]
    panels = up_w.shape[0]
    width = up_w.shape[2]
    half = width // 2
    y = jnp.zeros_like(middle)
    dh = jnp.zeros_like(middle)
    for panel in range(panels):
        hidden = plain_dot(normed, up_w[panel]) + bias_up[panel : panel + 1]
        passed = 0.5 + 0.5 * lax.erf(hidden * (0.5**0.5))
        z = (hidden * passed).astype(jnp.bfloat16)
        slope = passed + hidden * (jnp.exp(-0.5 * hidden * hidden) * 0.3989422804014327)
        back = jnp.concatenate([plain_dot(grad_rows, down_w[2 * panel]), plain_dot(grad_rows, down_w[2 * panel + 1])], axis=1)
        du = (slope * back).astype(jnp.bfloat16)
        active[:, panel * width : (panel + 1) * width] = z
        hidden_grad[:, panel * width : (panel + 1) * width] = du
        y = y + last_dot(z[:, :half], down_w[2 * panel]) + last_dot(z[:, half:], down_w[2 * panel + 1])
        dh = dh + last_dot(du, up_w[panel])
    layer[...] = (middle + y + bias_down).astype(jnp.bfloat16)
    wide = grad_rows.astype(jnp.float32)
    total = wide + norm_back(dh, unit, spread, gain)
    low = total.astype(jnp.bfloat16)
    middle_grad[...] = total
    branch_grad[...] = low
    attended_grad[...] = last_dot(low, out_w[...]).astype(jnp.bfloat16)

    @pl.when(pl.program_id(0) == 0)
    def _():
        sums[...] = jnp.zeros_like(sums)

    sums[0:1] += jnp.sum(dh * unit, axis=0, keepdims=True)
    sums[1:2] += jnp.sum(dh, axis=0, keepdims=True)
    sums[2:3] += jnp.sum(wide, axis=0, keepdims=True)


def middle_layer(tokens, attended, cotangent, out_w, up_w, down_w, rows, bias_up, block=256):
    count, d = tokens.shape
    ff = up_w.shape[0] * up_w.shape[2]
    row = lambda width: pl.BlockSpec((block, width), lambda r: (r, 0))
    whole = lambda array: pl.BlockSpec(array.shape, lambda r: (0,) * array.ndim)
    low, wide = jnp.bfloat16, jnp.float32
    shape = jax.ShapeDtypeStruct
    return pl.pallas_call(
        middle_kernel,
        out_shape=[shape((count, d), low), shape((count, d), low), shape((count, ff), low), shape((count, ff), low),
                   shape((count, d), wide), shape((count, d), low), shape((count, d), low), shape((8, d), wide)],
        grid=(count // block,),
        in_specs=[row(d), row(d), row(d)] + [whole(a) for a in (out_w, up_w, down_w, rows, bias_up)],
        out_specs=[row(d), row(d), row(ff), row(ff), row(d), row(d), row(d), pl.BlockSpec((8, d), lambda r: (0, 0))],
        compiler_params=pltpu.CompilerParams(vmem_limit_bytes=60 * 1024 * 1024),
        name="middle_layer",
    )(tokens, attended, cotangent, out_w, up_w, down_w, rows, bias_up)


D = 768
HEADS = 12
HD = 64
FF = 3072
BLOCKS = 12


masked_score = -1000000000.0
decay_rate = 0.5
step_rate = 1.0
small_rate = 0.3
highest = lax.Precision.HIGHEST


def broadcast(value, axis, source):
    kept = jnp.where(lax.axis_index(axis) == source, value, 0).astype(value.dtype)
    return lax.psum(kept, axis)


def layer_norm(values, scale_row, shift_row):
    center = values - jnp.mean(values, axis=-1, keepdims=True)
    spread = jnp.mean(center * center, axis=-1, keepdims=True)
    return center * lax.rsqrt(spread + 1e-06) * scale_row + shift_row


def unpack(small_params):
    pieces = [small_params[number * D : (number + 1) * D] for number in range(8)]
    return pieces + [small_params[8 * D : 8 * D + FF]]


def row_dot(left, right):
    return jnp.dot(left, right, preferred_element_type=jnp.float32)


def column_dot(left, right):
    return lax.dot_general(
        left, right, (((0,), (0,)), ((), ())), preferred_element_type=jnp.float32
    )


def transposed_dot(left, right):
    return lax.dot_general(
        left, right, (((1,), (1,)), ((), ())), preferred_element_type=jnp.float32
    )


def block_split(array, block_rows):
    slots = array.shape[-1]
    return array.reshape(HEADS, HD, slots // block_rows, block_rows).transpose(2, 0, 1, 3)


def block_join(array):
    return array.transpose(0, 3, 1, 2).reshape(-1, D)


def attend_clip(queries, key_rows, value_rows, length):
    slots = queries.shape[-1]
    block_rows = min(512, slots)
    score_scale = float(HD) ** (-0.5)
    visible = (jnp.arange(slots) < length)[None, None, :]

    def one_block(query_block):
        scores = (
            jnp.einsum("hdq,hdk->hqk", query_block, key_rows, preferred_element_type=jnp.float32)
            * score_scale
        )
        scores = jnp.where(visible, scores, masked_score)
        row_top = jnp.max(scores, axis=-1, keepdims=True)
        raised = jnp.exp(scores - row_top)
        row_total = jnp.sum(raised, axis=-1, keepdims=True)
        softmax_weights = (raised / row_total).astype(jnp.bfloat16)
        attended = jnp.einsum(
            "hqk,hdk->hdq", softmax_weights, value_rows, preferred_element_type=jnp.float32
        )
        return (attended.astype(jnp.bfloat16), (row_top + jnp.log(row_total))[:, :, 0])

    attended, log_totals = lax.map(one_block, block_split(queries, block_rows))
    return (block_join(attended), log_totals)


def attend_back(queries, key_rows, value_rows, length, log_totals, out_grads):
    slots = queries.shape[-1]
    block_rows = min(512, slots)
    score_scale = float(HD) ** (-0.5)
    visible = (jnp.arange(slots) < length)[None, None, :]

    def one_block(carry, pieces):
        key_grad, value_grad = carry
        query_block, grad_block, log_block = pieces
        scores = (
            jnp.einsum("hdq,hdk->hqk", query_block, key_rows, preferred_element_type=jnp.float32)
            * score_scale
        )
        scores = jnp.where(visible, scores, masked_score)
        softmax_weights = jnp.exp(scores - log_block[:, :, None])
        weight_grad = jnp.einsum(
            "hdq,hdk->hqk", grad_block, value_rows, preferred_element_type=jnp.float32
        )
        inner_sum = jnp.sum(softmax_weights * weight_grad, axis=-1, keepdims=True)
        score_grad = (softmax_weights * (weight_grad - inner_sum)).astype(jnp.bfloat16)
        query_grad = (
            jnp.einsum("hqk,hdk->hdq", score_grad, key_rows, preferred_element_type=jnp.float32)
            * score_scale
        )
        key_grad = (
            key_grad
            + jnp.einsum(
                "hqk,hdq->hdk", score_grad, query_block, preferred_element_type=jnp.float32
            )
            * score_scale
        )
        value_grad = value_grad + jnp.einsum(
            "hqk,hdq->hdk",
            softmax_weights.astype(jnp.bfloat16),
            grad_block,
            preferred_element_type=jnp.float32,
        )
        return ((key_grad, value_grad), query_grad)

    blank = jnp.zeros((HEADS, HD, slots), jnp.float32)
    (key_grad, value_grad), query_grad = lax.scan(
        one_block,
        (blank, blank),
        (block_split(queries, block_rows), block_split(out_grads, block_rows), log_totals),
    )
    key_rows_grad = key_grad.transpose(2, 0, 1).reshape(slots, D)
    value_rows_grad = value_grad.transpose(2, 0, 1).reshape(slots, D)
    return (block_join(query_grad), key_rows_grad, value_rows_grad)


def take_columns(operands, member, start):
    return lax.slice_in_dim(operands[member], start, start + D, axis=1)


def take_rows(operands, member, start):
    return lax.slice_in_dim(operands[member], start, start + D, axis=0)


def block_pickers():
    pickers = [partial(take_columns, member=0, start=column * D) for column in range(3)]
    pickers.append(partial(take_columns, member=1, start=0))
    pickers = pickers + [
        partial(take_columns, member=2, start=column * D) for column in range(FF // D)
    ]
    pickers = pickers + [
        partial(take_rows, member=3, start=column * D) for column in range(FF // D)
    ]
    return pickers


def fetch_update(update, root):
    return broadcast(update.astype(jnp.bfloat16), ("dp", "fsdp"), root).astype(update.dtype)


def band_tile(band, like, column_index):
    columns_here = like.shape[1]
    return lax.dynamic_slice_in_dim(band, column_index * columns_here, columns_here, 1)


def row_band(pieces, like, row_index):
    rows_here = like.shape[0]
    start = row_index * rows_here
    return jnp.concatenate(
        [lax.dynamic_slice_in_dim(piece, start, rows_here, 0) for piece in pieces], axis=1
    )


def stacked_band(pieces, like, row_index):
    rows_here = like.shape[0]
    start = row_index * rows_here
    owner_block = start // D
    picked = jnp.zeros((rows_here, D), jnp.float32)
    for number in range(len(pieces)):
        inside = jnp.clip(start - number * D, 0, D - rows_here)
        piece = lax.dynamic_slice_in_dim(pieces[number], inside, rows_here, 0)
        picked = jnp.where(owner_block == number, piece, picked)
    return picked


def local_any(
    tokens,
    counts,
    cotangent,
    qkv_weight,
    out_weight,
    up_weight,
    down_weight,
    small_params,
    statistics,
    inverse_roots,
    owners,
):
    clips_here = counts.shape[0]
    slots = tokens.shape[0] // clips_here
    qkv_low = qkv_weight.astype(jnp.bfloat16)
    out_low = out_weight.astype(jnp.bfloat16)
    up_low = up_weight.astype(jnp.bfloat16)
    down_low = down_weight.astype(jnp.bfloat16)
    qkv_cols, out_cols, up_cols, down_cols = (
        lax.all_gather(qkv_low, "fsdp", axis=1, tiled=True),
        lax.all_gather(out_low, "fsdp", axis=1, tiled=True),
        lax.all_gather(up_low, "fsdp", axis=1, tiled=True),
        lax.all_gather(down_low, "fsdp", axis=1, tiled=True),
    )
    qkv_full, out_full, up_full, down_full = (
        lax.all_gather(qkv_cols, "dp", axis=0, tiled=True),
        lax.all_gather(out_cols, "dp", axis=0, tiled=True),
        lax.all_gather(up_cols, "dp", axis=0, tiled=True),
        lax.all_gather(down_cols, "dp", axis=0, tiled=True),
    )
    (
        gain_one,
        shift_one,
        gain_two,
        shift_two,
        bias_query,
        bias_value,
        bias_out,
        bias_down,
        bias_up,
    ) = unpack(small_params)

    def heads_view(array):
        return array.reshape(clips_here, slots, HEADS, HD).transpose(0, 2, 3, 1)

    def clip_forward(clip_group):
        return attend_clip(clip_group[0], clip_group[1], clip_group[2], clip_group[3])

    def clip_backward(clip_group):
        return attend_back(
            clip_group[0], clip_group[1], clip_group[2], clip_group[3], clip_group[4], clip_group[5]
        )

    inputs = tokens.astype(jnp.float32)
    normed = layer_norm(inputs, gain_one, shift_one).astype(jnp.bfloat16)
    projected = row_dot(normed, qkv_full)
    queries = heads_view((projected[:, :D] + bias_query).astype(jnp.bfloat16))
    key_rows = heads_view(projected[:, D : 2 * D].astype(jnp.bfloat16))
    value_rows = heads_view((projected[:, 2 * D :] + bias_value).astype(jnp.bfloat16))
    attended, log_totals = lax.map(clip_forward, (queries, key_rows, value_rows, counts))
    attended = attended.reshape(-1, D)
    middle = inputs + (row_dot(attended, out_full) + bias_out)
    normed_two = layer_norm(middle, gain_two, shift_two).astype(jnp.bfloat16)
    hidden = row_dot(normed_two, up_full) + bias_up
    active = jax.nn.gelu(hidden, approximate=False).astype(jnp.bfloat16)
    layer_rows = (middle + row_dot(active, down_full) + bias_down).astype(jnp.bfloat16)
    qkv_part, out_part, up_part, down_part = (
        lax.all_gather(qkv_low, "fsdp", axis=1, tiled=True),
        lax.all_gather(out_low, "fsdp", axis=1, tiled=True),
        lax.all_gather(up_low, "fsdp", axis=1, tiled=True),
        lax.all_gather(down_low, "fsdp", axis=1, tiled=True),
    )
    qkv_back, out_back, up_back, down_back = (
        lax.all_gather(qkv_part, "dp", axis=0, tiled=True),
        lax.all_gather(out_part, "dp", axis=0, tiled=True),
        lax.all_gather(up_part, "dp", axis=0, tiled=True),
        lax.all_gather(down_part, "dp", axis=0, tiled=True),
    )
    grad_down = column_dot(active, cotangent)
    grad_bias_down = jnp.sum(cotangent.astype(jnp.float32), axis=0)
    active_grad = transposed_dot(cotangent, down_back)
    unused_value, gelu_pull = jax.vjp(partial(jax.nn.gelu, approximate=False), hidden)
    hidden_grad = gelu_pull(active_grad)[0].astype(jnp.bfloat16)
    grad_up = column_dot(normed_two, hidden_grad)
    grad_bias_up = jnp.sum(hidden_grad.astype(jnp.float32), axis=0)
    normed_two_grad = transposed_dot(hidden_grad, up_back)
    unused_norm, norm_two_pull = jax.vjp(layer_norm, middle, gain_two, shift_two)
    middle_grad, grad_gain_two, grad_shift_two = norm_two_pull(normed_two_grad)
    middle_grad = middle_grad + cotangent.astype(jnp.float32)
    branch_grad = middle_grad.astype(jnp.bfloat16)
    grad_out = column_dot(attended, branch_grad)
    grad_bias_out = jnp.sum(branch_grad.astype(jnp.float32), axis=0)
    attended_grad = transposed_dot(branch_grad, out_back).astype(jnp.bfloat16)
    query_grad, key_grad, value_grad = lax.map(
        clip_backward,
        (queries, key_rows, value_rows, counts, log_totals, heads_view(attended_grad)),
    )
    projected_grad = (
        jnp.concatenate([query_grad, key_grad, value_grad], axis=-1)
        .reshape(-1, 3 * D)
        .astype(jnp.bfloat16)
    )
    grad_qkv = column_dot(normed, projected_grad)
    grad_bias_query = jnp.sum(projected_grad[:, :D].astype(jnp.float32), axis=0)
    grad_bias_value = jnp.sum(projected_grad[:, 2 * D :].astype(jnp.float32), axis=0)
    normed_grad = transposed_dot(projected_grad, qkv_back)
    unused_first, norm_one_pull = jax.vjp(layer_norm, inputs, gain_one, shift_one)
    input_rows_grad, grad_gain_one, grad_shift_one = norm_one_pull(normed_grad)
    input_grad = (middle_grad + input_rows_grad).astype(jnp.bfloat16)
    small_grad = jnp.concatenate(
        [
            grad_gain_one,
            grad_shift_one,
            grad_gain_two,
            grad_shift_two,
            grad_bias_query,
            grad_bias_value,
            grad_bias_out,
            grad_bias_down,
            grad_bias_up,
        ]
    )
    row_qkv, row_out, row_up, row_down, row_small = (
        lax.psum_scatter(
            grad_qkv.astype(jnp.bfloat16), "dp", scatter_dimension=0, tiled=True
        ).astype(jnp.float32),
        lax.psum_scatter(
            grad_out.astype(jnp.bfloat16), "dp", scatter_dimension=0, tiled=True
        ).astype(jnp.float32),
        lax.psum_scatter(
            grad_up.astype(jnp.bfloat16), "dp", scatter_dimension=0, tiled=True
        ).astype(jnp.float32),
        lax.psum_scatter(
            grad_down.astype(jnp.bfloat16), "dp", scatter_dimension=0, tiled=True
        ).astype(jnp.float32),
        lax.psum_scatter(
            small_grad.astype(jnp.bfloat16), "dp", scatter_dimension=0, tiled=True
        ).astype(jnp.float32),
    )
    shard_qkv, shard_out, shard_up, shard_down, shard_small = (
        lax.psum_scatter(
            row_qkv.astype(jnp.bfloat16), "fsdp", scatter_dimension=1, tiled=True
        ).astype(jnp.float32),
        lax.psum_scatter(
            row_out.astype(jnp.bfloat16), "fsdp", scatter_dimension=1, tiled=True
        ).astype(jnp.float32),
        lax.psum_scatter(
            row_up.astype(jnp.bfloat16), "fsdp", scatter_dimension=1, tiled=True
        ).astype(jnp.float32),
        lax.psum_scatter(
            row_down.astype(jnp.bfloat16), "fsdp", scatter_dimension=1, tiled=True
        ).astype(jnp.float32),
        lax.psum_scatter(
            row_small.astype(jnp.bfloat16), "fsdp", scatter_dimension=0, tiled=True
        ).astype(jnp.float32),
    )
    band_qkv, band_out, band_up, band_down, band_small = (
        lax.all_gather(shard_qkv.astype(jnp.bfloat16), "fsdp", axis=1, tiled=True).astype(
            shard_qkv.dtype
        ),
        lax.all_gather(shard_out.astype(jnp.bfloat16), "fsdp", axis=1, tiled=True).astype(
            shard_out.dtype
        ),
        lax.all_gather(shard_up.astype(jnp.bfloat16), "fsdp", axis=1, tiled=True).astype(
            shard_up.dtype
        ),
        lax.all_gather(shard_down.astype(jnp.bfloat16), "fsdp", axis=1, tiled=True).astype(
            shard_down.dtype
        ),
        lax.all_gather(shard_small.astype(jnp.bfloat16), "fsdp", axis=0, tiled=True).astype(
            shard_small.dtype
        ),
    )
    rank = lax.axis_index(("dp", "fsdp"))
    row_index = lax.axis_index("dp")
    column_index = lax.axis_index("fsdp")
    numbers = jnp.arange(BLOCKS, dtype=jnp.int32)
    matches = owners == rank
    mine = jnp.sum(jnp.where(matches, numbers, 0))
    owning = jnp.any(matches)

    def update_slot(gradient):
        left_stat = decay_rate * statistics[0, 0] + (1.0 - decay_rate) * jnp.dot(
            gradient, gradient.T, precision=highest, preferred_element_type=jnp.float32
        )
        right_stat = decay_rate * statistics[0, 1] + (1.0 - decay_rate) * jnp.dot(
            gradient.T, gradient, precision=highest, preferred_element_type=jnp.float32
        )
        left_step = jnp.dot(
            inverse_roots[0, 0], gradient, precision=highest, preferred_element_type=jnp.float32
        )
        update = jnp.dot(
            left_step, inverse_roots[0, 1], precision=highest, preferred_element_type=jnp.float32
        )
        return (jnp.stack([left_stat, right_stat])[None], update)

    def keep_slot(gradient):
        return (statistics, jnp.zeros((D, D), jnp.float32))

    whole_qkv, whole_out, whole_up, whole_down, whole_small = (
        lax.all_gather(band_qkv.astype(jnp.bfloat16), "dp", axis=0, tiled=True).astype(
            band_qkv.dtype
        ),
        lax.all_gather(band_out.astype(jnp.bfloat16), "dp", axis=0, tiled=True).astype(
            band_out.dtype
        ),
        lax.all_gather(band_up.astype(jnp.bfloat16), "dp", axis=0, tiled=True).astype(
            band_up.dtype
        ),
        lax.all_gather(band_down.astype(jnp.bfloat16), "dp", axis=0, tiled=True).astype(
            band_down.dtype
        ),
        lax.all_gather(band_small.astype(jnp.bfloat16), "dp", axis=0, tiled=True).astype(
            band_small.dtype
        ),
    )
    gradient = lax.switch(mine, block_pickers(), (whole_qkv, whole_out, whole_up, whole_down))
    new_statistics, update = lax.cond(owning, update_slot, keep_slot, gradient)
    arrivals = []
    for number in range(BLOCKS):
        arrivals.append(fetch_update(update, owners[number]))
    tile_qkv = band_tile(row_band(arrivals[0:3], qkv_weight, row_index), qkv_weight, column_index)
    tile_out = band_tile(row_band(arrivals[3:4], out_weight, row_index), out_weight, column_index)
    tile_up = band_tile(
        row_band(arrivals[4 : 4 + FF // D], up_weight, row_index), up_weight, column_index
    )
    tile_down = band_tile(
        stacked_band(arrivals[4 + FF // D :], down_weight, row_index), down_weight, column_index
    )
    new_qkv = qkv_weight - step_rate * tile_qkv
    new_out = out_weight - step_rate * tile_out
    new_up = up_weight - step_rate * tile_up
    new_down = down_weight - step_rate * tile_down
    new_small = small_params - small_rate * whole_small * lax.rsqrt(
        jnp.mean(whole_small * whole_small) + 1e-06
    )
    return (
        layer_rows,
        input_grad,
        shard_qkv,
        shard_out,
        shard_up,
        shard_down,
        whole_small,
        new_statistics,
        new_qkv,
        new_out,
        new_up,
        new_down,
        new_small,
    )


def local_staged(
    sizes,
    tokens,
    counts,
    cotangent,
    qkv_weight,
    out_weight,
    up_weight,
    down_weight,
    small_params,
    statistics,
    inverse_roots,
    owners,
):
    n_dp, n_fsdp = sizes
    qkv_low = qkv_weight.astype(jnp.bfloat16)
    later = (
        out_weight.astype(jnp.bfloat16),
        up_weight.astype(jnp.bfloat16),
        down_weight.astype(jnp.bfloat16).T,
    )
    (
        gain_one,
        shift_one,
        gain_two,
        shift_two,
        bias_query,
        bias_value,
        bias_out,
        bias_down,
        bias_up,
    ) = unpack(small_params)
    orders = ("j", "j", "j", "i")
    qkv_pieces, *begun = gather_first(n_dp, n_fsdp, (qkv_low,) + later[:2], orders[:3], 0, 1)
    qkv_full = whole_of(qkv_pieces)
    inputs = tokens.astype(jnp.float32)
    normed = layer_norm(inputs, gain_one, shift_one).astype(jnp.bfloat16)
    bias_qkv = jnp.concatenate([bias_query, jnp.zeros((D,), jnp.float32), bias_value])
    projected = (row_dot(normed, qkv_full) + bias_qkv).astype(jnp.bfloat16)
    attended, log_totals, out_pieces, up_pieces, down_pieces = attend_gather(
        n_dp, n_fsdp, counts, projected, begun, later[2:], orders[1:], FORWARD_PLAN, 2
    )
    layer_rows, normed_two, active, hidden_grad, middle_grad, branch_grad, attended_grad, sums = middle_layer(
        tokens,
        attended,
        cotangent,
        whole_of(out_pieces),
        up_pieces.reshape(n_fsdp, D, FF // n_fsdp),
        down_pieces.reshape(n_dp, D, FF // n_dp),
        jnp.stack([gain_two, shift_two, bias_out, bias_down]),
        bias_up.reshape(n_fsdp, FF // n_fsdp),
    )
    grad_gain_two, grad_shift_two, grad_bias_down = sums[0], sums[1], sums[2]
    projected_grad, mine_down, mine_up, mine_out, grad_bias_up, grad_bias_out = grads_attend_back(
        n_dp, n_fsdp, counts, projected, attended, attended_grad, log_totals,
        cotangent, active, normed_two, hidden_grad, branch_grad, BACKWARD_PLAN, 3,
    )
    split_qkv, grad_bias_qkv = block_grads(normed, projected_grad, False)
    normed_grad = sum(
        transposed_dot(projected_grad[part], qkv_full[:, part * D : (part + 1) * D]) for part in range(3)
    )
    unused_first, norm_one_pull = jax.vjp(layer_norm, inputs, gain_one, shift_one)
    input_rows_grad, grad_gain_one, grad_shift_one = norm_one_pull(normed_grad)
    input_grad = (middle_grad + input_rows_grad).astype(jnp.bfloat16)
    small_grad = jnp.concatenate(
        [
            grad_gain_one,
            grad_shift_one,
            grad_gain_two,
            grad_shift_two,
            grad_bias_qkv[0, 0],
            grad_bias_qkv[2, 0],
            grad_bias_out.reshape(-1),
            grad_bias_down,
            grad_bias_up.reshape(-1),
        ]
    )
    devices = n_dp * n_fsdp
    small_split = jnp.pad(small_grad.astype(jnp.bfloat16).reshape(devices, -1), ((0, 0), (0, 2048 - 9216 // devices)))
    small_split = small_split.reshape(4, 2, 2, 2, 16, 128).transpose(2, 3, 0, 1, 4, 5)
    mine_qkv, mine_small = scatter_all(n_dp, n_fsdp, (split_qkv, small_split), ("j", "j"), 4)
    mine = jnp.concatenate([mine_qkv.astype(jnp.bfloat16), mine_out, mine_up, mine_down], axis=0)
    numbers = jnp.arange(BLOCKS, dtype=jnp.int32)
    ranks = jnp.arange(devices, dtype=jnp.int32)
    blocks_of = jnp.sum(jnp.where(owners[None, :] == ranks[:, None], numbers[None, :], 0), axis=1).astype(jnp.int32)
    rank = lax.axis_index(("dp", "fsdp"))
    owning = jnp.any(owners == rank)
    flags = jnp.stack([owning, blocks_of[rank] >= 4 + FF // D]).astype(jnp.int32)
    small_pieces, *tiles, new_statistics = owner_exchange(
        n_dp, n_fsdp, blocks_of, owners, flags, mine.reshape(BLOCKS, 48, 384), mine_small[:8],
        statistics[0], inverse_roots[0], 5,
    )
    grad_tiles, step_tiles = tiles[:4], tiles[4:]
    column_index = lax.axis_index("fsdp")
    shard_qkv, shard_out, shard_up, shard_down = tiles_of(grad_tiles, column_index)
    tile_qkv, tile_out, tile_up, tile_down = tiles_of(step_tiles, column_index)
    new_qkv = qkv_weight - step_rate * tile_qkv
    new_out = out_weight - step_rate * tile_out
    new_up = up_weight - step_rate * tile_up
    new_down = down_weight - step_rate * tile_down
    whole_small = small_pieces.reshape(devices, 1024)[:, : 9216 // devices].reshape(-1)
    new_small = small_params - small_rate * whole_small * lax.rsqrt(
        jnp.mean(whole_small * whole_small) + 1e-06
    )
    return (
        layer_rows,
        input_grad,
        shard_qkv,
        shard_out,
        shard_up,
        shard_down,
        whole_small,
        new_statistics[None],
        new_qkv,
        new_out,
        new_up,
        new_down,
        new_small,
    )


def whole_of(pieces):
    rows, columns = pieces.shape[-2:]
    folded = pieces.reshape(pieces.shape[0] * pieces.shape[1], -1, columns)
    return folded.transpose(1, 0, 2).reshape(folded.shape[1], -1)


def tiles_of(tiles, column_index):
    qkv, out, up, down = tiles
    band = lambda halves: halves.astype(jnp.float32).transpose(1, 0, 2).reshape(96, D)
    qkv, out = band(qkv), band(out)
    qkv = jnp.where(column_index % 2 == 1, qkv[:, 192:], qkv[:, : D - 192])
    out = lax.dynamic_slice_in_dim(out, column_index * 192, 192, 1)
    return qkv, out, band(up), down.astype(jnp.float32).T


def solution(mesh):
    placed = (
        P(("dp", "fsdp"), None),
        P(("dp", "fsdp")),
        P(("dp", "fsdp"), None),
        P("dp", "fsdp"),
        P("dp", "fsdp"),
        P("dp", "fsdp"),
        P("dp", "fsdp"),
        P(),
        P(("dp", "fsdp"), None, None, None),
        P(("dp", "fsdp"), None, None, None),
        P(),
    )
    sizes = (mesh.shape["dp"], mesh.shape["fsdp"])
    local = partial(local_staged, sizes) if sizes == (8, 4) else local_any
    return jax.shard_map(
        local,
        mesh=mesh,
        in_specs=placed,
        out_specs=(
            P(("dp", "fsdp"), None),
            P(("dp", "fsdp"), None),
            P("dp", "fsdp"),
            P("dp", "fsdp"),
            P("dp", "fsdp"),
            P("dp", "fsdp"),
            P(),
            P(("dp", "fsdp"), None, None, None),
            P("dp", "fsdp"),
            P("dp", "fsdp"),
            P("dp", "fsdp"),
            P("dp", "fsdp"),
            P(),
        ),
        check_vma=False,
    )
```

```python
from functools import partial

import jax
import jax.numpy as jnp
from jax import lax
from jax.experimental import pallas as pl
from jax.experimental.pallas import tpu as pltpu
from jax.sharding import PartitionSpec as P

MESH = pl.DeviceIdType.MESH
ANY = pl.BlockSpec(memory_space=pl.ANY)
VM = pl.BlockSpec(memory_space=pltpu.VMEM)


class Grid:
    def __init__(self, n_dp, n_fsdp):
        self.Z = 4
        self.X = n_dp // 4
        self.Y = n_fsdp // 2
        self.swap = self.X == self.Y
        self.A, self.B = self.X, self.Y

    def here(self):
        dp, fs = lax.axis_index("dp"), lax.axis_index("fsdp")
        self.z, self.x = dp // self.X, dp % self.X
        self.y, self.c = fs // 2, fs % 2
        if self.swap:
            self.a = self.x + self.c * (self.y - self.x)
            self.b = self.y + self.c * (self.x - self.y)
        else:
            self.a, self.b = self.x, self.y
        return self

    def xy(self, a, b, c):
        if self.swap:
            return a + c * (b - a), b + c * (a - b)
        return a, b

    def device(self, z, a, b, c, frame=None):
        x, y = self.xy(a, b, self.c if frame is None else frame)
        return {"dp": z * self.X + x, "fsdp": y * 2 + c}

    def shape(self, order, r, w):
        if order == "j":
            return (self.Y, 2, self.Z, self.X, r, w)
        return (self.Z, self.X, self.Y, 2, r, w)

    def at(self, ref, order, y, c, z, x):
        return ref.at[y, c, z, x] if order == "j" else ref.at[z, x, y, c]

    def peers(self):
        out = [self.device((self.z + k) % self.Z, self.a, self.b, self.c) for k in range(1, self.Z)]
        out += [self.device(self.z, (self.a + k) % self.A, self.b, self.c) for k in range(1, self.A)]
        out += [self.device(self.z, self.a, (self.b + k) % self.B, self.c) for k in range(1, self.B)]
        out += [{"dp": self.z * self.X + self.x, "fsdp": self.y * 2 + 1 - self.c}]
        return out

    def barrier(self):
        sem = pltpu.get_barrier_semaphore()
        peers = self.peers()
        for peer in peers:
            pl.semaphore_signal(sem, inc=1, device_id=peer, device_id_type=MESH)
        pl.semaphore_wait(sem, len(peers))


def remote(src, dst, send, recv, slot, device):
    return pltpu.make_async_remote_copy(
        src_ref=src, dst_ref=dst, send_sem=send.at[slot], recv_sem=recv.at[slot], device_id=device, device_id_type=MESH
    )


def start_all(copies):
    for copy in copies:
        copy.start()


def arrived(copies):
    for copy in copies:
        copy.wait_recv()


def sent(copies):
    for copy in copies:
        copy.wait_send()


class Copies:
    def __init__(self, send, recv):
        self.send, self.recv, self.slot = send, recv, 0

    def add(self, group, describe):
        group.append((self.slot, describe))
        self.slot += 1

    def made(self, group):
        out = []
        for slot, describe in group:
            start, end, device = describe()
            out.append(remote(start, end, self.send, self.recv, slot, device))
        return out

    def start(self, group):
        start_all(self.made(group))

    def arrived(self, group):
        arrived(self.made(group))

    def sent(self, group):
        sent(self.made(group))


class Gather:
    def __init__(self, g, order, path, rows, src, out, local, send, recv):
        size = {"z": g.Z, "a": g.A, "b": g.B}
        self.copies = Copies(send, recv)

        def at(name, shift):
            place = {"z": g.z, "a": g.a, "b": g.b}[name]
            return (place + shift + size[name]) % size[name] if shift else place

        def piece(cell):
            where = {name: (at(name, value[1]) if isinstance(value, tuple) else value) for name, value in cell.items()}
            x, y = g.xy(where["a"], where["b"], g.c)
            return g.at(out, order, y, g.c, where["z"], x).at[..., rows, :]

        own_cell = {"z": ("own", 0), "a": ("own", 0), "b": ("own", 0)}

        def cells(full):
            out = [dict(own_cell)]
            for axis in full:
                if axis == "z":
                    out = [dict(cell, z=slice(None)) for cell in out]
                else:
                    out = [dict(cell, **{axis: n}) for cell in out for n in range(size[axis])]
            return out

        def near():
            return {"dp": g.z * g.X + g.x, "fsdp": g.y * 2 + 1 - g.c}

        def far(axis, k):
            return g.device(*[at(name, k if name == axis else 0) for name in "zab"], g.c)

        def own():
            return src.at[rows, :]

        self.own = lambda: pltpu.make_async_copy(own(), piece(own_cell), local)
        self.stages, self.near = [], [[]]
        self.copies.add(self.near[0], lambda: (own(), piece(own_cell), near()))
        full = ""
        for axis in path:
            self.stages.append([])
            self.near.append([])
            for cell in cells(full):
                for k in range(1, size[axis]):
                    from_src = not full
                    self.copies.add(self.stages[-1], lambda cell=cell, k=k, axis=axis, from_src=from_src: (
                        own() if from_src else piece(cell), piece(cell), far(axis, k)))
                    came = dict(cell, **{axis: ("own", -k)})
                    self.copies.add(self.near[-1], lambda came=came: (piece(came), piece(came), near()))
            full += axis

    @staticmethod
    def slots(g):
        zab = (g.Z - 1) + (g.A - 1) + g.A * (g.B - 1)
        abz = (g.A - 1) + g.A * (g.B - 1) + g.A * g.B * (g.Z - 1)
        return 1 + 2 * max(zab, abz)

    def step(self, number):
        if number == 0:
            self.own().start()
        else:
            if number == 1:
                self.own().wait()
            self.copies.arrived(self.stages[number - 1])
        if number < 3:
            self.copies.start(self.stages[number])
        self.copies.start(self.near[number])

    def pause(self):
        self.own().wait()
        for group in (self.stages[0], self.near[0]):
            self.copies.arrived(group)
            self.copies.sent(group)

    def resume(self):
        self.copies.start(self.stages[1])
        self.copies.start(self.near[1])

    def finish(self, first=0):
        for group in self.near[first:]:
            self.copies.arrived(group)
        for group in self.near[first:] + self.stages[first:]:
            self.copies.sent(group)


class Scatter:
    def __init__(self, g, order, path, rows, src, bufs, send, recv):
        self.g, self.path, self.order, self.rows, self.src = g, path, order, rows, src
        self.work = bufs[0]
        self.recv = dict(zip(path, bufs[1:]))
        work = self.work
        size = {"z": g.Z, "a": g.A, "b": g.B}
        self.size = size
        self.copies = Copies(send, recv)
        places = lambda: {"z": g.z, "a": g.a, "b": g.b}

        def other(b, a):
            x, y = g.xy(a, b, 1 - g.c)
            return (g.at(src, order, y, 1 - g.c, slice(None), x).at[:, rows, :], work.at[b, :, a],
                    {"dp": g.z * g.X + g.x, "fsdp": g.y * 2 + 1 - g.c})

        def onward(axis, k, done):
            place = places()
            to = dict(place, **{axis: (place[axis] + k) % size[axis]})
            where = {name: (place[name] if name in done else slice(None)) for name in "bza"}
            where[axis] = to[axis]
            return (work.at[where["b"], where["z"], where["a"]], self.recv[axis].at[k - 1],
                    g.device(to["z"], to["a"], to["b"], g.c))

        self.stages = [[]]
        for b in range(g.B):
            for a in range(g.A):
                self.copies.add(self.stages[0], partial(other, b, a))
        done = ""
        for axis in path:
            self.stages.append([])
            for k in range(1, size[axis]):
                self.copies.add(self.stages[-1], partial(onward, axis, k, done))
            done += axis

    @staticmethod
    def slots(g):
        return g.A * g.B + (g.B - 1) + (g.A - 1) + (g.Z - 1)

    @staticmethod
    def scratch(g, path, r, w):
        size = {"z": g.Z, "a": g.A, "b": g.B}
        out = [pltpu.VMEM((g.B, g.Z, g.A, r, w), jnp.bfloat16)]
        done = ""
        for axis in path:
            done += axis
            out.append(pltpu.VMEM((size[axis] - 1,) + tuple(size[n] for n in "bza" if n not in done) + (r, w), jnp.bfloat16))
        return out

    def _cell(self, index, done):
        place = {"z": self.g.z, "a": self.g.a, "b": self.g.b}
        return [place[n] if n in done else index[n] for n in "bza"]

    def _add(self, number):
        g, done = self.g, self.path[:number]
        left = [n for n in "bza" if n not in done]
        total = 1
        for name in left:
            total *= self.size[name]

        def add(n, carry):
            index = {}
            for name in reversed(left):
                index[name] = n % self.size[name]
                n = n // self.size[name]
            b, z, a = self._cell(index, done)
            if number == 0:
                x, y = g.xy(a, b, g.c)
                mine = g.at(self.src, self.order, y, g.c, z, x)[self.rows, :]
                summed = self.work[b, z, a].astype(jnp.float32) + mine.astype(jnp.float32)
            else:
                summed = self._sum(number, b, z, a, [index[name] for name in left])
            self.work[b, z, a] = summed.astype(jnp.bfloat16)
            return carry

        lax.fori_loop(0, total, add, 0)

    def _sum(self, number, b, z, a, index):
        axis = self.path[number - 1]
        summed = self.work[b, z, a].astype(jnp.float32)
        for k in range(self.size[axis] - 1):
            summed = summed + self.recv[axis][tuple([k] + index)].astype(jnp.float32)
        return summed

    def step(self, number):
        if number > 0:
            self.copies.arrived(self.stages[number - 1])
            self._add(number - 1)
        self.copies.start(self.stages[number])

    def total(self):
        self.copies.arrived(self.stages[3])
        return self._sum(3, self.g.b, self.g.z, self.g.a, [])

    def finish(self):
        for group in self.stages:
            self.copies.sent(group)


GATHER_PATHS = ("zab", "abz")
SCATTER_PATHS = ("baz", "zba")


def row_parts(rows, share=0):
    second = rows * share // 6 // 16 * 16
    parts = [(0, pl.ds(0, rows - second))]
    return parts + ([(1, pl.ds(rows - second, second))] if second else [])


def job_list(sizes, share=0):
    return [(n, path, rows) for n, (r, _) in enumerate(sizes) for path, rows in row_parts(r, share)]


def rounds(jobs, last):
    return [(n, step) for step in range(last + 1) for n in range(len(jobs))]


def gather_scratch(g, count):
    lanes = Gather.slots(g)
    dma = pltpu.SemaphoreType.DMA
    return [dma((count,)), dma((count, lanes)), dma((count, lanes))]


def gather_jobs(g, orders, jobs, ins, outs, scratch):
    local, send, recv = scratch
    return [Gather(g, orders[n], GATHER_PATHS[path], rows, ins[n], outs[n], local.at[j], send.at[j], recv.at[j])
            for j, (n, path, rows) in enumerate(jobs)]


def gather_first(n_dp, n_fsdp, shards, orders, share, collective_id):
    grid = Grid(n_dp, n_fsdp)
    count = len(shards)
    jobs = job_list([shards[0].shape]) + [(n + 1, p, r) for n, p, r in job_list([s.shape for s in shards[1:]], share)]

    def kernel(*refs):
        g = grid.here()
        g.barrier()
        whole, *others = gather_jobs(g, orders, jobs, refs[:count], refs[count : 2 * count], refs[2 * count :])
        whole.step(0)
        whole.step(1)
        for job in others:
            job.step(0)
        whole.step(2)
        whole.step(3)
        for job in others:
            job.pause()
        whole.finish()

    return pl.pallas_call(
        kernel,
        out_shape=[jax.ShapeDtypeStruct(grid.shape(o, *s.shape), s.dtype) for s, o in zip(shards, orders)],
        in_specs=[ANY] * count,
        out_specs=[ANY] * count,
        scratch_shapes=gather_scratch(grid, len(jobs)),
        compiler_params=pltpu.CompilerParams(collective_id=collective_id, has_side_effects=True),
        name="gather_first",
    )(*shards)


def scatter_scratch(g, sizes, jobs):
    out = []
    for n, path, rows in jobs:
        out += Scatter.scratch(g, SCATTER_PATHS[path], rows.size, sizes[n][1])
    dma = pltpu.SemaphoreType.DMA
    lanes = Scatter.slots(g)
    return out + [dma((len(jobs), lanes)), dma((len(jobs), lanes))]


def scatter_jobs(g, orders, jobs, ins, scratch):
    send, recv = scratch[4 * len(jobs) :]
    return [Scatter(g, orders[n], SCATTER_PATHS[path], rows, ins[n], scratch[4 * j : 4 * j + 4], send.at[j], recv.at[j])
            for j, (n, path, rows) in enumerate(jobs)]


def scatter_all(n_dp, n_fsdp, wholes, orders, collective_id, dtype=jnp.float32):
    grid = Grid(n_dp, n_fsdp)
    count = len(wholes)
    sizes = [w.shape[-2:] for w in wholes]
    jobs = job_list(sizes, 2)

    def kernel(*refs):
        ins, outs, scratch = refs[:count], refs[count : 2 * count], refs[2 * count :]
        g = grid.here()
        g.barrier()
        work = scatter_jobs(g, orders, jobs, ins, scratch)
        for j, step in rounds(jobs, 3):
            work[j].step(step)
        for job, (n, path, rows) in zip(work, jobs):
            outs[n][rows, :] = job.total().astype(dtype)
        for job in work:
            job.finish()

    return pl.pallas_call(
        kernel,
        out_shape=[jax.ShapeDtypeStruct(s, dtype) for s in sizes],
        in_specs=[VM] * count,
        out_specs=[VM] * count,
        scratch_shapes=scatter_scratch(grid, sizes, jobs),
        compiler_params=pltpu.CompilerParams(collective_id=collective_id, has_side_effects=True,
                                             vmem_limit_bytes=60 * 1024 * 1024),
        name="scatter_all",
    )(*wholes)


HEAD = 64
PAIR = 128


def last_dot(left, right):
    return lax.dot_general(left, right, (((1,), (1,)), ((), ())), preferred_element_type=jnp.float32)


def plain_dot(left, right):
    return lax.dot_general(left, right, (((1,), (0,)), ((), ())), preferred_element_type=jnp.float32)


def attend_block(length, start, size, q_heads, k_ref, v_turned, o_ref, lse_ref):
    slots = k_ref.shape[0]
    half = slots // 2
    keys = k_ref[...]
    key_index = lax.broadcasted_iota(jnp.int32, (slots - half, size), 0) + half
    scores, tops = [], []
    for head in range(2):
        q = q_heads[head, pl.ds(start, size), :]
        low = last_dot(keys[:half], q)
        high = jnp.where(key_index < length, last_dot(keys[half:], q), -1000000000.0)
        tops.append(jnp.maximum(jnp.max(low, axis=0, keepdims=True), jnp.max(high, axis=0, keepdims=True)))
        scores.append((low, high))
    raised = [[jnp.exp(s - tops[head]).astype(jnp.bfloat16) for s in scores[head]] for head in range(2)]
    parts = []
    for head in range(2):
        summed = plain_dot(v_turned[head][:, :half], raised[head][0])
        summed = summed + plain_dot(v_turned[head][:, half:], raised[head][1])
        mine = summed[head * HEAD : (head + 1) * HEAD]
        total = summed[(1 - head) * HEAD : (1 - head) * HEAD + 1]
        parts.append(mine * (1.0 / total))
        lse_ref[head, pl.ds(start, size)] = (tops[head] + jnp.log(total))[0]
    o_ref[pl.ds(start, size), :] = jnp.concatenate(parts, axis=0).T.astype(jnp.bfloat16)


def attend_prepare(q_ref, v_ref, q_heads, v_turned):
    slots = q_ref.shape[0]
    lane = lax.broadcasted_iota(jnp.int32, (slots, PAIR), 1)
    row = lax.broadcasted_iota(jnp.int32, (PAIR, slots), 0)
    q = q_ref[...].astype(jnp.float32) * (HEAD ** (-0.5))
    v = v_ref[...].astype(jnp.float32).T
    for head in range(2):
        q_heads[head] = jnp.where(lane // HEAD == head, q, 0.0).astype(jnp.bfloat16)
        v_turned[head] = jnp.where(row // HEAD == head, v, 1.0).astype(jnp.bfloat16)


def attend_kernel(size, count_ref, q_ref, k_ref, v_ref, o_ref, lse_ref, q_heads, v_turned):
    attend_prepare(q_ref, v_ref, q_heads, v_turned)
    length = count_ref[0]

    def step(n, carry):
        attend_block(length, pl.multiple_of(n * size, size), size, q_heads, k_ref, v_turned, o_ref, lse_ref.at[0])
        return carry

    lax.fori_loop(0, q_ref.shape[0] // size, step, 0)


def attend(counts, projected, size=256):
    slots, width = projected.shape
    d = width // 3
    pairs = d // PAIR
    spec = lambda part: pl.BlockSpec((slots, PAIR), lambda p, n, part=part: (0, part * pairs + p))
    return pl.pallas_call(
        partial(attend_kernel, size),
        out_shape=[jax.ShapeDtypeStruct((slots, d), jnp.bfloat16),
                   jax.ShapeDtypeStruct((pairs, 2, slots), jnp.float32)],
        grid_spec=pltpu.PrefetchScalarGridSpec(
            num_scalar_prefetch=1, grid=(pairs,),
            in_specs=[spec(0), spec(1), spec(2)],
            out_specs=[pl.BlockSpec((slots, PAIR), lambda p, n: (0, p)),
                       pl.BlockSpec((1, 2, slots), lambda p, n: (p, 0, 0))],
            scratch_shapes=[pltpu.VMEM((2, slots, PAIR), jnp.bfloat16), pltpu.VMEM((2, PAIR, slots), jnp.bfloat16)]),
        compiler_params=pltpu.CompilerParams(vmem_limit_bytes=48 * 1024 * 1024),
        name="attend",
    )(counts, projected, projected, projected)


def attend_back_scratch(slots):
    return [pltpu.VMEM((2, slots, PAIR), jnp.bfloat16), pltpu.VMEM((2, slots, PAIR), jnp.bfloat16),
            pltpu.VMEM((2, PAIR, slots), jnp.bfloat16), pltpu.VMEM((2, slots), jnp.float32),
            pltpu.VMEM((slots, PAIR), jnp.float32), pltpu.VMEM((slots, PAIR), jnp.float32)]


def attend_back_body(size, count_ref, q_ref, k_ref, v_ref, o_ref, do_ref, lse_ref, out_ref,
                     q_heads, do_heads, k_turned, inner, dk_sum, dv_sum, hook):
    slots = q_ref.shape[0]
    length = count_ref[0]
    lane = lax.broadcasted_iota(jnp.int32, (slots, PAIR), 1)
    row = lax.broadcasted_iota(jnp.int32, (PAIR, slots), 0)
    q = q_ref[...].astype(jnp.float32) * (HEAD ** (-0.5))
    do = do_ref[...].astype(jnp.float32)
    k = k_ref[...].astype(jnp.float32).T * (HEAD ** (-0.5))
    product = (do * o_ref[...].astype(jnp.float32)).T
    for head in range(2):
        q_heads[head] = jnp.where(lane // HEAD == head, q, 0.0).astype(jnp.bfloat16)
        do_heads[head] = jnp.where(lane // HEAD == head, do, 0.0).astype(jnp.bfloat16)
        k_turned[head] = jnp.where(row // HEAD == head, k, 0.0).astype(jnp.bfloat16)
        inner[head] = jnp.sum(product[head * HEAD : (head + 1) * HEAD], axis=0)
    dk_sum[...] = jnp.zeros_like(dk_sum)
    dv_sum[...] = jnp.zeros_like(dv_sum)
    key_index = lax.broadcasted_iota(jnp.int32, (slots, size), 0)

    def step(n, carry):
        rows = pl.ds(n * size, size)
        keys, values = k_ref[...], v_ref[...]
        dq = jnp.zeros((PAIR, size), jnp.float32)
        for head in range(2):
            q_block, do_block = q_heads[head, rows, :], do_heads[head, rows, :]
            scores = last_dot(keys, q_block)
            weights = jnp.exp(scores - lse_ref[0, head, rows][None, :])
            weights = jnp.where(key_index < length, weights, 0.0)
            weight_grad = last_dot(values, do_block)
            score_grad = (weights * (weight_grad - inner[head, rows][None, :])).astype(jnp.bfloat16)
            dv_sum[...] += plain_dot(weights.astype(jnp.bfloat16), do_block)
            dk_sum[...] += plain_dot(score_grad, q_block)
            dq = dq + plain_dot(k_turned[head], score_grad)
        out_ref[0, rows, :] = dq.T.astype(jnp.bfloat16)
        return carry

    for n in range(slots // size):
        hook(n)
        step(n, 0)
    out_ref[1] = dk_sum[...].astype(jnp.bfloat16)
    out_ref[2] = dv_sum[...].astype(jnp.bfloat16)


def project_attend(n_dp, n_fsdp, counts, tokens, weight_pieces, norm_rows, bias, pieces, fresh, orders, plan, collective_id,
                   size=512, block=256):
    slots, d = tokens.shape
    width = weight_pieces.shape[0] * weight_pieces.shape[2]
    pairs = d // PAIR
    head = slots // block
    grid = Grid(n_dp, n_fsdp)
    begun, count = len(pieces), len(pieces) + len(fresh)
    jobs = plan["jobs"]
    waits = [job[0] < begun for job in jobs]
    shapes = [jax.ShapeDtypeStruct(p.shape, p.dtype) for p in pieces]
    shapes += [jax.ShapeDtypeStruct(grid.shape(o, *a.shape), a.dtype) for a, o in zip(fresh, orders[begun:])]

    def kernel(count_ref, x, w_pieces, rows, bias_ref, *refs):
        (h_ref, p_ref, w_ref, o_ref, lse_ref), outs = refs[count : count + 5], refs[count + 5 : 2 * count + 5]
        projected, q_heads, v_turned = refs[2 * count + 5 : 2 * count + 8]
        g = grid.here()
        work = gather_jobs(g, orders, jobs, outs[:begun] + refs[begun:count], outs, refs[2 * count + 8 :])
        step = pl.program_id(0)

        def run(when):
            for j, number in plan.get(when, []):
                if number == 1 and waits[j]:
                    work[j].resume()
                else:
                    work[j].step(number)

        @pl.when(step == 0)
        def _():
            g.barrier()

        for when in range(head + pairs):
            if when in plan:
                pl.when(step == when)(partial(run, when))

        @pl.when(step == 0)
        def _():
            part = w_pieces.shape[2]
            for n in range(w_pieces.shape[0]):
                w_ref[:, n * part : (n + 1) * part] = w_pieces[n]

        @pl.when(step < head)
        def _():
            unit, spread = centered(x[...].astype(jnp.float32))
            low = (unit * rows[0:1] + rows[1:2]).astype(jnp.bfloat16)
            h_ref[...] = low
            result = (plain_dot(low, w_ref[...]) + bias_ref[...]).astype(jnp.bfloat16)
            p_ref[...] = result
            projected[pl.ds(pl.multiple_of(step * block, block), block), :] = result

        @pl.when(step >= head)
        def _():
            lane = pl.multiple_of((step - head) * PAIR, PAIR)
            q_ref, k_ref, v_ref = (projected.at[:, pl.ds(lane + part * d, PAIR)] for part in range(3))
            attend_prepare(q_ref, v_ref, q_heads, v_turned)
            length = count_ref[0]
            for n in range(slots // size):
                attend_block(length, n * size, size, q_heads, k_ref, v_turned, o_ref, lse_ref.at[0])

        @pl.when(step == head + pairs - 1)
        def _():
            run("end")
            for j, job in enumerate(work):
                job.finish(1 if waits[j] else 0)

    low = jnp.bfloat16
    row_at = lambda s: jnp.minimum(s, head - 1)
    pair_at = lambda s: jnp.maximum(s - head, 0)
    row = lambda w: pl.BlockSpec((block, w), lambda s, n: (row_at(s), 0))
    whole = lambda array: pl.BlockSpec(array.shape, lambda s, n: (0,) * array.ndim, pipeline_mode=pl.Buffered(1))
    return pl.pallas_call(
        kernel,
        out_shape=[jax.ShapeDtypeStruct((slots, d), low), jax.ShapeDtypeStruct((slots, width), low),
                   jax.ShapeDtypeStruct((d, width), low), jax.ShapeDtypeStruct((slots, d), low),
                   jax.ShapeDtypeStruct((pairs, 2, slots), jnp.float32)] + shapes,
        grid_spec=pltpu.PrefetchScalarGridSpec(
            num_scalar_prefetch=1, grid=(head + pairs,),
            in_specs=[row(d), whole(weight_pieces), whole(norm_rows), whole(bias)] + [ANY] * count,
            out_specs=[row(d), row(width), pl.BlockSpec((d, width), lambda s, n: (0, 0)),
                       pl.BlockSpec((slots, PAIR), lambda s, n: (0, pair_at(s))),
                       pl.BlockSpec((1, 2, slots), lambda s, n: (pair_at(s), 0, 0))] + [ANY] * count,
            scratch_shapes=[pltpu.VMEM((slots, width), low), pltpu.VMEM((2, slots, PAIR), low),
                            pltpu.VMEM((2, PAIR, slots), low)] + gather_scratch(grid, len(jobs))),
        input_output_aliases={5 + n: 5 + n for n in range(begun)},
        compiler_params=pltpu.CompilerParams(vmem_limit_bytes=56 * 1024 * 1024, collective_id=collective_id,
                                             has_side_effects=True),
        name="project_attend",
    )(counts, tokens, weight_pieces, norm_rows, bias, *pieces, *fresh)


FORWARD_PLAN = {
    "jobs": [(0, 0, pl.ds(0, 96)), (1, 0, pl.ds(0, 96)), (2, 0, pl.ds(0, 192))],
    0: [(0, 1), (1, 1), (2, 0)],
    2: [(0, 2)],
    5: [(1, 2), (0, 3)],
    7: [(2, 1)],
    9: [(2, 2)],
    "end": [(1, 3), (2, 3)],
}


def cut_block(grad, turned_blocks, out, rows):
    for z, x, y, c in places():
        row, column = piece_rows(turned_blocks, z, x, y, c)
        out[y, c, z, x, rows, :] = grad[row : row + 48, column : column + 384]


def grads_attend_back(n_dp, n_fsdp, counts, projected, attended, attended_grad, lse, cotangent, active, normed, hidden_grad,
                      branch_grad, plan, collective_id, size=256):
    slots, width = projected.shape
    d = width // 3
    pairs = d // PAIR
    panels = active.shape[1] // d
    head = 2 * panels + 1
    grid = Grid(n_dp, n_fsdp)
    sizes = [(panels * 48, 384), (panels * 48, 384), (48, 384)]
    half = panels * 24
    jobs = [(n, 0, pl.ds(at, half)) for n in range(2) for at in (0, half)] + [(2, 0, pl.ds(0, 48))]
    steps = slots // size

    def kernel(count_ref, q_ref, k_ref, v_ref, o_ref, do_ref, lse_ref, dy, z, h2, du, o_all, db, out_ref, *refs):
        outs, sums, parts, left = refs[:3], refs[3:5], refs[5:8], refs[8]
        own, scratch = refs[9:15], refs[15:]
        g = grid.here()
        work = scatter_jobs(g, ["j"] * 3, jobs, parts, scratch)
        step = pl.program_id(0)

        def run(when):
            for j, number in plan.get(when, []):
                work[j].step(number)

        @pl.when(step == 0)
        def _():
            g.barrier()

        def turn(ref):
            left[...] = ref[...].astype(jnp.float32).T.astype(jnp.bfloat16)

        for first, ref in ((0, dy), (panels, h2), (2 * panels, o_all)):
            pl.when(step == first)(partial(turn, ref))

        def blocks(part, first, right, kind):
            @pl.when((step >= first) & (step < first + (1 if part == 2 else panels)))
            def _():
                values = right[...]
                grad = plain_dot(left[...], values).astype(jnp.bfloat16)
                at = 0 if part == 2 else pl.multiple_of((step - first) * 48, 16)
                cut_block(grad, kind, parts[part], pl.ds(at, 48))
                if part > 0:
                    sums[part - 1][...] = jnp.sum(values.astype(jnp.float32), axis=0).reshape(1, 1, d)

        for when in range(head):
            if (when, 0) in plan:
                pl.when(step == when)(partial(run, (when, 0)))
        blocks(0, 0, z, True)
        blocks(1, panels, du, False)
        blocks(2, 2 * panels, db, False)

        def hook(n):
            for p in range(head, head + pairs):
                if (p, n) in plan:
                    pl.when(step == p)(partial(run, (p, n)))

        @pl.when(step >= head)
        def _():
            attend_back_body(size, count_ref, q_ref, k_ref, v_ref, o_ref, do_ref, lse_ref, out_ref, *own, hook)

        @pl.when(step == head + pairs - 1)
        def _():
            run("end")
            for job, (n, path, rows) in zip(work, jobs):
                outs[n][rows, :] = job.total().astype(jnp.bfloat16)
            for job in work:
                job.finish()

    pair_at = lambda s: jnp.maximum(s - head, 0)
    spec = lambda part: pl.BlockSpec((slots, PAIR), lambda s, n, part=part: (0, part * pairs + pair_at(s)))
    once = pl.BlockSpec((slots, d), lambda s, n: (0, 0), pipeline_mode=pl.Buffered(1))
    panel = lambda first: pl.BlockSpec((slots, d), lambda s, n: (0, jnp.clip(s - first, 0, panels - 1)))
    low, wide = jnp.bfloat16, jnp.float32
    return pl.pallas_call(
        kernel,
        out_shape=[jax.ShapeDtypeStruct((3, slots, d), low)]
        + [jax.ShapeDtypeStruct(s, low) for s in sizes]
        + [jax.ShapeDtypeStruct((panels, 1, d), wide), jax.ShapeDtypeStruct((1, 1, d), wide)],
        grid_spec=pltpu.PrefetchScalarGridSpec(
            num_scalar_prefetch=1, grid=(head + pairs,),
            in_specs=[spec(0), spec(1), spec(2), spec(0), spec(0),
                      pl.BlockSpec((1, 2, slots), lambda s, n: (pair_at(s), 0, 0)),
                      once, panel(0), once, panel(panels), once, once],
            out_specs=[pl.BlockSpec((3, slots, PAIR), lambda s, n: (0, 0, pair_at(s)))] + [VM] * 3
            + [pl.BlockSpec((1, 1, d), lambda s, n: (jnp.clip(s - panels, 0, panels - 1), 0, 0)),
               pl.BlockSpec((1, 1, d), lambda s, n: (0, 0, 0))],
            scratch_shapes=[pltpu.VMEM(grid.shape("j", *s), low) for s in sizes] + [pltpu.VMEM((d, slots), low)]
            + attend_back_scratch(slots) + scatter_scratch(grid, sizes, jobs)),
        compiler_params=pltpu.CompilerParams(vmem_limit_bytes=62 * 1024 * 1024, collective_id=collective_id,
                                             has_side_effects=True),
        name="grads_attend_back",
    )(counts, projected, projected, projected, attended, attended_grad, lse, cotangent, active, normed, hidden_grad,
      attended, branch_grad)


BACKWARD_PLAN = {
    (2, 0): [(0, 0)],
    (4, 0): [(1, 0)],
    (5, 0): [(0, 1)],
    (7, 0): [(1, 1), (2, 0)],
    (8, 0): [(3, 0), (0, 2)],
    (9, 0): [(4, 0), (2, 1)],
    (10, 0): [(1, 2), (0, 3), (3, 1)],
    (11, 0): [(2, 2), (1, 3), (4, 1)],
    (12, 0): [(3, 2), (2, 3)],
    (13, 0): [(4, 2), (3, 3)],
    (14, 0): [(4, 3)],
}


PIECE = (48, 384)


class Spread:
    def __init__(self, g, u, tiles, send, recv, base):
        qkv, out, up, down = tiles
        me = g.y * 2 + g.c
        rows = pl.ds(pl.multiple_of(g.y * 48, 16), 48)
        self.g, self.u, self.tiles, self.rows, self.me = g, u, tiles, rows, me
        self.copies = []

        def copy(src, dst, device):
            self.copies.append(remote(src, dst, send, recv, base + len(self.copies), device))

        for k in range(1, 4):
            to = (me + k) % 4
            device = {"dp": g.z * 2 + g.x, "fsdp": to}
            block, half = self.qkv_place(to)
            copy(u.at[block], qkv.at[half, rows, :], device)
            copy(u.at[3], out.at[g.c, rows, :], device)
            copy(u.at[4 + to], up.at[g.c, rows, :], device)
        for k in range(1, 4):
            to = (g.z + k) % 4
            copy(u.at[8 + to], down.at[pl.ds(pl.multiple_of(g.z * 48, 16), 48), :], {"dp": to * 2 + g.x, "fsdp": me})

    def qkv_place(self, to):
        c = self.g.c
        middle = (to + 1) // 2 % 2
        return to - to // 3 - middle * c, middle + c - 2 * middle * c

    def start(self):
        start_all(self.copies)
        g, u = self.g, self.u
        qkv, out, up, down = self.tiles
        block, half = self.qkv_place(self.me)
        qkv[half, self.rows, :] = u[block]
        out[g.c, self.rows, :] = u[3]
        up[g.c, self.rows, :] = u[4 + self.me]
        down[pl.ds(pl.multiple_of(g.z * 48, 16), 48), :] = u[8 + g.z]

    def finish(self):
        arrived(self.copies)
        sent(self.copies)


TILES = [jax.ShapeDtypeStruct((2, 96, 384), jnp.bfloat16)] * 3 + [jax.ShapeDtypeStruct((192, 384), jnp.bfloat16)]


def meet_all(g, n_dp, n_fsdp):
    count = n_dp * n_fsdp
    me = (g.z * g.X + g.x) * n_fsdp + g.y * 2 + g.c
    sem = pltpu.get_barrier_semaphore()
    ranks = [(me + k) % count for k in range(1, count)]
    peers = [{"dp": rank // n_fsdp, "fsdp": rank % n_fsdp} for rank in ranks]
    for peer in peers:
        pl.semaphore_signal(sem, inc=1, device_id=peer, device_id_type=MESH)
    pl.semaphore_wait(sem, count - 1)
    return me, ranks, peers


def piece_rows(turned, z, x, y, c):
    if turned:
        return 192 * (2 * y + c) + 48 * z, 384 * x
    return 96 * (2 * z + x) + 48 * y, 384 * c


def places():
    return [(z, x, y, c) for z in range(4) for x in range(2) for y in range(2) for c in range(2)]


def tile_values(g, tiles):
    qkv, out, up, down = tiles
    odd = (g.y * 2 + g.c) % 2 == 1
    wide = jnp.float32
    band = jnp.concatenate([qkv[0].astype(wide), qkv[1].astype(wide)], axis=1)
    half = out[g.y].astype(wide)
    return [jnp.where(odd, band[:, 192:], band[:, :576]), jnp.where(odd, half[:, 192:], half[:, :192]),
            jnp.concatenate([up[0].astype(wide), up[1].astype(wide)], axis=1), down[...].astype(wide).T]


def owner_exchange(n_dp, n_fsdp, blocks_of, owners, flags, u, small, stats, roots, masters, small_params, rates, collective_id):
    grid = Grid(n_dp, n_fsdp)
    count = n_dp * n_fsdp
    spread_lanes = 12

    def kernel(of_ref, owners_ref, flags_ref, u_ref, small_ref, w_qkv, w_out, w_up, w_down, params, stats_hbm, roots_hbm,
               g_qkv, g_out, g_up, g_down, n_qkv, n_out, n_up, n_down, g_small, n_small, new_stats_hbm,
               all_small, qkv, out, up, down, s_qkv, s_out, s_up, s_down, slots, got, got_steps, u_steps, stats, roots, block, turned, local, send, recv):
        g = grid.here()
        me, ranks, peers = meet_all(g, n_dp, n_fsdp)
        loads = [pltpu.make_async_copy(stats_hbm, stats, local.at[0]), pltpu.make_async_copy(roots_hbm, roots, local.at[1])]

        def fill(n, carry):
            slots[n] = u_ref[of_ref[n]]
            return carry

        lax.fori_loop(0, count, fill, 0)
        lane = 0
        copies, small_copies, step_copies = [], [], []
        for rank, peer in zip(ranks, peers):
            copies.append(remote(slots.at[rank], got.at[me], send, recv, lane, peer))
            small_copies.append(remote(small_ref, all_small.at[me], send, recv, lane + 1, peer))
            step_copies.append(remote(slots.at[rank], got_steps.at[me], send, recv, lane + 2, peer))
            lane += 3
        start_all(copies)
        for load in loads:
            load.start()
        got[me] = slots[me]
        all_small[me] = small_ref[...]
        for load in loads:
            load.wait()
        arrived(copies)
        sent(copies)
        spread = Spread(g, u_ref, (qkv, out, up, down), send, recv, lane)
        spread.start()
        start_all(small_copies)

        own, kind = flags_ref[0] == 1, flags_ref[1]
        for turn in range(2):
            for n, place in enumerate(places()):
                row, column = piece_rows(turn, *place)
                (turned if turn else block)[row : row + 48, column : column + 384] = got[n]
        block[...] = jnp.where(kind == 1, turned[...], block[...])
        turned[...] = block[...].astype(jnp.float32).T.astype(jnp.bfloat16)
        left = plain_dot(roots[kind].astype(jnp.bfloat16), block[...]).astype(jnp.bfloat16)
        step = plain_dot(left, roots[1 - kind].astype(jnp.bfloat16)).astype(jnp.bfloat16)
        for n, place in enumerate(places()):
            row, column = piece_rows(0, *place)
            other_row, other_column = piece_rows(1, *place)
            slots[n] = jnp.where(kind == 1, step[other_row : other_row + 48, other_column : other_column + 384],
                                 step[row : row + 48, column : column + 384])
        start_all(step_copies)
        got_steps[me] = slots[me]
        rows_by = last_dot(block[...], block[...])
        columns_by = last_dot(turned[...], turned[...])
        for side in range(2):
            mine, other = (rows_by, columns_by) if side == 0 else (columns_by, rows_by)
            moved = 0.5 * stats[side] + 0.5 * jnp.where(kind == 1, other, mine)
            stats[side] = jnp.where(own, moved, stats[side])
        store = pltpu.make_async_copy(stats, new_stats_hbm, local.at[0])
        store.start()
        spread.finish()
        for ref, value in zip((g_qkv, g_out, g_up, g_down), tile_values(g, (qkv, out, up, down))):
            ref[...] = value
        arrived(small_copies)
        lines = params.shape[0]
        total = jnp.concatenate([all_small[n].astype(jnp.float32) for n in range(-(-lines // 16))], axis=0)[:lines]
        g_small[...] = total
        mean = jnp.sum(total * total) * (1.0 / (lines * 128))
        n_small[...] = params[...] - rates[1] * total * lax.rsqrt(jnp.full((1, 128), mean + 1e-06, jnp.float32))
        arrived(step_copies)

        def pick(n, carry):
            u_steps[n] = got_steps[owners_ref[n]]
            return carry

        lax.fori_loop(0, 12, pick, 0)
        back = Spread(g, u_steps, (s_qkv, s_out, s_up, s_down), send, recv, lane + spread_lanes)
        back.start()
        sent(small_copies + step_copies)
        back.finish()
        new = tile_values(g, (s_qkv, s_out, s_up, s_down))
        for ref, master, value in zip((n_qkv, n_out, n_up, n_down), (w_qkv, w_out, w_up, w_down), new):
            ref[...] = master[...] - rates[0] * value
        store.wait()

    lanes = 3 * (count - 1) + 2 * spread_lanes
    low = jnp.bfloat16
    smem = pl.BlockSpec(memory_space=pltpu.SMEM)
    return pl.pallas_call(
        kernel,
        out_shape=[jax.ShapeDtypeStruct(a.shape, jnp.float32) for a in (*masters, *masters, small_params, small_params, stats)],
        in_specs=[smem, smem, smem] + [VM] * 7 + [ANY, ANY],
        out_specs=[VM] * 10 + [ANY],
        scratch_shapes=[pltpu.VMEM((count,) + small.shape, low)] + [pltpu.VMEM(t.shape, low) for t in TILES * 2]
        + [pltpu.VMEM((count,) + PIECE, low), pltpu.VMEM((count,) + PIECE, low),
                        pltpu.VMEM((count,) + PIECE, low), pltpu.VMEM((12,) + PIECE, low),
                        pltpu.VMEM(stats.shape, jnp.float32), pltpu.VMEM(roots.shape, jnp.float32),
                        pltpu.VMEM(stats.shape[1:], low), pltpu.VMEM(stats.shape[1:], low),
                        pltpu.SemaphoreType.DMA((2,)), pltpu.SemaphoreType.DMA((lanes,)), pltpu.SemaphoreType.DMA((lanes,))],
        compiler_params=pltpu.CompilerParams(collective_id=collective_id, has_side_effects=True,
                                             vmem_limit_bytes=56 * 1024 * 1024),
        name="owner_exchange",
    )(blocks_of, owners, flags, u, small, *masters, small_params, stats, roots)


def block_grads_kernel(turned_blocks, left, right, out, sums, left_turned):
    @pl.when(pl.program_id(0) == 0)
    def _():
        left_turned[...] = left[...].astype(jnp.float32).T.astype(jnp.bfloat16)

    values = right[...].reshape(right.shape[-2:])
    grad = plain_dot(left_turned[...], values).astype(jnp.bfloat16)
    for z, x, y, c in places():
        row, column = piece_rows(turned_blocks, z, x, y, c)
        out[y, c, z, x] = grad[row : row + 48, column : column + 384]
    sums[...] = jnp.sum(values.astype(jnp.float32), axis=0).reshape(sums.shape)


def block_grads(left, right, turned_blocks):
    rows, d = left.shape
    if right.ndim == 3:
        count = right.shape[0]
        spec = pl.BlockSpec((1, rows, d), lambda b: (b, 0, 0))
    else:
        count = right.shape[1] // d
        spec = pl.BlockSpec((rows, d), lambda b: (0, b))
    return pl.pallas_call(
        partial(block_grads_kernel, turned_blocks),
        out_shape=[jax.ShapeDtypeStruct((2, 2, 4, 2, count * 48, 384), jnp.bfloat16),
                   jax.ShapeDtypeStruct((count, 1, d), jnp.float32)],
        grid=(count,),
        in_specs=[pl.BlockSpec((rows, d), lambda b: (0, 0)), spec],
        out_specs=[pl.BlockSpec((2, 2, 4, 2, 48, 384), lambda b: (0, 0, 0, 0, b, 0)),
                   pl.BlockSpec((1, 1, d), lambda b: (b, 0, 0))],
        scratch_shapes=[pltpu.VMEM((d, rows), jnp.bfloat16)],
        compiler_params=pltpu.CompilerParams(vmem_limit_bytes=56 * 1024 * 1024),
        name="block_grads",
    )(left, right)


def centered(values):
    center = values - jnp.mean(values, axis=-1, keepdims=True)
    spread = lax.rsqrt(jnp.mean(center * center, axis=-1, keepdims=True) + 1e-06)
    return center * spread, spread


def norm_back(grads, unit, spread, gain):
    scaled = grads * gain
    mean = jnp.mean(scaled, axis=-1, keepdims=True)
    along = jnp.mean(scaled * unit, axis=-1, keepdims=True)
    return (scaled - mean - unit * along) * spread


def middle_kernel(x, attended, dy, out_w, up_w, down_w, rows, bias_up,
                  layer, h2, active, hidden_grad, middle_grad, branch_grad, attended_grad, sums):
    gain, shift, bias_out, bias_down = rows[0:1], rows[1:2], rows[2:3], rows[3:4]
    middle = x[...].astype(jnp.float32) + (plain_dot(attended[...], out_w[...]) + bias_out)
    unit, spread = centered(middle)
    normed = (unit * gain + shift).astype(jnp.bfloat16)
    h2[...] = normed
    grad_rows = dy[...]
    panels = up_w.shape[0]
    width = up_w.shape[2]
    half = width // 2
    y = jnp.zeros_like(middle)
    dh = jnp.zeros_like(middle)
    for panel in range(panels):
        hidden = plain_dot(normed, up_w[panel]) + bias_up[panel : panel + 1]
        passed = 0.5 + 0.5 * lax.erf(hidden * (0.5**0.5))
        z = (hidden * passed).astype(jnp.bfloat16)
        slope = passed + hidden * (jnp.exp(-0.5 * hidden * hidden) * 0.3989422804014327)
        back = jnp.concatenate([plain_dot(grad_rows, down_w[2 * panel]), plain_dot(grad_rows, down_w[2 * panel + 1])], axis=1)
        du = (slope * back).astype(jnp.bfloat16)
        active[:, panel * width : (panel + 1) * width] = z
        hidden_grad[:, panel * width : (panel + 1) * width] = du
        y = y + last_dot(z[:, :half], down_w[2 * panel]) + last_dot(z[:, half:], down_w[2 * panel + 1])
        dh = dh + last_dot(du, up_w[panel])
    layer[...] = (middle + y + bias_down).astype(jnp.bfloat16)
    wide = grad_rows.astype(jnp.float32)
    total = wide + norm_back(dh, unit, spread, gain)
    low = total.astype(jnp.bfloat16)
    middle_grad[...] = total
    branch_grad[...] = low
    attended_grad[...] = last_dot(low, out_w[...]).astype(jnp.bfloat16)

    @pl.when(pl.program_id(0) == 0)
    def _():
        sums[...] = jnp.zeros_like(sums)

    sums[0:1] += jnp.sum(dh * unit, axis=0, keepdims=True)
    sums[1:2] += jnp.sum(dh, axis=0, keepdims=True)
    sums[2:3] += jnp.sum(wide, axis=0, keepdims=True)


def middle_layer(tokens, attended, cotangent, out_w, up_w, down_w, rows, bias_up, block=256):
    count, d = tokens.shape
    ff = up_w.shape[0] * up_w.shape[2]
    row = lambda width: pl.BlockSpec((block, width), lambda r: (r, 0))
    whole = lambda array: pl.BlockSpec(array.shape, lambda r: (0,) * array.ndim)
    low, wide = jnp.bfloat16, jnp.float32
    shape = jax.ShapeDtypeStruct
    return pl.pallas_call(
        middle_kernel,
        out_shape=[shape((count, d), low), shape((count, d), low), shape((count, ff), low), shape((count, ff), low),
                   shape((count, d), wide), shape((count, d), low), shape((count, d), low), shape((8, d), wide)],
        grid=(count // block,),
        in_specs=[row(d), row(d), row(d)] + [whole(a) for a in (out_w, up_w, down_w, rows, bias_up)],
        out_specs=[row(d), row(d), row(ff), row(ff), row(d), row(d), row(d), pl.BlockSpec((8, d), lambda r: (0, 0))],
        compiler_params=pltpu.CompilerParams(vmem_limit_bytes=60 * 1024 * 1024),
        name="middle_layer",
    )(tokens, attended, cotangent, out_w, up_w, down_w, rows, bias_up)


def project_back(n_dp, n_fsdp, tokens, normed, projected_grad, weight, middle_grad, gain, others, collective_id, block=256):
    grid = Grid(n_dp, n_fsdp)
    count, d = tokens.shape
    n_blocks = projected_grad.shape[0]
    lines = others.shape[0]
    sizes = [(48, 384)] * n_blocks + [(16, 128)]
    jobs = job_list(sizes)
    low, wide = jnp.bfloat16, jnp.float32

    def kernel(x_h, normed_h, dp_h, weight_h, middle_h, gain_ref, others_ref, mine, small, input_grad_h, *refs):
        x, h, dp, w, middle, out = refs[:6]
        left, parts, small_parts, rows, packed, local = refs[6:12]
        scratch = refs[12:]
        g = grid.here()
        g.barrier()
        loads = [pltpu.make_async_copy(a, b, local.at[n])
                 for n, (a, b) in enumerate(((normed_h, h), (dp_h, dp), (weight_h, w), (x_h, x), (middle_h, middle)))]
        for load in loads:
            load.start()
        loads[0].wait()
        left[...] = h[...].astype(wide).T.astype(low)
        loads[1].wait()
        work = scatter_jobs(g, ["j"] * (n_blocks + 1), jobs, [parts.at[n] for n in range(n_blocks)] + [small_parts], scratch)
        for n in range(n_blocks):
            values = dp[n]
            grad = plain_dot(left[...], values).astype(low)
            for z, px, y, c in places():
                row, column = piece_rows(False, z, px, y, c)
                parts[n, y, c, z, px] = grad[row : row + 48, column : column + 384]
            work[n].step(0)
        for line in range(lines):
            rows[line : line + 1] = others_ref[line : line + 1]
        rows[4:5] = jnp.sum(dp[0].astype(wide), axis=0, keepdims=True)
        rows[5:6] = jnp.sum(dp[2].astype(wide), axis=0, keepdims=True)
        for load in loads[2:]:
            load.wait()

        def back(n):
            at = slice(n * block, (n + 1) * block)
            dh = last_dot(dp[0, at], w[:, :d]) + last_dot(dp[1, at], w[:, d : 2 * d]) + last_dot(dp[2, at], w[:, 2 * d :])
            unit, spread = centered(x[at].astype(wide))
            out[at] = (middle[at] + norm_back(dh, unit, spread, gain_ref[...])).astype(low)
            scaled, shifted = jnp.sum(dh * unit, axis=0, keepdims=True), jnp.sum(dh, axis=0, keepdims=True)
            rows[0:1] = scaled if n == 0 else rows[0:1] + scaled
            rows[1:2] = shifted if n == 0 else rows[1:2] + shifted

        plan = {0: [(0, 1)], 1: [(1, 1), (2, 1)], 2: [(0, 2)], 3: [(1, 2), (2, 2)]}
        for n in range(count // block):
            for j, step in plan.get(n, []):
                work[j].step(step)
            back(n)
        store = pltpu.make_async_copy(out, input_grad_h, local.at[0])
        store.start()
        packed[...] = jnp.zeros_like(packed)
        for line in range(lines):
            for part in range(d // 128):
                at = line * (d // 128) + part
                packed[at : at + 1] = rows[line : line + 1, part * 128 : (part + 1) * 128]
        small_parts[...] = jnp.zeros_like(small_parts)
        for n, (z, px, y, c) in enumerate(places()):
            if n < packed.shape[0] // 16:
                small_parts[y, c, z, px] = packed[16 * n : 16 * n + 16].astype(low)
        work[n_blocks].step(0)
        for j in range(n_blocks):
            work[j].step(3)
            work[n_blocks].step(j + 1)
        for n in range(n_blocks):
            mine[n] = work[n].total().astype(low)
        small[...] = work[n_blocks].total().astype(low)
        for job in work:
            job.finish()
        store.wait()

    shape = jax.ShapeDtypeStruct
    return pl.pallas_call(
        kernel,
        out_shape=[shape((n_blocks, 48, 384), low), shape((16, 128), low), shape((count, d), low)],
        in_specs=[ANY] * 5 + [VM, VM],
        out_specs=[VM, VM, ANY],
        scratch_shapes=[pltpu.VMEM((count, d), low), pltpu.VMEM((count, d), low), pltpu.VMEM(projected_grad.shape, low),
                        pltpu.VMEM(weight.shape, low), pltpu.VMEM((count, d), wide), pltpu.VMEM((count, d), low),
                        pltpu.VMEM((d, count), low), pltpu.VMEM((n_blocks,) + grid.shape("j", 48, 384), low),
                        pltpu.VMEM(grid.shape("j", 16, 128), low), pltpu.VMEM((16, d), wide), pltpu.VMEM((80, 128), wide),
                        pltpu.SemaphoreType.DMA((5,))] + scatter_scratch(grid, sizes, jobs),
        compiler_params=pltpu.CompilerParams(vmem_limit_bytes=60 * 1024 * 1024, collective_id=collective_id,
                                             has_side_effects=True),
        name="project_back",
    )(tokens, normed, projected_grad, weight, middle_grad, gain, others)


D = 768
HEADS = 12
HD = 64
FF = 3072
BLOCKS = 12


masked_score = -1000000000.0
decay_rate = 0.5
step_rate = 1.0
small_rate = 0.3
highest = lax.Precision.HIGHEST


def broadcast(value, axis, source):
    kept = jnp.where(lax.axis_index(axis) == source, value, 0).astype(value.dtype)
    return lax.psum(kept, axis)


def layer_norm(values, scale_row, shift_row):
    center = values - jnp.mean(values, axis=-1, keepdims=True)
    spread = jnp.mean(center * center, axis=-1, keepdims=True)
    return center * lax.rsqrt(spread + 1e-06) * scale_row + shift_row


def unpack(small_params):
    pieces = [small_params[number * D : (number + 1) * D] for number in range(8)]
    return pieces + [small_params[8 * D : 8 * D + FF]]


def row_dot(left, right):
    return jnp.dot(left, right, preferred_element_type=jnp.float32)


def column_dot(left, right):
    return lax.dot_general(
        left, right, (((0,), (0,)), ((), ())), preferred_element_type=jnp.float32
    )


def transposed_dot(left, right):
    return lax.dot_general(
        left, right, (((1,), (1,)), ((), ())), preferred_element_type=jnp.float32
    )


def block_split(array, block_rows):
    slots = array.shape[-1]
    return array.reshape(HEADS, HD, slots // block_rows, block_rows).transpose(2, 0, 1, 3)


def block_join(array):
    return array.transpose(0, 3, 1, 2).reshape(-1, D)


def attend_clip(queries, key_rows, value_rows, length):
    slots = queries.shape[-1]
    block_rows = min(512, slots)
    score_scale = float(HD) ** (-0.5)
    visible = (jnp.arange(slots) < length)[None, None, :]

    def one_block(query_block):
        scores = (
            jnp.einsum("hdq,hdk->hqk", query_block, key_rows, preferred_element_type=jnp.float32)
            * score_scale
        )
        scores = jnp.where(visible, scores, masked_score)
        row_top = jnp.max(scores, axis=-1, keepdims=True)
        raised = jnp.exp(scores - row_top)
        row_total = jnp.sum(raised, axis=-1, keepdims=True)
        softmax_weights = (raised / row_total).astype(jnp.bfloat16)
        attended = jnp.einsum(
            "hqk,hdk->hdq", softmax_weights, value_rows, preferred_element_type=jnp.float32
        )
        return (attended.astype(jnp.bfloat16), (row_top + jnp.log(row_total))[:, :, 0])

    attended, log_totals = lax.map(one_block, block_split(queries, block_rows))
    return (block_join(attended), log_totals)


def attend_back(queries, key_rows, value_rows, length, log_totals, out_grads):
    slots = queries.shape[-1]
    block_rows = min(512, slots)
    score_scale = float(HD) ** (-0.5)
    visible = (jnp.arange(slots) < length)[None, None, :]

    def one_block(carry, pieces):
        key_grad, value_grad = carry
        query_block, grad_block, log_block = pieces
        scores = (
            jnp.einsum("hdq,hdk->hqk", query_block, key_rows, preferred_element_type=jnp.float32)
            * score_scale
        )
        scores = jnp.where(visible, scores, masked_score)
        softmax_weights = jnp.exp(scores - log_block[:, :, None])
        weight_grad = jnp.einsum(
            "hdq,hdk->hqk", grad_block, value_rows, preferred_element_type=jnp.float32
        )
        inner_sum = jnp.sum(softmax_weights * weight_grad, axis=-1, keepdims=True)
        score_grad = (softmax_weights * (weight_grad - inner_sum)).astype(jnp.bfloat16)
        query_grad = (
            jnp.einsum("hqk,hdk->hdq", score_grad, key_rows, preferred_element_type=jnp.float32)
            * score_scale
        )
        key_grad = (
            key_grad
            + jnp.einsum(
                "hqk,hdq->hdk", score_grad, query_block, preferred_element_type=jnp.float32
            )
            * score_scale
        )
        value_grad = value_grad + jnp.einsum(
            "hqk,hdq->hdk",
            softmax_weights.astype(jnp.bfloat16),
            grad_block,
            preferred_element_type=jnp.float32,
        )
        return ((key_grad, value_grad), query_grad)

    blank = jnp.zeros((HEADS, HD, slots), jnp.float32)
    (key_grad, value_grad), query_grad = lax.scan(
        one_block,
        (blank, blank),
        (block_split(queries, block_rows), block_split(out_grads, block_rows), log_totals),
    )
    key_rows_grad = key_grad.transpose(2, 0, 1).reshape(slots, D)
    value_rows_grad = value_grad.transpose(2, 0, 1).reshape(slots, D)
    return (block_join(query_grad), key_rows_grad, value_rows_grad)


def take_columns(operands, member, start):
    return lax.slice_in_dim(operands[member], start, start + D, axis=1)


def take_rows(operands, member, start):
    return lax.slice_in_dim(operands[member], start, start + D, axis=0)


def block_pickers():
    pickers = [partial(take_columns, member=0, start=column * D) for column in range(3)]
    pickers.append(partial(take_columns, member=1, start=0))
    pickers = pickers + [
        partial(take_columns, member=2, start=column * D) for column in range(FF // D)
    ]
    pickers = pickers + [
        partial(take_rows, member=3, start=column * D) for column in range(FF // D)
    ]
    return pickers


def fetch_update(update, root):
    return broadcast(update.astype(jnp.bfloat16), ("dp", "fsdp"), root).astype(update.dtype)


def band_tile(band, like, column_index):
    columns_here = like.shape[1]
    return lax.dynamic_slice_in_dim(band, column_index * columns_here, columns_here, 1)


def row_band(pieces, like, row_index):
    rows_here = like.shape[0]
    start = row_index * rows_here
    return jnp.concatenate(
        [lax.dynamic_slice_in_dim(piece, start, rows_here, 0) for piece in pieces], axis=1
    )


def stacked_band(pieces, like, row_index):
    rows_here = like.shape[0]
    start = row_index * rows_here
    owner_block = start // D
    picked = jnp.zeros((rows_here, D), jnp.float32)
    for number in range(len(pieces)):
        inside = jnp.clip(start - number * D, 0, D - rows_here)
        piece = lax.dynamic_slice_in_dim(pieces[number], inside, rows_here, 0)
        picked = jnp.where(owner_block == number, piece, picked)
    return picked


def local_any(
    tokens,
    counts,
    cotangent,
    qkv_weight,
    out_weight,
    up_weight,
    down_weight,
    small_params,
    statistics,
    inverse_roots,
    owners,
):
    clips_here = counts.shape[0]
    slots = tokens.shape[0] // clips_here
    qkv_low = qkv_weight.astype(jnp.bfloat16)
    out_low = out_weight.astype(jnp.bfloat16)
    up_low = up_weight.astype(jnp.bfloat16)
    down_low = down_weight.astype(jnp.bfloat16)
    qkv_cols, out_cols, up_cols, down_cols = (
        lax.all_gather(qkv_low, "fsdp", axis=1, tiled=True),
        lax.all_gather(out_low, "fsdp", axis=1, tiled=True),
        lax.all_gather(up_low, "fsdp", axis=1, tiled=True),
        lax.all_gather(down_low, "fsdp", axis=1, tiled=True),
    )
    qkv_full, out_full, up_full, down_full = (
        lax.all_gather(qkv_cols, "dp", axis=0, tiled=True),
        lax.all_gather(out_cols, "dp", axis=0, tiled=True),
        lax.all_gather(up_cols, "dp", axis=0, tiled=True),
        lax.all_gather(down_cols, "dp", axis=0, tiled=True),
    )
    (
        gain_one,
        shift_one,
        gain_two,
        shift_two,
        bias_query,
        bias_value,
        bias_out,
        bias_down,
        bias_up,
    ) = unpack(small_params)

    def heads_view(array):
        return array.reshape(clips_here, slots, HEADS, HD).transpose(0, 2, 3, 1)

    def clip_forward(clip_group):
        return attend_clip(clip_group[0], clip_group[1], clip_group[2], clip_group[3])

    def clip_backward(clip_group):
        return attend_back(
            clip_group[0], clip_group[1], clip_group[2], clip_group[3], clip_group[4], clip_group[5]
        )

    inputs = tokens.astype(jnp.float32)
    normed = layer_norm(inputs, gain_one, shift_one).astype(jnp.bfloat16)
    projected = row_dot(normed, qkv_full)
    queries = heads_view((projected[:, :D] + bias_query).astype(jnp.bfloat16))
    key_rows = heads_view(projected[:, D : 2 * D].astype(jnp.bfloat16))
    value_rows = heads_view((projected[:, 2 * D :] + bias_value).astype(jnp.bfloat16))
    attended, log_totals = lax.map(clip_forward, (queries, key_rows, value_rows, counts))
    attended = attended.reshape(-1, D)
    middle = inputs + (row_dot(attended, out_full) + bias_out)
    normed_two = layer_norm(middle, gain_two, shift_two).astype(jnp.bfloat16)
    hidden = row_dot(normed_two, up_full) + bias_up
    active = jax.nn.gelu(hidden, approximate=False).astype(jnp.bfloat16)
    layer_rows = (middle + row_dot(active, down_full) + bias_down).astype(jnp.bfloat16)
    qkv_part, out_part, up_part, down_part = (
        lax.all_gather(qkv_low, "fsdp", axis=1, tiled=True),
        lax.all_gather(out_low, "fsdp", axis=1, tiled=True),
        lax.all_gather(up_low, "fsdp", axis=1, tiled=True),
        lax.all_gather(down_low, "fsdp", axis=1, tiled=True),
    )
    qkv_back, out_back, up_back, down_back = (
        lax.all_gather(qkv_part, "dp", axis=0, tiled=True),
        lax.all_gather(out_part, "dp", axis=0, tiled=True),
        lax.all_gather(up_part, "dp", axis=0, tiled=True),
        lax.all_gather(down_part, "dp", axis=0, tiled=True),
    )
    grad_down = column_dot(active, cotangent)
    grad_bias_down = jnp.sum(cotangent.astype(jnp.float32), axis=0)
    active_grad = transposed_dot(cotangent, down_back)
    unused_value, gelu_pull = jax.vjp(partial(jax.nn.gelu, approximate=False), hidden)
    hidden_grad = gelu_pull(active_grad)[0].astype(jnp.bfloat16)
    grad_up = column_dot(normed_two, hidden_grad)
    grad_bias_up = jnp.sum(hidden_grad.astype(jnp.float32), axis=0)
    normed_two_grad = transposed_dot(hidden_grad, up_back)
    unused_norm, norm_two_pull = jax.vjp(layer_norm, middle, gain_two, shift_two)
    middle_grad, grad_gain_two, grad_shift_two = norm_two_pull(normed_two_grad)
    middle_grad = middle_grad + cotangent.astype(jnp.float32)
    branch_grad = middle_grad.astype(jnp.bfloat16)
    grad_out = column_dot(attended, branch_grad)
    grad_bias_out = jnp.sum(branch_grad.astype(jnp.float32), axis=0)
    attended_grad = transposed_dot(branch_grad, out_back).astype(jnp.bfloat16)
    query_grad, key_grad, value_grad = lax.map(
        clip_backward,
        (queries, key_rows, value_rows, counts, log_totals, heads_view(attended_grad)),
    )
    projected_grad = (
        jnp.concatenate([query_grad, key_grad, value_grad], axis=-1)
        .reshape(-1, 3 * D)
        .astype(jnp.bfloat16)
    )
    grad_qkv = column_dot(normed, projected_grad)
    grad_bias_query = jnp.sum(projected_grad[:, :D].astype(jnp.float32), axis=0)
    grad_bias_value = jnp.sum(projected_grad[:, 2 * D :].astype(jnp.float32), axis=0)
    normed_grad = transposed_dot(projected_grad, qkv_back)
    unused_first, norm_one_pull = jax.vjp(layer_norm, inputs, gain_one, shift_one)
    input_rows_grad, grad_gain_one, grad_shift_one = norm_one_pull(normed_grad)
    input_grad = (middle_grad + input_rows_grad).astype(jnp.bfloat16)
    small_grad = jnp.concatenate(
        [
            grad_gain_one,
            grad_shift_one,
            grad_gain_two,
            grad_shift_two,
            grad_bias_query,
            grad_bias_value,
            grad_bias_out,
            grad_bias_down,
            grad_bias_up,
        ]
    )
    row_qkv, row_out, row_up, row_down, row_small = (
        lax.psum_scatter(
            grad_qkv.astype(jnp.bfloat16), "dp", scatter_dimension=0, tiled=True
        ).astype(jnp.float32),
        lax.psum_scatter(
            grad_out.astype(jnp.bfloat16), "dp", scatter_dimension=0, tiled=True
        ).astype(jnp.float32),
        lax.psum_scatter(
            grad_up.astype(jnp.bfloat16), "dp", scatter_dimension=0, tiled=True
        ).astype(jnp.float32),
        lax.psum_scatter(
            grad_down.astype(jnp.bfloat16), "dp", scatter_dimension=0, tiled=True
        ).astype(jnp.float32),
        lax.psum_scatter(
            small_grad.astype(jnp.bfloat16), "dp", scatter_dimension=0, tiled=True
        ).astype(jnp.float32),
    )
    shard_qkv, shard_out, shard_up, shard_down, shard_small = (
        lax.psum_scatter(
            row_qkv.astype(jnp.bfloat16), "fsdp", scatter_dimension=1, tiled=True
        ).astype(jnp.float32),
        lax.psum_scatter(
            row_out.astype(jnp.bfloat16), "fsdp", scatter_dimension=1, tiled=True
        ).astype(jnp.float32),
        lax.psum_scatter(
            row_up.astype(jnp.bfloat16), "fsdp", scatter_dimension=1, tiled=True
        ).astype(jnp.float32),
        lax.psum_scatter(
            row_down.astype(jnp.bfloat16), "fsdp", scatter_dimension=1, tiled=True
        ).astype(jnp.float32),
        lax.psum_scatter(
            row_small.astype(jnp.bfloat16), "fsdp", scatter_dimension=0, tiled=True
        ).astype(jnp.float32),
    )
    band_qkv, band_out, band_up, band_down, band_small = (
        lax.all_gather(shard_qkv.astype(jnp.bfloat16), "fsdp", axis=1, tiled=True).astype(
            shard_qkv.dtype
        ),
        lax.all_gather(shard_out.astype(jnp.bfloat16), "fsdp", axis=1, tiled=True).astype(
            shard_out.dtype
        ),
        lax.all_gather(shard_up.astype(jnp.bfloat16), "fsdp", axis=1, tiled=True).astype(
            shard_up.dtype
        ),
        lax.all_gather(shard_down.astype(jnp.bfloat16), "fsdp", axis=1, tiled=True).astype(
            shard_down.dtype
        ),
        lax.all_gather(shard_small.astype(jnp.bfloat16), "fsdp", axis=0, tiled=True).astype(
            shard_small.dtype
        ),
    )
    rank = lax.axis_index(("dp", "fsdp"))
    row_index = lax.axis_index("dp")
    column_index = lax.axis_index("fsdp")
    numbers = jnp.arange(BLOCKS, dtype=jnp.int32)
    matches = owners == rank
    mine = jnp.sum(jnp.where(matches, numbers, 0))
    owning = jnp.any(matches)

    def update_slot(gradient):
        left_stat = decay_rate * statistics[0, 0] + (1.0 - decay_rate) * jnp.dot(
            gradient, gradient.T, precision=highest, preferred_element_type=jnp.float32
        )
        right_stat = decay_rate * statistics[0, 1] + (1.0 - decay_rate) * jnp.dot(
            gradient.T, gradient, precision=highest, preferred_element_type=jnp.float32
        )
        left_step = jnp.dot(
            inverse_roots[0, 0], gradient, precision=highest, preferred_element_type=jnp.float32
        )
        update = jnp.dot(
            left_step, inverse_roots[0, 1], precision=highest, preferred_element_type=jnp.float32
        )
        return (jnp.stack([left_stat, right_stat])[None], update)

    def keep_slot(gradient):
        return (statistics, jnp.zeros((D, D), jnp.float32))

    whole_qkv, whole_out, whole_up, whole_down, whole_small = (
        lax.all_gather(band_qkv.astype(jnp.bfloat16), "dp", axis=0, tiled=True).astype(
            band_qkv.dtype
        ),
        lax.all_gather(band_out.astype(jnp.bfloat16), "dp", axis=0, tiled=True).astype(
            band_out.dtype
        ),
        lax.all_gather(band_up.astype(jnp.bfloat16), "dp", axis=0, tiled=True).astype(
            band_up.dtype
        ),
        lax.all_gather(band_down.astype(jnp.bfloat16), "dp", axis=0, tiled=True).astype(
            band_down.dtype
        ),
        lax.all_gather(band_small.astype(jnp.bfloat16), "dp", axis=0, tiled=True).astype(
            band_small.dtype
        ),
    )
    gradient = lax.switch(mine, block_pickers(), (whole_qkv, whole_out, whole_up, whole_down))
    new_statistics, update = lax.cond(owning, update_slot, keep_slot, gradient)
    arrivals = []
    for number in range(BLOCKS):
        arrivals.append(fetch_update(update, owners[number]))
    tile_qkv = band_tile(row_band(arrivals[0:3], qkv_weight, row_index), qkv_weight, column_index)
    tile_out = band_tile(row_band(arrivals[3:4], out_weight, row_index), out_weight, column_index)
    tile_up = band_tile(
        row_band(arrivals[4 : 4 + FF // D], up_weight, row_index), up_weight, column_index
    )
    tile_down = band_tile(
        stacked_band(arrivals[4 + FF // D :], down_weight, row_index), down_weight, column_index
    )
    new_qkv = qkv_weight - step_rate * tile_qkv
    new_out = out_weight - step_rate * tile_out
    new_up = up_weight - step_rate * tile_up
    new_down = down_weight - step_rate * tile_down
    new_small = small_params - small_rate * whole_small * lax.rsqrt(
        jnp.mean(whole_small * whole_small) + 1e-06
    )
    return (
        layer_rows,
        input_grad,
        shard_qkv,
        shard_out,
        shard_up,
        shard_down,
        whole_small,
        new_statistics,
        new_qkv,
        new_out,
        new_up,
        new_down,
        new_small,
    )


def local_staged(
    sizes,
    tokens,
    counts,
    cotangent,
    qkv_weight,
    out_weight,
    up_weight,
    down_weight,
    small_params,
    statistics,
    inverse_roots,
    owners,
):
    n_dp, n_fsdp = sizes
    qkv_low = qkv_weight.astype(jnp.bfloat16)
    later = (
        out_weight.astype(jnp.bfloat16),
        up_weight.astype(jnp.bfloat16),
        down_weight.astype(jnp.bfloat16).T,
    )
    (
        gain_one,
        shift_one,
        gain_two,
        shift_two,
        bias_query,
        bias_value,
        bias_out,
        bias_down,
        bias_up,
    ) = unpack(small_params)
    orders = ("j", "j", "j", "i")
    qkv_pieces, *begun = gather_first(n_dp, n_fsdp, (qkv_low,) + later[:2], orders[:3], 0, 1)
    bias_qkv = jnp.concatenate([bias_query, jnp.zeros((D,), jnp.float32), bias_value])
    normed, projected, qkv_full, attended, log_totals, out_pieces, up_pieces, down_pieces = project_attend(
        n_dp, n_fsdp, counts, tokens, qkv_pieces.reshape(n_fsdp, D, 3 * D // n_fsdp), jnp.stack([gain_one, shift_one]),
        bias_qkv[None], begun, later[2:], orders[1:], FORWARD_PLAN, 2,
    )
    layer_rows, normed_two, active, hidden_grad, middle_grad, branch_grad, attended_grad, sums = middle_layer(
        tokens,
        attended,
        cotangent,
        whole_of(out_pieces),
        up_pieces.reshape(n_fsdp, D, FF // n_fsdp),
        down_pieces.reshape(n_dp, D, FF // n_dp),
        jnp.stack([gain_two, shift_two, bias_out, bias_down]),
        bias_up.reshape(n_fsdp, FF // n_fsdp),
    )
    projected_grad, mine_down, mine_up, mine_out, grad_bias_up, grad_bias_out = grads_attend_back(
        n_dp, n_fsdp, counts, projected, attended, attended_grad, log_totals,
        cotangent, active, normed_two, hidden_grad, branch_grad, BACKWARD_PLAN, 3,
    )
    blank = jnp.zeros((2, D), jnp.float32)
    others = jnp.concatenate(
        [blank, sums[0:2], blank, grad_bias_out[0], sums[2:3], grad_bias_up[:, 0]], axis=0
    )
    mine_qkv, mine_small, input_grad = project_back(
        n_dp, n_fsdp, tokens, normed, projected_grad, qkv_full, middle_grad, gain_one[None], others, 4
    )
    devices = n_dp * n_fsdp
    mine = jnp.concatenate([mine_qkv] + [part.reshape(-1, 48, 384) for part in (mine_out, mine_up, mine_down)], axis=0)
    numbers = jnp.arange(BLOCKS, dtype=jnp.int32)
    ranks = jnp.arange(devices, dtype=jnp.int32)
    blocks_of = jnp.sum(jnp.where(owners[None, :] == ranks[:, None], numbers[None, :], 0), axis=1).astype(jnp.int32)
    rank = lax.axis_index(("dp", "fsdp"))
    owning = jnp.any(owners == rank)
    flags = jnp.stack([owning, blocks_of[rank] >= 4 + FF // D]).astype(jnp.int32)
    masters = (qkv_weight, out_weight, up_weight, down_weight)
    *results, whole_small, new_small, new_statistics = owner_exchange(
        n_dp, n_fsdp, blocks_of, owners, flags, mine, mine_small, statistics[0], inverse_roots[0],
        masters, small_params.reshape(-1, 128), (step_rate, small_rate), 5,
    )
    shard_qkv, shard_out, shard_up, shard_down, new_qkv, new_out, new_up, new_down = results
    whole_small, new_small = whole_small.reshape(-1), new_small.reshape(-1)
    return (
        layer_rows,
        input_grad,
        shard_qkv,
        shard_out,
        shard_up,
        shard_down,
        whole_small,
        new_statistics[None],
        new_qkv,
        new_out,
        new_up,
        new_down,
        new_small,
    )


def whole_of(pieces):
    rows, columns = pieces.shape[-2:]
    folded = pieces.reshape(pieces.shape[0] * pieces.shape[1], -1, columns)
    return folded.transpose(1, 0, 2).reshape(folded.shape[1], -1)


def solution(mesh):
    placed = (
        P(("dp", "fsdp"), None),
        P(("dp", "fsdp")),
        P(("dp", "fsdp"), None),
        P("dp", "fsdp"),
        P("dp", "fsdp"),
        P("dp", "fsdp"),
        P("dp", "fsdp"),
        P(),
        P(("dp", "fsdp"), None, None, None),
        P(("dp", "fsdp"), None, None, None),
        P(),
    )
    sizes = (mesh.shape["dp"], mesh.shape["fsdp"])
    local = partial(local_staged, sizes) if sizes == (8, 4) else local_any
    return jax.shard_map(
        local,
        mesh=mesh,
        in_specs=placed,
        out_specs=(
            P(("dp", "fsdp"), None),
            P(("dp", "fsdp"), None),
            P("dp", "fsdp"),
            P("dp", "fsdp"),
            P("dp", "fsdp"),
            P("dp", "fsdp"),
            P(),
            P(("dp", "fsdp"), None, None, None),
            P("dp", "fsdp"),
            P("dp", "fsdp"),
            P("dp", "fsdp"),
            P("dp", "fsdp"),
            P(),
        ),
        check_vma=False,
    )
```

```python
from functools import partial

import jax
import jax.numpy as jnp
from jax import lax
from jax.experimental import pallas as pl
from jax.experimental.pallas import tpu as pltpu
from jax.sharding import PartitionSpec as P

MESH = pl.DeviceIdType.MESH
ANY = pl.BlockSpec(memory_space=pl.ANY)
VM = pl.BlockSpec(memory_space=pltpu.VMEM)


class Grid:
    def __init__(self, n_dp, n_fsdp):
        self.Z = 4
        self.X = n_dp // 4
        self.Y = n_fsdp // 2
        self.swap = self.X == self.Y
        self.A, self.B = self.X, self.Y

    def here(self):
        dp, fs = lax.axis_index("dp"), lax.axis_index("fsdp")
        self.z, self.x = dp // self.X, dp % self.X
        self.y, self.c = fs // 2, fs % 2
        if self.swap:
            self.a = self.x + self.c * (self.y - self.x)
            self.b = self.y + self.c * (self.x - self.y)
        else:
            self.a, self.b = self.x, self.y
        return self

    def xy(self, a, b, c):
        if self.swap:
            return a + c * (b - a), b + c * (a - b)
        return a, b

    def device(self, z, a, b, c, frame=None):
        x, y = self.xy(a, b, self.c if frame is None else frame)
        return {"dp": z * self.X + x, "fsdp": y * 2 + c}

    def shape(self, order, r, w):
        if order == "j":
            return (self.Y, 2, self.Z, self.X, r, w)
        return (self.Z, self.X, self.Y, 2, r, w)

    def at(self, ref, order, y, c, z, x):
        return ref.at[y, c, z, x] if order == "j" else ref.at[z, x, y, c]

    def peers(self):
        out = [self.device((self.z + k) % self.Z, self.a, self.b, self.c) for k in range(1, self.Z)]
        out += [self.device(self.z, (self.a + k) % self.A, self.b, self.c) for k in range(1, self.A)]
        out += [self.device(self.z, self.a, (self.b + k) % self.B, self.c) for k in range(1, self.B)]
        out += [{"dp": self.z * self.X + self.x, "fsdp": self.y * 2 + 1 - self.c}]
        return out

    def barrier(self):
        sem = pltpu.get_barrier_semaphore()
        peers = self.peers()
        for peer in peers:
            pl.semaphore_signal(sem, inc=1, device_id=peer, device_id_type=MESH)
        pl.semaphore_wait(sem, len(peers))


def remote(src, dst, send, recv, slot, device):
    return pltpu.make_async_remote_copy(
        src_ref=src, dst_ref=dst, send_sem=send.at[slot], recv_sem=recv.at[slot], device_id=device, device_id_type=MESH
    )


def start_all(copies):
    for copy in copies:
        copy.start()


def arrived(copies):
    for copy in copies:
        copy.wait_recv()


def sent(copies):
    for copy in copies:
        copy.wait_send()


class Copies:
    def __init__(self, send, recv):
        self.send, self.recv, self.slot = send, recv, 0

    def add(self, group, describe):
        group.append((self.slot, describe))
        self.slot += 1

    def made(self, group):
        out = []
        for slot, describe in group:
            start, end, device = describe()
            out.append(remote(start, end, self.send, self.recv, slot, device))
        return out

    def start(self, group):
        start_all(self.made(group))

    def arrived(self, group):
        arrived(self.made(group))

    def sent(self, group):
        sent(self.made(group))


class Gather:
    def __init__(self, g, order, path, rows, src, out, local, send, recv):
        size = {"z": g.Z, "a": g.A, "b": g.B}
        self.copies = Copies(send, recv)

        def at(name, shift):
            place = {"z": g.z, "a": g.a, "b": g.b}[name]
            return (place + shift + size[name]) % size[name] if shift else place

        def piece(cell):
            where = {name: (at(name, value[1]) if isinstance(value, tuple) else value) for name, value in cell.items()}
            x, y = g.xy(where["a"], where["b"], g.c)
            return g.at(out, order, y, g.c, where["z"], x).at[..., rows, :]

        own_cell = {"z": ("own", 0), "a": ("own", 0), "b": ("own", 0)}

        def cells(full):
            out = [dict(own_cell)]
            for axis in full:
                if axis == "z":
                    out = [dict(cell, z=slice(None)) for cell in out]
                else:
                    out = [dict(cell, **{axis: n}) for cell in out for n in range(size[axis])]
            return out

        def near():
            return {"dp": g.z * g.X + g.x, "fsdp": g.y * 2 + 1 - g.c}

        def far(axis, k):
            return g.device(*[at(name, k if name == axis else 0) for name in "zab"], g.c)

        def own():
            return src.at[rows, :]

        self.own = lambda: pltpu.make_async_copy(own(), piece(own_cell), local)
        self.stages, self.near = [], [[]]
        self.copies.add(self.near[0], lambda: (own(), piece(own_cell), near()))
        full = ""
        for axis in path:
            self.stages.append([])
            self.near.append([])
            for cell in cells(full):
                for k in range(1, size[axis]):
                    from_src = not full
                    self.copies.add(self.stages[-1], lambda cell=cell, k=k, axis=axis, from_src=from_src: (
                        own() if from_src else piece(cell), piece(cell), far(axis, k)))
                    came = dict(cell, **{axis: ("own", -k)})
                    self.copies.add(self.near[-1], lambda came=came: (piece(came), piece(came), near()))
            full += axis

    @staticmethod
    def slots(g):
        zab = (g.Z - 1) + (g.A - 1) + g.A * (g.B - 1)
        abz = (g.A - 1) + g.A * (g.B - 1) + g.A * g.B * (g.Z - 1)
        return 1 + 2 * max(zab, abz)

    def step(self, number):
        if number == 0:
            self.own().start()
        else:
            if number == 1:
                self.own().wait()
            self.copies.arrived(self.stages[number - 1])
        if number < 3:
            self.copies.start(self.stages[number])
        self.copies.start(self.near[number])

    def pause(self):
        self.own().wait()
        for group in (self.stages[0], self.near[0]):
            self.copies.arrived(group)
            self.copies.sent(group)

    def resume(self):
        self.copies.start(self.stages[1])
        self.copies.start(self.near[1])

    def finish(self, first=0):
        for group in self.near[first:]:
            self.copies.arrived(group)
        for group in self.near[first:] + self.stages[first:]:
            self.copies.sent(group)


class Scatter:
    def __init__(self, g, order, path, rows, src, bufs, send, recv):
        self.g, self.path, self.order, self.rows, self.src = g, path, order, rows, src
        self.work = bufs[0]
        self.recv = dict(zip(path, bufs[1:]))
        work = self.work
        size = {"z": g.Z, "a": g.A, "b": g.B}
        self.size = size
        self.copies = Copies(send, recv)
        places = lambda: {"z": g.z, "a": g.a, "b": g.b}

        def other(b, a):
            x, y = g.xy(a, b, 1 - g.c)
            return (g.at(src, order, y, 1 - g.c, slice(None), x).at[:, rows, :], work.at[b, :, a],
                    {"dp": g.z * g.X + g.x, "fsdp": g.y * 2 + 1 - g.c})

        def onward(axis, k, done):
            place = places()
            to = dict(place, **{axis: (place[axis] + k) % size[axis]})
            where = {name: (place[name] if name in done else slice(None)) for name in "bza"}
            where[axis] = to[axis]
            return (work.at[where["b"], where["z"], where["a"]], self.recv[axis].at[k - 1],
                    g.device(to["z"], to["a"], to["b"], g.c))

        self.stages = [[]]
        for b in range(g.B):
            for a in range(g.A):
                self.copies.add(self.stages[0], partial(other, b, a))
        done = ""
        for axis in path:
            self.stages.append([])
            for k in range(1, size[axis]):
                self.copies.add(self.stages[-1], partial(onward, axis, k, done))
            done += axis

    @staticmethod
    def slots(g):
        return g.A * g.B + (g.B - 1) + (g.A - 1) + (g.Z - 1)

    @staticmethod
    def scratch(g, path, r, w):
        size = {"z": g.Z, "a": g.A, "b": g.B}
        out = [pltpu.VMEM((g.B, g.Z, g.A, r, w), jnp.bfloat16)]
        done = ""
        for axis in path:
            done += axis
            out.append(pltpu.VMEM((size[axis] - 1,) + tuple(size[n] for n in "bza" if n not in done) + (r, w), jnp.bfloat16))
        return out

    def _cell(self, index, done):
        place = {"z": self.g.z, "a": self.g.a, "b": self.g.b}
        return [place[n] if n in done else index[n] for n in "bza"]

    def _add(self, number):
        g, done = self.g, self.path[:number]
        left = [n for n in "bza" if n not in done]
        total = 1
        for name in left:
            total *= self.size[name]

        def add(n, carry):
            index = {}
            for name in reversed(left):
                index[name] = n % self.size[name]
                n = n // self.size[name]
            b, z, a = self._cell(index, done)
            if number == 0:
                x, y = g.xy(a, b, g.c)
                mine = g.at(self.src, self.order, y, g.c, z, x)[self.rows, :]
                summed = self.work[b, z, a].astype(jnp.float32) + mine.astype(jnp.float32)
            else:
                summed = self._sum(number, b, z, a, [index[name] for name in left])
            self.work[b, z, a] = summed.astype(jnp.bfloat16)
            return carry

        lax.fori_loop(0, total, add, 0)

    def _sum(self, number, b, z, a, index):
        axis = self.path[number - 1]
        summed = self.work[b, z, a].astype(jnp.float32)
        for k in range(self.size[axis] - 1):
            summed = summed + self.recv[axis][tuple([k] + index)].astype(jnp.float32)
        return summed

    def step(self, number):
        if number > 0:
            self.copies.arrived(self.stages[number - 1])
            self._add(number - 1)
        self.copies.start(self.stages[number])

    def total(self):
        self.copies.arrived(self.stages[3])
        return self._sum(3, self.g.b, self.g.z, self.g.a, [])

    def finish(self):
        for group in self.stages:
            self.copies.sent(group)


GATHER_PATHS = ("zab", "abz")
SCATTER_PATHS = ("baz", "zba")


def row_parts(rows, share=0):
    second = rows * share // 6 // 16 * 16
    parts = [(0, pl.ds(0, rows - second))]
    return parts + ([(1, pl.ds(rows - second, second))] if second else [])


def job_list(sizes, share=0):
    return [(n, path, rows) for n, (r, _) in enumerate(sizes) for path, rows in row_parts(r, share)]


def rounds(jobs, last):
    return [(n, step) for step in range(last + 1) for n in range(len(jobs))]


def gather_scratch(g, count):
    lanes = Gather.slots(g)
    dma = pltpu.SemaphoreType.DMA
    return [dma((count,)), dma((count, lanes)), dma((count, lanes))]


def gather_jobs(g, orders, jobs, ins, outs, scratch):
    local, send, recv = scratch
    return [Gather(g, orders[n], GATHER_PATHS[path], rows, ins[n], outs[n], local.at[j], send.at[j], recv.at[j])
            for j, (n, path, rows) in enumerate(jobs)]


def gather_first(n_dp, n_fsdp, shards, orders, plan, collective_id):
    grid = Grid(n_dp, n_fsdp)
    count = len(shards)
    jobs, order, wholes = plan

    def kernel(*refs):
        g = grid.here()
        low = refs[2 * count : 3 * count]
        low[0][...] = refs[0][...].astype(jnp.bfloat16)
        g.barrier()
        work = gather_jobs(g, orders, jobs, low, refs[count : 2 * count], refs[3 * count :])
        work[0].step(0)
        for n in range(1, count):
            low[n][...] = refs[n][...].astype(jnp.bfloat16)
        for job, step in order:
            work[job].step(step)
        for job in work[wholes:]:
            job.pause()
        for job in work[:wholes]:
            job.finish()

    return pl.pallas_call(
        kernel,
        out_shape=[jax.ShapeDtypeStruct(grid.shape(o, *s.shape), jnp.bfloat16) for s, o in zip(shards, orders)],
        in_specs=[VM] * count,
        out_specs=[ANY] * count,
        scratch_shapes=[pltpu.VMEM(s.shape, jnp.bfloat16) for s in shards] + gather_scratch(grid, len(jobs)),
        compiler_params=pltpu.CompilerParams(collective_id=collective_id, has_side_effects=True),
        name="gather_first",
    )(*shards)


def scatter_scratch(g, sizes, jobs):
    out = []
    for n, path, rows in jobs:
        out += Scatter.scratch(g, SCATTER_PATHS[path], rows.size, sizes[n][1])
    dma = pltpu.SemaphoreType.DMA
    lanes = Scatter.slots(g)
    return out + [dma((len(jobs), lanes)), dma((len(jobs), lanes))]


def scatter_jobs(g, orders, jobs, ins, scratch):
    send, recv = scratch[4 * len(jobs) :]
    return [Scatter(g, orders[n], SCATTER_PATHS[path], rows, ins[n], scratch[4 * j : 4 * j + 4], send.at[j], recv.at[j])
            for j, (n, path, rows) in enumerate(jobs)]


def scatter_all(n_dp, n_fsdp, wholes, orders, collective_id, dtype=jnp.float32):
    grid = Grid(n_dp, n_fsdp)
    count = len(wholes)
    sizes = [w.shape[-2:] for w in wholes]
    jobs = job_list(sizes, 2)

    def kernel(*refs):
        ins, outs, scratch = refs[:count], refs[count : 2 * count], refs[2 * count :]
        g = grid.here()
        g.barrier()
        work = scatter_jobs(g, orders, jobs, ins, scratch)
        for j, step in rounds(jobs, 3):
            work[j].step(step)
        for job, (n, path, rows) in zip(work, jobs):
            outs[n][rows, :] = job.total().astype(dtype)
        for job in work:
            job.finish()

    return pl.pallas_call(
        kernel,
        out_shape=[jax.ShapeDtypeStruct(s, dtype) for s in sizes],
        in_specs=[VM] * count,
        out_specs=[VM] * count,
        scratch_shapes=scatter_scratch(grid, sizes, jobs),
        compiler_params=pltpu.CompilerParams(collective_id=collective_id, has_side_effects=True,
                                             vmem_limit_bytes=60 * 1024 * 1024),
        name="scatter_all",
    )(*wholes)


HEAD = 64
PAIR = 128


def last_dot(left, right):
    return lax.dot_general(left, right, (((1,), (1,)), ((), ())), preferred_element_type=jnp.float32)


def plain_dot(left, right):
    return lax.dot_general(left, right, (((1,), (0,)), ((), ())), preferred_element_type=jnp.float32)


def attend_block(length, start, size, q_heads, k_ref, v_turned, o_ref, lse_ref):
    slots = k_ref.shape[0]
    half = slots // 2
    keys = k_ref[...]
    key_index = lax.broadcasted_iota(jnp.int32, (slots - half, size), 0) + half
    scores, tops = [], []
    for head in range(2):
        q = q_heads[head, pl.ds(start, size), :]
        low = last_dot(keys[:half], q)
        high = jnp.where(key_index < length, last_dot(keys[half:], q), -1000000000.0)
        tops.append(jnp.maximum(jnp.max(low, axis=0, keepdims=True), jnp.max(high, axis=0, keepdims=True)))
        scores.append((low, high))
    raised = [[jnp.exp(s - tops[head]).astype(jnp.bfloat16) for s in scores[head]] for head in range(2)]
    parts = []
    for head in range(2):
        summed = plain_dot(v_turned[head][:, :half], raised[head][0])
        summed = summed + plain_dot(v_turned[head][:, half:], raised[head][1])
        mine = summed[head * HEAD : (head + 1) * HEAD]
        total = summed[(1 - head) * HEAD : (1 - head) * HEAD + 1]
        parts.append(mine * (1.0 / total))
        lse_ref[head, pl.ds(start, size)] = (tops[head] + jnp.log(total))[0]
    o_ref[pl.ds(start, size), :] = jnp.concatenate(parts, axis=0).T.astype(jnp.bfloat16)


def attend_prepare(q_ref, v_ref, q_heads, v_turned):
    slots = q_ref.shape[0]
    lane = lax.broadcasted_iota(jnp.int32, (slots, PAIR), 1)
    row = lax.broadcasted_iota(jnp.int32, (PAIR, slots), 0)
    q = q_ref[...].astype(jnp.float32) * (HEAD ** (-0.5))
    v = v_ref[...].astype(jnp.float32).T
    for head in range(2):
        q_heads[head] = jnp.where(lane // HEAD == head, q, 0.0).astype(jnp.bfloat16)
        v_turned[head] = jnp.where(row // HEAD == head, v, 1.0).astype(jnp.bfloat16)


def attend_kernel(size, count_ref, q_ref, k_ref, v_ref, o_ref, lse_ref, q_heads, v_turned):
    attend_prepare(q_ref, v_ref, q_heads, v_turned)
    length = count_ref[0]

    def step(n, carry):
        attend_block(length, pl.multiple_of(n * size, size), size, q_heads, k_ref, v_turned, o_ref, lse_ref.at[0])
        return carry

    lax.fori_loop(0, q_ref.shape[0] // size, step, 0)


def attend(counts, projected, size=256):
    slots, width = projected.shape
    d = width // 3
    pairs = d // PAIR
    spec = lambda part: pl.BlockSpec((slots, PAIR), lambda p, n, part=part: (0, part * pairs + p))
    return pl.pallas_call(
        partial(attend_kernel, size),
        out_shape=[jax.ShapeDtypeStruct((slots, d), jnp.bfloat16),
                   jax.ShapeDtypeStruct((pairs, 2, slots), jnp.float32)],
        grid_spec=pltpu.PrefetchScalarGridSpec(
            num_scalar_prefetch=1, grid=(pairs,),
            in_specs=[spec(0), spec(1), spec(2)],
            out_specs=[pl.BlockSpec((slots, PAIR), lambda p, n: (0, p)),
                       pl.BlockSpec((1, 2, slots), lambda p, n: (p, 0, 0))],
            scratch_shapes=[pltpu.VMEM((2, slots, PAIR), jnp.bfloat16), pltpu.VMEM((2, PAIR, slots), jnp.bfloat16)]),
        compiler_params=pltpu.CompilerParams(vmem_limit_bytes=48 * 1024 * 1024),
        name="attend",
    )(counts, projected, projected, projected)


def attend_back_scratch(slots):
    return [pltpu.VMEM((2, slots, PAIR), jnp.bfloat16), pltpu.VMEM((2, slots, PAIR), jnp.bfloat16),
            pltpu.VMEM((2, PAIR, slots), jnp.bfloat16), pltpu.VMEM((2, slots), jnp.float32),
            pltpu.VMEM((slots, PAIR), jnp.float32), pltpu.VMEM((slots, PAIR), jnp.float32)]


def attend_back_body(size, count_ref, q_ref, k_ref, v_ref, o_ref, do_ref, lse_ref, out_ref,
                     q_heads, do_heads, k_turned, inner, dk_sum, dv_sum, hook):
    slots = q_ref.shape[0]
    length = count_ref[0]
    lane = lax.broadcasted_iota(jnp.int32, (slots, PAIR), 1)
    row = lax.broadcasted_iota(jnp.int32, (PAIR, slots), 0)
    q = q_ref[...].astype(jnp.float32) * (HEAD ** (-0.5))
    do = do_ref[...].astype(jnp.float32)
    k = k_ref[...].astype(jnp.float32).T * (HEAD ** (-0.5))
    product = (do * o_ref[...].astype(jnp.float32)).T
    for head in range(2):
        q_heads[head] = jnp.where(lane // HEAD == head, q, 0.0).astype(jnp.bfloat16)
        do_heads[head] = jnp.where(lane // HEAD == head, do, 0.0).astype(jnp.bfloat16)
        k_turned[head] = jnp.where(row // HEAD == head, k, 0.0).astype(jnp.bfloat16)
        inner[head] = jnp.sum(product[head * HEAD : (head + 1) * HEAD], axis=0)
    dk_sum[...] = jnp.zeros_like(dk_sum)
    dv_sum[...] = jnp.zeros_like(dv_sum)
    key_index = lax.broadcasted_iota(jnp.int32, (slots, size), 0)

    def step(n, carry):
        rows = pl.ds(n * size, size)
        keys, values = k_ref[...], v_ref[...]
        dq = jnp.zeros((PAIR, size), jnp.float32)
        for head in range(2):
            q_block, do_block = q_heads[head, rows, :], do_heads[head, rows, :]
            scores = last_dot(keys, q_block)
            weights = jnp.exp(scores - lse_ref[0, head, rows][None, :])
            weights = jnp.where(key_index < length, weights, 0.0)
            weight_grad = last_dot(values, do_block)
            score_grad = (weights * (weight_grad - inner[head, rows][None, :])).astype(jnp.bfloat16)
            dv_sum[...] += plain_dot(weights.astype(jnp.bfloat16), do_block)
            dk_sum[...] += plain_dot(score_grad, q_block)
            dq = dq + plain_dot(k_turned[head], score_grad)
        out_ref[0, rows, :] = dq.T.astype(jnp.bfloat16)
        return carry

    for n in range(slots // size):
        hook(n)
        step(n, 0)
    out_ref[1] = dk_sum[...].astype(jnp.bfloat16)
    out_ref[2] = dv_sum[...].astype(jnp.bfloat16)


def project_attend(n_dp, n_fsdp, counts, tokens, weight_pieces, norm_rows, bias, pieces, fresh, orders, plan, collective_id,
                   size=512, block=256):
    slots, d = tokens.shape
    width = weight_pieces.shape[0] * weight_pieces.shape[2]
    pairs = d // PAIR
    head = slots // block
    grid = Grid(n_dp, n_fsdp)
    begun, count = len(pieces), len(pieces) + len(fresh)
    jobs = plan["jobs"]
    waits = [job[0] < begun for job in jobs]
    shapes = [jax.ShapeDtypeStruct(p.shape, p.dtype) for p in pieces]
    turned = [a.shape[::-1] for a in fresh]
    shapes += [jax.ShapeDtypeStruct(grid.shape(o, *a), jnp.bfloat16) for a, o in zip(turned, orders[begun:])]

    def kernel(count_ref, x, w_pieces, rows, bias_ref, *refs):
        (h_ref, p_ref, w_ref, o_ref, lse_ref), outs = refs[count : count + 5], refs[count + 5 : 2 * count + 5]
        projected, q_heads, v_turned = refs[2 * count + 5 : 2 * count + 8]
        low_fresh = refs[2 * count + 8 : 2 * count + 8 + len(fresh)]
        g = grid.here()
        work = gather_jobs(g, orders, jobs, outs[:begun] + low_fresh, outs, refs[2 * count + 8 + len(fresh) :])
        step = pl.program_id(0)

        def run(when):
            for j, number in plan.get(when, []):
                if number == 1 and waits[j]:
                    work[j].resume()
                else:
                    work[j].step(number)

        @pl.when(step == 0)
        def _():
            for ref, master in zip(low_fresh, refs[begun:count]):
                ref[...] = master[...].T.astype(jnp.bfloat16)
            g.barrier()

        for when in range(head + pairs):
            if when in plan:
                pl.when(step == when)(partial(run, when))

        @pl.when(step == 0)
        def _():
            part = w_pieces.shape[2]
            for n in range(w_pieces.shape[0]):
                w_ref[:, n * part : (n + 1) * part] = w_pieces[n]

        @pl.when(step < head)
        def _():
            unit, spread = centered(x[...].astype(jnp.float32))
            low = (unit * rows[0:1] + rows[1:2]).astype(jnp.bfloat16)
            h_ref[...] = low
            result = (plain_dot(low, w_ref[...]) + bias_ref[...]).astype(jnp.bfloat16)
            p_ref[...] = result
            projected[pl.ds(pl.multiple_of(step * block, block), block), :] = result

        @pl.when(step >= head)
        def _():
            lane = pl.multiple_of((step - head) * PAIR, PAIR)
            q_ref, k_ref, v_ref = (projected.at[:, pl.ds(lane + part * d, PAIR)] for part in range(3))
            attend_prepare(q_ref, v_ref, q_heads, v_turned)
            length = count_ref[0]
            for n in range(slots // size):
                attend_block(length, n * size, size, q_heads, k_ref, v_turned, o_ref, lse_ref.at[0])

        @pl.when(step == head + pairs - 1)
        def _():
            run("end")
            for j, job in enumerate(work):
                job.finish(1 if waits[j] else 0)

    low = jnp.bfloat16
    row_at = lambda s: jnp.minimum(s, head - 1)
    pair_at = lambda s: jnp.maximum(s - head, 0)
    row = lambda w: pl.BlockSpec((block, w), lambda s, n: (row_at(s), 0))
    whole = lambda array: pl.BlockSpec(array.shape, lambda s, n: (0,) * array.ndim, pipeline_mode=pl.Buffered(1))
    return pl.pallas_call(
        kernel,
        out_shape=[jax.ShapeDtypeStruct((slots, d), low), jax.ShapeDtypeStruct((slots, width), low),
                   jax.ShapeDtypeStruct((d, width), low), jax.ShapeDtypeStruct((slots, d), low),
                   jax.ShapeDtypeStruct((pairs, 2, slots), jnp.float32)] + shapes,
        grid_spec=pltpu.PrefetchScalarGridSpec(
            num_scalar_prefetch=1, grid=(head + pairs,),
            in_specs=[row(d), whole(weight_pieces), whole(norm_rows), whole(bias)] + [ANY] * begun + [whole(a) for a in fresh],
            out_specs=[row(d), row(width), pl.BlockSpec((d, width), lambda s, n: (0, 0)),
                       pl.BlockSpec((slots, PAIR), lambda s, n: (0, pair_at(s))),
                       pl.BlockSpec((1, 2, slots), lambda s, n: (pair_at(s), 0, 0))] + [ANY] * count,
            scratch_shapes=[pltpu.VMEM((slots, width), low), pltpu.VMEM((2, slots, PAIR), low),
                            pltpu.VMEM((2, PAIR, slots), low)] + [pltpu.VMEM(a, low) for a in turned]
            + gather_scratch(grid, len(jobs))),
        input_output_aliases={5 + n: 5 + n for n in range(begun)},
        compiler_params=pltpu.CompilerParams(vmem_limit_bytes=56 * 1024 * 1024, collective_id=collective_id,
                                             has_side_effects=True),
        name="project_attend",
    )(counts, tokens, weight_pieces, norm_rows, bias, *pieces, *fresh)


FIRST_PLAN = (
    [(0, 0, pl.ds(0, 48)), (0, 0, pl.ds(48, 48)), (1, 0, pl.ds(0, 96)), (2, 0, pl.ds(0, 64)), (2, 1, pl.ds(64, 32))],
    [(0, 1), (1, 0), (0, 2), (1, 1), (2, 0), (3, 0), (4, 0), (0, 3), (1, 2), (1, 3)],
    2,
)
FORWARD_PLAN = {
    "jobs": [(0, 0, pl.ds(0, 96)), (1, 0, pl.ds(0, 64)), (1, 1, pl.ds(64, 32)), (2, 0, pl.ds(0, 192))],
    0: [(0, 1), (1, 1), (3, 0), (2, 1)],
    3: [(0, 2)],
    5: [(1, 2), (0, 3), (2, 2)],
    7: [(3, 1)],
    "end": [(1, 3), (3, 2), (2, 3), (3, 3)],
}


def cut_block(grad, turned_blocks, out, rows):
    for z, x, y, c in places():
        row, column = piece_rows(turned_blocks, z, x, y, c)
        out[y, c, z, x, rows, :] = grad[row : row + 48, column : column + 384]


def grads_attend_back(n_dp, n_fsdp, counts, projected, attended, attended_grad, lse, cotangent, active, normed, hidden_grad,
                      branch_grad, plan, collective_id, size=256):
    slots, width = projected.shape
    d = width // 3
    pairs = d // PAIR
    panels = active.shape[1] // d
    head = 2 * panels + 1
    grid = Grid(n_dp, n_fsdp)
    sizes = [(panels * 48, 384), (panels * 48, 384), (48, 384)]
    jobs = plan["jobs"]
    steps = slots // size

    def kernel(count_ref, q_ref, k_ref, v_ref, o_ref, do_ref, lse_ref, dy, z, h2, du, o_all, db, out_ref, *refs):
        outs, sums, parts, left = refs[:3], refs[3:5], refs[5:8], refs[8]
        own, scratch = refs[9:15], refs[15:]
        g = grid.here()
        work = scatter_jobs(g, ["j"] * 3, jobs, parts, scratch)
        step = pl.program_id(0)

        def run(when):
            for j, number in plan.get(when, []):
                work[j].step(number)

        @pl.when(step == 0)
        def _():
            g.barrier()

        def turn(ref):
            left[...] = ref[...].astype(jnp.float32).T.astype(jnp.bfloat16)

        for first, ref in ((0, dy), (panels, h2), (2 * panels, o_all)):
            pl.when(step == first)(partial(turn, ref))

        def blocks(part, first, right, kind):
            @pl.when((step >= first) & (step < first + (1 if part == 2 else panels)))
            def _():
                values = right[...]
                grad = plain_dot(left[...], values).astype(jnp.bfloat16)
                at = 0 if part == 2 else pl.multiple_of((step - first) * 48, 16)
                cut_block(grad, kind, parts[part], pl.ds(at, 48))
                if part > 0:
                    sums[part - 1][...] = jnp.sum(values.astype(jnp.float32), axis=0).reshape(1, 1, d)

        for when in range(head):
            if (when, 0) in plan:
                pl.when(step == when)(partial(run, (when, 0)))
        blocks(0, 0, z, True)
        blocks(1, panels, du, False)
        blocks(2, 2 * panels, db, False)

        def hook(n):
            for p in range(head, head + pairs):
                if (p, n) in plan:
                    pl.when(step == p)(partial(run, (p, n)))

        @pl.when(step >= head)
        def _():
            attend_back_body(size, count_ref, q_ref, k_ref, v_ref, o_ref, do_ref, lse_ref, out_ref, *own, hook)

        @pl.when(step == head + pairs - 1)
        def _():
            run("end")
            for job, (n, path, rows) in zip(work, jobs):
                outs[n][rows, :] = job.total().astype(jnp.bfloat16)
            for job in work:
                job.finish()

    pair_at = lambda s: jnp.maximum(s - head, 0)
    spec = lambda part: pl.BlockSpec((slots, PAIR), lambda s, n, part=part: (0, part * pairs + pair_at(s)))
    once = pl.BlockSpec((slots, d), lambda s, n: (0, 0), pipeline_mode=pl.Buffered(1))
    panel = lambda first: pl.BlockSpec((slots, d), lambda s, n: (0, jnp.clip(s - first, 0, panels - 1)))
    low, wide = jnp.bfloat16, jnp.float32
    return pl.pallas_call(
        kernel,
        out_shape=[jax.ShapeDtypeStruct((3, slots, d), low)]
        + [jax.ShapeDtypeStruct(s, low) for s in sizes]
        + [jax.ShapeDtypeStruct((panels, 1, d), wide), jax.ShapeDtypeStruct((1, 1, d), wide)],
        grid_spec=pltpu.PrefetchScalarGridSpec(
            num_scalar_prefetch=1, grid=(head + pairs,),
            in_specs=[spec(0), spec(1), spec(2), spec(0), spec(0),
                      pl.BlockSpec((1, 2, slots), lambda s, n: (pair_at(s), 0, 0)),
                      once, panel(0), once, panel(panels), once, once],
            out_specs=[pl.BlockSpec((3, slots, PAIR), lambda s, n: (0, 0, pair_at(s)))] + [VM] * 3
            + [pl.BlockSpec((1, 1, d), lambda s, n: (jnp.clip(s - panels, 0, panels - 1), 0, 0)),
               pl.BlockSpec((1, 1, d), lambda s, n: (0, 0, 0))],
            scratch_shapes=[pltpu.VMEM(grid.shape("j", *s), low) for s in sizes] + [pltpu.VMEM((d, slots), low)]
            + attend_back_scratch(slots) + scatter_scratch(grid, sizes, jobs)),
        compiler_params=pltpu.CompilerParams(vmem_limit_bytes=62 * 1024 * 1024, collective_id=collective_id,
                                             has_side_effects=True),
        name="grads_attend_back",
    )(counts, projected, projected, projected, attended, attended_grad, lse, cotangent, active, normed, hidden_grad,
      attended, branch_grad)


BACKWARD_PLAN = {
    "jobs": [(n, 0, pl.ds(at, 96)) for n in range(2) for at in (0, 96)] + [(2, 0, pl.ds(0, 48))],
    (2, 0): [(0, 0)],
    (4, 0): [(1, 0)],
    (5, 0): [(0, 1)],
    (7, 0): [(1, 1), (2, 0)],
    (8, 0): [(3, 0), (0, 2)],
    (9, 0): [(4, 0), (2, 1)],
    (10, 0): [(1, 2), (0, 3), (3, 1)],
    (11, 0): [(2, 2), (1, 3), (4, 1)],
    (12, 0): [(3, 2), (2, 3)],
    (13, 0): [(4, 2), (3, 3)],
    (14, 0): [(4, 3)],
}


PIECE = (48, 384)


class Spread:
    def __init__(self, g, u, tiles, send, recv, base):
        qkv, out, up, down = tiles
        me = g.y * 2 + g.c
        rows = pl.ds(pl.multiple_of(g.y * 48, 16), 48)
        self.g, self.u, self.tiles, self.rows, self.me = g, u, tiles, rows, me
        self.copies = []

        def copy(src, dst, device):
            self.copies.append(remote(src, dst, send, recv, base + len(self.copies), device))

        for k in range(1, 4):
            to = (me + k) % 4
            device = {"dp": g.z * 2 + g.x, "fsdp": to}
            block, half = self.qkv_place(to)
            copy(u.at[block], qkv.at[half, rows, :], device)
            copy(u.at[3], out.at[g.c, rows, :], device)
            copy(u.at[4 + to], up.at[g.c, rows, :], device)
        for k in range(1, 4):
            to = (g.z + k) % 4
            copy(u.at[8 + to], down.at[pl.ds(pl.multiple_of(g.z * 48, 16), 48), :], {"dp": to * 2 + g.x, "fsdp": me})

    def qkv_place(self, to):
        c = self.g.c
        middle = (to + 1) // 2 % 2
        return to - to // 3 - middle * c, middle + c - 2 * middle * c

    def start(self):
        start_all(self.copies)
        g, u = self.g, self.u
        qkv, out, up, down = self.tiles
        block, half = self.qkv_place(self.me)
        qkv[half, self.rows, :] = u[block]
        out[g.c, self.rows, :] = u[3]
        up[g.c, self.rows, :] = u[4 + self.me]
        down[pl.ds(pl.multiple_of(g.z * 48, 16), 48), :] = u[8 + g.z]

    def finish(self):
        arrived(self.copies)
        sent(self.copies)


TILES = [jax.ShapeDtypeStruct((2, 96, 384), jnp.bfloat16)] * 3 + [jax.ShapeDtypeStruct((192, 384), jnp.bfloat16)]


def meet_all(g, n_dp, n_fsdp):
    count = n_dp * n_fsdp
    me = (g.z * g.X + g.x) * n_fsdp + g.y * 2 + g.c
    sem = pltpu.get_barrier_semaphore()
    ranks = [(me + k) % count for k in range(1, count)]
    peers = [{"dp": rank // n_fsdp, "fsdp": rank % n_fsdp} for rank in ranks]
    for peer in peers:
        pl.semaphore_signal(sem, inc=1, device_id=peer, device_id_type=MESH)
    pl.semaphore_wait(sem, count - 1)
    return me, ranks, peers


def piece_rows(turned, z, x, y, c):
    if turned:
        return 192 * (2 * y + c) + 48 * z, 384 * x
    return 96 * (2 * z + x) + 48 * y, 384 * c


def places():
    return [(z, x, y, c) for z in range(4) for x in range(2) for y in range(2) for c in range(2)]


def tile_values(g, tiles):
    qkv, out, up, down = tiles
    odd = (g.y * 2 + g.c) % 2 == 1
    wide = jnp.float32
    band = jnp.concatenate([qkv[0].astype(wide), qkv[1].astype(wide)], axis=1)
    half = out[g.y].astype(wide)
    return [jnp.where(odd, band[:, 192:], band[:, :576]), jnp.where(odd, half[:, 192:], half[:, :192]),
            jnp.concatenate([up[0].astype(wide), up[1].astype(wide)], axis=1), down[...].astype(wide).T]


def owner_exchange(n_dp, n_fsdp, owners, mine, small, roots, collective_id):
    grid = Grid(n_dp, n_fsdp)
    count = n_dp * n_fsdp
    n_blocks = owners.shape[0]
    d = roots.shape[1]
    spread_lanes = 12

    def kernel(owners_ref, qkv_ref, out_ref, up_ref, down_ref, small_ref, roots_hbm,
               qkv, out, up, down, s_qkv, s_out, s_up, s_down, all_small, block, turned,
               u, slots, got, got_steps, u_steps, roots, local, send, recv):
        g = grid.here()
        me, ranks, peers = meet_all(g, n_dp, n_fsdp)
        load = pltpu.make_async_copy(roots_hbm, roots, local.at[0])
        load.start()
        first = 0
        for ref in (qkv_ref, out_ref, up_ref, down_ref):
            part = ref.shape[0] // 48
            u[first : first + part] = ref[...].reshape(part, 48, 384)
            first += part

        def owned(n):
            found = 0
            for b in range(n_blocks):
                found = jnp.where(owners_ref[b] == n, b, found)
            return found

        def fill(n, carry):
            slots[n] = u[owned(n)]
            return carry

        lax.fori_loop(0, count, fill, 0)
        lane = 0
        copies, small_copies, step_copies = [], [], []
        for rank, peer in zip(ranks, peers):
            copies.append(remote(slots.at[rank], got.at[me], send, recv, lane, peer))
            small_copies.append(remote(small_ref, all_small.at[me], send, recv, lane + 1, peer))
            step_copies.append(remote(slots.at[rank], got_steps.at[me], send, recv, lane + 2, peer))
            lane += 3
        start_all(copies)
        got[me] = slots[me]
        all_small[me] = small_ref[...]
        load.wait()
        kind = jnp.where(owned(me) >= 8, 1, 0)
        arrived(copies)
        sent(copies)
        spread = Spread(g, u, (qkv, out, up, down), send, recv, lane)
        spread.start()
        start_all(small_copies)
        for turn in range(2):
            for n, place in enumerate(places()):
                row, column = piece_rows(turn, *place)
                (turned if turn else block)[row : row + 48, column : column + 384] = got[n]
        block[...] = jnp.where(kind == 1, turned[...], block[...])
        left = plain_dot(roots[kind].astype(jnp.bfloat16), block[...]).astype(jnp.bfloat16)
        step = plain_dot(left, roots[1 - kind].astype(jnp.bfloat16)).astype(jnp.bfloat16)
        for n, place in enumerate(places()):
            row, column = piece_rows(0, *place)
            other_row, other_column = piece_rows(1, *place)
            slots[n] = jnp.where(kind == 1, step[other_row : other_row + 48, other_column : other_column + 384],
                                 step[row : row + 48, column : column + 384])
        start_all(step_copies)
        got_steps[me] = slots[me]
        wide = block[...].astype(jnp.float32)
        wide_turned = wide.T
        block[...] = jnp.where(kind == 1, wide_turned, wide).astype(jnp.bfloat16)
        turned[...] = jnp.where(kind == 1, wide, wide_turned).astype(jnp.bfloat16)
        spread.finish()
        arrived(small_copies)
        arrived(step_copies)

        def pick(n, carry):
            u_steps[n] = got_steps[owners_ref[n]]
            return carry

        lax.fori_loop(0, n_blocks, pick, 0)
        back = Spread(g, u_steps, (s_qkv, s_out, s_up, s_down), send, recv, lane + spread_lanes)
        back.start()
        sent(small_copies + step_copies)
        back.finish()

    lanes = 3 * (count - 1) + 2 * spread_lanes
    low = jnp.bfloat16
    pieces = pltpu.VMEM((count,) + PIECE, low)
    return pl.pallas_call(
        kernel,
        out_shape=TILES + TILES + [jax.ShapeDtypeStruct((count,) + small.shape, low), jax.ShapeDtypeStruct((d, d), low),
                                   jax.ShapeDtypeStruct((d, d), low)],
        in_specs=[pl.BlockSpec(memory_space=pltpu.SMEM)] + [VM] * 5 + [ANY],
        out_specs=[VM] * 11,
        scratch_shapes=[pltpu.VMEM((n_blocks,) + PIECE, low), pieces, pieces, pieces, pltpu.VMEM((n_blocks,) + PIECE, low),
                        pltpu.VMEM(roots.shape, jnp.float32), pltpu.SemaphoreType.DMA((1,)),
                        pltpu.SemaphoreType.DMA((lanes,)), pltpu.SemaphoreType.DMA((lanes,))],
        compiler_params=pltpu.CompilerParams(collective_id=collective_id, has_side_effects=True,
                                             vmem_limit_bytes=56 * 1024 * 1024),
        name="owner_exchange",
    )(owners, *mine, small, roots)


def finish_step(n_dp, n_fsdp, owners, exchanged, masters, small_params, stats, rates, parts=4):
    grid = Grid(n_dp, n_fsdp)
    tiles, all_small, block, turned = exchanged[:8], *exchanged[8:]
    d = block.shape[0]
    rows = d // parts

    def kernel(owners_ref, qkv, out, up, down, s_qkv, s_out, s_up, s_down, all_small, block, turned,
               w_qkv, w_out, w_up, w_down, params, stats_ref,
               g_qkv, g_out, g_up, g_down, n_qkv, n_out, n_up, n_down, g_small, n_small, new_stats):
        g = grid.here()
        step = pl.program_id(0)
        me = (g.z * g.X + g.x) * n_fsdp + g.y * 2 + g.c
        own = owners_ref[0] == me
        for n in range(1, owners.shape[0]):
            own = own | (owners_ref[n] == me)

        @pl.when(step == 0)
        def _():
            values = tile_values(g, (qkv, out, up, down))
            for ref, value in zip((g_qkv, g_out, g_up, g_down), values):
                ref[...] = value
            steps = tile_values(g, (s_qkv, s_out, s_up, s_down))
            for ref, master, value in zip((n_qkv, n_out, n_up, n_down), (w_qkv, w_out, w_up, w_down), steps):
                ref[...] = master[...] - rates[0] * value
            lines = params.shape[0]
            total = jnp.concatenate([all_small[n].astype(jnp.float32) for n in range(-(-lines // 16))], axis=0)[:lines]
            g_small[...] = total
            mean = jnp.sum(total * total) * (1.0 / (lines * 128))
            n_small[...] = params[...] - rates[1] * total * lax.rsqrt(jnp.full((1, 128), mean + 1e-06, jnp.float32))

        @pl.when(own)
        def _():
            at = pl.ds(pl.multiple_of(step * rows, rows), rows)
            new_stats[0] = 0.5 * stats_ref[0] + 0.5 * last_dot(block[at, :], block[...])
            new_stats[1] = 0.5 * stats_ref[1] + 0.5 * last_dot(turned[at, :], turned[...])

        @pl.when(jnp.logical_not(own))
        def _():
            new_stats[...] = stats_ref[...]

    whole = lambda a: pl.BlockSpec(a.shape, lambda s, n: (0,) * len(a.shape))
    banded = pl.BlockSpec((2, rows, d), lambda s, n: (0, s, 0))
    results = [jax.ShapeDtypeStruct(a.shape, jnp.float32) for a in (*masters, *masters, small_params, small_params)]
    return pl.pallas_call(
        kernel,
        out_shape=results + [jax.ShapeDtypeStruct(stats.shape, jnp.float32)],
        grid_spec=pltpu.PrefetchScalarGridSpec(
            num_scalar_prefetch=1, grid=(parts,),
            in_specs=[whole(a) for a in (*exchanged, *masters, small_params)] + [banded],
            out_specs=[whole(a) for a in results] + [banded]),
        compiler_params=pltpu.CompilerParams(vmem_limit_bytes=56 * 1024 * 1024),
        name="finish_step",
    )(owners, *exchanged, *masters, small_params, stats)


def centered(values):
    center = values - jnp.mean(values, axis=-1, keepdims=True)
    spread = lax.rsqrt(jnp.mean(center * center, axis=-1, keepdims=True) + 1e-06)
    return center * spread, spread


def norm_back(grads, unit, spread, gain):
    scaled = grads * gain
    mean = jnp.mean(scaled, axis=-1, keepdims=True)
    along = jnp.mean(scaled * unit, axis=-1, keepdims=True)
    return (scaled - mean - unit * along) * spread


def middle_kernel(x, attended, dy, out_pieces, up_w, down_w, rows, bias_up,
                  layer, h2, active, hidden_grad, middle_grad, branch_grad, attended_grad, sums, out_w):
    @pl.when(pl.program_id(0) == 0)
    def _():
        part = out_pieces.shape[2]
        for n in range(out_pieces.shape[0]):
            out_w[:, n * part : (n + 1) * part] = out_pieces[n]

    gain, shift, bias_out, bias_down = rows[0:1], rows[1:2], rows[2:3], rows[3:4]
    middle = x[...].astype(jnp.float32) + (plain_dot(attended[...], out_w[...]) + bias_out)
    unit, spread = centered(middle)
    normed = (unit * gain + shift).astype(jnp.bfloat16)
    h2[...] = normed
    grad_rows = dy[...]
    panels = up_w.shape[0]
    width = up_w.shape[2]
    half = width // 2
    y = jnp.zeros_like(middle)
    dh = jnp.zeros_like(middle)
    for panel in range(panels):
        hidden = plain_dot(normed, up_w[panel]) + bias_up[panel : panel + 1]
        passed = 0.5 + 0.5 * lax.erf(hidden * (0.5**0.5))
        z = (hidden * passed).astype(jnp.bfloat16)
        slope = passed + hidden * (jnp.exp(-0.5 * hidden * hidden) * 0.3989422804014327)
        back = jnp.concatenate([plain_dot(grad_rows, down_w[2 * panel]), plain_dot(grad_rows, down_w[2 * panel + 1])], axis=1)
        du = (slope * back).astype(jnp.bfloat16)
        active[:, panel * width : (panel + 1) * width] = z
        hidden_grad[:, panel * width : (panel + 1) * width] = du
        y = y + last_dot(z[:, :half], down_w[2 * panel]) + last_dot(z[:, half:], down_w[2 * panel + 1])
        dh = dh + last_dot(du, up_w[panel])
    layer[...] = (middle + y + bias_down).astype(jnp.bfloat16)
    wide = grad_rows.astype(jnp.float32)
    total = wide + norm_back(dh, unit, spread, gain)
    low = total.astype(jnp.bfloat16)
    middle_grad[...] = total
    branch_grad[...] = low
    attended_grad[...] = last_dot(low, out_w[...]).astype(jnp.bfloat16)

    @pl.when(pl.program_id(0) == 0)
    def _():
        sums[...] = jnp.zeros_like(sums)

    sums[0:1] += jnp.sum(dh * unit, axis=0, keepdims=True)
    sums[1:2] += jnp.sum(dh, axis=0, keepdims=True)
    sums[2:3] += jnp.sum(wide, axis=0, keepdims=True)


def middle_layer(tokens, attended, cotangent, out_w, up_w, down_w, rows, bias_up, block=256):
    count, d = tokens.shape
    ff = up_w.shape[0] * up_w.shape[2]
    row = lambda width: pl.BlockSpec((block, width), lambda r: (r, 0))
    whole = lambda array: pl.BlockSpec(array.shape, lambda r: (0,) * array.ndim)
    low, wide = jnp.bfloat16, jnp.float32
    shape = jax.ShapeDtypeStruct
    return pl.pallas_call(
        middle_kernel,
        out_shape=[shape((count, d), low), shape((count, d), low), shape((count, ff), low), shape((count, ff), low),
                   shape((count, d), wide), shape((count, d), low), shape((count, d), low), shape((8, d), wide)],
        grid=(count // block,),
        in_specs=[row(d), row(d), row(d)] + [whole(a) for a in (out_w, up_w, down_w, rows, bias_up)],
        out_specs=[row(d), row(d), row(ff), row(ff), row(d), row(d), row(d), pl.BlockSpec((8, d), lambda r: (0, 0))],
        scratch_shapes=[pltpu.VMEM((d, d), low)],
        compiler_params=pltpu.CompilerParams(vmem_limit_bytes=60 * 1024 * 1024),
        name="middle_layer",
    )(tokens, attended, cotangent, out_w, up_w, down_w, rows, bias_up)


def project_back(n_dp, n_fsdp, tokens, normed, projected_grad, weight, middle_grad, gain, sums, bias_out, bias_up, plan,
                 collective_id, block=256):
    grid = Grid(n_dp, n_fsdp)
    count, d = tokens.shape
    n_blocks = projected_grad.shape[0]
    lines = 8 + bias_up.shape[0]
    sizes = [(48, 384)] * n_blocks + [(16, 128)]
    jobs = plan["jobs"]
    low, wide = jnp.bfloat16, jnp.float32

    def kernel(x_h, normed_h, dp_h, weight_h, middle_h, gain_ref, sums_ref, bias_out_ref, bias_up_ref, mine, small, input_grad_h, *refs):
        x, h, dp, w, middle, out = refs[:6]
        left, parts, small_parts, rows, packed, local = refs[6:12]
        scratch = refs[12:]
        g = grid.here()
        g.barrier()
        loads = [pltpu.make_async_copy(a, b, local.at[n])
                 for n, (a, b) in enumerate(((normed_h, h), (dp_h, dp), (weight_h, w), (x_h, x), (middle_h, middle)))]
        for load in loads:
            load.start()
        loads[0].wait()
        left[...] = h[...].astype(wide).T.astype(low)
        loads[1].wait()
        work = scatter_jobs(g, ["j"] * (n_blocks + 1), jobs, [parts.at[n] for n in range(n_blocks)] + [small_parts], scratch)
        for n in range(n_blocks):
            values = dp[n]
            grad = plain_dot(left[...], values).astype(low)
            for z, px, y, c in places():
                row, column = piece_rows(False, z, px, y, c)
                parts[n, y, c, z, px] = grad[row : row + 48, column : column + 384]
            for j, job in enumerate(jobs):
                if job[0] == n:
                    work[j].step(0)
        rows[2:4] = sums_ref[0:2]
        rows[6:7] = bias_out_ref[0]
        rows[7:8] = sums_ref[2:3]
        for n in range(lines - 8):
            rows[8 + n : 9 + n] = bias_up_ref[n]
        rows[4:5] = jnp.sum(dp[0].astype(wide), axis=0, keepdims=True)
        rows[5:6] = jnp.sum(dp[2].astype(wide), axis=0, keepdims=True)
        for load in loads[2:]:
            load.wait()

        def back(n):
            at = slice(n * block, (n + 1) * block)
            dh = last_dot(dp[0, at], w[:, :d]) + last_dot(dp[1, at], w[:, d : 2 * d]) + last_dot(dp[2, at], w[:, 2 * d :])
            unit, spread = centered(x[at].astype(wide))
            out[at] = (middle[at] + norm_back(dh, unit, spread, gain_ref[...])).astype(low)
            scaled, shifted = jnp.sum(dh * unit, axis=0, keepdims=True), jnp.sum(dh, axis=0, keepdims=True)
            rows[0:1] = scaled if n == 0 else rows[0:1] + scaled
            rows[1:2] = shifted if n == 0 else rows[1:2] + shifted

        for n in range(count // block):
            for j, step in plan.get(n, []):
                work[j].step(step)
            back(n)
        store = pltpu.make_async_copy(out, input_grad_h, local.at[0])
        store.start()
        packed[...] = jnp.zeros_like(packed)
        for line in range(lines):
            for part in range(d // 128):
                at = line * (d // 128) + part
                packed[at : at + 1] = rows[line : line + 1, part * 128 : (part + 1) * 128]
        small_parts[...] = jnp.zeros_like(small_parts)
        for n, (z, px, y, c) in enumerate(places()):
            if n < packed.shape[0] // 16:
                small_parts[y, c, z, px] = packed[16 * n : 16 * n + 16].astype(low)
        for j, step in plan["end"]:
            work[j].step(step)
        for job, (n, path, at) in zip(work, jobs):
            if n < n_blocks:
                mine[n, at, :] = job.total().astype(low)
            else:
                small[...] = job.total().astype(low)
        for job in work:
            job.finish()
        store.wait()

    shape = jax.ShapeDtypeStruct
    return pl.pallas_call(
        kernel,
        out_shape=[shape((n_blocks, 48, 384), low), shape((16, 128), low), shape((count, d), low)],
        in_specs=[ANY] * 5 + [VM] * 4,
        out_specs=[VM, VM, ANY],
        scratch_shapes=[pltpu.VMEM((count, d), low), pltpu.VMEM((count, d), low), pltpu.VMEM(projected_grad.shape, low),
                        pltpu.VMEM(weight.shape, low), pltpu.VMEM((count, d), wide), pltpu.VMEM((count, d), low),
                        pltpu.VMEM((d, count), low), pltpu.VMEM((n_blocks,) + grid.shape("j", 48, 384), low),
                        pltpu.VMEM(grid.shape("j", 16, 128), low), pltpu.VMEM((16, d), wide), pltpu.VMEM((80, 128), wide),
                        pltpu.SemaphoreType.DMA((5,))] + scatter_scratch(grid, sizes, jobs),
        compiler_params=pltpu.CompilerParams(vmem_limit_bytes=60 * 1024 * 1024, collective_id=collective_id,
                                             has_side_effects=True),
        name="project_back",
    )(tokens, normed, projected_grad, weight, middle_grad, gain, sums, bias_out, bias_up)


TAIL_PLAN = {
    "jobs": [(0, 0, pl.ds(0, 48)), (1, 0, pl.ds(0, 48)), (2, 0, pl.ds(0, 48)), (3, 0, pl.ds(0, 16))],
    0: [(0, 1)],
    1: [(1, 1), (0, 2)],
    2: [(2, 1)],
    3: [(1, 2), (0, 3)],
    "end": [(3, 0), (2, 2), (3, 1), (1, 3), (3, 2), (2, 3), (3, 3)],
}


D = 768
HEADS = 12
HD = 64
FF = 3072
BLOCKS = 12


masked_score = -1000000000.0
decay_rate = 0.5
step_rate = 1.0
small_rate = 0.3
highest = lax.Precision.HIGHEST


def broadcast(value, axis, source):
    kept = jnp.where(lax.axis_index(axis) == source, value, 0).astype(value.dtype)
    return lax.psum(kept, axis)


def layer_norm(values, scale_row, shift_row):
    center = values - jnp.mean(values, axis=-1, keepdims=True)
    spread = jnp.mean(center * center, axis=-1, keepdims=True)
    return center * lax.rsqrt(spread + 1e-06) * scale_row + shift_row


def unpack(small_params):
    pieces = [small_params[number * D : (number + 1) * D] for number in range(8)]
    return pieces + [small_params[8 * D : 8 * D + FF]]


def row_dot(left, right):
    return jnp.dot(left, right, preferred_element_type=jnp.float32)


def column_dot(left, right):
    return lax.dot_general(
        left, right, (((0,), (0,)), ((), ())), preferred_element_type=jnp.float32
    )


def transposed_dot(left, right):
    return lax.dot_general(
        left, right, (((1,), (1,)), ((), ())), preferred_element_type=jnp.float32
    )


def block_split(array, block_rows):
    slots = array.shape[-1]
    return array.reshape(HEADS, HD, slots // block_rows, block_rows).transpose(2, 0, 1, 3)


def block_join(array):
    return array.transpose(0, 3, 1, 2).reshape(-1, D)


def attend_clip(queries, key_rows, value_rows, length):
    slots = queries.shape[-1]
    block_rows = min(512, slots)
    score_scale = float(HD) ** (-0.5)
    visible = (jnp.arange(slots) < length)[None, None, :]

    def one_block(query_block):
        scores = (
            jnp.einsum("hdq,hdk->hqk", query_block, key_rows, preferred_element_type=jnp.float32)
            * score_scale
        )
        scores = jnp.where(visible, scores, masked_score)
        row_top = jnp.max(scores, axis=-1, keepdims=True)
        raised = jnp.exp(scores - row_top)
        row_total = jnp.sum(raised, axis=-1, keepdims=True)
        softmax_weights = (raised / row_total).astype(jnp.bfloat16)
        attended = jnp.einsum(
            "hqk,hdk->hdq", softmax_weights, value_rows, preferred_element_type=jnp.float32
        )
        return (attended.astype(jnp.bfloat16), (row_top + jnp.log(row_total))[:, :, 0])

    attended, log_totals = lax.map(one_block, block_split(queries, block_rows))
    return (block_join(attended), log_totals)


def attend_back(queries, key_rows, value_rows, length, log_totals, out_grads):
    slots = queries.shape[-1]
    block_rows = min(512, slots)
    score_scale = float(HD) ** (-0.5)
    visible = (jnp.arange(slots) < length)[None, None, :]

    def one_block(carry, pieces):
        key_grad, value_grad = carry
        query_block, grad_block, log_block = pieces
        scores = (
            jnp.einsum("hdq,hdk->hqk", query_block, key_rows, preferred_element_type=jnp.float32)
            * score_scale
        )
        scores = jnp.where(visible, scores, masked_score)
        softmax_weights = jnp.exp(scores - log_block[:, :, None])
        weight_grad = jnp.einsum(
            "hdq,hdk->hqk", grad_block, value_rows, preferred_element_type=jnp.float32
        )
        inner_sum = jnp.sum(softmax_weights * weight_grad, axis=-1, keepdims=True)
        score_grad = (softmax_weights * (weight_grad - inner_sum)).astype(jnp.bfloat16)
        query_grad = (
            jnp.einsum("hqk,hdk->hdq", score_grad, key_rows, preferred_element_type=jnp.float32)
            * score_scale
        )
        key_grad = (
            key_grad
            + jnp.einsum(
                "hqk,hdq->hdk", score_grad, query_block, preferred_element_type=jnp.float32
            )
            * score_scale
        )
        value_grad = value_grad + jnp.einsum(
            "hqk,hdq->hdk",
            softmax_weights.astype(jnp.bfloat16),
            grad_block,
            preferred_element_type=jnp.float32,
        )
        return ((key_grad, value_grad), query_grad)

    blank = jnp.zeros((HEADS, HD, slots), jnp.float32)
    (key_grad, value_grad), query_grad = lax.scan(
        one_block,
        (blank, blank),
        (block_split(queries, block_rows), block_split(out_grads, block_rows), log_totals),
    )
    key_rows_grad = key_grad.transpose(2, 0, 1).reshape(slots, D)
    value_rows_grad = value_grad.transpose(2, 0, 1).reshape(slots, D)
    return (block_join(query_grad), key_rows_grad, value_rows_grad)


def take_columns(operands, member, start):
    return lax.slice_in_dim(operands[member], start, start + D, axis=1)


def take_rows(operands, member, start):
    return lax.slice_in_dim(operands[member], start, start + D, axis=0)


def block_pickers():
    pickers = [partial(take_columns, member=0, start=column * D) for column in range(3)]
    pickers.append(partial(take_columns, member=1, start=0))
    pickers = pickers + [
        partial(take_columns, member=2, start=column * D) for column in range(FF // D)
    ]
    pickers = pickers + [
        partial(take_rows, member=3, start=column * D) for column in range(FF // D)
    ]
    return pickers


def fetch_update(update, root):
    return broadcast(update.astype(jnp.bfloat16), ("dp", "fsdp"), root).astype(update.dtype)


def band_tile(band, like, column_index):
    columns_here = like.shape[1]
    return lax.dynamic_slice_in_dim(band, column_index * columns_here, columns_here, 1)


def row_band(pieces, like, row_index):
    rows_here = like.shape[0]
    start = row_index * rows_here
    return jnp.concatenate(
        [lax.dynamic_slice_in_dim(piece, start, rows_here, 0) for piece in pieces], axis=1
    )


def stacked_band(pieces, like, row_index):
    rows_here = like.shape[0]
    start = row_index * rows_here
    owner_block = start // D
    picked = jnp.zeros((rows_here, D), jnp.float32)
    for number in range(len(pieces)):
        inside = jnp.clip(start - number * D, 0, D - rows_here)
        piece = lax.dynamic_slice_in_dim(pieces[number], inside, rows_here, 0)
        picked = jnp.where(owner_block == number, piece, picked)
    return picked


def local_any(
    tokens,
    counts,
    cotangent,
    qkv_weight,
    out_weight,
    up_weight,
    down_weight,
    small_params,
    statistics,
    inverse_roots,
    owners,
):
    clips_here = counts.shape[0]
    slots = tokens.shape[0] // clips_here
    qkv_low = qkv_weight.astype(jnp.bfloat16)
    out_low = out_weight.astype(jnp.bfloat16)
    up_low = up_weight.astype(jnp.bfloat16)
    down_low = down_weight.astype(jnp.bfloat16)
    qkv_cols, out_cols, up_cols, down_cols = (
        lax.all_gather(qkv_low, "fsdp", axis=1, tiled=True),
        lax.all_gather(out_low, "fsdp", axis=1, tiled=True),
        lax.all_gather(up_low, "fsdp", axis=1, tiled=True),
        lax.all_gather(down_low, "fsdp", axis=1, tiled=True),
    )
    qkv_full, out_full, up_full, down_full = (
        lax.all_gather(qkv_cols, "dp", axis=0, tiled=True),
        lax.all_gather(out_cols, "dp", axis=0, tiled=True),
        lax.all_gather(up_cols, "dp", axis=0, tiled=True),
        lax.all_gather(down_cols, "dp", axis=0, tiled=True),
    )
    (
        gain_one,
        shift_one,
        gain_two,
        shift_two,
        bias_query,
        bias_value,
        bias_out,
        bias_down,
        bias_up,
    ) = unpack(small_params)

    def heads_view(array):
        return array.reshape(clips_here, slots, HEADS, HD).transpose(0, 2, 3, 1)

    def clip_forward(clip_group):
        return attend_clip(clip_group[0], clip_group[1], clip_group[2], clip_group[3])

    def clip_backward(clip_group):
        return attend_back(
            clip_group[0], clip_group[1], clip_group[2], clip_group[3], clip_group[4], clip_group[5]
        )

    inputs = tokens.astype(jnp.float32)
    normed = layer_norm(inputs, gain_one, shift_one).astype(jnp.bfloat16)
    projected = row_dot(normed, qkv_full)
    queries = heads_view((projected[:, :D] + bias_query).astype(jnp.bfloat16))
    key_rows = heads_view(projected[:, D : 2 * D].astype(jnp.bfloat16))
    value_rows = heads_view((projected[:, 2 * D :] + bias_value).astype(jnp.bfloat16))
    attended, log_totals = lax.map(clip_forward, (queries, key_rows, value_rows, counts))
    attended = attended.reshape(-1, D)
    middle = inputs + (row_dot(attended, out_full) + bias_out)
    normed_two = layer_norm(middle, gain_two, shift_two).astype(jnp.bfloat16)
    hidden = row_dot(normed_two, up_full) + bias_up
    active = jax.nn.gelu(hidden, approximate=False).astype(jnp.bfloat16)
    layer_rows = (middle + row_dot(active, down_full) + bias_down).astype(jnp.bfloat16)
    qkv_part, out_part, up_part, down_part = (
        lax.all_gather(qkv_low, "fsdp", axis=1, tiled=True),
        lax.all_gather(out_low, "fsdp", axis=1, tiled=True),
        lax.all_gather(up_low, "fsdp", axis=1, tiled=True),
        lax.all_gather(down_low, "fsdp", axis=1, tiled=True),
    )
    qkv_back, out_back, up_back, down_back = (
        lax.all_gather(qkv_part, "dp", axis=0, tiled=True),
        lax.all_gather(out_part, "dp", axis=0, tiled=True),
        lax.all_gather(up_part, "dp", axis=0, tiled=True),
        lax.all_gather(down_part, "dp", axis=0, tiled=True),
    )
    grad_down = column_dot(active, cotangent)
    grad_bias_down = jnp.sum(cotangent.astype(jnp.float32), axis=0)
    active_grad = transposed_dot(cotangent, down_back)
    unused_value, gelu_pull = jax.vjp(partial(jax.nn.gelu, approximate=False), hidden)
    hidden_grad = gelu_pull(active_grad)[0].astype(jnp.bfloat16)
    grad_up = column_dot(normed_two, hidden_grad)
    grad_bias_up = jnp.sum(hidden_grad.astype(jnp.float32), axis=0)
    normed_two_grad = transposed_dot(hidden_grad, up_back)
    unused_norm, norm_two_pull = jax.vjp(layer_norm, middle, gain_two, shift_two)
    middle_grad, grad_gain_two, grad_shift_two = norm_two_pull(normed_two_grad)
    middle_grad = middle_grad + cotangent.astype(jnp.float32)
    branch_grad = middle_grad.astype(jnp.bfloat16)
    grad_out = column_dot(attended, branch_grad)
    grad_bias_out = jnp.sum(branch_grad.astype(jnp.float32), axis=0)
    attended_grad = transposed_dot(branch_grad, out_back).astype(jnp.bfloat16)
    query_grad, key_grad, value_grad = lax.map(
        clip_backward,
        (queries, key_rows, value_rows, counts, log_totals, heads_view(attended_grad)),
    )
    projected_grad = (
        jnp.concatenate([query_grad, key_grad, value_grad], axis=-1)
        .reshape(-1, 3 * D)
        .astype(jnp.bfloat16)
    )
    grad_qkv = column_dot(normed, projected_grad)
    grad_bias_query = jnp.sum(projected_grad[:, :D].astype(jnp.float32), axis=0)
    grad_bias_value = jnp.sum(projected_grad[:, 2 * D :].astype(jnp.float32), axis=0)
    normed_grad = transposed_dot(projected_grad, qkv_back)
    unused_first, norm_one_pull = jax.vjp(layer_norm, inputs, gain_one, shift_one)
    input_rows_grad, grad_gain_one, grad_shift_one = norm_one_pull(normed_grad)
    input_grad = (middle_grad + input_rows_grad).astype(jnp.bfloat16)
    small_grad = jnp.concatenate(
        [
            grad_gain_one,
            grad_shift_one,
            grad_gain_two,
            grad_shift_two,
            grad_bias_query,
            grad_bias_value,
            grad_bias_out,
            grad_bias_down,
            grad_bias_up,
        ]
    )
    row_qkv, row_out, row_up, row_down, row_small = (
        lax.psum_scatter(
            grad_qkv.astype(jnp.bfloat16), "dp", scatter_dimension=0, tiled=True
        ).astype(jnp.float32),
        lax.psum_scatter(
            grad_out.astype(jnp.bfloat16), "dp", scatter_dimension=0, tiled=True
        ).astype(jnp.float32),
        lax.psum_scatter(
            grad_up.astype(jnp.bfloat16), "dp", scatter_dimension=0, tiled=True
        ).astype(jnp.float32),
        lax.psum_scatter(
            grad_down.astype(jnp.bfloat16), "dp", scatter_dimension=0, tiled=True
        ).astype(jnp.float32),
        lax.psum_scatter(
            small_grad.astype(jnp.bfloat16), "dp", scatter_dimension=0, tiled=True
        ).astype(jnp.float32),
    )
    shard_qkv, shard_out, shard_up, shard_down, shard_small = (
        lax.psum_scatter(
            row_qkv.astype(jnp.bfloat16), "fsdp", scatter_dimension=1, tiled=True
        ).astype(jnp.float32),
        lax.psum_scatter(
            row_out.astype(jnp.bfloat16), "fsdp", scatter_dimension=1, tiled=True
        ).astype(jnp.float32),
        lax.psum_scatter(
            row_up.astype(jnp.bfloat16), "fsdp", scatter_dimension=1, tiled=True
        ).astype(jnp.float32),
        lax.psum_scatter(
            row_down.astype(jnp.bfloat16), "fsdp", scatter_dimension=1, tiled=True
        ).astype(jnp.float32),
        lax.psum_scatter(
            row_small.astype(jnp.bfloat16), "fsdp", scatter_dimension=0, tiled=True
        ).astype(jnp.float32),
    )
    band_qkv, band_out, band_up, band_down, band_small = (
        lax.all_gather(shard_qkv.astype(jnp.bfloat16), "fsdp", axis=1, tiled=True).astype(
            shard_qkv.dtype
        ),
        lax.all_gather(shard_out.astype(jnp.bfloat16), "fsdp", axis=1, tiled=True).astype(
            shard_out.dtype
        ),
        lax.all_gather(shard_up.astype(jnp.bfloat16), "fsdp", axis=1, tiled=True).astype(
            shard_up.dtype
        ),
        lax.all_gather(shard_down.astype(jnp.bfloat16), "fsdp", axis=1, tiled=True).astype(
            shard_down.dtype
        ),
        lax.all_gather(shard_small.astype(jnp.bfloat16), "fsdp", axis=0, tiled=True).astype(
            shard_small.dtype
        ),
    )
    rank = lax.axis_index(("dp", "fsdp"))
    row_index = lax.axis_index("dp")
    column_index = lax.axis_index("fsdp")
    numbers = jnp.arange(BLOCKS, dtype=jnp.int32)
    matches = owners == rank
    mine = jnp.sum(jnp.where(matches, numbers, 0))
    owning = jnp.any(matches)

    def update_slot(gradient):
        left_stat = decay_rate * statistics[0, 0] + (1.0 - decay_rate) * jnp.dot(
            gradient, gradient.T, precision=highest, preferred_element_type=jnp.float32
        )
        right_stat = decay_rate * statistics[0, 1] + (1.0 - decay_rate) * jnp.dot(
            gradient.T, gradient, precision=highest, preferred_element_type=jnp.float32
        )
        left_step = jnp.dot(
            inverse_roots[0, 0], gradient, precision=highest, preferred_element_type=jnp.float32
        )
        update = jnp.dot(
            left_step, inverse_roots[0, 1], precision=highest, preferred_element_type=jnp.float32
        )
        return (jnp.stack([left_stat, right_stat])[None], update)

    def keep_slot(gradient):
        return (statistics, jnp.zeros((D, D), jnp.float32))

    whole_qkv, whole_out, whole_up, whole_down, whole_small = (
        lax.all_gather(band_qkv.astype(jnp.bfloat16), "dp", axis=0, tiled=True).astype(
            band_qkv.dtype
        ),
        lax.all_gather(band_out.astype(jnp.bfloat16), "dp", axis=0, tiled=True).astype(
            band_out.dtype
        ),
        lax.all_gather(band_up.astype(jnp.bfloat16), "dp", axis=0, tiled=True).astype(
            band_up.dtype
        ),
        lax.all_gather(band_down.astype(jnp.bfloat16), "dp", axis=0, tiled=True).astype(
            band_down.dtype
        ),
        lax.all_gather(band_small.astype(jnp.bfloat16), "dp", axis=0, tiled=True).astype(
            band_small.dtype
        ),
    )
    gradient = lax.switch(mine, block_pickers(), (whole_qkv, whole_out, whole_up, whole_down))
    new_statistics, update = lax.cond(owning, update_slot, keep_slot, gradient)
    arrivals = []
    for number in range(BLOCKS):
        arrivals.append(fetch_update(update, owners[number]))
    tile_qkv = band_tile(row_band(arrivals[0:3], qkv_weight, row_index), qkv_weight, column_index)
    tile_out = band_tile(row_band(arrivals[3:4], out_weight, row_index), out_weight, column_index)
    tile_up = band_tile(
        row_band(arrivals[4 : 4 + FF // D], up_weight, row_index), up_weight, column_index
    )
    tile_down = band_tile(
        stacked_band(arrivals[4 + FF // D :], down_weight, row_index), down_weight, column_index
    )
    new_qkv = qkv_weight - step_rate * tile_qkv
    new_out = out_weight - step_rate * tile_out
    new_up = up_weight - step_rate * tile_up
    new_down = down_weight - step_rate * tile_down
    new_small = small_params - small_rate * whole_small * lax.rsqrt(
        jnp.mean(whole_small * whole_small) + 1e-06
    )
    return (
        layer_rows,
        input_grad,
        shard_qkv,
        shard_out,
        shard_up,
        shard_down,
        whole_small,
        new_statistics,
        new_qkv,
        new_out,
        new_up,
        new_down,
        new_small,
    )


def local_staged(
    sizes,
    tokens,
    counts,
    cotangent,
    qkv_weight,
    out_weight,
    up_weight,
    down_weight,
    small_params,
    statistics,
    inverse_roots,
    owners,
):
    n_dp, n_fsdp = sizes
    (
        gain_one,
        shift_one,
        gain_two,
        shift_two,
        bias_query,
        bias_value,
        bias_out,
        bias_down,
        bias_up,
    ) = unpack(small_params)
    orders = ("j", "j", "j", "i")
    qkv_pieces, *begun = gather_first(n_dp, n_fsdp, (qkv_weight, out_weight, up_weight), orders[:3], FIRST_PLAN, 1)
    bias_qkv = jnp.concatenate([bias_query, jnp.zeros((D,), jnp.float32), bias_value])
    normed, projected, qkv_full, attended, log_totals, out_pieces, up_pieces, down_pieces = project_attend(
        n_dp, n_fsdp, counts, tokens, qkv_pieces.reshape(n_fsdp, D, 3 * D // n_fsdp), jnp.stack([gain_one, shift_one]),
        bias_qkv[None], begun, (down_weight,), orders[1:], FORWARD_PLAN, 2,
    )
    layer_rows, normed_two, active, hidden_grad, middle_grad, branch_grad, attended_grad, sums = middle_layer(
        tokens,
        attended,
        cotangent,
        out_pieces.reshape(n_fsdp, D, D // n_fsdp),
        up_pieces.reshape(n_fsdp, D, FF // n_fsdp),
        down_pieces.reshape(n_dp, D, FF // n_dp),
        jnp.stack([gain_two, shift_two, bias_out, bias_down]),
        bias_up.reshape(n_fsdp, FF // n_fsdp),
    )
    projected_grad, mine_down, mine_up, mine_out, grad_bias_up, grad_bias_out = grads_attend_back(
        n_dp, n_fsdp, counts, projected, attended, attended_grad, log_totals,
        cotangent, active, normed_two, hidden_grad, branch_grad, BACKWARD_PLAN, 3,
    )
    mine_qkv, mine_small, input_grad = project_back(
        n_dp, n_fsdp, tokens, normed, projected_grad, qkv_full, middle_grad, gain_one[None],
        sums, grad_bias_out, grad_bias_up, TAIL_PLAN, 4
    )
    exchanged = owner_exchange(
        n_dp, n_fsdp, owners, (mine_qkv.reshape(-1, 384), mine_out, mine_up, mine_down), mine_small, inverse_roots[0], 5
    )
    masters = (qkv_weight, out_weight, up_weight, down_weight)
    *results, whole_small, new_small, new_statistics = finish_step(
        n_dp, n_fsdp, owners, exchanged, masters, small_params.reshape(-1, 128), statistics[0], (step_rate, small_rate)
    )
    shard_qkv, shard_out, shard_up, shard_down, new_qkv, new_out, new_up, new_down = results
    whole_small, new_small = whole_small.reshape(-1), new_small.reshape(-1)
    return (
        layer_rows,
        input_grad,
        shard_qkv,
        shard_out,
        shard_up,
        shard_down,
        whole_small,
        new_statistics[None],
        new_qkv,
        new_out,
        new_up,
        new_down,
        new_small,
    )


def solution(mesh):
    placed = (
        P(("dp", "fsdp"), None),
        P(("dp", "fsdp")),
        P(("dp", "fsdp"), None),
        P("dp", "fsdp"),
        P("dp", "fsdp"),
        P("dp", "fsdp"),
        P("dp", "fsdp"),
        P(),
        P(("dp", "fsdp"), None, None, None),
        P(("dp", "fsdp"), None, None, None),
        P(),
    )
    sizes = (mesh.shape["dp"], mesh.shape["fsdp"])
    local = partial(local_staged, sizes) if sizes == (8, 4) else local_any
    return jax.shard_map(
        local,
        mesh=mesh,
        in_specs=placed,
        out_specs=(
            P(("dp", "fsdp"), None),
            P(("dp", "fsdp"), None),
            P("dp", "fsdp"),
            P("dp", "fsdp"),
            P("dp", "fsdp"),
            P("dp", "fsdp"),
            P(),
            P(("dp", "fsdp"), None, None, None),
            P("dp", "fsdp"),
            P("dp", "fsdp"),
            P("dp", "fsdp"),
            P("dp", "fsdp"),
            P(),
        ),
        check_vma=False,
    )
```

```python
from functools import partial

import jax
import jax.numpy as jnp
from jax import lax
from jax.experimental import pallas as pl
from jax.experimental.pallas import tpu as pltpu
from jax.sharding import PartitionSpec as P

MESH = pl.DeviceIdType.MESH
ANY = pl.BlockSpec(memory_space=pl.ANY)
VM = pl.BlockSpec(memory_space=pltpu.VMEM)


class Grid:
    def __init__(self, n_dp, n_fsdp):
        self.Z = 4
        self.X = n_dp // 4
        self.Y = n_fsdp // 2
        self.swap = self.X == self.Y
        self.A, self.B = self.X, self.Y

    def here(self):
        dp, fs = lax.axis_index("dp"), lax.axis_index("fsdp")
        self.z, self.x = dp // self.X, dp % self.X
        self.y, self.c = fs // 2, fs % 2
        if self.swap:
            self.a = self.x + self.c * (self.y - self.x)
            self.b = self.y + self.c * (self.x - self.y)
        else:
            self.a, self.b = self.x, self.y
        return self

    def xy(self, a, b, c):
        if self.swap:
            return a + c * (b - a), b + c * (a - b)
        return a, b

    def device(self, z, a, b, c, frame=None):
        x, y = self.xy(a, b, self.c if frame is None else frame)
        return {"dp": z * self.X + x, "fsdp": y * 2 + c}

    def shape(self, order, r, w):
        if order == "j":
            return (self.Y, 2, self.Z, self.X, r, w)
        return (self.Z, self.X, self.Y, 2, r, w)

    def at(self, ref, order, y, c, z, x):
        return ref.at[y, c, z, x] if order == "j" else ref.at[z, x, y, c]

    def peers(self):
        out = [self.device((self.z + k) % self.Z, self.a, self.b, self.c) for k in range(1, self.Z)]
        out += [self.device(self.z, (self.a + k) % self.A, self.b, self.c) for k in range(1, self.A)]
        out += [self.device(self.z, self.a, (self.b + k) % self.B, self.c) for k in range(1, self.B)]
        out += [{"dp": self.z * self.X + self.x, "fsdp": self.y * 2 + 1 - self.c}]
        return out

    def barrier(self, between=None):
        sem = pltpu.get_barrier_semaphore()
        peers = self.peers()
        for peer in peers:
            pl.semaphore_signal(sem, inc=1, device_id=peer, device_id_type=MESH)
        if between is not None:
            between()
        pl.semaphore_wait(sem, len(peers))


def remote(src, dst, send, recv, slot, device):
    return pltpu.make_async_remote_copy(
        src_ref=src, dst_ref=dst, send_sem=send.at[slot], recv_sem=recv.at[slot], device_id=device, device_id_type=MESH
    )


def start_all(copies):
    for copy in copies:
        copy.start()


def arrived(copies):
    for copy in copies:
        copy.wait_recv()


def sent(copies):
    for copy in copies:
        copy.wait_send()


class Copies:
    def __init__(self, send, recv):
        self.send, self.recv, self.slot = send, recv, 0

    def add(self, group, describe):
        group.append((self.slot, describe))
        self.slot += 1

    def made(self, group):
        out = []
        for slot, describe in group:
            start, end, device = describe()
            out.append(remote(start, end, self.send, self.recv, slot, device))
        return out

    def start(self, group):
        start_all(self.made(group))

    def arrived(self, group):
        arrived(self.made(group))

    def sent(self, group):
        sent(self.made(group))


class Gather:
    def __init__(self, g, order, path, rows, src, out, local, send, recv):
        size = {"z": g.Z, "a": g.A, "b": g.B}
        self.copies = Copies(send, recv)

        def at(name, shift):
            place = {"z": g.z, "a": g.a, "b": g.b}[name]
            return (place + shift + size[name]) % size[name] if shift else place

        def piece(cell):
            where = {name: (at(name, value[1]) if isinstance(value, tuple) else value) for name, value in cell.items()}
            x, y = g.xy(where["a"], where["b"], g.c)
            return g.at(out, order, y, g.c, where["z"], x).at[..., rows, :]

        own_cell = {"z": ("own", 0), "a": ("own", 0), "b": ("own", 0)}

        def cells(full):
            out = [dict(own_cell)]
            for axis in full:
                if axis == "z":
                    out = [dict(cell, z=slice(None)) for cell in out]
                else:
                    out = [dict(cell, **{axis: n}) for cell in out for n in range(size[axis])]
            return out

        def near():
            return {"dp": g.z * g.X + g.x, "fsdp": g.y * 2 + 1 - g.c}

        def far(axis, k):
            return g.device(*[at(name, k if name == axis else 0) for name in "zab"], g.c)

        def own():
            return src.at[rows, :]

        self.own = lambda: pltpu.make_async_copy(own(), piece(own_cell), local)
        self.stages, self.near = [], [[]]
        self.copies.add(self.near[0], lambda: (own(), piece(own_cell), near()))
        full = ""
        for axis in path:
            self.stages.append([])
            self.near.append([])
            for cell in cells(full):
                for k in range(1, size[axis]):
                    from_src = not full
                    self.copies.add(self.stages[-1], lambda cell=cell, k=k, axis=axis, from_src=from_src: (
                        own() if from_src else piece(cell), piece(cell), far(axis, k)))
                    came = dict(cell, **{axis: ("own", -k)})
                    self.copies.add(self.near[-1], lambda came=came: (piece(came), piece(came), near()))
            full += axis

    @staticmethod
    def slots(g):
        zab = (g.Z - 1) + (g.A - 1) + g.A * (g.B - 1)
        abz = (g.A - 1) + g.A * (g.B - 1) + g.A * g.B * (g.Z - 1)
        return 1 + 2 * max(zab, abz)

    def step(self, number):
        if number == 0:
            self.own().start()
        else:
            if number == 1:
                self.own().wait()
            self.copies.arrived(self.stages[number - 1])
        if number < 3:
            self.copies.start(self.stages[number])
        self.copies.start(self.near[number])

    def pause(self):
        self.own().wait()
        for group in (self.stages[0], self.near[0]):
            self.copies.arrived(group)
            self.copies.sent(group)

    def resume(self):
        self.copies.start(self.stages[1])
        self.copies.start(self.near[1])

    def finish(self, first=0):
        for group in self.near[first:]:
            self.copies.arrived(group)
        for group in self.near[first:] + self.stages[first:]:
            self.copies.sent(group)


class Scatter:
    def __init__(self, g, order, path, rows, src, bufs, send, recv):
        self.g, self.path, self.order, self.rows, self.src = g, path, order, rows, src
        self.work = bufs[0]
        self.recv = dict(zip(path, bufs[1:]))
        work = self.work
        size = {"z": g.Z, "a": g.A, "b": g.B}
        self.size = size
        self.copies = Copies(send, recv)
        places = lambda: {"z": g.z, "a": g.a, "b": g.b}

        def other(b, a):
            x, y = g.xy(a, b, 1 - g.c)
            return (g.at(src, order, y, 1 - g.c, slice(None), x).at[:, rows, :], work.at[b, :, a],
                    {"dp": g.z * g.X + g.x, "fsdp": g.y * 2 + 1 - g.c})

        def onward(axis, k, done):
            place = places()
            to = dict(place, **{axis: (place[axis] + k) % size[axis]})
            where = {name: (place[name] if name in done else slice(None)) for name in "bza"}
            where[axis] = to[axis]
            return (work.at[where["b"], where["z"], where["a"]], self.recv[axis].at[k - 1],
                    g.device(to["z"], to["a"], to["b"], g.c))

        self.stages = [[]]
        for b in range(g.B):
            for a in range(g.A):
                self.copies.add(self.stages[0], partial(other, b, a))
        done = ""
        for axis in path:
            self.stages.append([])
            for k in range(1, size[axis]):
                self.copies.add(self.stages[-1], partial(onward, axis, k, done))
            done += axis

    @staticmethod
    def slots(g):
        return g.A * g.B + (g.B - 1) + (g.A - 1) + (g.Z - 1)

    @staticmethod
    def scratch(g, path, r, w):
        size = {"z": g.Z, "a": g.A, "b": g.B}
        out = [pltpu.VMEM((g.B, g.Z, g.A, r, w), jnp.bfloat16)]
        done = ""
        for axis in path:
            done += axis
            out.append(pltpu.VMEM((size[axis] - 1,) + tuple(size[n] for n in "bza" if n not in done) + (r, w), jnp.bfloat16))
        return out

    def _cell(self, index, done):
        place = {"z": self.g.z, "a": self.g.a, "b": self.g.b}
        return [place[n] if n in done else index[n] for n in "bza"]

    def _add(self, number):
        g, done = self.g, self.path[:number]
        left = [n for n in "bza" if n not in done]
        total = 1
        for name in left:
            total *= self.size[name]

        def add(n, carry):
            index = {}
            for name in reversed(left):
                index[name] = n % self.size[name]
                n = n // self.size[name]
            b, z, a = self._cell(index, done)
            if number == 0:
                x, y = g.xy(a, b, g.c)
                mine = g.at(self.src, self.order, y, g.c, z, x)[self.rows, :]
                summed = self.work[b, z, a].astype(jnp.float32) + mine.astype(jnp.float32)
            else:
                summed = self._sum(number, b, z, a, [index[name] for name in left])
            self.work[b, z, a] = summed.astype(jnp.bfloat16)
            return carry

        lax.fori_loop(0, total, add, 0)

    def _sum(self, number, b, z, a, index):
        axis = self.path[number - 1]
        summed = self.work[b, z, a].astype(jnp.float32)
        for k in range(self.size[axis] - 1):
            summed = summed + self.recv[axis][tuple([k] + index)].astype(jnp.float32)
        return summed

    def step(self, number):
        if number > 0:
            self.copies.arrived(self.stages[number - 1])
            self._add(number - 1)
        self.copies.start(self.stages[number])

    def total(self):
        self.copies.arrived(self.stages[3])
        return self._sum(3, self.g.b, self.g.z, self.g.a, [])

    def finish(self):
        for group in self.stages:
            self.copies.sent(group)


GATHER_PATHS = ("zab", "abz")
SCATTER_PATHS = ("baz", "zba")


def row_parts(rows, share=0):
    second = rows * share // 6 // 16 * 16
    parts = [(0, pl.ds(0, rows - second))]
    return parts + ([(1, pl.ds(rows - second, second))] if second else [])


def job_list(sizes, share=0):
    return [(n, path, rows) for n, (r, _) in enumerate(sizes) for path, rows in row_parts(r, share)]


def rounds(jobs, last):
    return [(n, step) for step in range(last + 1) for n in range(len(jobs))]


def gather_scratch(g, count):
    lanes = Gather.slots(g)
    dma = pltpu.SemaphoreType.DMA
    return [dma((count,)), dma((count, lanes)), dma((count, lanes))]


def gather_jobs(g, orders, jobs, ins, outs, scratch):
    local, send, recv = scratch
    return [Gather(g, orders[n], GATHER_PATHS[path], rows, ins[n], outs[n], local.at[j], send.at[j], recv.at[j])
            for j, (n, path, rows) in enumerate(jobs)]


def gather_first(n_dp, n_fsdp, shards, orders, plan, collective_id):
    grid = Grid(n_dp, n_fsdp)
    count = len(shards)
    jobs, order, wholes = plan

    def kernel(*refs):
        g = grid.here()
        low = refs[2 * count : 3 * count]

        def first():
            low[0][...] = refs[0][...].astype(jnp.bfloat16)

        g.barrier(first)
        work = gather_jobs(g, orders, jobs, low, refs[count : 2 * count], refs[3 * count :])
        work[0].step(0)
        for n in range(1, count):
            low[n][...] = refs[n][...].astype(jnp.bfloat16)
        for job, step in order:
            work[job].step(step)
        for job in work[wholes:]:
            job.pause()
        for job in work[:wholes]:
            job.finish()

    return pl.pallas_call(
        kernel,
        out_shape=[jax.ShapeDtypeStruct(grid.shape(o, *s.shape), jnp.bfloat16) for s, o in zip(shards, orders)],
        in_specs=[VM] * count,
        out_specs=[ANY] * count,
        scratch_shapes=[pltpu.VMEM(s.shape, jnp.bfloat16) for s in shards] + gather_scratch(grid, len(jobs)),
        compiler_params=pltpu.CompilerParams(collective_id=collective_id, has_side_effects=True),
        name="gather_first",
    )(*shards)


def scatter_scratch(g, sizes, jobs):
    out = []
    for n, path, rows in jobs:
        out += Scatter.scratch(g, SCATTER_PATHS[path], rows.size, sizes[n][1])
    dma = pltpu.SemaphoreType.DMA
    lanes = Scatter.slots(g)
    return out + [dma((len(jobs), lanes)), dma((len(jobs), lanes))]


def scatter_jobs(g, orders, jobs, ins, scratch):
    send, recv = scratch[4 * len(jobs) :]
    return [Scatter(g, orders[n], SCATTER_PATHS[path], rows, ins[n], scratch[4 * j : 4 * j + 4], send.at[j], recv.at[j])
            for j, (n, path, rows) in enumerate(jobs)]


def scatter_all(n_dp, n_fsdp, wholes, orders, collective_id, dtype=jnp.float32):
    grid = Grid(n_dp, n_fsdp)
    count = len(wholes)
    sizes = [w.shape[-2:] for w in wholes]
    jobs = job_list(sizes, 2)

    def kernel(*refs):
        ins, outs, scratch = refs[:count], refs[count : 2 * count], refs[2 * count :]
        g = grid.here()
        g.barrier()
        work = scatter_jobs(g, orders, jobs, ins, scratch)
        for j, step in rounds(jobs, 3):
            work[j].step(step)
        for job, (n, path, rows) in zip(work, jobs):
            outs[n][rows, :] = job.total().astype(dtype)
        for job in work:
            job.finish()

    return pl.pallas_call(
        kernel,
        out_shape=[jax.ShapeDtypeStruct(s, dtype) for s in sizes],
        in_specs=[VM] * count,
        out_specs=[VM] * count,
        scratch_shapes=scatter_scratch(grid, sizes, jobs),
        compiler_params=pltpu.CompilerParams(collective_id=collective_id, has_side_effects=True,
                                             vmem_limit_bytes=60 * 1024 * 1024),
        name="scatter_all",
    )(*wholes)


HEAD = 64
PAIR = 128


def last_dot(left, right):
    return lax.dot_general(left, right, (((1,), (1,)), ((), ())), preferred_element_type=jnp.float32)


def plain_dot(left, right):
    return lax.dot_general(left, right, (((1,), (0,)), ((), ())), preferred_element_type=jnp.float32)


def attend_block(length, start, size, q_heads, k_ref, v_turned, o_ref, lse_ref):
    slots = k_ref.shape[0]
    half = slots // 2
    keys = k_ref[...]
    key_index = lax.broadcasted_iota(jnp.int32, (slots - half, size), 0) + half
    scores, tops = [], []
    for head in range(2):
        q = q_heads[head, pl.ds(start, size), :]
        low = last_dot(keys[:half], q)
        high = jnp.where(key_index < length, last_dot(keys[half:], q), -1000000000.0)
        tops.append(jnp.maximum(jnp.max(low, axis=0, keepdims=True), jnp.max(high, axis=0, keepdims=True)))
        scores.append((low, high))
    raised = [[jnp.exp(s - tops[head]).astype(jnp.bfloat16) for s in scores[head]] for head in range(2)]
    parts = []
    for head in range(2):
        summed = plain_dot(v_turned[head][:, :half], raised[head][0])
        summed = summed + plain_dot(v_turned[head][:, half:], raised[head][1])
        mine = summed[head * HEAD : (head + 1) * HEAD]
        total = summed[(1 - head) * HEAD : (1 - head) * HEAD + 1]
        parts.append(mine * (1.0 / total))
        lse_ref[head, pl.ds(start, size)] = (tops[head] + jnp.log(total))[0]
    o_ref[pl.ds(start, size), :] = jnp.concatenate(parts, axis=0).T.astype(jnp.bfloat16)


def attend_prepare(q_ref, v_ref, q_heads, v_turned):
    slots = q_ref.shape[0]
    lane = lax.broadcasted_iota(jnp.int32, (slots, PAIR), 1)
    row = lax.broadcasted_iota(jnp.int32, (PAIR, slots), 0)
    q = q_ref[...].astype(jnp.float32) * (HEAD ** (-0.5))
    v = v_ref[...].astype(jnp.float32).T
    for head in range(2):
        q_heads[head] = jnp.where(lane // HEAD == head, q, 0.0).astype(jnp.bfloat16)
        v_turned[head] = jnp.where(row // HEAD == head, v, 1.0).astype(jnp.bfloat16)


def attend_kernel(size, count_ref, q_ref, k_ref, v_ref, o_ref, lse_ref, q_heads, v_turned):
    attend_prepare(q_ref, v_ref, q_heads, v_turned)
    length = count_ref[0]

    def step(n, carry):
        attend_block(length, pl.multiple_of(n * size, size), size, q_heads, k_ref, v_turned, o_ref, lse_ref.at[0])
        return carry

    lax.fori_loop(0, q_ref.shape[0] // size, step, 0)


def attend(counts, projected, size=256):
    slots, width = projected.shape
    d = width // 3
    pairs = d // PAIR
    spec = lambda part: pl.BlockSpec((slots, PAIR), lambda p, n, part=part: (0, part * pairs + p))
    return pl.pallas_call(
        partial(attend_kernel, size),
        out_shape=[jax.ShapeDtypeStruct((slots, d), jnp.bfloat16),
                   jax.ShapeDtypeStruct((pairs, 2, slots), jnp.float32)],
        grid_spec=pltpu.PrefetchScalarGridSpec(
            num_scalar_prefetch=1, grid=(pairs,),
            in_specs=[spec(0), spec(1), spec(2)],
            out_specs=[pl.BlockSpec((slots, PAIR), lambda p, n: (0, p)),
                       pl.BlockSpec((1, 2, slots), lambda p, n: (p, 0, 0))],
            scratch_shapes=[pltpu.VMEM((2, slots, PAIR), jnp.bfloat16), pltpu.VMEM((2, PAIR, slots), jnp.bfloat16)]),
        compiler_params=pltpu.CompilerParams(vmem_limit_bytes=48 * 1024 * 1024),
        name="attend",
    )(counts, projected, projected, projected)


def attend_back_scratch(slots):
    return [pltpu.VMEM((2, slots, PAIR), jnp.bfloat16), pltpu.VMEM((2, slots, PAIR), jnp.bfloat16),
            pltpu.VMEM((2, PAIR, slots), jnp.bfloat16), pltpu.VMEM((2, slots), jnp.float32),
            pltpu.VMEM((slots, PAIR), jnp.float32), pltpu.VMEM((slots, PAIR), jnp.float32)]


def attend_back_body(size, count_ref, q_ref, k_ref, v_ref, o_ref, do_ref, lse_ref, out_ref,
                     q_heads, do_heads, k_turned, inner, dk_sum, dv_sum, hook):
    slots = q_ref.shape[0]
    length = count_ref[0]
    lane = lax.broadcasted_iota(jnp.int32, (slots, PAIR), 1)
    row = lax.broadcasted_iota(jnp.int32, (PAIR, slots), 0)
    q = q_ref[...].astype(jnp.float32) * (HEAD ** (-0.5))
    do = do_ref[...].astype(jnp.float32)
    k = k_ref[...].astype(jnp.float32).T * (HEAD ** (-0.5))
    product = (do * o_ref[...].astype(jnp.float32)).T
    for head in range(2):
        q_heads[head] = jnp.where(lane // HEAD == head, q, 0.0).astype(jnp.bfloat16)
        do_heads[head] = jnp.where(lane // HEAD == head, do, 0.0).astype(jnp.bfloat16)
        k_turned[head] = jnp.where(row // HEAD == head, k, 0.0).astype(jnp.bfloat16)
        inner[head] = jnp.sum(product[head * HEAD : (head + 1) * HEAD], axis=0)
    dk_sum[...] = jnp.zeros_like(dk_sum)
    dv_sum[...] = jnp.zeros_like(dv_sum)
    key_index = lax.broadcasted_iota(jnp.int32, (slots, size), 0)

    def step(n, carry):
        rows = pl.ds(n * size, size)
        keys, values = k_ref[...], v_ref[...]
        dq = jnp.zeros((PAIR, size), jnp.float32)
        for head in range(2):
            q_block, do_block = q_heads[head, rows, :], do_heads[head, rows, :]
            scores = last_dot(keys, q_block)
            weights = jnp.exp(scores - lse_ref[0, head, rows][None, :])
            weights = jnp.where(key_index < length, weights, 0.0)
            weight_grad = last_dot(values, do_block)
            score_grad = (weights * (weight_grad - inner[head, rows][None, :])).astype(jnp.bfloat16)
            dv_sum[...] += plain_dot(weights.astype(jnp.bfloat16), do_block)
            dk_sum[...] += plain_dot(score_grad, q_block)
            dq = dq + plain_dot(k_turned[head], score_grad)
        out_ref[0, rows, :] = dq.T.astype(jnp.bfloat16)
        return carry

    for n in range(slots // size):
        hook(n)
        step(n, 0)
    out_ref[1] = dk_sum[...].astype(jnp.bfloat16)
    out_ref[2] = dv_sum[...].astype(jnp.bfloat16)


def project_attend(n_dp, n_fsdp, counts, tokens, weight_pieces, small_rows, pieces, fresh, orders, plan, collective_id,
                   size=512, block=256):
    slots, d = tokens.shape
    width = weight_pieces.shape[0] * weight_pieces.shape[2]
    pairs = d // PAIR
    head = slots // block
    grid = Grid(n_dp, n_fsdp)
    begun, count = len(pieces), len(pieces) + len(fresh)
    jobs = plan["jobs"]
    waits = [job[0] < begun for job in jobs]
    shapes = [jax.ShapeDtypeStruct(p.shape, p.dtype) for p in pieces]
    shapes += [jax.ShapeDtypeStruct(grid.shape(o, *a.shape), jnp.bfloat16) for a, o in zip(fresh, orders[begun:])]

    def kernel(count_ref, x, w_pieces, rows, *refs):
        (h_ref, p_ref, w_ref, o_ref, lse_ref), outs = refs[count : count + 5], refs[count + 5 : 2 * count + 5]
        projected, q_heads, v_turned = refs[2 * count + 5 : 2 * count + 8]
        low_fresh = refs[2 * count + 8 : 2 * count + 8 + len(fresh)]
        g = grid.here()
        work = gather_jobs(g, orders, jobs, outs[:begun] + low_fresh, outs, refs[2 * count + 8 + len(fresh) :])
        step = pl.program_id(0)

        def run(when):
            for j, number in plan.get(when, []):
                if number == 1 and waits[j]:
                    work[j].resume()
                else:
                    work[j].step(number)

        @pl.when(step == 0)
        def _():
            def first():
                for ref, master in zip(low_fresh, refs[begun:count]):
                    ref[...] = master[...].astype(jnp.bfloat16)

            g.barrier(first)

        for when in range(head + pairs):
            if when in plan:
                pl.when(step == when)(partial(run, when))

        @pl.when(step == 0)
        def _():
            part = w_pieces.shape[2]
            for n in range(w_pieces.shape[0]):
                w_ref[:, n * part : (n + 1) * part] = w_pieces[n]

        @pl.when(step < head)
        def _():
            unit, spread = centered(x[...].astype(jnp.float32))
            low = (unit * rows[0:1] + rows[1:2]).astype(jnp.bfloat16)
            h_ref[...] = low
            bias = jnp.concatenate([rows[4:5], jnp.zeros((1, d), jnp.float32), rows[5:6]], axis=1)
            result = (plain_dot(low, w_ref[...]) + bias).astype(jnp.bfloat16)
            p_ref[...] = result
            projected[pl.ds(pl.multiple_of(step * block, block), block), :] = result

        @pl.when(step >= head)
        def _():
            lane = pl.multiple_of((step - head) * PAIR, PAIR)
            q_ref, k_ref, v_ref = (projected.at[:, pl.ds(lane + part * d, PAIR)] for part in range(3))
            attend_prepare(q_ref, v_ref, q_heads, v_turned)
            length = count_ref[0]
            for n in range(slots // size):
                attend_block(length, n * size, size, q_heads, k_ref, v_turned, o_ref, lse_ref.at[0])

        @pl.when(step == head + pairs - 1)
        def _():
            run("end")
            for j, job in enumerate(work):
                job.finish(1 if waits[j] else 0)

    low = jnp.bfloat16
    row_at = lambda s: jnp.minimum(s, head - 1)
    pair_at = lambda s: jnp.maximum(s - head, 0)
    row = lambda w: pl.BlockSpec((block, w), lambda s, n: (row_at(s), 0))
    whole = lambda array: pl.BlockSpec(array.shape, lambda s, n: (0,) * array.ndim, pipeline_mode=pl.Buffered(1))
    return pl.pallas_call(
        kernel,
        out_shape=[jax.ShapeDtypeStruct((slots, d), low), jax.ShapeDtypeStruct((slots, width), low),
                   jax.ShapeDtypeStruct((d, width), low), jax.ShapeDtypeStruct((slots, d), low),
                   jax.ShapeDtypeStruct((pairs, 2, slots), jnp.float32)] + shapes,
        grid_spec=pltpu.PrefetchScalarGridSpec(
            num_scalar_prefetch=1, grid=(head + pairs,),
            in_specs=[row(d), whole(weight_pieces), whole(small_rows)] + [ANY] * begun + [whole(a) for a in fresh],
            out_specs=[row(d), row(width), pl.BlockSpec((d, width), lambda s, n: (0, 0)),
                       pl.BlockSpec((slots, PAIR), lambda s, n: (0, pair_at(s))),
                       pl.BlockSpec((1, 2, slots), lambda s, n: (pair_at(s), 0, 0))] + [ANY] * count,
            scratch_shapes=[pltpu.VMEM((slots, width), low), pltpu.VMEM((2, slots, PAIR), low),
                            pltpu.VMEM((2, PAIR, slots), low)] + [pltpu.VMEM(a.shape, low) for a in fresh]
            + gather_scratch(grid, len(jobs))),
        input_output_aliases={4 + n: 5 + n for n in range(begun)},
        compiler_params=pltpu.CompilerParams(vmem_limit_bytes=56 * 1024 * 1024, collective_id=collective_id,
                                             has_side_effects=True),
        name="project_attend",
    )(counts, tokens, weight_pieces, small_rows, *pieces, *fresh)


FIRST_PLAN = (
    [(0, 0, pl.ds(0, 48)), (0, 0, pl.ds(48, 48)), (1, 0, pl.ds(0, 96)), (2, 0, pl.ds(0, 64)), (2, 1, pl.ds(64, 32))],
    [(0, 1), (1, 0), (0, 2), (1, 1), (2, 0), (3, 0), (4, 0), (0, 3), (1, 2), (1, 3)],
    2,
)
FORWARD_PLAN = {
    "jobs": [(0, 0, pl.ds(0, 96)), (1, 0, pl.ds(0, 64)), (1, 1, pl.ds(64, 32)), (2, 0, pl.ds(0, 192))],
    0: [(0, 1), (1, 1), (3, 0), (2, 1)],
    3: [(0, 2)],
    5: [(1, 2), (0, 3), (2, 2)],
    7: [(3, 1)],
    "end": [(1, 3), (3, 2), (2, 3), (3, 3)],
}


def cut_block(grad, turned_blocks, out, rows):
    for z, x, y, c in places():
        row, column = piece_rows(turned_blocks, z, x, y, c)
        out[y, c, z, x, rows, :] = grad[row : row + 48, column : column + 384]


def grads_attend_back(n_dp, n_fsdp, counts, projected, attended, attended_grad, lse, cotangent, active, normed, hidden_grad,
                      branch_grad, plan, collective_id, size=256):
    slots, width = projected.shape
    d = width // 3
    pairs = d // PAIR
    panels = active.shape[1] // d
    head = 2 * panels + 1
    grid = Grid(n_dp, n_fsdp)
    sizes = [(panels * 48, 384), (panels * 48, 384), (48, 384)]
    jobs = plan["jobs"]
    steps = slots // size

    def kernel(count_ref, q_ref, k_ref, v_ref, o_ref, do_ref, lse_ref, dy, z, h2, du, o_all, db, out_ref, *refs):
        outs, sums, parts, left = refs[:3], refs[3:5], refs[5:8], refs[8]
        own, scratch = refs[9:15], refs[15:]
        g = grid.here()
        work = scatter_jobs(g, ["j"] * 3, jobs, parts, scratch)
        step = pl.program_id(0)

        def run(when):
            for j, number in plan.get(when, []):
                work[j].step(number)

        @pl.when(step == 0)
        def _():
            g.barrier()

        def turn(ref):
            left[...] = ref[...].astype(jnp.float32).T.astype(jnp.bfloat16)

        for first, ref in ((0, dy), (panels, h2), (2 * panels, o_all)):
            pl.when(step == first)(partial(turn, ref))

        def blocks(part, first, right, kind):
            @pl.when((step >= first) & (step < first + (1 if part == 2 else panels)))
            def _():
                values = right[...]
                grad = plain_dot(left[...], values).astype(jnp.bfloat16)
                at = 0 if part == 2 else pl.multiple_of((step - first) * 48, 16)
                cut_block(grad, kind, parts[part], pl.ds(at, 48))
                if part > 0:
                    sums[part - 1][...] = jnp.sum(values.astype(jnp.float32), axis=0).reshape(1, 1, d)

        for when in range(head):
            if (when, 0) in plan:
                pl.when(step == when)(partial(run, (when, 0)))
        blocks(0, 0, z, True)
        blocks(1, panels, du, False)
        blocks(2, 2 * panels, db, False)

        def hook(n):
            for p in range(head, head + pairs):
                if (p, n) in plan:
                    pl.when(step == p)(partial(run, (p, n)))

        @pl.when(step >= head)
        def _():
            attend_back_body(size, count_ref, q_ref, k_ref, v_ref, o_ref, do_ref, lse_ref, out_ref, *own, hook)

        @pl.when(step == head + pairs - 1)
        def _():
            run("end")
            for job, (n, path, rows) in zip(work, jobs):
                outs[n][rows, :] = job.total().astype(jnp.bfloat16)
            for job in work:
                job.finish()

    pair_at = lambda s: jnp.maximum(s - head, 0)
    spec = lambda part: pl.BlockSpec((slots, PAIR), lambda s, n, part=part: (0, part * pairs + pair_at(s)))
    once = pl.BlockSpec((slots, d), lambda s, n: (0, 0), pipeline_mode=pl.Buffered(1))
    panel = lambda first: pl.BlockSpec((slots, d), lambda s, n: (0, jnp.clip(s - first, 0, panels - 1)))
    low, wide = jnp.bfloat16, jnp.float32
    return pl.pallas_call(
        kernel,
        out_shape=[jax.ShapeDtypeStruct((3, slots, d), low)]
        + [jax.ShapeDtypeStruct(s, low) for s in sizes]
        + [jax.ShapeDtypeStruct((panels, 1, d), wide), jax.ShapeDtypeStruct((1, 1, d), wide)],
        grid_spec=pltpu.PrefetchScalarGridSpec(
            num_scalar_prefetch=1, grid=(head + pairs,),
            in_specs=[spec(0), spec(1), spec(2), spec(0), spec(0),
                      pl.BlockSpec((1, 2, slots), lambda s, n: (pair_at(s), 0, 0)),
                      once, panel(0), once, panel(panels), once, once],
            out_specs=[pl.BlockSpec((3, slots, PAIR), lambda s, n: (0, 0, pair_at(s)))] + [VM] * 3
            + [pl.BlockSpec((1, 1, d), lambda s, n: (jnp.clip(s - panels, 0, panels - 1), 0, 0)),
               pl.BlockSpec((1, 1, d), lambda s, n: (0, 0, 0))],
            scratch_shapes=[pltpu.VMEM(grid.shape("j", *s), low) for s in sizes] + [pltpu.VMEM((d, slots), low)]
            + attend_back_scratch(slots) + scatter_scratch(grid, sizes, jobs)),
        compiler_params=pltpu.CompilerParams(vmem_limit_bytes=62 * 1024 * 1024, collective_id=collective_id,
                                             has_side_effects=True),
        name="grads_attend_back",
    )(counts, projected, projected, projected, attended, attended_grad, lse, cotangent, active, normed, hidden_grad,
      attended, branch_grad)


BACKWARD_PLAN = {
    "jobs": [(n, 0, pl.ds(at, 96)) for n in range(2) for at in (0, 96)] + [(2, 0, pl.ds(0, 48))],
    (2, 0): [(0, 0)],
    (4, 0): [(1, 0)],
    (5, 0): [(0, 1)],
    (7, 0): [(1, 1), (2, 0)],
    (8, 0): [(3, 0), (0, 2)],
    (9, 0): [(4, 0), (2, 1)],
    (10, 0): [(1, 2), (0, 3), (3, 1)],
    (11, 0): [(2, 2), (1, 3), (4, 1)],
    (12, 0): [(3, 2), (2, 3)],
    (13, 0): [(4, 2), (3, 3)],
    (14, 0): [(4, 3)],
}


PIECE = (48, 384)


class Spread:
    def __init__(self, g, u, tiles, send, recv, base):
        qkv, out, up, down = tiles
        me = g.y * 2 + g.c
        rows = pl.ds(pl.multiple_of(g.y * 48, 16), 48)
        self.g, self.u, self.tiles, self.rows, self.me = g, u, tiles, rows, me
        self.copies = []

        def copy(src, dst, device):
            self.copies.append(remote(src, dst, send, recv, base + len(self.copies), device))

        for k in range(1, 4):
            to = (me + k) % 4
            device = {"dp": g.z * 2 + g.x, "fsdp": to}
            block, half = self.qkv_place(to)
            copy(u.at[block], qkv.at[half, rows, :], device)
            copy(u.at[3], out.at[g.c, rows, :], device)
            copy(u.at[4 + to], up.at[g.c, rows, :], device)
        for k in range(1, 4):
            to = (g.z + k) % 4
            copy(u.at[8 + to], down.at[pl.ds(pl.multiple_of(g.z * 48, 16), 48), :], {"dp": to * 2 + g.x, "fsdp": me})

    def qkv_place(self, to):
        c = self.g.c
        middle = (to + 1) // 2 % 2
        return to - to // 3 - middle * c, middle + c - 2 * middle * c

    def start(self):
        start_all(self.copies)
        g, u = self.g, self.u
        qkv, out, up, down = self.tiles
        block, half = self.qkv_place(self.me)
        qkv[half, self.rows, :] = u[block]
        out[g.c, self.rows, :] = u[3]
        up[g.c, self.rows, :] = u[4 + self.me]
        down[pl.ds(pl.multiple_of(g.z * 48, 16), 48), :] = u[8 + g.z]

    def finish(self):
        arrived(self.copies)
        sent(self.copies)


TILES = [jax.ShapeDtypeStruct((2, 96, 384), jnp.bfloat16)] * 3 + [jax.ShapeDtypeStruct((192, 384), jnp.bfloat16)]


def meet_all(g, n_dp, n_fsdp, between):
    count = n_dp * n_fsdp
    me = (g.z * g.X + g.x) * n_fsdp + g.y * 2 + g.c
    sem = pltpu.get_barrier_semaphore()
    ranks = [(me + k) % count for k in range(1, count)]
    peers = [{"dp": rank // n_fsdp, "fsdp": rank % n_fsdp} for rank in ranks]
    for peer in peers:
        pl.semaphore_signal(sem, inc=1, device_id=peer, device_id_type=MESH)
    between(me)
    pl.semaphore_wait(sem, count - 1)
    return me, ranks, peers


def piece_rows(turned, z, x, y, c):
    if turned:
        return 192 * (2 * y + c) + 48 * z, 384 * x
    return 96 * (2 * z + x) + 48 * y, 384 * c


def places():
    return [(z, x, y, c) for z in range(4) for x in range(2) for y in range(2) for c in range(2)]


def tile_values(g, tiles):
    qkv, out, up, down = tiles
    odd = (g.y * 2 + g.c) % 2 == 1
    wide = jnp.float32
    band = jnp.concatenate([qkv[0].astype(wide), qkv[1].astype(wide)], axis=1)
    half = out[g.y].astype(wide)
    return [jnp.where(odd, band[:, 192:], band[:, :576]), jnp.where(odd, half[:, 192:], half[:, :192]),
            jnp.concatenate([up[0].astype(wide), up[1].astype(wide)], axis=1), down[...].astype(wide)]


def owner_exchange(n_dp, n_fsdp, owners, mine, small, roots, collective_id):
    grid = Grid(n_dp, n_fsdp)
    count = n_dp * n_fsdp
    n_blocks = owners.shape[0]
    d = roots.shape[1]
    spread_lanes = 12

    def kernel(owners_ref, qkv_ref, out_ref, up_ref, down_ref, small_ref, roots_hbm,
               qkv, out, up, down, s_qkv, s_out, s_up, s_down, all_small, block, turned,
               u, slots, got, got_steps, u_steps, roots, local, send, recv):
        g = grid.here()
        load = pltpu.make_async_copy(roots_hbm, roots, local.at[0])

        def owned(n):
            found = 0
            for b in range(n_blocks):
                found = jnp.where(owners_ref[b] == n, b, found)
            return found

        def first(me):
            load.start()
            at = 0
            for ref in (qkv_ref, out_ref, up_ref, down_ref):
                part = ref.shape[0] // 48
                u[at : at + part] = ref[...].reshape(part, 48, 384)
                at += part

            def fill(n, carry):
                slots[n] = u[owned(n)]
                return carry

            lax.fori_loop(0, count, fill, 0)
            got[me] = slots[me]
            all_small[me] = small_ref[...]

        me, ranks, peers = meet_all(g, n_dp, n_fsdp, first)
        lane = 0
        copies, small_copies, step_copies = [], [], []
        for rank, peer in zip(ranks, peers):
            copies.append(remote(slots.at[rank], got.at[me], send, recv, lane, peer))
            small_copies.append(remote(small_ref, all_small.at[me], send, recv, lane + 1, peer))
            step_copies.append(remote(slots.at[rank], got_steps.at[me], send, recv, lane + 2, peer))
            lane += 3
        start_all(copies)
        load.wait()
        kind = jnp.where(owned(me) >= 8, 1, 0)
        arrived(copies)
        sent(copies)
        spread = Spread(g, u, (qkv, out, up, down), send, recv, lane)
        spread.start()
        start_all(small_copies)
        for turn in range(2):
            for n, place in enumerate(places()):
                row, column = piece_rows(turn, *place)
                (turned if turn else block)[row : row + 48, column : column + 384] = got[n]
        block[...] = jnp.where(kind == 1, turned[...], block[...])
        left = plain_dot(roots[kind].astype(jnp.bfloat16), block[...]).astype(jnp.bfloat16)
        step = plain_dot(left, roots[1 - kind].astype(jnp.bfloat16)).astype(jnp.bfloat16)
        for n, place in enumerate(places()):
            row, column = piece_rows(0, *place)
            other_row, other_column = piece_rows(1, *place)
            slots[n] = jnp.where(kind == 1, step[other_row : other_row + 48, other_column : other_column + 384],
                                 step[row : row + 48, column : column + 384])
        start_all(step_copies)
        got_steps[me] = slots[me]
        wide = block[...].astype(jnp.float32)
        wide_turned = wide.T
        block[...] = jnp.where(kind == 1, wide_turned, wide).astype(jnp.bfloat16)
        turned[...] = jnp.where(kind == 1, wide, wide_turned).astype(jnp.bfloat16)
        spread.finish()
        arrived(small_copies)
        arrived(step_copies)

        def pick(n, carry):
            u_steps[n] = got_steps[owners_ref[n]]
            return carry

        lax.fori_loop(0, n_blocks, pick, 0)
        back = Spread(g, u_steps, (s_qkv, s_out, s_up, s_down), send, recv, lane + spread_lanes)
        back.start()
        sent(small_copies + step_copies)
        back.finish()

    lanes = 3 * (count - 1) + 2 * spread_lanes
    low = jnp.bfloat16
    pieces = pltpu.VMEM((count,) + PIECE, low)
    return pl.pallas_call(
        kernel,
        out_shape=TILES + TILES + [jax.ShapeDtypeStruct((count,) + small.shape, low), jax.ShapeDtypeStruct((d, d), low),
                                   jax.ShapeDtypeStruct((d, d), low)],
        in_specs=[pl.BlockSpec(memory_space=pltpu.SMEM)] + [VM] * 5 + [ANY],
        out_specs=[VM] * 11,
        scratch_shapes=[pltpu.VMEM((n_blocks,) + PIECE, low), pieces, pieces, pieces, pltpu.VMEM((n_blocks,) + PIECE, low),
                        pltpu.VMEM(roots.shape, jnp.float32), pltpu.SemaphoreType.DMA((1,)),
                        pltpu.SemaphoreType.DMA((lanes,)), pltpu.SemaphoreType.DMA((lanes,))],
        compiler_params=pltpu.CompilerParams(collective_id=collective_id, has_side_effects=True,
                                             vmem_limit_bytes=56 * 1024 * 1024),
        name="owner_exchange",
    )(owners, *mine, small, roots)


def finish_step(n_dp, n_fsdp, owners, exchanged, masters, small_params, stats, rates, parts=4):
    grid = Grid(n_dp, n_fsdp)
    tiles, all_small, block, turned = exchanged[:8], *exchanged[8:]
    d = block.shape[0]
    rows = d // parts

    def kernel(owners_ref, qkv, out, up, down, s_qkv, s_out, s_up, s_down, all_small, block, turned,
               w_qkv, w_out, w_up, w_down, params, stats_ref,
               g_qkv, g_out, g_up, g_down, n_qkv, n_out, n_up, n_down, g_small, n_small, new_stats):
        g = grid.here()
        step = pl.program_id(0)
        me = (g.z * g.X + g.x) * n_fsdp + g.y * 2 + g.c
        own = owners_ref[0] == me
        for n in range(1, owners.shape[0]):
            own = own | (owners_ref[n] == me)

        @pl.when(step == 0)
        def _():
            values = tile_values(g, (qkv, out, up, down))
            for ref, value in zip((g_qkv, g_out, g_up, g_down), values):
                ref[...] = value
            steps = tile_values(g, (s_qkv, s_out, s_up, s_down))
            for ref, master, value in zip((n_qkv, n_out, n_up, n_down), (w_qkv, w_out, w_up, w_down), steps):
                ref[...] = master[...] - rates[0] * value
            lines = params.shape[0]
            total = jnp.concatenate([all_small[n].astype(jnp.float32) for n in range(-(-lines // 16))], axis=0)[:lines]
            g_small[...] = total
            mean = jnp.sum(total * total) * (1.0 / (lines * 128))
            n_small[...] = params[...] - rates[1] * total * lax.rsqrt(jnp.full((1, 128), mean + 1e-06, jnp.float32))

        @pl.when(own)
        def _():
            at = pl.ds(pl.multiple_of(step * rows, rows), rows)
            new_stats[0] = 0.5 * stats_ref[0] + 0.5 * last_dot(block[at, :], block[...])
            new_stats[1] = 0.5 * stats_ref[1] + 0.5 * last_dot(turned[at, :], turned[...])

        @pl.when(jnp.logical_not(own))
        def _():
            new_stats[...] = stats_ref[...]

    whole = lambda a: pl.BlockSpec(a.shape, lambda s, n: (0,) * len(a.shape))
    banded = pl.BlockSpec((2, rows, d), lambda s, n: (0, s, 0))
    results = [jax.ShapeDtypeStruct(a.shape, jnp.float32) for a in (*masters, *masters, small_params, small_params)]
    return pl.pallas_call(
        kernel,
        out_shape=results + [jax.ShapeDtypeStruct(stats.shape, jnp.float32)],
        grid_spec=pltpu.PrefetchScalarGridSpec(
            num_scalar_prefetch=1, grid=(parts,),
            in_specs=[whole(a) for a in (*exchanged, *masters, small_params)] + [banded],
            out_specs=[whole(a) for a in results] + [banded]),
        compiler_params=pltpu.CompilerParams(vmem_limit_bytes=56 * 1024 * 1024),
        name="finish_step",
    )(owners, *exchanged, *masters, small_params, stats)


def centered(values):
    center = values - jnp.mean(values, axis=-1, keepdims=True)
    spread = lax.rsqrt(jnp.mean(center * center, axis=-1, keepdims=True) + 1e-06)
    return center * spread, spread


def norm_back(grads, unit, spread, gain):
    scaled = grads * gain
    mean = jnp.mean(scaled, axis=-1, keepdims=True)
    along = jnp.mean(scaled * unit, axis=-1, keepdims=True)
    return (scaled - mean - unit * along) * spread


def middle_kernel(x, attended, dy, out_pieces, up_w, down_w, rows,
                  layer, h2, active, hidden_grad, middle_grad, branch_grad, attended_grad, sums, out_w):
    @pl.when(pl.program_id(0) == 0)
    def _():
        part = out_pieces.shape[2]
        for n in range(out_pieces.shape[0]):
            out_w[:, n * part : (n + 1) * part] = out_pieces[n]

    gain, shift, bias_out, bias_down = rows[2:3], rows[3:4], rows[6:7], rows[7:8]
    middle = x[...].astype(jnp.float32) + (plain_dot(attended[...], out_w[...]) + bias_out)
    unit, spread = centered(middle)
    normed = (unit * gain + shift).astype(jnp.bfloat16)
    h2[...] = normed
    grad_rows = dy[...]
    panels = up_w.shape[0]
    width = up_w.shape[2]
    half = width // 2
    y = jnp.zeros_like(middle)
    dh = jnp.zeros_like(middle)
    for panel in range(panels):
        hidden = plain_dot(normed, up_w[panel]) + rows[8 + panel : 9 + panel]
        passed = 0.5 + 0.5 * lax.erf(hidden * (0.5**0.5))
        z = (hidden * passed).astype(jnp.bfloat16)
        slope = passed + hidden * (jnp.exp(-0.5 * hidden * hidden) * 0.3989422804014327)
        back = jnp.concatenate([plain_dot(grad_rows, down_w[2 * panel]), plain_dot(grad_rows, down_w[2 * panel + 1])], axis=1)
        du = (slope * back).astype(jnp.bfloat16)
        active[:, panel * width : (panel + 1) * width] = z
        hidden_grad[:, panel * width : (panel + 1) * width] = du
        y = y + last_dot(z[:, :half], down_w[2 * panel]) + last_dot(z[:, half:], down_w[2 * panel + 1])
        dh = dh + last_dot(du, up_w[panel])
    layer[...] = (middle + y + bias_down).astype(jnp.bfloat16)
    wide = grad_rows.astype(jnp.float32)
    total = wide + norm_back(dh, unit, spread, gain)
    low = total.astype(jnp.bfloat16)
    middle_grad[...] = total
    branch_grad[...] = low
    attended_grad[...] = last_dot(low, out_w[...]).astype(jnp.bfloat16)

    @pl.when(pl.program_id(0) == 0)
    def _():
        sums[...] = jnp.zeros_like(sums)

    sums[0:1] += jnp.sum(dh * unit, axis=0, keepdims=True)
    sums[1:2] += jnp.sum(dh, axis=0, keepdims=True)
    sums[2:3] += jnp.sum(wide, axis=0, keepdims=True)


def middle_layer(tokens, attended, cotangent, out_w, up_w, down_w, rows, block=256):
    count, d = tokens.shape
    ff = up_w.shape[0] * up_w.shape[2]
    row = lambda width: pl.BlockSpec((block, width), lambda r: (r, 0))
    whole = lambda array: pl.BlockSpec(array.shape, lambda r: (0,) * array.ndim)
    low, wide = jnp.bfloat16, jnp.float32
    shape = jax.ShapeDtypeStruct
    return pl.pallas_call(
        middle_kernel,
        out_shape=[shape((count, d), low), shape((count, d), low), shape((count, ff), low), shape((count, ff), low),
                   shape((count, d), wide), shape((count, d), low), shape((count, d), low), shape((8, d), wide)],
        grid=(count // block,),
        in_specs=[row(d), row(d), row(d)] + [whole(a) for a in (out_w, up_w, down_w, rows)],
        out_specs=[row(d), row(d), row(ff), row(ff), row(d), row(d), row(d), pl.BlockSpec((8, d), lambda r: (0, 0))],
        scratch_shapes=[pltpu.VMEM((d, d), low)],
        compiler_params=pltpu.CompilerParams(vmem_limit_bytes=60 * 1024 * 1024),
        name="middle_layer",
    )(tokens, attended, cotangent, out_w, up_w, down_w, rows)


def project_back(n_dp, n_fsdp, tokens, normed, projected_grad, weight, middle_grad, gain, sums, bias_out, bias_up, plan,
                 collective_id, block=256):
    grid = Grid(n_dp, n_fsdp)
    count, d = tokens.shape
    n_blocks = projected_grad.shape[0]
    lines = 8 + bias_up.shape[0]
    sizes = [(48, 384)] * n_blocks + [(16, 128)]
    jobs = plan["jobs"]
    low, wide = jnp.bfloat16, jnp.float32

    def kernel(x_h, normed_h, dp_h, weight_h, middle_h, gain_ref, sums_ref, bias_out_ref, bias_up_ref, mine, small, input_grad_h, *refs):
        x, h, dp, w, middle, out = refs[:6]
        left, parts, small_parts, rows, packed, local = refs[6:12]
        scratch = refs[12:]
        g = grid.here()
        loads = [pltpu.make_async_copy(a, b, local.at[n])
                 for n, (a, b) in enumerate(((normed_h, h), (dp_h, dp), (weight_h, w), (x_h, x), (middle_h, middle)))]

        def first():
            for load in loads:
                load.start()
            loads[0].wait()
            left[...] = h[...].astype(wide).T.astype(low)

        g.barrier(first)
        loads[1].wait()
        work = scatter_jobs(g, ["j"] * (n_blocks + 1), jobs, [parts.at[n] for n in range(n_blocks)] + [small_parts], scratch)
        for n in range(n_blocks):
            values = dp[n]
            grad = plain_dot(left[...], values).astype(low)
            for z, px, y, c in places():
                row, column = piece_rows(False, z, px, y, c)
                parts[n, y, c, z, px] = grad[row : row + 48, column : column + 384]
            for j, job in enumerate(jobs):
                if job[0] == n:
                    work[j].step(0)
        rows[2:4] = sums_ref[0:2]
        rows[6:7] = bias_out_ref[0]
        rows[7:8] = sums_ref[2:3]
        for n in range(lines - 8):
            rows[8 + n : 9 + n] = bias_up_ref[n]
        rows[4:5] = jnp.sum(dp[0].astype(wide), axis=0, keepdims=True)
        rows[5:6] = jnp.sum(dp[2].astype(wide), axis=0, keepdims=True)
        for load in loads[2:]:
            load.wait()

        def back(n):
            at = slice(n * block, (n + 1) * block)
            dh = last_dot(dp[0, at], w[:, :d]) + last_dot(dp[1, at], w[:, d : 2 * d]) + last_dot(dp[2, at], w[:, 2 * d :])
            unit, spread = centered(x[at].astype(wide))
            out[at] = (middle[at] + norm_back(dh, unit, spread, gain_ref[0:1])).astype(low)
            scaled, shifted = jnp.sum(dh * unit, axis=0, keepdims=True), jnp.sum(dh, axis=0, keepdims=True)
            rows[0:1] = scaled if n == 0 else rows[0:1] + scaled
            rows[1:2] = shifted if n == 0 else rows[1:2] + shifted

        for n in range(count // block):
            for j, step in plan.get(n, []):
                work[j].step(step)
            back(n)
        store = pltpu.make_async_copy(out, input_grad_h, local.at[0])
        store.start()
        packed[...] = jnp.zeros_like(packed)
        for line in range(lines):
            for part in range(d // 128):
                at = line * (d // 128) + part
                packed[at : at + 1] = rows[line : line + 1, part * 128 : (part + 1) * 128]
        small_parts[...] = jnp.zeros_like(small_parts)
        for n, (z, px, y, c) in enumerate(places()):
            if n < packed.shape[0] // 16:
                small_parts[y, c, z, px] = packed[16 * n : 16 * n + 16].astype(low)
        for j, step in plan["end"]:
            work[j].step(step)
        for job, (n, path, at) in zip(work, jobs):
            if n < n_blocks:
                mine[n, at, :] = job.total().astype(low)
            else:
                small[...] = job.total().astype(low)
        for job in work:
            job.finish()
        store.wait()

    shape = jax.ShapeDtypeStruct
    return pl.pallas_call(
        kernel,
        out_shape=[shape((n_blocks, 48, 384), low), shape((16, 128), low), shape((count, d), low)],
        in_specs=[ANY] * 5 + [VM] * 4,
        out_specs=[VM, VM, ANY],
        scratch_shapes=[pltpu.VMEM((count, d), low), pltpu.VMEM((count, d), low), pltpu.VMEM(projected_grad.shape, low),
                        pltpu.VMEM(weight.shape, low), pltpu.VMEM((count, d), wide), pltpu.VMEM((count, d), low),
                        pltpu.VMEM((d, count), low), pltpu.VMEM((n_blocks,) + grid.shape("j", 48, 384), low),
                        pltpu.VMEM(grid.shape("j", 16, 128), low), pltpu.VMEM((16, d), wide), pltpu.VMEM((80, 128), wide),
                        pltpu.SemaphoreType.DMA((5,))] + scatter_scratch(grid, sizes, jobs),
        compiler_params=pltpu.CompilerParams(vmem_limit_bytes=60 * 1024 * 1024, collective_id=collective_id,
                                             has_side_effects=True),
        name="project_back",
    )(tokens, normed, projected_grad, weight, middle_grad, gain, sums, bias_out, bias_up)


TAIL_PLAN = {
    "jobs": [(0, 0, pl.ds(0, 48)), (1, 0, pl.ds(0, 48)), (2, 0, pl.ds(0, 48)), (3, 0, pl.ds(0, 16))],
    0: [(0, 1)],
    1: [(1, 1), (0, 2)],
    2: [(2, 1)],
    3: [(1, 2), (0, 3)],
    "end": [(3, 0), (2, 2), (3, 1), (1, 3), (3, 2), (2, 3), (3, 3)],
}


D = 768
HEADS = 12
HD = 64
FF = 3072
BLOCKS = 12


masked_score = -1000000000.0
decay_rate = 0.5
step_rate = 1.0
small_rate = 0.3
highest = lax.Precision.HIGHEST


def broadcast(value, axis, source):
    kept = jnp.where(lax.axis_index(axis) == source, value, 0).astype(value.dtype)
    return lax.psum(kept, axis)


def layer_norm(values, scale_row, shift_row):
    center = values - jnp.mean(values, axis=-1, keepdims=True)
    spread = jnp.mean(center * center, axis=-1, keepdims=True)
    return center * lax.rsqrt(spread + 1e-06) * scale_row + shift_row


def unpack(small_params):
    pieces = [small_params[number * D : (number + 1) * D] for number in range(8)]
    return pieces + [small_params[8 * D : 8 * D + FF]]


def row_dot(left, right):
    return jnp.dot(left, right, preferred_element_type=jnp.float32)


def column_dot(left, right):
    return lax.dot_general(
        left, right, (((0,), (0,)), ((), ())), preferred_element_type=jnp.float32
    )


def transposed_dot(left, right):
    return lax.dot_general(
        left, right, (((1,), (1,)), ((), ())), preferred_element_type=jnp.float32
    )


def block_split(array, block_rows):
    slots = array.shape[-1]
    return array.reshape(HEADS, HD, slots // block_rows, block_rows).transpose(2, 0, 1, 3)


def block_join(array):
    return array.transpose(0, 3, 1, 2).reshape(-1, D)


def attend_clip(queries, key_rows, value_rows, length):
    slots = queries.shape[-1]
    block_rows = min(512, slots)
    score_scale = float(HD) ** (-0.5)
    visible = (jnp.arange(slots) < length)[None, None, :]

    def one_block(query_block):
        scores = (
            jnp.einsum("hdq,hdk->hqk", query_block, key_rows, preferred_element_type=jnp.float32)
            * score_scale
        )
        scores = jnp.where(visible, scores, masked_score)
        row_top = jnp.max(scores, axis=-1, keepdims=True)
        raised = jnp.exp(scores - row_top)
        row_total = jnp.sum(raised, axis=-1, keepdims=True)
        softmax_weights = (raised / row_total).astype(jnp.bfloat16)
        attended = jnp.einsum(
            "hqk,hdk->hdq", softmax_weights, value_rows, preferred_element_type=jnp.float32
        )
        return (attended.astype(jnp.bfloat16), (row_top + jnp.log(row_total))[:, :, 0])

    attended, log_totals = lax.map(one_block, block_split(queries, block_rows))
    return (block_join(attended), log_totals)


def attend_back(queries, key_rows, value_rows, length, log_totals, out_grads):
    slots = queries.shape[-1]
    block_rows = min(512, slots)
    score_scale = float(HD) ** (-0.5)
    visible = (jnp.arange(slots) < length)[None, None, :]

    def one_block(carry, pieces):
        key_grad, value_grad = carry
        query_block, grad_block, log_block = pieces
        scores = (
            jnp.einsum("hdq,hdk->hqk", query_block, key_rows, preferred_element_type=jnp.float32)
            * score_scale
        )
        scores = jnp.where(visible, scores, masked_score)
        softmax_weights = jnp.exp(scores - log_block[:, :, None])
        weight_grad = jnp.einsum(
            "hdq,hdk->hqk", grad_block, value_rows, preferred_element_type=jnp.float32
        )
        inner_sum = jnp.sum(softmax_weights * weight_grad, axis=-1, keepdims=True)
        score_grad = (softmax_weights * (weight_grad - inner_sum)).astype(jnp.bfloat16)
        query_grad = (
            jnp.einsum("hqk,hdk->hdq", score_grad, key_rows, preferred_element_type=jnp.float32)
            * score_scale
        )
        key_grad = (
            key_grad
            + jnp.einsum(
                "hqk,hdq->hdk", score_grad, query_block, preferred_element_type=jnp.float32
            )
            * score_scale
        )
        value_grad = value_grad + jnp.einsum(
            "hqk,hdq->hdk",
            softmax_weights.astype(jnp.bfloat16),
            grad_block,
            preferred_element_type=jnp.float32,
        )
        return ((key_grad, value_grad), query_grad)

    blank = jnp.zeros((HEADS, HD, slots), jnp.float32)
    (key_grad, value_grad), query_grad = lax.scan(
        one_block,
        (blank, blank),
        (block_split(queries, block_rows), block_split(out_grads, block_rows), log_totals),
    )
    key_rows_grad = key_grad.transpose(2, 0, 1).reshape(slots, D)
    value_rows_grad = value_grad.transpose(2, 0, 1).reshape(slots, D)
    return (block_join(query_grad), key_rows_grad, value_rows_grad)


def take_columns(operands, member, start):
    return lax.slice_in_dim(operands[member], start, start + D, axis=1)


def take_rows(operands, member, start):
    return lax.slice_in_dim(operands[member], start, start + D, axis=0)


def block_pickers():
    pickers = [partial(take_columns, member=0, start=column * D) for column in range(3)]
    pickers.append(partial(take_columns, member=1, start=0))
    pickers = pickers + [
        partial(take_columns, member=2, start=column * D) for column in range(FF // D)
    ]
    pickers = pickers + [
        partial(take_rows, member=3, start=column * D) for column in range(FF // D)
    ]
    return pickers


def fetch_update(update, root):
    return broadcast(update.astype(jnp.bfloat16), ("dp", "fsdp"), root).astype(update.dtype)


def band_tile(band, like, column_index):
    columns_here = like.shape[1]
    return lax.dynamic_slice_in_dim(band, column_index * columns_here, columns_here, 1)


def row_band(pieces, like, row_index):
    rows_here = like.shape[0]
    start = row_index * rows_here
    return jnp.concatenate(
        [lax.dynamic_slice_in_dim(piece, start, rows_here, 0) for piece in pieces], axis=1
    )


def stacked_band(pieces, like, row_index):
    rows_here = like.shape[0]
    start = row_index * rows_here
    owner_block = start // D
    picked = jnp.zeros((rows_here, D), jnp.float32)
    for number in range(len(pieces)):
        inside = jnp.clip(start - number * D, 0, D - rows_here)
        piece = lax.dynamic_slice_in_dim(pieces[number], inside, rows_here, 0)
        picked = jnp.where(owner_block == number, piece, picked)
    return picked


def local_any(
    tokens,
    counts,
    cotangent,
    qkv_weight,
    out_weight,
    up_weight,
    down_weight,
    small_params,
    statistics,
    inverse_roots,
    owners,
):
    clips_here = counts.shape[0]
    slots = tokens.shape[0] // clips_here
    qkv_low = qkv_weight.astype(jnp.bfloat16)
    out_low = out_weight.astype(jnp.bfloat16)
    up_low = up_weight.astype(jnp.bfloat16)
    down_low = down_weight.astype(jnp.bfloat16)
    qkv_cols, out_cols, up_cols, down_cols = (
        lax.all_gather(qkv_low, "fsdp", axis=1, tiled=True),
        lax.all_gather(out_low, "fsdp", axis=1, tiled=True),
        lax.all_gather(up_low, "fsdp", axis=1, tiled=True),
        lax.all_gather(down_low, "fsdp", axis=1, tiled=True),
    )
    qkv_full, out_full, up_full, down_full = (
        lax.all_gather(qkv_cols, "dp", axis=0, tiled=True),
        lax.all_gather(out_cols, "dp", axis=0, tiled=True),
        lax.all_gather(up_cols, "dp", axis=0, tiled=True),
        lax.all_gather(down_cols, "dp", axis=0, tiled=True),
    )
    (
        gain_one,
        shift_one,
        gain_two,
        shift_two,
        bias_query,
        bias_value,
        bias_out,
        bias_down,
        bias_up,
    ) = unpack(small_params)

    def heads_view(array):
        return array.reshape(clips_here, slots, HEADS, HD).transpose(0, 2, 3, 1)

    def clip_forward(clip_group):
        return attend_clip(clip_group[0], clip_group[1], clip_group[2], clip_group[3])

    def clip_backward(clip_group):
        return attend_back(
            clip_group[0], clip_group[1], clip_group[2], clip_group[3], clip_group[4], clip_group[5]
        )

    inputs = tokens.astype(jnp.float32)
    normed = layer_norm(inputs, gain_one, shift_one).astype(jnp.bfloat16)
    projected = row_dot(normed, qkv_full)
    queries = heads_view((projected[:, :D] + bias_query).astype(jnp.bfloat16))
    key_rows = heads_view(projected[:, D : 2 * D].astype(jnp.bfloat16))
    value_rows = heads_view((projected[:, 2 * D :] + bias_value).astype(jnp.bfloat16))
    attended, log_totals = lax.map(clip_forward, (queries, key_rows, value_rows, counts))
    attended = attended.reshape(-1, D)
    middle = inputs + (row_dot(attended, out_full) + bias_out)
    normed_two = layer_norm(middle, gain_two, shift_two).astype(jnp.bfloat16)
    hidden = row_dot(normed_two, up_full) + bias_up
    active = jax.nn.gelu(hidden, approximate=False).astype(jnp.bfloat16)
    layer_rows = (middle + row_dot(active, down_full) + bias_down).astype(jnp.bfloat16)
    qkv_part, out_part, up_part, down_part = (
        lax.all_gather(qkv_low, "fsdp", axis=1, tiled=True),
        lax.all_gather(out_low, "fsdp", axis=1, tiled=True),
        lax.all_gather(up_low, "fsdp", axis=1, tiled=True),
        lax.all_gather(down_low, "fsdp", axis=1, tiled=True),
    )
    qkv_back, out_back, up_back, down_back = (
        lax.all_gather(qkv_part, "dp", axis=0, tiled=True),
        lax.all_gather(out_part, "dp", axis=0, tiled=True),
        lax.all_gather(up_part, "dp", axis=0, tiled=True),
        lax.all_gather(down_part, "dp", axis=0, tiled=True),
    )
    grad_down = column_dot(active, cotangent)
    grad_bias_down = jnp.sum(cotangent.astype(jnp.float32), axis=0)
    active_grad = transposed_dot(cotangent, down_back)
    unused_value, gelu_pull = jax.vjp(partial(jax.nn.gelu, approximate=False), hidden)
    hidden_grad = gelu_pull(active_grad)[0].astype(jnp.bfloat16)
    grad_up = column_dot(normed_two, hidden_grad)
    grad_bias_up = jnp.sum(hidden_grad.astype(jnp.float32), axis=0)
    normed_two_grad = transposed_dot(hidden_grad, up_back)
    unused_norm, norm_two_pull = jax.vjp(layer_norm, middle, gain_two, shift_two)
    middle_grad, grad_gain_two, grad_shift_two = norm_two_pull(normed_two_grad)
    middle_grad = middle_grad + cotangent.astype(jnp.float32)
    branch_grad = middle_grad.astype(jnp.bfloat16)
    grad_out = column_dot(attended, branch_grad)
    grad_bias_out = jnp.sum(branch_grad.astype(jnp.float32), axis=0)
    attended_grad = transposed_dot(branch_grad, out_back).astype(jnp.bfloat16)
    query_grad, key_grad, value_grad = lax.map(
        clip_backward,
        (queries, key_rows, value_rows, counts, log_totals, heads_view(attended_grad)),
    )
    projected_grad = (
        jnp.concatenate([query_grad, key_grad, value_grad], axis=-1)
        .reshape(-1, 3 * D)
        .astype(jnp.bfloat16)
    )
    grad_qkv = column_dot(normed, projected_grad)
    grad_bias_query = jnp.sum(projected_grad[:, :D].astype(jnp.float32), axis=0)
    grad_bias_value = jnp.sum(projected_grad[:, 2 * D :].astype(jnp.float32), axis=0)
    normed_grad = transposed_dot(projected_grad, qkv_back)
    unused_first, norm_one_pull = jax.vjp(layer_norm, inputs, gain_one, shift_one)
    input_rows_grad, grad_gain_one, grad_shift_one = norm_one_pull(normed_grad)
    input_grad = (middle_grad + input_rows_grad).astype(jnp.bfloat16)
    small_grad = jnp.concatenate(
        [
            grad_gain_one,
            grad_shift_one,
            grad_gain_two,
            grad_shift_two,
            grad_bias_query,
            grad_bias_value,
            grad_bias_out,
            grad_bias_down,
            grad_bias_up,
        ]
    )
    row_qkv, row_out, row_up, row_down, row_small = (
        lax.psum_scatter(
            grad_qkv.astype(jnp.bfloat16), "dp", scatter_dimension=0, tiled=True
        ).astype(jnp.float32),
        lax.psum_scatter(
            grad_out.astype(jnp.bfloat16), "dp", scatter_dimension=0, tiled=True
        ).astype(jnp.float32),
        lax.psum_scatter(
            grad_up.astype(jnp.bfloat16), "dp", scatter_dimension=0, tiled=True
        ).astype(jnp.float32),
        lax.psum_scatter(
            grad_down.astype(jnp.bfloat16), "dp", scatter_dimension=0, tiled=True
        ).astype(jnp.float32),
        lax.psum_scatter(
            small_grad.astype(jnp.bfloat16), "dp", scatter_dimension=0, tiled=True
        ).astype(jnp.float32),
    )
    shard_qkv, shard_out, shard_up, shard_down, shard_small = (
        lax.psum_scatter(
            row_qkv.astype(jnp.bfloat16), "fsdp", scatter_dimension=1, tiled=True
        ).astype(jnp.float32),
        lax.psum_scatter(
            row_out.astype(jnp.bfloat16), "fsdp", scatter_dimension=1, tiled=True
        ).astype(jnp.float32),
        lax.psum_scatter(
            row_up.astype(jnp.bfloat16), "fsdp", scatter_dimension=1, tiled=True
        ).astype(jnp.float32),
        lax.psum_scatter(
            row_down.astype(jnp.bfloat16), "fsdp", scatter_dimension=1, tiled=True
        ).astype(jnp.float32),
        lax.psum_scatter(
            row_small.astype(jnp.bfloat16), "fsdp", scatter_dimension=0, tiled=True
        ).astype(jnp.float32),
    )
    band_qkv, band_out, band_up, band_down, band_small = (
        lax.all_gather(shard_qkv.astype(jnp.bfloat16), "fsdp", axis=1, tiled=True).astype(
            shard_qkv.dtype
        ),
        lax.all_gather(shard_out.astype(jnp.bfloat16), "fsdp", axis=1, tiled=True).astype(
            shard_out.dtype
        ),
        lax.all_gather(shard_up.astype(jnp.bfloat16), "fsdp", axis=1, tiled=True).astype(
            shard_up.dtype
        ),
        lax.all_gather(shard_down.astype(jnp.bfloat16), "fsdp", axis=1, tiled=True).astype(
            shard_down.dtype
        ),
        lax.all_gather(shard_small.astype(jnp.bfloat16), "fsdp", axis=0, tiled=True).astype(
            shard_small.dtype
        ),
    )
    rank = lax.axis_index(("dp", "fsdp"))
    row_index = lax.axis_index("dp")
    column_index = lax.axis_index("fsdp")
    numbers = jnp.arange(BLOCKS, dtype=jnp.int32)
    matches = owners == rank
    mine = jnp.sum(jnp.where(matches, numbers, 0))
    owning = jnp.any(matches)

    def update_slot(gradient):
        left_stat = decay_rate * statistics[0, 0] + (1.0 - decay_rate) * jnp.dot(
            gradient, gradient.T, precision=highest, preferred_element_type=jnp.float32
        )
        right_stat = decay_rate * statistics[0, 1] + (1.0 - decay_rate) * jnp.dot(
            gradient.T, gradient, precision=highest, preferred_element_type=jnp.float32
        )
        left_step = jnp.dot(
            inverse_roots[0, 0], gradient, precision=highest, preferred_element_type=jnp.float32
        )
        update = jnp.dot(
            left_step, inverse_roots[0, 1], precision=highest, preferred_element_type=jnp.float32
        )
        return (jnp.stack([left_stat, right_stat])[None], update)

    def keep_slot(gradient):
        return (statistics, jnp.zeros((D, D), jnp.float32))

    whole_qkv, whole_out, whole_up, whole_down, whole_small = (
        lax.all_gather(band_qkv.astype(jnp.bfloat16), "dp", axis=0, tiled=True).astype(
            band_qkv.dtype
        ),
        lax.all_gather(band_out.astype(jnp.bfloat16), "dp", axis=0, tiled=True).astype(
            band_out.dtype
        ),
        lax.all_gather(band_up.astype(jnp.bfloat16), "dp", axis=0, tiled=True).astype(
            band_up.dtype
        ),
        lax.all_gather(band_down.astype(jnp.bfloat16), "dp", axis=0, tiled=True).astype(
            band_down.dtype
        ),
        lax.all_gather(band_small.astype(jnp.bfloat16), "dp", axis=0, tiled=True).astype(
            band_small.dtype
        ),
    )
    gradient = lax.switch(mine, block_pickers(), (whole_qkv, whole_out, whole_up, whole_down))
    new_statistics, update = lax.cond(owning, update_slot, keep_slot, gradient)
    arrivals = []
    for number in range(BLOCKS):
        arrivals.append(fetch_update(update, owners[number]))
    tile_qkv = band_tile(row_band(arrivals[0:3], qkv_weight, row_index), qkv_weight, column_index)
    tile_out = band_tile(row_band(arrivals[3:4], out_weight, row_index), out_weight, column_index)
    tile_up = band_tile(
        row_band(arrivals[4 : 4 + FF // D], up_weight, row_index), up_weight, column_index
    )
    tile_down = band_tile(
        stacked_band(arrivals[4 + FF // D :], down_weight, row_index), down_weight, column_index
    )
    new_qkv = qkv_weight - step_rate * tile_qkv
    new_out = out_weight - step_rate * tile_out
    new_up = up_weight - step_rate * tile_up
    new_down = down_weight - step_rate * tile_down
    new_small = small_params - small_rate * whole_small * lax.rsqrt(
        jnp.mean(whole_small * whole_small) + 1e-06
    )
    return (
        layer_rows,
        input_grad,
        shard_qkv,
        shard_out,
        shard_up,
        shard_down,
        whole_small,
        new_statistics,
        new_qkv,
        new_out,
        new_up,
        new_down,
        new_small,
    )


def local_staged(
    sizes,
    tokens,
    counts,
    cotangent,
    qkv_weight,
    out_weight,
    up_weight,
    down_weight,
    small_params,
    statistics,
    inverse_roots,
    owners,
):
    n_dp, n_fsdp = sizes
    small_rows = small_params.reshape(-1, D)
    down_turned = down_weight.T
    orders = ("j", "j", "j", "i")
    qkv_pieces, *begun = gather_first(n_dp, n_fsdp, (qkv_weight, out_weight, up_weight), orders[:3], FIRST_PLAN, 1)
    normed, projected, qkv_full, attended, log_totals, out_pieces, up_pieces, down_pieces = project_attend(
        n_dp, n_fsdp, counts, tokens, qkv_pieces.reshape(n_fsdp, D, 3 * D // n_fsdp), small_rows,
        begun, (down_turned,), orders[1:], FORWARD_PLAN, 2,
    )
    layer_rows, normed_two, active, hidden_grad, middle_grad, branch_grad, attended_grad, sums = middle_layer(
        tokens,
        attended,
        cotangent,
        out_pieces.reshape(n_fsdp, D, D // n_fsdp),
        up_pieces.reshape(n_fsdp, D, FF // n_fsdp),
        down_pieces.reshape(n_dp, D, FF // n_dp),
        small_rows,
    )
    projected_grad, mine_down, mine_up, mine_out, grad_bias_up, grad_bias_out = grads_attend_back(
        n_dp, n_fsdp, counts, projected, attended, attended_grad, log_totals,
        cotangent, active, normed_two, hidden_grad, branch_grad, BACKWARD_PLAN, 3,
    )
    mine_qkv, mine_small, input_grad = project_back(
        n_dp, n_fsdp, tokens, normed, projected_grad, qkv_full, middle_grad, small_rows,
        sums, grad_bias_out, grad_bias_up, TAIL_PLAN, 4
    )
    exchanged = owner_exchange(
        n_dp, n_fsdp, owners, (mine_qkv.reshape(-1, 384), mine_out, mine_up, mine_down), mine_small, inverse_roots[0], 5
    )
    masters = (qkv_weight, out_weight, up_weight, down_turned)
    *results, whole_small, new_small, new_statistics = finish_step(
        n_dp, n_fsdp, owners, exchanged, masters, small_params.reshape(-1, 128), statistics[0], (step_rate, small_rate)
    )
    shard_qkv, shard_out, shard_up, shard_down, new_qkv, new_out, new_up, new_down = results
    whole_small, new_small = whole_small.reshape(-1), new_small.reshape(-1)
    return (
        layer_rows,
        input_grad,
        shard_qkv,
        shard_out,
        shard_up,
        shard_down.T,
        whole_small,
        new_statistics[None],
        new_qkv,
        new_out,
        new_up,
        new_down.T,
        new_small,
    )


def solution(mesh):
    placed = (
        P(("dp", "fsdp"), None),
        P(("dp", "fsdp")),
        P(("dp", "fsdp"), None),
        P("dp", "fsdp"),
        P("dp", "fsdp"),
        P("dp", "fsdp"),
        P("dp", "fsdp"),
        P(),
        P(("dp", "fsdp"), None, None, None),
        P(("dp", "fsdp"), None, None, None),
        P(),
    )
    sizes = (mesh.shape["dp"], mesh.shape["fsdp"])
    local = partial(local_staged, sizes) if sizes == (8, 4) else local_any
    return jax.shard_map(
        local,
        mesh=mesh,
        in_specs=placed,
        out_specs=(
            P(("dp", "fsdp"), None),
            P(("dp", "fsdp"), None),
            P("dp", "fsdp"),
            P("dp", "fsdp"),
            P("dp", "fsdp"),
            P("dp", "fsdp"),
            P(),
            P(("dp", "fsdp"), None, None, None),
            P("dp", "fsdp"),
            P("dp", "fsdp"),
            P("dp", "fsdp"),
            P("dp", "fsdp"),
            P(),
        ),
        check_vma=False,
    )
```

```python
from functools import partial

import jax
import jax.numpy as jnp
from jax import lax
from jax.experimental import pallas as pl
from jax.experimental.pallas import tpu as pltpu
from jax.sharding import PartitionSpec as P

MESH = pl.DeviceIdType.MESH
ANY = pl.BlockSpec(memory_space=pl.ANY)
VM = pl.BlockSpec(memory_space=pltpu.VMEM)


class Grid:
    def __init__(self, n_dp, n_fsdp):
        self.Z = 4
        self.X = n_dp // 4
        self.Y = n_fsdp // 2
        self.swap = self.X == self.Y
        self.A, self.B = self.X, self.Y

    def here(self):
        dp, fs = lax.axis_index("dp"), lax.axis_index("fsdp")
        self.z, self.x = dp // self.X, dp % self.X
        self.y, self.c = fs // 2, fs % 2
        if self.swap:
            self.a = self.x + self.c * (self.y - self.x)
            self.b = self.y + self.c * (self.x - self.y)
        else:
            self.a, self.b = self.x, self.y
        return self

    def xy(self, a, b, c):
        if self.swap:
            return a + c * (b - a), b + c * (a - b)
        return a, b

    def device(self, z, a, b, c, frame=None):
        x, y = self.xy(a, b, self.c if frame is None else frame)
        return {"dp": z * self.X + x, "fsdp": y * 2 + c}

    def shape(self, order, r, w):
        if order == "j":
            return (self.Y, 2, self.Z, self.X, r, w)
        return (self.Z, self.X, self.Y, 2, r, w)

    def at(self, ref, order, y, c, z, x):
        return ref.at[y, c, z, x] if order == "j" else ref.at[z, x, y, c]

    def peers(self):
        out = [self.device((self.z + k) % self.Z, self.a, self.b, self.c) for k in range(1, self.Z)]
        out += [self.device(self.z, (self.a + k) % self.A, self.b, self.c) for k in range(1, self.A)]
        out += [self.device(self.z, self.a, (self.b + k) % self.B, self.c) for k in range(1, self.B)]
        out += [{"dp": self.z * self.X + self.x, "fsdp": self.y * 2 + 1 - self.c}]
        return out

    def barrier(self, between=None):
        sem = pltpu.get_barrier_semaphore()
        peers = self.peers()
        for peer in peers:
            pl.semaphore_signal(sem, inc=1, device_id=peer, device_id_type=MESH)
        if between is not None:
            between()
        pl.semaphore_wait(sem, len(peers))


def remote(src, dst, send, recv, slot, device):
    return pltpu.make_async_remote_copy(
        src_ref=src, dst_ref=dst, send_sem=send.at[slot], recv_sem=recv.at[slot], device_id=device, device_id_type=MESH
    )


def start_all(copies):
    for copy in copies:
        copy.start()


def arrived(copies):
    for copy in copies:
        copy.wait_recv()


def sent(copies):
    for copy in copies:
        copy.wait_send()


class Copies:
    def __init__(self, send, recv):
        self.send, self.recv, self.slot = send, recv, 0

    def add(self, group, describe):
        group.append((self.slot, describe))
        self.slot += 1

    def made(self, group):
        out = []
        for slot, describe in group:
            start, end, device = describe()
            out.append(remote(start, end, self.send, self.recv, slot, device))
        return out

    def start(self, group):
        start_all(self.made(group))

    def arrived(self, group):
        arrived(self.made(group))

    def sent(self, group):
        sent(self.made(group))


class Gather:
    def __init__(self, g, order, path, rows, src, out, local, send, recv):
        size = {"z": g.Z, "a": g.A, "b": g.B}
        self.copies = Copies(send, recv)

        def at(name, shift):
            place = {"z": g.z, "a": g.a, "b": g.b}[name]
            return (place + shift + size[name]) % size[name] if shift else place

        def piece(cell):
            where = {name: (at(name, value[1]) if isinstance(value, tuple) else value) for name, value in cell.items()}
            x, y = g.xy(where["a"], where["b"], g.c)
            return g.at(out, order, y, g.c, where["z"], x).at[..., rows, :]

        own_cell = {"z": ("own", 0), "a": ("own", 0), "b": ("own", 0)}

        def cells(full):
            out = [dict(own_cell)]
            for axis in full:
                if axis == "z":
                    out = [dict(cell, z=slice(None)) for cell in out]
                else:
                    out = [dict(cell, **{axis: n}) for cell in out for n in range(size[axis])]
            return out

        def near():
            return {"dp": g.z * g.X + g.x, "fsdp": g.y * 2 + 1 - g.c}

        def far(axis, k):
            return g.device(*[at(name, k if name == axis else 0) for name in "zab"], g.c)

        def own():
            return src.at[rows, :]

        self.own = lambda: pltpu.make_async_copy(own(), piece(own_cell), local)
        self.stages, self.near = [], [[]]
        self.copies.add(self.near[0], lambda: (own(), piece(own_cell), near()))
        full = ""
        for axis in path:
            self.stages.append([])
            self.near.append([])
            for cell in cells(full):
                for k in range(1, size[axis]):
                    from_src = not full
                    self.copies.add(self.stages[-1], lambda cell=cell, k=k, axis=axis, from_src=from_src: (
                        own() if from_src else piece(cell), piece(cell), far(axis, k)))
                    came = dict(cell, **{axis: ("own", -k)})
                    self.copies.add(self.near[-1], lambda came=came: (piece(came), piece(came), near()))
            full += axis

    @staticmethod
    def slots(g):
        zab = (g.Z - 1) + (g.A - 1) + g.A * (g.B - 1)
        abz = (g.A - 1) + g.A * (g.B - 1) + g.A * g.B * (g.Z - 1)
        return 1 + 2 * max(zab, abz)

    def step(self, number):
        if number == 0:
            self.own().start()
        else:
            if number == 1:
                self.own().wait()
            self.copies.arrived(self.stages[number - 1])
        if number < 3:
            self.copies.start(self.stages[number])
        self.copies.start(self.near[number])

    def pause(self):
        self.own().wait()
        for group in (self.stages[0], self.near[0]):
            self.copies.arrived(group)
            self.copies.sent(group)

    def resume(self):
        self.copies.start(self.stages[1])
        self.copies.start(self.near[1])

    def finish(self, first=0):
        for group in self.near[first:]:
            self.copies.arrived(group)
        for group in self.near[first:] + self.stages[first:]:
            self.copies.sent(group)


class Scatter:
    def __init__(self, g, order, path, rows, src, bufs, send, recv):
        self.g, self.path, self.order, self.rows, self.src = g, path, order, rows, src
        self.work = bufs[0]
        self.recv = dict(zip(path, bufs[1:]))
        work = self.work
        size = {"z": g.Z, "a": g.A, "b": g.B}
        self.size = size
        self.copies = Copies(send, recv)
        places = lambda: {"z": g.z, "a": g.a, "b": g.b}

        def other(b, a):
            x, y = g.xy(a, b, 1 - g.c)
            return (g.at(src, order, y, 1 - g.c, slice(None), x).at[:, rows, :], work.at[b, :, a],
                    {"dp": g.z * g.X + g.x, "fsdp": g.y * 2 + 1 - g.c})

        def onward(axis, k, done):
            place = places()
            to = dict(place, **{axis: (place[axis] + k) % size[axis]})
            where = {name: (place[name] if name in done else slice(None)) for name in "bza"}
            where[axis] = to[axis]
            return (work.at[where["b"], where["z"], where["a"]], self.recv[axis].at[k - 1],
                    g.device(to["z"], to["a"], to["b"], g.c))

        self.stages = [[]]
        for b in range(g.B):
            for a in range(g.A):
                self.copies.add(self.stages[0], partial(other, b, a))
        done = ""
        for axis in path:
            self.stages.append([])
            for k in range(1, size[axis]):
                self.copies.add(self.stages[-1], partial(onward, axis, k, done))
            done += axis

    @staticmethod
    def slots(g):
        return g.A * g.B + (g.B - 1) + (g.A - 1) + (g.Z - 1)

    @staticmethod
    def scratch(g, path, r, w):
        size = {"z": g.Z, "a": g.A, "b": g.B}
        out = [pltpu.VMEM((g.B, g.Z, g.A, r, w), jnp.bfloat16)]
        done = ""
        for axis in path:
            done += axis
            out.append(pltpu.VMEM((size[axis] - 1,) + tuple(size[n] for n in "bza" if n not in done) + (r, w), jnp.bfloat16))
        return out

    def _cell(self, index, done):
        place = {"z": self.g.z, "a": self.g.a, "b": self.g.b}
        return [place[n] if n in done else index[n] for n in "bza"]

    def _add(self, number):
        g, done = self.g, self.path[:number]
        left = [n for n in "bza" if n not in done]
        total = 1
        for name in left:
            total *= self.size[name]

        def add(n, carry):
            index = {}
            for name in reversed(left):
                index[name] = n % self.size[name]
                n = n // self.size[name]
            b, z, a = self._cell(index, done)
            if number == 0:
                x, y = g.xy(a, b, g.c)
                mine = g.at(self.src, self.order, y, g.c, z, x)[self.rows, :]
                summed = self.work[b, z, a].astype(jnp.float32) + mine.astype(jnp.float32)
            else:
                summed = self._sum(number, b, z, a, [index[name] for name in left])
            self.work[b, z, a] = summed.astype(jnp.bfloat16)
            return carry

        lax.fori_loop(0, total, add, 0)

    def _sum(self, number, b, z, a, index):
        axis = self.path[number - 1]
        summed = self.work[b, z, a].astype(jnp.float32)
        for k in range(self.size[axis] - 1):
            summed = summed + self.recv[axis][tuple([k] + index)].astype(jnp.float32)
        return summed

    def step(self, number):
        if number > 0:
            self.copies.arrived(self.stages[number - 1])
            self._add(number - 1)
        self.copies.start(self.stages[number])

    def total(self):
        self.copies.arrived(self.stages[3])
        return self._sum(3, self.g.b, self.g.z, self.g.a, [])

    def finish(self):
        for group in self.stages:
            self.copies.sent(group)


GATHER_PATHS = ("zab", "abz")
SCATTER_PATHS = ("baz", "zba")


def row_parts(rows, share=0):
    second = rows * share // 6 // 16 * 16
    parts = [(0, pl.ds(0, rows - second))]
    return parts + ([(1, pl.ds(rows - second, second))] if second else [])


def job_list(sizes, share=0):
    return [(n, path, rows) for n, (r, _) in enumerate(sizes) for path, rows in row_parts(r, share)]


def rounds(jobs, last):
    return [(n, step) for step in range(last + 1) for n in range(len(jobs))]


def gather_scratch(g, count):
    lanes = Gather.slots(g)
    dma = pltpu.SemaphoreType.DMA
    return [dma((count,)), dma((count, lanes)), dma((count, lanes))]


def gather_jobs(g, orders, jobs, ins, outs, scratch):
    local, send, recv = scratch
    return [Gather(g, orders[n], GATHER_PATHS[path], rows, ins[n], outs[n], local.at[j], send.at[j], recv.at[j])
            for j, (n, path, rows) in enumerate(jobs)]


def gather_first(n_dp, n_fsdp, shards, orders, plan, collective_id):
    grid = Grid(n_dp, n_fsdp)
    count = len(shards)
    jobs, order, wholes = plan

    def kernel(*refs):
        g = grid.here()
        low = refs[2 * count : 3 * count]

        def first():
            low[0][...] = refs[0][...].astype(jnp.bfloat16)

        g.barrier(first)
        work = gather_jobs(g, orders, jobs, low, refs[count : 2 * count], refs[3 * count :])
        work[0].step(0)
        for n in range(1, count):
            low[n][...] = refs[n][...].astype(jnp.bfloat16)
        for job, step in order:
            work[job].step(step)
        for job in work[wholes:]:
            job.pause()
        for job in work[:wholes]:
            job.finish()

    return pl.pallas_call(
        kernel,
        out_shape=[jax.ShapeDtypeStruct(grid.shape(o, *s.shape), jnp.bfloat16) for s, o in zip(shards, orders)],
        in_specs=[VM] * count,
        out_specs=[ANY] * count,
        scratch_shapes=[pltpu.VMEM(s.shape, jnp.bfloat16) for s in shards] + gather_scratch(grid, len(jobs)),
        compiler_params=pltpu.CompilerParams(collective_id=collective_id, has_side_effects=True),
        name="gather_first",
    )(*shards)


def scatter_scratch(g, sizes, jobs):
    out = []
    for n, path, rows in jobs:
        out += Scatter.scratch(g, SCATTER_PATHS[path], rows.size, sizes[n][1])
    dma = pltpu.SemaphoreType.DMA
    lanes = Scatter.slots(g)
    return out + [dma((len(jobs), lanes)), dma((len(jobs), lanes))]


def scatter_jobs(g, orders, jobs, ins, scratch):
    send, recv = scratch[4 * len(jobs) :]
    return [Scatter(g, orders[n], SCATTER_PATHS[path], rows, ins[n], scratch[4 * j : 4 * j + 4], send.at[j], recv.at[j])
            for j, (n, path, rows) in enumerate(jobs)]


def scatter_all(n_dp, n_fsdp, wholes, orders, collective_id, dtype=jnp.float32):
    grid = Grid(n_dp, n_fsdp)
    count = len(wholes)
    sizes = [w.shape[-2:] for w in wholes]
    jobs = job_list(sizes, 2)

    def kernel(*refs):
        ins, outs, scratch = refs[:count], refs[count : 2 * count], refs[2 * count :]
        g = grid.here()
        g.barrier()
        work = scatter_jobs(g, orders, jobs, ins, scratch)
        for j, step in rounds(jobs, 3):
            work[j].step(step)
        for job, (n, path, rows) in zip(work, jobs):
            outs[n][rows, :] = job.total().astype(dtype)
        for job in work:
            job.finish()

    return pl.pallas_call(
        kernel,
        out_shape=[jax.ShapeDtypeStruct(s, dtype) for s in sizes],
        in_specs=[VM] * count,
        out_specs=[VM] * count,
        scratch_shapes=scatter_scratch(grid, sizes, jobs),
        compiler_params=pltpu.CompilerParams(collective_id=collective_id, has_side_effects=True,
                                             vmem_limit_bytes=60 * 1024 * 1024),
        name="scatter_all",
    )(*wholes)


HEAD = 64
PAIR = 128


def last_dot(left, right):
    return lax.dot_general(left, right, (((1,), (1,)), ((), ())), preferred_element_type=jnp.float32)


def plain_dot(left, right):
    return lax.dot_general(left, right, (((1,), (0,)), ((), ())), preferred_element_type=jnp.float32)


def attend_block(length, start, size, q_heads, k_ref, v_turned, o_ref, lse_ref):
    slots = k_ref.shape[0]
    half = slots // 2
    keys = k_ref[...]
    key_index = lax.broadcasted_iota(jnp.int32, (slots - half, size), 0) + half
    scores, tops = [], []
    for head in range(2):
        q = q_heads[head, pl.ds(start, size), :]
        low = last_dot(keys[:half], q)
        high = jnp.where(key_index < length, last_dot(keys[half:], q), -1000000000.0)
        tops.append(jnp.maximum(jnp.max(low, axis=0, keepdims=True), jnp.max(high, axis=0, keepdims=True)))
        scores.append((low, high))
    raised = [[jnp.exp(s - tops[head]).astype(jnp.bfloat16) for s in scores[head]] for head in range(2)]
    parts = []
    for head in range(2):
        summed = plain_dot(v_turned[head][:, :half], raised[head][0])
        summed = summed + plain_dot(v_turned[head][:, half:], raised[head][1])
        mine = summed[head * HEAD : (head + 1) * HEAD]
        total = summed[(1 - head) * HEAD : (1 - head) * HEAD + 1]
        parts.append(mine * (1.0 / total))
        lse_ref[head, pl.ds(start, size)] = (tops[head] + jnp.log(total))[0]
    o_ref[pl.ds(start, size), :] = jnp.concatenate(parts, axis=0).T.astype(jnp.bfloat16)


def attend_prepare(q_ref, v_ref, q_heads, v_turned):
    slots = q_ref.shape[0]
    lane = lax.broadcasted_iota(jnp.int32, (slots, PAIR), 1)
    row = lax.broadcasted_iota(jnp.int32, (PAIR, slots), 0)
    q = q_ref[...].astype(jnp.float32) * (HEAD ** (-0.5))
    v = v_ref[...].astype(jnp.float32).T
    for head in range(2):
        q_heads[head] = jnp.where(lane // HEAD == head, q, 0.0).astype(jnp.bfloat16)
        v_turned[head] = jnp.where(row // HEAD == head, v, 1.0).astype(jnp.bfloat16)


def attend_kernel(size, count_ref, q_ref, k_ref, v_ref, o_ref, lse_ref, q_heads, v_turned):
    attend_prepare(q_ref, v_ref, q_heads, v_turned)
    length = count_ref[0]

    def step(n, carry):
        attend_block(length, pl.multiple_of(n * size, size), size, q_heads, k_ref, v_turned, o_ref, lse_ref.at[0])
        return carry

    lax.fori_loop(0, q_ref.shape[0] // size, step, 0)


def attend(counts, projected, size=256):
    slots, width = projected.shape
    d = width // 3
    pairs = d // PAIR
    spec = lambda part: pl.BlockSpec((slots, PAIR), lambda p, n, part=part: (0, part * pairs + p))
    return pl.pallas_call(
        partial(attend_kernel, size),
        out_shape=[jax.ShapeDtypeStruct((slots, d), jnp.bfloat16),
                   jax.ShapeDtypeStruct((pairs, 2, slots), jnp.float32)],
        grid_spec=pltpu.PrefetchScalarGridSpec(
            num_scalar_prefetch=1, grid=(pairs,),
            in_specs=[spec(0), spec(1), spec(2)],
            out_specs=[pl.BlockSpec((slots, PAIR), lambda p, n: (0, p)),
                       pl.BlockSpec((1, 2, slots), lambda p, n: (p, 0, 0))],
            scratch_shapes=[pltpu.VMEM((2, slots, PAIR), jnp.bfloat16), pltpu.VMEM((2, PAIR, slots), jnp.bfloat16)]),
        compiler_params=pltpu.CompilerParams(vmem_limit_bytes=48 * 1024 * 1024),
        name="attend",
    )(counts, projected, projected, projected)


def attend_back_scratch(slots):
    return [pltpu.VMEM((2, slots, PAIR), jnp.bfloat16), pltpu.VMEM((2, slots, PAIR), jnp.bfloat16),
            pltpu.VMEM((2, PAIR, slots), jnp.bfloat16), pltpu.VMEM((2, slots), jnp.float32),
            pltpu.VMEM((slots, PAIR), jnp.float32), pltpu.VMEM((slots, PAIR), jnp.float32)]


def attend_back_body(size, count_ref, q_ref, k_ref, v_ref, o_ref, do_ref, lse_ref, out_ref,
                     q_heads, do_heads, k_turned, inner, dk_sum, dv_sum, hook):
    slots = q_ref.shape[0]
    length = count_ref[0]
    lane = lax.broadcasted_iota(jnp.int32, (slots, PAIR), 1)
    row = lax.broadcasted_iota(jnp.int32, (PAIR, slots), 0)
    q = q_ref[...].astype(jnp.float32) * (HEAD ** (-0.5))
    do = do_ref[...].astype(jnp.float32)
    k = k_ref[...].astype(jnp.float32).T * (HEAD ** (-0.5))
    product = (do * o_ref[...].astype(jnp.float32)).T
    for head in range(2):
        q_heads[head] = jnp.where(lane // HEAD == head, q, 0.0).astype(jnp.bfloat16)
        do_heads[head] = jnp.where(lane // HEAD == head, do, 0.0).astype(jnp.bfloat16)
        k_turned[head] = jnp.where(row // HEAD == head, k, 0.0).astype(jnp.bfloat16)
        inner[head] = jnp.sum(product[head * HEAD : (head + 1) * HEAD], axis=0)
    dk_sum[...] = jnp.zeros_like(dk_sum)
    dv_sum[...] = jnp.zeros_like(dv_sum)
    key_index = lax.broadcasted_iota(jnp.int32, (slots, size), 0)

    def step(n, carry):
        rows = pl.ds(n * size, size)
        keys, values = k_ref[...], v_ref[...]
        dq = jnp.zeros((PAIR, size), jnp.float32)
        for head in range(2):
            q_block, do_block = q_heads[head, rows, :], do_heads[head, rows, :]
            scores = last_dot(keys, q_block)
            weights = jnp.exp(scores - lse_ref[0, head, rows][None, :])
            weights = jnp.where(key_index < length, weights, 0.0)
            weight_grad = last_dot(values, do_block)
            score_grad = (weights * (weight_grad - inner[head, rows][None, :])).astype(jnp.bfloat16)
            dv_sum[...] += plain_dot(weights.astype(jnp.bfloat16), do_block)
            dk_sum[...] += plain_dot(score_grad, q_block)
            dq = dq + plain_dot(k_turned[head], score_grad)
        out_ref[0, rows, :] = dq.T.astype(jnp.bfloat16)
        return carry

    for n in range(slots // size):
        hook(n)
        step(n, 0)
    out_ref[1] = dk_sum[...].astype(jnp.bfloat16)
    out_ref[2] = dv_sum[...].astype(jnp.bfloat16)


def project_attend(n_dp, n_fsdp, counts, tokens, weight_pieces, small_rows, pieces, fresh, orders, plan, collective_id,
                   size=512, block=256):
    slots, d = tokens.shape
    width = weight_pieces.shape[0] * weight_pieces.shape[2]
    pairs = d // PAIR
    head = slots // block
    grid = Grid(n_dp, n_fsdp)
    begun, count = len(pieces), len(pieces) + len(fresh)
    jobs = plan["jobs"]
    waits = [job[0] < begun for job in jobs]
    shapes = [jax.ShapeDtypeStruct(p.shape, p.dtype) for p in pieces]
    shapes += [jax.ShapeDtypeStruct(grid.shape(o, *a.shape), jnp.bfloat16) for a, o in zip(fresh, orders[begun:])]

    def kernel(count_ref, x, w_pieces, rows, *refs):
        (h_ref, p_ref, w_ref, o_ref, lse_ref), outs = refs[count : count + 5], refs[count + 5 : 2 * count + 5]
        projected, q_heads, v_turned = refs[2 * count + 5 : 2 * count + 8]
        low_fresh = refs[2 * count + 8 : 2 * count + 8 + len(fresh)]
        g = grid.here()
        work = gather_jobs(g, orders, jobs, outs[:begun] + low_fresh, outs, refs[2 * count + 8 + len(fresh) :])
        step = pl.program_id(0)

        def run(when):
            for j, number in plan.get(when, []):
                if number == 1 and waits[j]:
                    work[j].resume()
                else:
                    work[j].step(number)

        @pl.when(step == 0)
        def _():
            def first():
                for ref, master in zip(low_fresh, refs[begun:count]):
                    ref[...] = master[...].astype(jnp.bfloat16)

            g.barrier(first)

        for when in range(head + pairs):
            if when in plan:
                pl.when(step == when)(partial(run, when))

        @pl.when(step == 0)
        def _():
            part = w_pieces.shape[2]
            for n in range(w_pieces.shape[0]):
                w_ref[:, n * part : (n + 1) * part] = w_pieces[n]

        @pl.when(step < head)
        def _():
            unit, spread = centered(x[...].astype(jnp.float32))
            low = (unit * rows[0:1] + rows[1:2]).astype(jnp.bfloat16)
            h_ref[...] = low
            bias = jnp.concatenate([rows[4:5], jnp.zeros((1, d), jnp.float32), rows[5:6]], axis=1)
            result = (plain_dot(low, w_ref[...]) + bias).astype(jnp.bfloat16)
            p_ref[...] = result
            projected[pl.ds(pl.multiple_of(step * block, block), block), :] = result

        @pl.when(step >= head)
        def _():
            lane = pl.multiple_of((step - head) * PAIR, PAIR)
            q_ref, k_ref, v_ref = (projected.at[:, pl.ds(lane + part * d, PAIR)] for part in range(3))
            attend_prepare(q_ref, v_ref, q_heads, v_turned)
            length = count_ref[0]
            for n in range(slots // size):
                attend_block(length, n * size, size, q_heads, k_ref, v_turned, o_ref, lse_ref.at[0])

        @pl.when(step == head + pairs - 1)
        def _():
            run("end")
            for j, job in enumerate(work):
                job.finish(1 if waits[j] else 0)

    low = jnp.bfloat16
    row_at = lambda s: jnp.minimum(s, head - 1)
    pair_at = lambda s: jnp.maximum(s - head, 0)
    row = lambda w: pl.BlockSpec((block, w), lambda s, n: (row_at(s), 0))
    whole = lambda array: pl.BlockSpec(array.shape, lambda s, n: (0,) * array.ndim, pipeline_mode=pl.Buffered(1))
    return pl.pallas_call(
        kernel,
        out_shape=[jax.ShapeDtypeStruct((slots, d), low), jax.ShapeDtypeStruct((slots, width), low),
                   jax.ShapeDtypeStruct((d, width), low), jax.ShapeDtypeStruct((slots, d), low),
                   jax.ShapeDtypeStruct((pairs, 2, slots), jnp.float32)] + shapes,
        grid_spec=pltpu.PrefetchScalarGridSpec(
            num_scalar_prefetch=1, grid=(head + pairs,),
            in_specs=[row(d), whole(weight_pieces), whole(small_rows)] + [ANY] * begun + [whole(a) for a in fresh],
            out_specs=[row(d), row(width), pl.BlockSpec((d, width), lambda s, n: (0, 0)),
                       pl.BlockSpec((slots, PAIR), lambda s, n: (0, pair_at(s))),
                       pl.BlockSpec((1, 2, slots), lambda s, n: (pair_at(s), 0, 0))] + [ANY] * count,
            scratch_shapes=[pltpu.VMEM((slots, width), low), pltpu.VMEM((2, slots, PAIR), low),
                            pltpu.VMEM((2, PAIR, slots), low)] + [pltpu.VMEM(a.shape, low) for a in fresh]
            + gather_scratch(grid, len(jobs))),
        input_output_aliases={4 + n: 5 + n for n in range(begun)},
        compiler_params=pltpu.CompilerParams(vmem_limit_bytes=56 * 1024 * 1024, collective_id=collective_id,
                                             has_side_effects=True),
        name="project_attend",
    )(counts, tokens, weight_pieces, small_rows, *pieces, *fresh)


FIRST_PLAN = (
    [(0, 0, pl.ds(0, 32)), (0, 0, pl.ds(32, 32)), (0, 0, pl.ds(64, 32)), (1, 0, pl.ds(0, 96)), (2, 0, pl.ds(0, 64)),
     (2, 1, pl.ds(64, 32))],
    [(1, 0), (0, 1), (2, 0), (1, 1), (0, 2), (2, 1), (3, 0), (4, 0), (5, 0), (1, 2), (0, 3), (2, 2), (1, 3), (2, 3)],
    3,
)
FORWARD_PLAN = {
    "jobs": [(0, 0, pl.ds(0, 96)), (1, 0, pl.ds(0, 64)), (1, 1, pl.ds(64, 32)), (2, 0, pl.ds(0, 192))],
    0: [(0, 1), (1, 1), (3, 0), (2, 1)],
    3: [(0, 2)],
    5: [(1, 2), (0, 3), (2, 2)],
    7: [(3, 1)],
    "end": [(1, 3), (3, 2), (2, 3), (3, 3)],
}


def cut_block(grad, turned_blocks, out, rows):
    for z, x, y, c in places():
        row, column = piece_rows(turned_blocks, z, x, y, c)
        out[y, c, z, x, rows, :] = grad[row : row + 48, column : column + 384]


def grads_attend_back(n_dp, n_fsdp, counts, projected, attended, attended_grad, lse, cotangent, active, normed, hidden_grad,
                      branch_grad, plan, collective_id, size=256):
    slots, width = projected.shape
    d = width // 3
    pairs = d // PAIR
    panels = active.shape[1] // d
    head = 2 * panels + 1
    grid = Grid(n_dp, n_fsdp)
    sizes = [(panels * 48, 384), (panels * 48, 384), (48, 384)]
    jobs = plan["jobs"]
    steps = slots // size

    def kernel(count_ref, q_ref, k_ref, v_ref, o_ref, do_ref, lse_ref, dy, z, h2, du, o_all, db, out_ref, *refs):
        outs, sums, parts, left = refs[:3], refs[3:5], refs[5:8], refs[8]
        own, scratch = refs[9:15], refs[15:]
        g = grid.here()
        work = scatter_jobs(g, ["j"] * 3, jobs, parts, scratch)
        step = pl.program_id(0)

        def run(when):
            for j, number in plan.get(when, []):
                work[j].step(number)

        @pl.when(step == 0)
        def _():
            g.barrier()

        def turn(ref):
            left[...] = ref[...].astype(jnp.float32).T.astype(jnp.bfloat16)

        for first, ref in ((0, dy), (panels, h2), (2 * panels, o_all)):
            pl.when(step == first)(partial(turn, ref))

        def blocks(part, first, right, kind):
            @pl.when((step >= first) & (step < first + (1 if part == 2 else panels)))
            def _():
                values = right[...]
                grad = plain_dot(left[...], values).astype(jnp.bfloat16)
                at = 0 if part == 2 else pl.multiple_of((step - first) * 48, 16)
                cut_block(grad, kind, parts[part], pl.ds(at, 48))
                if part > 0:
                    sums[part - 1][...] = jnp.sum(values.astype(jnp.float32), axis=0).reshape(1, 1, d)

        for when in range(head):
            if (when, 0) in plan:
                pl.when(step == when)(partial(run, (when, 0)))
        blocks(0, 0, z, True)
        blocks(1, panels, du, False)
        blocks(2, 2 * panels, db, False)

        def hook(n):
            for p in range(head, head + pairs):
                if (p, n) in plan:
                    pl.when(step == p)(partial(run, (p, n)))

        @pl.when(step >= head)
        def _():
            attend_back_body(size, count_ref, q_ref, k_ref, v_ref, o_ref, do_ref, lse_ref, out_ref, *own, hook)

        @pl.when(step == head + pairs - 1)
        def _():
            run("end")
            for job, (n, path, rows) in zip(work, jobs):
                outs[n][rows, :] = job.total().astype(jnp.bfloat16)
            for job in work:
                job.finish()

    pair_at = lambda s: jnp.maximum(s - head, 0)
    spec = lambda part: pl.BlockSpec((slots, PAIR), lambda s, n, part=part: (0, part * pairs + pair_at(s)))
    once = pl.BlockSpec((slots, d), lambda s, n: (0, 0), pipeline_mode=pl.Buffered(1))
    panel = lambda first: pl.BlockSpec((slots, d), lambda s, n: (0, jnp.clip(s - first, 0, panels - 1)))
    low, wide = jnp.bfloat16, jnp.float32
    return pl.pallas_call(
        kernel,
        out_shape=[jax.ShapeDtypeStruct((3, slots, d), low)]
        + [jax.ShapeDtypeStruct(s, low) for s in sizes]
        + [jax.ShapeDtypeStruct((panels, 1, d), wide), jax.ShapeDtypeStruct((1, 1, d), wide)],
        grid_spec=pltpu.PrefetchScalarGridSpec(
            num_scalar_prefetch=1, grid=(head + pairs,),
            in_specs=[spec(0), spec(1), spec(2), spec(0), spec(0),
                      pl.BlockSpec((1, 2, slots), lambda s, n: (pair_at(s), 0, 0)),
                      once, panel(0), once, panel(panels), once, once],
            out_specs=[pl.BlockSpec((3, slots, PAIR), lambda s, n: (0, 0, pair_at(s)))] + [VM] * 3
            + [pl.BlockSpec((1, 1, d), lambda s, n: (jnp.clip(s - panels, 0, panels - 1), 0, 0)),
               pl.BlockSpec((1, 1, d), lambda s, n: (0, 0, 0))],
            scratch_shapes=[pltpu.VMEM(grid.shape("j", *s), low) for s in sizes] + [pltpu.VMEM((d, slots), low)]
            + attend_back_scratch(slots) + scatter_scratch(grid, sizes, jobs)),
        compiler_params=pltpu.CompilerParams(vmem_limit_bytes=62 * 1024 * 1024, collective_id=collective_id,
                                             has_side_effects=True),
        name="grads_attend_back",
    )(counts, projected, projected, projected, attended, attended_grad, lse, cotangent, active, normed, hidden_grad,
      attended, branch_grad)


BACKWARD_PLAN = {
    "jobs": [(n, 0, pl.ds(at, 96)) for n in range(2) for at in (0, 96)] + [(2, 0, pl.ds(0, 48))],
    (2, 0): [(0, 0)],
    (4, 0): [(1, 0)],
    (5, 0): [(0, 1)],
    (7, 0): [(1, 1), (2, 0)],
    (8, 0): [(3, 0), (0, 2)],
    (9, 0): [(4, 0), (2, 1)],
    (10, 0): [(1, 2), (0, 3), (3, 1)],
    (11, 0): [(2, 2), (1, 3), (4, 1)],
    (12, 0): [(3, 2), (2, 3)],
    (13, 0): [(4, 2), (3, 3)],
    (14, 0): [(4, 3)],
}


PIECE = (48, 384)


class Spread:
    def __init__(self, g, u, tiles, send, recv, base):
        qkv, out, up, down = tiles
        me = g.y * 2 + g.c
        rows = pl.ds(pl.multiple_of(g.y * 48, 16), 48)
        self.g, self.u, self.tiles, self.rows, self.me = g, u, tiles, rows, me
        self.copies = []

        def copy(src, dst, device):
            self.copies.append(remote(src, dst, send, recv, base + len(self.copies), device))

        for k in range(1, 4):
            to = (me + k) % 4
            device = {"dp": g.z * 2 + g.x, "fsdp": to}
            block, half = self.qkv_place(to)
            copy(u.at[block], qkv.at[half, rows, :], device)
            copy(u.at[3], out.at[g.c, rows, :], device)
            copy(u.at[4 + to], up.at[g.c, rows, :], device)
        for k in range(1, 4):
            to = (g.z + k) % 4
            copy(u.at[8 + to], down.at[pl.ds(pl.multiple_of(g.z * 48, 16), 48), :], {"dp": to * 2 + g.x, "fsdp": me})

    def qkv_place(self, to):
        c = self.g.c
        middle = (to + 1) // 2 % 2
        return to - to // 3 - middle * c, middle + c - 2 * middle * c

    def start(self):
        start_all(self.copies)
        g, u = self.g, self.u
        qkv, out, up, down = self.tiles
        block, half = self.qkv_place(self.me)
        qkv[half, self.rows, :] = u[block]
        out[g.c, self.rows, :] = u[3]
        up[g.c, self.rows, :] = u[4 + self.me]
        down[pl.ds(pl.multiple_of(g.z * 48, 16), 48), :] = u[8 + g.z]

    def finish(self):
        arrived(self.copies)
        sent(self.copies)


TILES = [jax.ShapeDtypeStruct((2, 96, 384), jnp.bfloat16)] * 3 + [jax.ShapeDtypeStruct((192, 384), jnp.bfloat16)]


def meet_all(g, n_dp, n_fsdp, between):
    count = n_dp * n_fsdp
    me = (g.z * g.X + g.x) * n_fsdp + g.y * 2 + g.c
    sem = pltpu.get_barrier_semaphore()
    ranks = [(me + k) % count for k in range(1, count)]
    peers = [{"dp": rank // n_fsdp, "fsdp": rank % n_fsdp} for rank in ranks]
    for peer in peers:
        pl.semaphore_signal(sem, inc=1, device_id=peer, device_id_type=MESH)
    between(me)
    pl.semaphore_wait(sem, count - 1)
    return me, ranks, peers


def piece_rows(turned, z, x, y, c):
    if turned:
        return 192 * (2 * y + c) + 48 * z, 384 * x
    return 96 * (2 * z + x) + 48 * y, 384 * c


def places():
    return [(z, x, y, c) for z in range(4) for x in range(2) for y in range(2) for c in range(2)]


def tile_values(g, tiles):
    qkv, out, up, down = tiles
    odd = (g.y * 2 + g.c) % 2 == 1
    wide = jnp.float32
    band = jnp.concatenate([qkv[0].astype(wide), qkv[1].astype(wide)], axis=1)
    half = out[g.y].astype(wide)
    return [jnp.where(odd, band[:, 192:], band[:, :576]), jnp.where(odd, half[:, 192:], half[:, :192]),
            jnp.concatenate([up[0].astype(wide), up[1].astype(wide)], axis=1), down[...].astype(wide)]


def owner_exchange(n_dp, n_fsdp, owners, mine, small, roots, collective_id):
    grid = Grid(n_dp, n_fsdp)
    count = n_dp * n_fsdp
    n_blocks = owners.shape[0]
    d = roots.shape[1]
    spread_lanes = 12

    def kernel(owners_ref, qkv_ref, out_ref, up_ref, down_ref, small_ref, roots_hbm,
               qkv, out, up, down, s_qkv, s_out, s_up, s_down, all_small, block, turned,
               u, slots, got, got_steps, u_steps, roots, local, send, recv):
        g = grid.here()
        load = pltpu.make_async_copy(roots_hbm, roots, local.at[0])

        def owned(n):
            found = 0
            for b in range(n_blocks):
                found = jnp.where(owners_ref[b] == n, b, found)
            return found

        def first(me):
            load.start()
            at = 0
            for ref in (qkv_ref, out_ref, up_ref, down_ref):
                part = ref.shape[0] // 48
                u[at : at + part] = ref[...].reshape(part, 48, 384)
                at += part

            def fill(n, carry):
                slots[n] = u[owned(n)]
                return carry

            lax.fori_loop(0, count, fill, 0)
            got[me] = slots[me]
            all_small[me] = small_ref[...]

        me, ranks, peers = meet_all(g, n_dp, n_fsdp, first)
        lane = 0
        copies, small_copies, step_copies = [], [], []
        for rank, peer in zip(ranks, peers):
            copies.append(remote(slots.at[rank], got.at[me], send, recv, lane, peer))
            small_copies.append(remote(small_ref, all_small.at[me], send, recv, lane + 1, peer))
            step_copies.append(remote(slots.at[rank], got_steps.at[me], send, recv, lane + 2, peer))
            lane += 3
        start_all(copies)
        load.wait()
        kind = jnp.where(owned(me) >= 8, 1, 0)
        arrived(copies)
        sent(copies)
        spread = Spread(g, u, (qkv, out, up, down), send, recv, lane)
        spread.start()
        start_all(small_copies)
        for turn in range(2):
            for n, place in enumerate(places()):
                row, column = piece_rows(turn, *place)
                (turned if turn else block)[row : row + 48, column : column + 384] = got[n]
        block[...] = jnp.where(kind == 1, turned[...], block[...])
        left = plain_dot(roots[kind].astype(jnp.bfloat16), block[...]).astype(jnp.bfloat16)
        step = plain_dot(left, roots[1 - kind].astype(jnp.bfloat16)).astype(jnp.bfloat16)
        for n, place in enumerate(places()):
            row, column = piece_rows(0, *place)
            other_row, other_column = piece_rows(1, *place)
            slots[n] = jnp.where(kind == 1, step[other_row : other_row + 48, other_column : other_column + 384],
                                 step[row : row + 48, column : column + 384])
        start_all(step_copies)
        got_steps[me] = slots[me]
        wide = block[...].astype(jnp.float32)
        wide_turned = wide.T
        block[...] = jnp.where(kind == 1, wide_turned, wide).astype(jnp.bfloat16)
        turned[...] = jnp.where(kind == 1, wide, wide_turned).astype(jnp.bfloat16)
        spread.finish()
        arrived(small_copies)
        arrived(step_copies)

        def pick(n, carry):
            u_steps[n] = got_steps[owners_ref[n]]
            return carry

        lax.fori_loop(0, n_blocks, pick, 0)
        back = Spread(g, u_steps, (s_qkv, s_out, s_up, s_down), send, recv, lane + spread_lanes)
        back.start()
        sent(small_copies + step_copies)
        back.finish()

    lanes = 3 * (count - 1) + 2 * spread_lanes
    low = jnp.bfloat16
    pieces = pltpu.VMEM((count,) + PIECE, low)
    return pl.pallas_call(
        kernel,
        out_shape=TILES + TILES + [jax.ShapeDtypeStruct((count,) + small.shape, low), jax.ShapeDtypeStruct((d, d), low),
                                   jax.ShapeDtypeStruct((d, d), low)],
        in_specs=[pl.BlockSpec(memory_space=pltpu.SMEM)] + [VM] * 5 + [ANY],
        out_specs=[VM] * 11,
        scratch_shapes=[pltpu.VMEM((n_blocks,) + PIECE, low), pieces, pieces, pieces, pltpu.VMEM((n_blocks,) + PIECE, low),
                        pltpu.VMEM(roots.shape, jnp.float32), pltpu.SemaphoreType.DMA((1,)),
                        pltpu.SemaphoreType.DMA((lanes,)), pltpu.SemaphoreType.DMA((lanes,))],
        compiler_params=pltpu.CompilerParams(collective_id=collective_id, has_side_effects=True,
                                             vmem_limit_bytes=56 * 1024 * 1024),
        name="owner_exchange",
    )(owners, *mine, small, roots)


def finish_step(n_dp, n_fsdp, owners, exchanged, masters, small_params, stats, rates, parts=2):
    grid = Grid(n_dp, n_fsdp)
    tiles, all_small, block, turned = exchanged[:8], *exchanged[8:]
    d = block.shape[0]
    rows = d // parts

    def kernel(owners_ref, qkv, out, up, down, s_qkv, s_out, s_up, s_down, all_small, block, turned,
               w_qkv, w_out, w_up, w_down, params, stats_ref,
               g_qkv, g_out, g_up, g_down, n_qkv, n_out, n_up, n_down, g_small, n_small, new_stats):
        g = grid.here()
        step = pl.program_id(0)
        me = (g.z * g.X + g.x) * n_fsdp + g.y * 2 + g.c
        own = owners_ref[0] == me
        for n in range(1, owners.shape[0]):
            own = own | (owners_ref[n] == me)

        @pl.when(step == 0)
        def _():
            values = tile_values(g, (qkv, out, up, down))
            for ref, value in zip((g_qkv, g_out, g_up, g_down), values):
                ref[...] = value
            steps = tile_values(g, (s_qkv, s_out, s_up, s_down))
            for ref, master, value in zip((n_qkv, n_out, n_up, n_down), (w_qkv, w_out, w_up, w_down), steps):
                ref[...] = master[...] - rates[0] * value
            lines = params.shape[0]
            total = jnp.concatenate([all_small[n].astype(jnp.float32) for n in range(-(-lines // 16))], axis=0)[:lines]
            g_small[...] = total
            mean = jnp.sum(total * total) * (1.0 / (lines * 128))
            n_small[...] = params[...] - rates[1] * total * lax.rsqrt(jnp.full((1, 128), mean + 1e-06, jnp.float32))

        @pl.when(own)
        def _():
            at = pl.ds(pl.multiple_of(step * rows, rows), rows)
            new_stats[0] = 0.5 * stats_ref[0] + 0.5 * last_dot(block[at, :], block[...])
            new_stats[1] = 0.5 * stats_ref[1] + 0.5 * last_dot(turned[at, :], turned[...])

        @pl.when(jnp.logical_not(own))
        def _():
            new_stats[...] = stats_ref[...]

    whole = lambda a: pl.BlockSpec(a.shape, lambda s, n: (0,) * len(a.shape))
    banded = pl.BlockSpec((2, rows, d), lambda s, n: (0, s, 0))
    results = [jax.ShapeDtypeStruct(a.shape, jnp.float32) for a in (*masters, *masters, small_params, small_params)]
    return pl.pallas_call(
        kernel,
        out_shape=results + [jax.ShapeDtypeStruct(stats.shape, jnp.float32)],
        grid_spec=pltpu.PrefetchScalarGridSpec(
            num_scalar_prefetch=1, grid=(parts,),
            in_specs=[whole(a) for a in (*exchanged, *masters, small_params)] + [banded],
            out_specs=[whole(a) for a in results] + [banded]),
        compiler_params=pltpu.CompilerParams(vmem_limit_bytes=56 * 1024 * 1024),
        name="finish_step",
    )(owners, *exchanged, *masters, small_params, stats)


def centered(values):
    center = values - jnp.mean(values, axis=-1, keepdims=True)
    spread = lax.rsqrt(jnp.mean(center * center, axis=-1, keepdims=True) + 1e-06)
    return center * spread, spread


def norm_back(grads, unit, spread, gain):
    scaled = grads * gain
    mean = jnp.mean(scaled, axis=-1, keepdims=True)
    along = jnp.mean(scaled * unit, axis=-1, keepdims=True)
    return (scaled - mean - unit * along) * spread


def middle_kernel(x, attended, dy, out_pieces, up_w, down_w, rows,
                  layer, h2, active, hidden_grad, middle_grad, branch_grad, attended_grad, sums, out_w):
    @pl.when(pl.program_id(0) == 0)
    def _():
        part = out_pieces.shape[2]
        for n in range(out_pieces.shape[0]):
            out_w[:, n * part : (n + 1) * part] = out_pieces[n]

    gain, shift, bias_out, bias_down = rows[2:3], rows[3:4], rows[6:7], rows[7:8]
    middle = x[...].astype(jnp.float32) + (plain_dot(attended[...], out_w[...]) + bias_out)
    unit, spread = centered(middle)
    normed = (unit * gain + shift).astype(jnp.bfloat16)
    h2[...] = normed
    grad_rows = dy[...]
    panels = up_w.shape[0]
    width = up_w.shape[2]
    half = width // 2
    y = jnp.zeros_like(middle)
    dh = jnp.zeros_like(middle)
    for panel in range(panels):
        hidden = plain_dot(normed, up_w[panel]) + rows[8 + panel : 9 + panel]
        passed = 0.5 + 0.5 * lax.erf(hidden * (0.5**0.5))
        z = (hidden * passed).astype(jnp.bfloat16)
        slope = passed + hidden * (jnp.exp(-0.5 * hidden * hidden) * 0.3989422804014327)
        back = jnp.concatenate([plain_dot(grad_rows, down_w[2 * panel]), plain_dot(grad_rows, down_w[2 * panel + 1])], axis=1)
        du = (slope * back).astype(jnp.bfloat16)
        active[:, panel * width : (panel + 1) * width] = z
        hidden_grad[:, panel * width : (panel + 1) * width] = du
        y = y + last_dot(z[:, :half], down_w[2 * panel]) + last_dot(z[:, half:], down_w[2 * panel + 1])
        dh = dh + last_dot(du, up_w[panel])
    layer[...] = (middle + y + bias_down).astype(jnp.bfloat16)
    wide = grad_rows.astype(jnp.float32)
    total = wide + norm_back(dh, unit, spread, gain)
    low = total.astype(jnp.bfloat16)
    middle_grad[...] = total
    branch_grad[...] = low
    attended_grad[...] = last_dot(low, out_w[...]).astype(jnp.bfloat16)

    @pl.when(pl.program_id(0) == 0)
    def _():
        sums[...] = jnp.zeros_like(sums)

    sums[0:1] += jnp.sum(dh * unit, axis=0, keepdims=True)
    sums[1:2] += jnp.sum(dh, axis=0, keepdims=True)
    sums[2:3] += jnp.sum(wide, axis=0, keepdims=True)


def middle_layer(tokens, attended, cotangent, out_w, up_w, down_w, rows, block=256):
    count, d = tokens.shape
    ff = up_w.shape[0] * up_w.shape[2]
    row = lambda width: pl.BlockSpec((block, width), lambda r: (r, 0))
    whole = lambda array: pl.BlockSpec(array.shape, lambda r: (0,) * array.ndim)
    low, wide = jnp.bfloat16, jnp.float32
    shape = jax.ShapeDtypeStruct
    return pl.pallas_call(
        middle_kernel,
        out_shape=[shape((count, d), low), shape((count, d), low), shape((count, ff), low), shape((count, ff), low),
                   shape((count, d), wide), shape((count, d), low), shape((count, d), low), shape((8, d), wide)],
        grid=(count // block,),
        in_specs=[row(d), row(d), row(d)] + [whole(a) for a in (out_w, up_w, down_w, rows)],
        out_specs=[row(d), row(d), row(ff), row(ff), row(d), row(d), row(d), pl.BlockSpec((8, d), lambda r: (0, 0))],
        scratch_shapes=[pltpu.VMEM((d, d), low)],
        compiler_params=pltpu.CompilerParams(vmem_limit_bytes=60 * 1024 * 1024),
        name="middle_layer",
    )(tokens, attended, cotangent, out_w, up_w, down_w, rows)


def project_back(n_dp, n_fsdp, tokens, normed, projected_grad, weight, middle_grad, gain, sums, bias_out, bias_up, plan,
                 collective_id, block=256):
    grid = Grid(n_dp, n_fsdp)
    count, d = tokens.shape
    n_blocks = projected_grad.shape[0]
    lines = 8 + bias_up.shape[0]
    sizes = [(48, 384)] * n_blocks + [(16, 128)]
    jobs = plan["jobs"]
    low, wide = jnp.bfloat16, jnp.float32

    def kernel(x_h, normed_h, dp_h, weight_h, middle_h, gain_ref, sums_ref, bias_out_ref, bias_up_ref, mine, small, input_grad_h, *refs):
        x, h, dp, w, middle, out = refs[:6]
        left, parts, small_parts, rows, packed, local = refs[6:12]
        scratch = refs[12:]
        g = grid.here()
        loads = [pltpu.make_async_copy(a, b, local.at[n])
                 for n, (a, b) in enumerate(((normed_h, h), (dp_h, dp), (weight_h, w), (x_h, x), (middle_h, middle)))]

        def first():
            for load in loads:
                load.start()
            loads[0].wait()
            left[...] = h[...].astype(wide).T.astype(low)

        g.barrier(first)
        loads[1].wait()
        work = scatter_jobs(g, ["j"] * (n_blocks + 1), jobs, [parts.at[n] for n in range(n_blocks)] + [small_parts], scratch)
        for n in range(n_blocks):
            values = dp[n]
            grad = plain_dot(left[...], values).astype(low)
            for z, px, y, c in places():
                row, column = piece_rows(False, z, px, y, c)
                parts[n, y, c, z, px] = grad[row : row + 48, column : column + 384]
            for j, job in enumerate(jobs):
                if job[0] == n:
                    work[j].step(0)
        rows[2:4] = sums_ref[0:2]
        rows[6:7] = bias_out_ref[0]
        rows[7:8] = sums_ref[2:3]
        for n in range(lines - 8):
            rows[8 + n : 9 + n] = bias_up_ref[n]
        rows[4:5] = jnp.sum(dp[0].astype(wide), axis=0, keepdims=True)
        rows[5:6] = jnp.sum(dp[2].astype(wide), axis=0, keepdims=True)
        for load in loads[2:]:
            load.wait()

        def back(n):
            at = slice(n * block, (n + 1) * block)
            dh = last_dot(dp[0, at], w[:, :d]) + last_dot(dp[1, at], w[:, d : 2 * d]) + last_dot(dp[2, at], w[:, 2 * d :])
            unit, spread = centered(x[at].astype(wide))
            out[at] = (middle[at] + norm_back(dh, unit, spread, gain_ref[0:1])).astype(low)
            scaled, shifted = jnp.sum(dh * unit, axis=0, keepdims=True), jnp.sum(dh, axis=0, keepdims=True)
            rows[0:1] = scaled if n == 0 else rows[0:1] + scaled
            rows[1:2] = shifted if n == 0 else rows[1:2] + shifted

        for n in range(count // block):
            for j, step in plan.get(n, []):
                work[j].step(step)
            back(n)
        store = pltpu.make_async_copy(out, input_grad_h, local.at[0])
        store.start()
        packed[...] = jnp.zeros_like(packed)
        for line in range(lines):
            for part in range(d // 128):
                at = line * (d // 128) + part
                packed[at : at + 1] = rows[line : line + 1, part * 128 : (part + 1) * 128]
        small_parts[...] = jnp.zeros_like(small_parts)
        for n, (z, px, y, c) in enumerate(places()):
            if n < packed.shape[0] // 16:
                small_parts[y, c, z, px] = packed[16 * n : 16 * n + 16].astype(low)
        for j, step in plan["end"]:
            work[j].step(step)
        for job, (n, path, at) in zip(work, jobs):
            if n < n_blocks:
                mine[n, at, :] = job.total().astype(low)
            else:
                small[...] = job.total().astype(low)
        for job in work:
            job.finish()
        store.wait()

    shape = jax.ShapeDtypeStruct
    return pl.pallas_call(
        kernel,
        out_shape=[shape((n_blocks, 48, 384), low), shape((16, 128), low), shape((count, d), low)],
        in_specs=[ANY] * 5 + [VM] * 4,
        out_specs=[VM, VM, ANY],
        scratch_shapes=[pltpu.VMEM((count, d), low), pltpu.VMEM((count, d), low), pltpu.VMEM(projected_grad.shape, low),
                        pltpu.VMEM(weight.shape, low), pltpu.VMEM((count, d), wide), pltpu.VMEM((count, d), low),
                        pltpu.VMEM((d, count), low), pltpu.VMEM((n_blocks,) + grid.shape("j", 48, 384), low),
                        pltpu.VMEM(grid.shape("j", 16, 128), low), pltpu.VMEM((16, d), wide), pltpu.VMEM((80, 128), wide),
                        pltpu.SemaphoreType.DMA((5,))] + scatter_scratch(grid, sizes, jobs),
        compiler_params=pltpu.CompilerParams(vmem_limit_bytes=60 * 1024 * 1024, collective_id=collective_id,
                                             has_side_effects=True),
        name="project_back",
    )(tokens, normed, projected_grad, weight, middle_grad, gain, sums, bias_out, bias_up)


TAIL_PLAN = {
    "jobs": [(0, 0, pl.ds(0, 48)), (1, 0, pl.ds(0, 48)), (2, 0, pl.ds(0, 48)), (3, 0, pl.ds(0, 16))],
    0: [(0, 1)],
    1: [(1, 1), (0, 2)],
    2: [(2, 1)],
    3: [(1, 2), (0, 3)],
    "end": [(3, 0), (2, 2), (3, 1), (1, 3), (3, 2), (2, 3), (3, 3)],
}


D = 768
HEADS = 12
HD = 64
FF = 3072
BLOCKS = 12


masked_score = -1000000000.0
decay_rate = 0.5
step_rate = 1.0
small_rate = 0.3
highest = lax.Precision.HIGHEST


def broadcast(value, axis, source):
    kept = jnp.where(lax.axis_index(axis) == source, value, 0).astype(value.dtype)
    return lax.psum(kept, axis)


def layer_norm(values, scale_row, shift_row):
    center = values - jnp.mean(values, axis=-1, keepdims=True)
    spread = jnp.mean(center * center, axis=-1, keepdims=True)
    return center * lax.rsqrt(spread + 1e-06) * scale_row + shift_row


def unpack(small_params):
    pieces = [small_params[number * D : (number + 1) * D] for number in range(8)]
    return pieces + [small_params[8 * D : 8 * D + FF]]


def row_dot(left, right):
    return jnp.dot(left, right, preferred_element_type=jnp.float32)


def column_dot(left, right):
    return lax.dot_general(
        left, right, (((0,), (0,)), ((), ())), preferred_element_type=jnp.float32
    )


def transposed_dot(left, right):
    return lax.dot_general(
        left, right, (((1,), (1,)), ((), ())), preferred_element_type=jnp.float32
    )


def block_split(array, block_rows):
    slots = array.shape[-1]
    return array.reshape(HEADS, HD, slots // block_rows, block_rows).transpose(2, 0, 1, 3)


def block_join(array):
    return array.transpose(0, 3, 1, 2).reshape(-1, D)


def attend_clip(queries, key_rows, value_rows, length):
    slots = queries.shape[-1]
    block_rows = min(512, slots)
    score_scale = float(HD) ** (-0.5)
    visible = (jnp.arange(slots) < length)[None, None, :]

    def one_block(query_block):
        scores = (
            jnp.einsum("hdq,hdk->hqk", query_block, key_rows, preferred_element_type=jnp.float32)
            * score_scale
        )
        scores = jnp.where(visible, scores, masked_score)
        row_top = jnp.max(scores, axis=-1, keepdims=True)
        raised = jnp.exp(scores - row_top)
        row_total = jnp.sum(raised, axis=-1, keepdims=True)
        softmax_weights = (raised / row_total).astype(jnp.bfloat16)
        attended = jnp.einsum(
            "hqk,hdk->hdq", softmax_weights, value_rows, preferred_element_type=jnp.float32
        )
        return (attended.astype(jnp.bfloat16), (row_top + jnp.log(row_total))[:, :, 0])

    attended, log_totals = lax.map(one_block, block_split(queries, block_rows))
    return (block_join(attended), log_totals)


def attend_back(queries, key_rows, value_rows, length, log_totals, out_grads):
    slots = queries.shape[-1]
    block_rows = min(512, slots)
    score_scale = float(HD) ** (-0.5)
    visible = (jnp.arange(slots) < length)[None, None, :]

    def one_block(carry, pieces):
        key_grad, value_grad = carry
        query_block, grad_block, log_block = pieces
        scores = (
            jnp.einsum("hdq,hdk->hqk", query_block, key_rows, preferred_element_type=jnp.float32)
            * score_scale
        )
        scores = jnp.where(visible, scores, masked_score)
        softmax_weights = jnp.exp(scores - log_block[:, :, None])
        weight_grad = jnp.einsum(
            "hdq,hdk->hqk", grad_block, value_rows, preferred_element_type=jnp.float32
        )
        inner_sum = jnp.sum(softmax_weights * weight_grad, axis=-1, keepdims=True)
        score_grad = (softmax_weights * (weight_grad - inner_sum)).astype(jnp.bfloat16)
        query_grad = (
            jnp.einsum("hqk,hdk->hdq", score_grad, key_rows, preferred_element_type=jnp.float32)
            * score_scale
        )
        key_grad = (
            key_grad
            + jnp.einsum(
                "hqk,hdq->hdk", score_grad, query_block, preferred_element_type=jnp.float32
            )
            * score_scale
        )
        value_grad = value_grad + jnp.einsum(
            "hqk,hdq->hdk",
            softmax_weights.astype(jnp.bfloat16),
            grad_block,
            preferred_element_type=jnp.float32,
        )
        return ((key_grad, value_grad), query_grad)

    blank = jnp.zeros((HEADS, HD, slots), jnp.float32)
    (key_grad, value_grad), query_grad = lax.scan(
        one_block,
        (blank, blank),
        (block_split(queries, block_rows), block_split(out_grads, block_rows), log_totals),
    )
    key_rows_grad = key_grad.transpose(2, 0, 1).reshape(slots, D)
    value_rows_grad = value_grad.transpose(2, 0, 1).reshape(slots, D)
    return (block_join(query_grad), key_rows_grad, value_rows_grad)


def take_columns(operands, member, start):
    return lax.slice_in_dim(operands[member], start, start + D, axis=1)


def take_rows(operands, member, start):
    return lax.slice_in_dim(operands[member], start, start + D, axis=0)


def block_pickers():
    pickers = [partial(take_columns, member=0, start=column * D) for column in range(3)]
    pickers.append(partial(take_columns, member=1, start=0))
    pickers = pickers + [
        partial(take_columns, member=2, start=column * D) for column in range(FF // D)
    ]
    pickers = pickers + [
        partial(take_rows, member=3, start=column * D) for column in range(FF // D)
    ]
    return pickers


def fetch_update(update, root):
    return broadcast(update.astype(jnp.bfloat16), ("dp", "fsdp"), root).astype(update.dtype)


def band_tile(band, like, column_index):
    columns_here = like.shape[1]
    return lax.dynamic_slice_in_dim(band, column_index * columns_here, columns_here, 1)


def row_band(pieces, like, row_index):
    rows_here = like.shape[0]
    start = row_index * rows_here
    return jnp.concatenate(
        [lax.dynamic_slice_in_dim(piece, start, rows_here, 0) for piece in pieces], axis=1
    )


def stacked_band(pieces, like, row_index):
    rows_here = like.shape[0]
    start = row_index * rows_here
    owner_block = start // D
    picked = jnp.zeros((rows_here, D), jnp.float32)
    for number in range(len(pieces)):
        inside = jnp.clip(start - number * D, 0, D - rows_here)
        piece = lax.dynamic_slice_in_dim(pieces[number], inside, rows_here, 0)
        picked = jnp.where(owner_block == number, piece, picked)
    return picked


def local_any(
    tokens,
    counts,
    cotangent,
    qkv_weight,
    out_weight,
    up_weight,
    down_weight,
    small_params,
    statistics,
    inverse_roots,
    owners,
):
    clips_here = counts.shape[0]
    slots = tokens.shape[0] // clips_here
    qkv_low = qkv_weight.astype(jnp.bfloat16)
    out_low = out_weight.astype(jnp.bfloat16)
    up_low = up_weight.astype(jnp.bfloat16)
    down_low = down_weight.astype(jnp.bfloat16)
    qkv_cols, out_cols, up_cols, down_cols = (
        lax.all_gather(qkv_low, "fsdp", axis=1, tiled=True),
        lax.all_gather(out_low, "fsdp", axis=1, tiled=True),
        lax.all_gather(up_low, "fsdp", axis=1, tiled=True),
        lax.all_gather(down_low, "fsdp", axis=1, tiled=True),
    )
    qkv_full, out_full, up_full, down_full = (
        lax.all_gather(qkv_cols, "dp", axis=0, tiled=True),
        lax.all_gather(out_cols, "dp", axis=0, tiled=True),
        lax.all_gather(up_cols, "dp", axis=0, tiled=True),
        lax.all_gather(down_cols, "dp", axis=0, tiled=True),
    )
    (
        gain_one,
        shift_one,
        gain_two,
        shift_two,
        bias_query,
        bias_value,
        bias_out,
        bias_down,
        bias_up,
    ) = unpack(small_params)

    def heads_view(array):
        return array.reshape(clips_here, slots, HEADS, HD).transpose(0, 2, 3, 1)

    def clip_forward(clip_group):
        return attend_clip(clip_group[0], clip_group[1], clip_group[2], clip_group[3])

    def clip_backward(clip_group):
        return attend_back(
            clip_group[0], clip_group[1], clip_group[2], clip_group[3], clip_group[4], clip_group[5]
        )

    inputs = tokens.astype(jnp.float32)
    normed = layer_norm(inputs, gain_one, shift_one).astype(jnp.bfloat16)
    projected = row_dot(normed, qkv_full)
    queries = heads_view((projected[:, :D] + bias_query).astype(jnp.bfloat16))
    key_rows = heads_view(projected[:, D : 2 * D].astype(jnp.bfloat16))
    value_rows = heads_view((projected[:, 2 * D :] + bias_value).astype(jnp.bfloat16))
    attended, log_totals = lax.map(clip_forward, (queries, key_rows, value_rows, counts))
    attended = attended.reshape(-1, D)
    middle = inputs + (row_dot(attended, out_full) + bias_out)
    normed_two = layer_norm(middle, gain_two, shift_two).astype(jnp.bfloat16)
    hidden = row_dot(normed_two, up_full) + bias_up
    active = jax.nn.gelu(hidden, approximate=False).astype(jnp.bfloat16)
    layer_rows = (middle + row_dot(active, down_full) + bias_down).astype(jnp.bfloat16)
    qkv_part, out_part, up_part, down_part = (
        lax.all_gather(qkv_low, "fsdp", axis=1, tiled=True),
        lax.all_gather(out_low, "fsdp", axis=1, tiled=True),
        lax.all_gather(up_low, "fsdp", axis=1, tiled=True),
        lax.all_gather(down_low, "fsdp", axis=1, tiled=True),
    )
    qkv_back, out_back, up_back, down_back = (
        lax.all_gather(qkv_part, "dp", axis=0, tiled=True),
        lax.all_gather(out_part, "dp", axis=0, tiled=True),
        lax.all_gather(up_part, "dp", axis=0, tiled=True),
        lax.all_gather(down_part, "dp", axis=0, tiled=True),
    )
    grad_down = column_dot(active, cotangent)
    grad_bias_down = jnp.sum(cotangent.astype(jnp.float32), axis=0)
    active_grad = transposed_dot(cotangent, down_back)
    unused_value, gelu_pull = jax.vjp(partial(jax.nn.gelu, approximate=False), hidden)
    hidden_grad = gelu_pull(active_grad)[0].astype(jnp.bfloat16)
    grad_up = column_dot(normed_two, hidden_grad)
    grad_bias_up = jnp.sum(hidden_grad.astype(jnp.float32), axis=0)
    normed_two_grad = transposed_dot(hidden_grad, up_back)
    unused_norm, norm_two_pull = jax.vjp(layer_norm, middle, gain_two, shift_two)
    middle_grad, grad_gain_two, grad_shift_two = norm_two_pull(normed_two_grad)
    middle_grad = middle_grad + cotangent.astype(jnp.float32)
    branch_grad = middle_grad.astype(jnp.bfloat16)
    grad_out = column_dot(attended, branch_grad)
    grad_bias_out = jnp.sum(branch_grad.astype(jnp.float32), axis=0)
    attended_grad = transposed_dot(branch_grad, out_back).astype(jnp.bfloat16)
    query_grad, key_grad, value_grad = lax.map(
        clip_backward,
        (queries, key_rows, value_rows, counts, log_totals, heads_view(attended_grad)),
    )
    projected_grad = (
        jnp.concatenate([query_grad, key_grad, value_grad], axis=-1)
        .reshape(-1, 3 * D)
        .astype(jnp.bfloat16)
    )
    grad_qkv = column_dot(normed, projected_grad)
    grad_bias_query = jnp.sum(projected_grad[:, :D].astype(jnp.float32), axis=0)
    grad_bias_value = jnp.sum(projected_grad[:, 2 * D :].astype(jnp.float32), axis=0)
    normed_grad = transposed_dot(projected_grad, qkv_back)
    unused_first, norm_one_pull = jax.vjp(layer_norm, inputs, gain_one, shift_one)
    input_rows_grad, grad_gain_one, grad_shift_one = norm_one_pull(normed_grad)
    input_grad = (middle_grad + input_rows_grad).astype(jnp.bfloat16)
    small_grad = jnp.concatenate(
        [
            grad_gain_one,
            grad_shift_one,
            grad_gain_two,
            grad_shift_two,
            grad_bias_query,
            grad_bias_value,
            grad_bias_out,
            grad_bias_down,
            grad_bias_up,
        ]
    )
    row_qkv, row_out, row_up, row_down, row_small = (
        lax.psum_scatter(
            grad_qkv.astype(jnp.bfloat16), "dp", scatter_dimension=0, tiled=True
        ).astype(jnp.float32),
        lax.psum_scatter(
            grad_out.astype(jnp.bfloat16), "dp", scatter_dimension=0, tiled=True
        ).astype(jnp.float32),
        lax.psum_scatter(
            grad_up.astype(jnp.bfloat16), "dp", scatter_dimension=0, tiled=True
        ).astype(jnp.float32),
        lax.psum_scatter(
            grad_down.astype(jnp.bfloat16), "dp", scatter_dimension=0, tiled=True
        ).astype(jnp.float32),
        lax.psum_scatter(
            small_grad.astype(jnp.bfloat16), "dp", scatter_dimension=0, tiled=True
        ).astype(jnp.float32),
    )
    shard_qkv, shard_out, shard_up, shard_down, shard_small = (
        lax.psum_scatter(
            row_qkv.astype(jnp.bfloat16), "fsdp", scatter_dimension=1, tiled=True
        ).astype(jnp.float32),
        lax.psum_scatter(
            row_out.astype(jnp.bfloat16), "fsdp", scatter_dimension=1, tiled=True
        ).astype(jnp.float32),
        lax.psum_scatter(
            row_up.astype(jnp.bfloat16), "fsdp", scatter_dimension=1, tiled=True
        ).astype(jnp.float32),
        lax.psum_scatter(
            row_down.astype(jnp.bfloat16), "fsdp", scatter_dimension=1, tiled=True
        ).astype(jnp.float32),
        lax.psum_scatter(
            row_small.astype(jnp.bfloat16), "fsdp", scatter_dimension=0, tiled=True
        ).astype(jnp.float32),
    )
    band_qkv, band_out, band_up, band_down, band_small = (
        lax.all_gather(shard_qkv.astype(jnp.bfloat16), "fsdp", axis=1, tiled=True).astype(
            shard_qkv.dtype
        ),
        lax.all_gather(shard_out.astype(jnp.bfloat16), "fsdp", axis=1, tiled=True).astype(
            shard_out.dtype
        ),
        lax.all_gather(shard_up.astype(jnp.bfloat16), "fsdp", axis=1, tiled=True).astype(
            shard_up.dtype
        ),
        lax.all_gather(shard_down.astype(jnp.bfloat16), "fsdp", axis=1, tiled=True).astype(
            shard_down.dtype
        ),
        lax.all_gather(shard_small.astype(jnp.bfloat16), "fsdp", axis=0, tiled=True).astype(
            shard_small.dtype
        ),
    )
    rank = lax.axis_index(("dp", "fsdp"))
    row_index = lax.axis_index("dp")
    column_index = lax.axis_index("fsdp")
    numbers = jnp.arange(BLOCKS, dtype=jnp.int32)
    matches = owners == rank
    mine = jnp.sum(jnp.where(matches, numbers, 0))
    owning = jnp.any(matches)

    def update_slot(gradient):
        left_stat = decay_rate * statistics[0, 0] + (1.0 - decay_rate) * jnp.dot(
            gradient, gradient.T, precision=highest, preferred_element_type=jnp.float32
        )
        right_stat = decay_rate * statistics[0, 1] + (1.0 - decay_rate) * jnp.dot(
            gradient.T, gradient, precision=highest, preferred_element_type=jnp.float32
        )
        left_step = jnp.dot(
            inverse_roots[0, 0], gradient, precision=highest, preferred_element_type=jnp.float32
        )
        update = jnp.dot(
            left_step, inverse_roots[0, 1], precision=highest, preferred_element_type=jnp.float32
        )
        return (jnp.stack([left_stat, right_stat])[None], update)

    def keep_slot(gradient):
        return (statistics, jnp.zeros((D, D), jnp.float32))

    whole_qkv, whole_out, whole_up, whole_down, whole_small = (
        lax.all_gather(band_qkv.astype(jnp.bfloat16), "dp", axis=0, tiled=True).astype(
            band_qkv.dtype
        ),
        lax.all_gather(band_out.astype(jnp.bfloat16), "dp", axis=0, tiled=True).astype(
            band_out.dtype
        ),
        lax.all_gather(band_up.astype(jnp.bfloat16), "dp", axis=0, tiled=True).astype(
            band_up.dtype
        ),
        lax.all_gather(band_down.astype(jnp.bfloat16), "dp", axis=0, tiled=True).astype(
            band_down.dtype
        ),
        lax.all_gather(band_small.astype(jnp.bfloat16), "dp", axis=0, tiled=True).astype(
            band_small.dtype
        ),
    )
    gradient = lax.switch(mine, block_pickers(), (whole_qkv, whole_out, whole_up, whole_down))
    new_statistics, update = lax.cond(owning, update_slot, keep_slot, gradient)
    arrivals = []
    for number in range(BLOCKS):
        arrivals.append(fetch_update(update, owners[number]))
    tile_qkv = band_tile(row_band(arrivals[0:3], qkv_weight, row_index), qkv_weight, column_index)
    tile_out = band_tile(row_band(arrivals[3:4], out_weight, row_index), out_weight, column_index)
    tile_up = band_tile(
        row_band(arrivals[4 : 4 + FF // D], up_weight, row_index), up_weight, column_index
    )
    tile_down = band_tile(
        stacked_band(arrivals[4 + FF // D :], down_weight, row_index), down_weight, column_index
    )
    new_qkv = qkv_weight - step_rate * tile_qkv
    new_out = out_weight - step_rate * tile_out
    new_up = up_weight - step_rate * tile_up
    new_down = down_weight - step_rate * tile_down
    new_small = small_params - small_rate * whole_small * lax.rsqrt(
        jnp.mean(whole_small * whole_small) + 1e-06
    )
    return (
        layer_rows,
        input_grad,
        shard_qkv,
        shard_out,
        shard_up,
        shard_down,
        whole_small,
        new_statistics,
        new_qkv,
        new_out,
        new_up,
        new_down,
        new_small,
    )


def local_staged(
    sizes,
    tokens,
    counts,
    cotangent,
    qkv_weight,
    out_weight,
    up_weight,
    down_weight,
    small_params,
    statistics,
    inverse_roots,
    owners,
):
    n_dp, n_fsdp = sizes
    small_rows = small_params.reshape(-1, D)
    down_turned = down_weight.T
    orders = ("j", "j", "j", "i")
    qkv_pieces, *begun = gather_first(n_dp, n_fsdp, (qkv_weight, out_weight, up_weight), orders[:3], FIRST_PLAN, 1)
    normed, projected, qkv_full, attended, log_totals, out_pieces, up_pieces, down_pieces = project_attend(
        n_dp, n_fsdp, counts, tokens, qkv_pieces.reshape(n_fsdp, D, 3 * D // n_fsdp), small_rows,
        begun, (down_turned,), orders[1:], FORWARD_PLAN, 2,
    )
    layer_rows, normed_two, active, hidden_grad, middle_grad, branch_grad, attended_grad, sums = middle_layer(
        tokens,
        attended,
        cotangent,
        out_pieces.reshape(n_fsdp, D, D // n_fsdp),
        up_pieces.reshape(n_fsdp, D, FF // n_fsdp),
        down_pieces.reshape(n_dp, D, FF // n_dp),
        small_rows,
    )
    projected_grad, mine_down, mine_up, mine_out, grad_bias_up, grad_bias_out = grads_attend_back(
        n_dp, n_fsdp, counts, projected, attended, attended_grad, log_totals,
        cotangent, active, normed_two, hidden_grad, branch_grad, BACKWARD_PLAN, 3,
    )
    mine_qkv, mine_small, input_grad = project_back(
        n_dp, n_fsdp, tokens, normed, projected_grad, qkv_full, middle_grad, small_rows,
        sums, grad_bias_out, grad_bias_up, TAIL_PLAN, 4
    )
    exchanged = owner_exchange(
        n_dp, n_fsdp, owners, (mine_qkv.reshape(-1, 384), mine_out, mine_up, mine_down), mine_small, inverse_roots[0], 5
    )
    masters = (qkv_weight, out_weight, up_weight, down_turned)
    *results, whole_small, new_small, new_statistics = finish_step(
        n_dp, n_fsdp, owners, exchanged, masters, small_params.reshape(-1, 128), statistics[0], (step_rate, small_rate)
    )
    shard_qkv, shard_out, shard_up, shard_down, new_qkv, new_out, new_up, new_down = results
    whole_small, new_small = whole_small.reshape(-1), new_small.reshape(-1)
    return (
        layer_rows,
        input_grad,
        shard_qkv,
        shard_out,
        shard_up,
        shard_down.T,
        whole_small,
        new_statistics[None],
        new_qkv,
        new_out,
        new_up,
        new_down.T,
        new_small,
    )


def solution(mesh):
    placed = (
        P(("dp", "fsdp"), None),
        P(("dp", "fsdp")),
        P(("dp", "fsdp"), None),
        P("dp", "fsdp"),
        P("dp", "fsdp"),
        P("dp", "fsdp"),
        P("dp", "fsdp"),
        P(),
        P(("dp", "fsdp"), None, None, None),
        P(("dp", "fsdp"), None, None, None),
        P(),
    )
    sizes = (mesh.shape["dp"], mesh.shape["fsdp"])
    local = partial(local_staged, sizes) if sizes == (8, 4) else local_any
    return jax.shard_map(
        local,
        mesh=mesh,
        in_specs=placed,
        out_specs=(
            P(("dp", "fsdp"), None),
            P(("dp", "fsdp"), None),
            P("dp", "fsdp"),
            P("dp", "fsdp"),
            P("dp", "fsdp"),
            P("dp", "fsdp"),
            P(),
            P(("dp", "fsdp"), None, None, None),
            P("dp", "fsdp"),
            P("dp", "fsdp"),
            P("dp", "fsdp"),
            P("dp", "fsdp"),
            P(),
        ),
        check_vma=False,
    )
```
